32 devices in a mesh: dp: 8 (over y, x, core), mp: 4 (over z).
Axes of the slice: x: 2, y: 2, z: 4, core: 2. Of those that a mesh axis runs over, the one named last changes fastest.
Arguments:
- layer_in: bfloat16 [8, 1024, 1472], P('dp', 'mp'), may hold values from -6 to 6
- segment_ids: int32 [8, 1024], P('dp'), may hold values from 0 to 7, never falling along the last dimension, each value on 1 to 512 neighbouring positions
- bucket_table: int32 [2047], replicated, may hold values from 0 to 31
- attn_gain: float32 [1472], replicated, may hold values from 0.25 to 1.75
- query_weight: float32 [1472, 512], P(None, 'mp'), may hold values from -0.01953125 to 0.01953125
- key_weight: float32 [1472, 512], P(None, 'mp'), may hold values from -0.15625 to 0.15625
- value_weight: float32 [1472, 512], P(None, 'mp'), may hold values from -0.15625 to 0.15625
- out_weight: float32 [512, 1472], P('mp'), may hold values from -1 to 1
- rel_bias: float32 [32, 8], P(None, 'mp'), may hold values from -4 to 4
- ff_gain: float32 [1472], replicated, may hold values from 0.25 to 1.75
- gate_weight: float32 [1472, 3584], P(None, 'mp'), may hold values from -0.15625 to 0.15625
- up_weight: float32 [1472, 3584], P(None, 'mp'), may hold values from -0.15625 to 0.15625
- down_weight: float32 [3584, 1472], P('mp'), may hold values from -0.09375 to 0.09375
- cotangent: bfloat16 [8, 1024, 1472], P('dp', 'mp'), may hold values from -6 to 6
Outputs:
- layer_out: bfloat16 [8, 1024, 1472], P('dp', 'mp')
- input_grad: bfloat16 [8, 1024, 1472], P('dp', 'mp')
- new_attn_gain: float32 [1472], replicated
- attn_gain_moment: float32 [1472], replicated
- new_query_weight: float32 [1472, 512], P(None, 'mp')
- query_row_moment: float32 [1472], replicated
- query_col_moment: float32 [512], P('mp')
- new_key_weight: float32 [1472, 512], P(None, 'mp')
- key_row_moment: float32 [1472], replicated
- key_col_moment: float32 [512], P('mp')
- new_value_weight: float32 [1472, 512], P(None, 'mp')
- value_row_moment: float32 [1472], replicated
- value_col_moment: float32 [512], P('mp')
- new_out_weight: float32 [512, 1472], P('mp')
- out_row_moment: float32 [512], P('mp')
- out_col_moment: float32 [1472], replicated
- new_rel_bias: float32 [32, 8], P(None, 'mp')
- rel_row_moment: float32 [32], replicated
- rel_col_moment: float32 [8], P('mp')
- new_ff_gain: float32 [1472], replicated
- ff_gain_moment: float32 [1472], replicated
- new_gate_weight: float32 [1472, 3584], P(None, 'mp')
- gate_row_moment: float32 [1472], replicated
- gate_col_moment: float32 [3584], P('mp')
- new_up_weight: float32 [1472, 3584], P(None, 'mp')
- up_row_moment: float32 [1472], replicated
- up_col_moment: float32 [3584], P('mp')
- new_down_weight: float32 [3584, 1472], P('mp')
- down_row_moment: float32 [3584], P('mp')
- down_col_moment: float32 [1472], replicated
The draws below stay inside these ranges and needn't reach their ends.
Inputs may be any that keep to these rules, and one draw needn't show every extreme that they name: `segment_ids`: along each row the numbers never fall; a document holds 1 to 512 bytes.
All inputs are finite; a program needn't handle non-finite values.
Results may differ from the reference program's by a relative error of at most 0.029.
Values may be sent and summed in bfloat16 or wider, within the bound.
A program may use at most 256 MiB of HBM per device.

```python
import math
import jax
import jax.numpy as jnp
import numpy as np
from jax import lax

D = 1472
HD = 64
FF = 3584
BUCKETS = 32
SEQ = 1024
SLOTS = 8
ROWS = 8


def plant(result, own_key, low, high):
    dims = result.shape
    spot = [jax.random.randint(jax.random.fold_in(own_key, axis), (), 0, dims[axis]) for axis in range(len(dims))]
    result = result.at[tuple(spot)].set(low)
    longest = dims.index(max(dims))
    spot[longest] = (spot[longest] + 1) % dims[longest]
    return result.at[tuple(spot)].set(high)


def block_scale(key, dims, split, low, high):
    factor_of = 1.0
    for position, parts in split:
        steps = jax.random.uniform(jax.random.fold_in(jax.random.fold_in(key, 6), position), (parts,), jnp.float32, low / len(split), high / len(split))
        factor_of = factor_of * jnp.repeat(jnp.exp(steps), dims[position] // parts).reshape((-1,) + (1,) * (len(dims) - 1 - position))
    return factor_of


def length_profile(amount, total, bound, lean):
    portions = [(1 << 20) // math.isqrt(rank ** lean) + 1 for rank in range(2, amount + 1)]
    rest, given = total - bound - (amount - 1), [1] * (amount - 1)
    while rest > 0:
        free = [i for i in range(amount - 1) if given[i] < bound]
        pool, left = sum([portions[i] for i in free]), rest
        for i in free:
            extra = min(bound - given[i], max(1, left * portions[i] // pool), rest)
            given[i] = given[i] + extra
            rest = rest - extra
    return np.array([bound] + given)


def ragged_sizes(rng, number_of, total, most, slope):
    if number_of == 2:
        one = jax.random.randint(rng, (), max(1, total - most), min(most, total - 1) + 1)
        return jnp.stack([one, total - one])
    lengths = jnp.asarray(length_profile(number_of, total, most, slope), jnp.int32)
    twos = (number_of - 1) // 2
    source_of, sink = lengths[1:1 + 2 * twos:2], lengths[2:2 + 2 * twos:2]
    slack = jnp.minimum(source_of - 1, most - sink)
    passed = jax.random.randint(jax.random.fold_in(rng, 1), (twos,), 0, 1 << 20) % (slack + 1)
    lengths = lengths.at[1:1 + 2 * twos:2].set(source_of - passed).at[2:2 + 2 * twos:2].set(sink + passed)
    return lengths[jax.random.permutation(jax.random.fold_in(rng, 2), number_of)]


def scatter_about(own_key, dims, scale, limit, split=(), held_as=jnp.bfloat16):
    level = block_scale(own_key, dims, split, -0.22, 0.18) if split else 1.0
    values = jax.random.normal(own_key, dims, jnp.float32) * scale * level
    return jnp.minimum(jnp.maximum(values, -limit), limit).astype(held_as)


def setup_inputs(seed: int = 0) -> dict:
    key_list = jax.random.split(jax.random.key(seed), 15)
    return {
        "layer_in": scatter_about(key_list[0], (ROWS, SEQ, D), 1.0, 6.0, ((0, 8), (1, 4))),
        "segment_ids": jax.vmap(lambda own: jnp.searchsorted(jnp.cumsum(ragged_sizes(own, 8, SEQ, SEQ // 2, 2)), jnp.arange(SEQ), side="right"))(jax.random.split(key_list[1], ROWS)).reshape((ROWS, SEQ)).astype(jnp.int32),
        "bucket_table": plant(jax.random.randint(key_list[2], (2 * SEQ - 1,), 0, BUCKETS), jax.random.fold_in(key_list[2], 1), 0, BUCKETS - 1).astype(jnp.int32),
        "attn_gain": jnp.clip(1.0 + 0.15 * jax.random.normal(key_list[3], (D,), jnp.float32), 0.25, 1.75),
        "query_weight": scatter_about(key_list[4], (D, SLOTS * HD), (D * HD) ** -0.5, 0.01953125, ((1, 4),), jnp.float32),
        "key_weight": scatter_about(key_list[5], (D, SLOTS * HD), D ** -0.5, 0.15625, ((1, 4),), jnp.float32),
        "value_weight": scatter_about(key_list[6], (D, SLOTS * HD), D ** -0.5, 0.15625, ((1, 4),), jnp.float32),
        "out_weight": scatter_about(key_list[7], (SLOTS * HD, D), 32 ** -0.5, 1.0, ((0, 4),), jnp.float32),
        "rel_bias": scatter_about(key_list[8], (BUCKETS, SLOTS), 1.0, 4.0, ((1, 4),), jnp.float32),
        "ff_gain": jnp.clip(1.0 + 0.15 * jax.random.normal(key_list[9], (D,), jnp.float32), 0.25, 1.75),
        "gate_weight": scatter_about(key_list[10], (D, FF), D ** -0.5, 0.15625, ((1, 4),), jnp.float32),
        "up_weight": scatter_about(key_list[11], (D, FF), D ** -0.5, 0.15625, ((1, 4),), jnp.float32),
        "down_weight": scatter_about(key_list[12], (FF, D), FF ** -0.5, 0.09375, ((0, 4),), jnp.float32),
        "cotangent": scatter_about(key_list[13], (ROWS, SEQ, D), 1.0, 6.0, ((0, 8), (1, 4))),
    }


@jax.custom_vjp
def low(v):
    return lax.optimization_barrier(v.astype(jnp.bfloat16)).astype(jnp.float32)

@jax.custom_vjp
def low_back(v):
    return v

def low_keep(v):
    return (low(v), None)

def low_pass(kept, grad):
    return (grad,)

def back_keep(v):
    return (v, None)

def back_low(kept, grad):
    return (low(grad),)
low.defvjp(low_keep, low_pass)
low_back.defvjp(back_keep, back_low)
highest = lax.Precision.HIGHEST
step_scale = 0.3

def rms_norm(values, gain):
    return values * lax.rsqrt(lax.optimization_barrier(jnp.mean(values * values, axis=-1, keepdims=True)) + 1e-06) * gain

def product(left_side, right_side):
    return jnp.dot(left_side, right_side, precision=highest, preferred_element_type=jnp.float32)

def lane_mask():
    slot_ids = jnp.arange(SLOTS)
    slot_valid = ((slot_ids < 5) | (slot_ids == 6)).astype(jnp.float32)
    return jnp.repeat(slot_valid, HD)

def forward(block_in, block_segments, bucket_table, attn_gain, query_weight, key_weight, value_weight, out_weight, rel_bias, ff_gain, gate_weight, up_weight, down_weight):
    group_rows = block_in.shape[0]
    flat_in = block_in.reshape(group_rows * SEQ, D)
    lanes = lane_mask()
    normed = low(rms_norm(flat_in, attn_gain))
    queries = low(low_back(product(normed, low(query_weight) * lanes))).reshape(group_rows, SEQ, SLOTS, HD)
    key_rows = low(low_back(product(normed, low(key_weight) * lanes))).reshape(group_rows, SEQ, SLOTS, HD)
    value_rows = low(low_back(product(normed, low(value_weight) * lanes))).reshape(group_rows, SEQ, SLOTS, HD)
    offsets = jnp.arange(SEQ)[None, :] - jnp.arange(SEQ)[:, None] + SEQ - 1
    bias_table = jnp.transpose(rel_bias[bucket_table[offsets]], (2, 0, 1))

    def attend_row(row_item):
        row_query, row_keys, row_values, row_segments = row_item
        scores = jnp.einsum('ihd,jhd->hij', row_query, row_keys, precision=highest) + bias_table
        scores = low_back(scores)
        same_doc = row_segments[:, None] == row_segments[None, :]
        scores = jnp.where(same_doc[None], scores, -1e+30)
        soft_probs = jax.nn.softmax(scores, axis=-1)
        mixed_row = jnp.einsum('hij,jhd->ihd', low(soft_probs), row_values, precision=highest)
        return low(low_back(mixed_row.reshape(SEQ, SLOTS * HD)))
    attended = lax.map(jax.checkpoint(attend_row), (queries, key_rows, value_rows, block_segments))
    attended = attended.reshape(group_rows * SEQ, SLOTS * HD)
    attn_branch = low_back(product(attended, low(out_weight) * lanes[:, None]))
    middle = flat_in + attn_branch
    normed_ff = low(rms_norm(middle, ff_gain))
    gate_act = low_back(product(normed_ff, low(gate_weight)))
    up_act = low_back(product(normed_ff, low(up_weight)))
    hidden = low(jax.nn.gelu(gate_act, approximate=True) * up_act)
    ff_branch = low_back(product(hidden, low(down_weight)))
    return (middle + ff_branch).reshape(group_rows, SEQ, D)

def factored(weight, gradient):
    squares = gradient * gradient + 1e-30
    row_moment = lax.optimization_barrier(jnp.mean(squares, axis=1))
    col_moment = lax.optimization_barrier(jnp.mean(squares, axis=0))
    update = gradient * lax.rsqrt(row_moment / jnp.mean(row_moment))[:, None] * lax.rsqrt(col_moment)[None, :]
    step_rate = step_scale * jnp.sqrt(jnp.mean(weight * weight))
    return (weight - step_rate * update, row_moment, col_moment)

def vector_step(weight, gradient):
    squares = gradient * gradient + 1e-30
    step_rate = step_scale * jnp.sqrt(jnp.mean(weight * weight))
    return (weight - step_rate * gradient * lax.rsqrt(jnp.mean(squares)), squares)

def reference(layer_in, segment_ids, bucket_table, attn_gain, query_weight, key_weight, value_weight, out_weight, rel_bias, ff_gain, gate_weight, up_weight, down_weight, cotangent):
    params = (attn_gain, query_weight, key_weight, value_weight, out_weight, rel_bias, ff_gain, gate_weight, up_weight, down_weight)
    group_rows = 4
    block_count = layer_in.shape[0] // group_rows
    inputs = layer_in.astype(jnp.float32).reshape(block_count, group_rows, SEQ, D)
    cot_blocks = cotangent.astype(jnp.float32).reshape(block_count, group_rows, SEQ, D)
    segments = segment_ids.reshape(block_count, group_rows, SEQ)

    def scan_block(running, block_item):
        block_in, block_cot, block_segments = block_item

        def apply_layer(inner_in, *weights):
            return forward(inner_in, block_segments, bucket_table, *weights)
        block_out, pullback = jax.vjp(apply_layer, block_in, *params)
        increments = pullback(block_cot)
        running = tuple((accum_term + new_term for accum_term, new_term in zip(running, increments[1:])))
        return (running, (block_out, increments[0]))
    zero_grads = tuple((jnp.zeros_like(weight) for weight in params))
    gradients, (block_outs, block_grads) = lax.scan(scan_block, zero_grads, (inputs, cot_blocks, segments))
    layer_out = block_outs.reshape(layer_in.shape).astype(jnp.bfloat16)
    input_grad = block_grads.reshape(layer_in.shape).astype(jnp.bfloat16)
    new_attn_gain, attn_gain_moment = vector_step(attn_gain, gradients[0])
    new_query, query_row, query_col = factored(query_weight, gradients[1])
    new_key, key_row, key_col = factored(key_weight, gradients[2])
    new_value, value_row, value_col = factored(value_weight, gradients[3])
    new_out, out_row, out_col = factored(out_weight, gradients[4])
    new_rel, rel_row, rel_col = factored(rel_bias, gradients[5])
    new_ff_gain, ff_gain_moment = vector_step(ff_gain, gradients[6])
    new_gate, gate_row, gate_col = factored(gate_weight, gradients[7])
    new_up, up_row, up_col = factored(up_weight, gradients[8])
    new_down, down_row, down_col = factored(down_weight, gradients[9])
    return (layer_out, input_grad, new_attn_gain, attn_gain_moment, new_query, query_row, query_col, new_key, key_row, key_col, new_value, value_row, value_col, new_out, out_row, out_col, new_rel, rel_row, rel_col, new_ff_gain, ff_gain_moment, new_gate, gate_row, gate_col, new_up, up_row, up_col, new_down, down_row, down_col)
```

```python
import functools

import jax
import jax.numpy as jnp
from jax import lax
from jax.experimental import pallas as pl
from jax.experimental.pallas import tpu as pltpu
from jax.sharding import PartitionSpec as P

HD = 64
BUCKETS = 32
BLOCK = 128


highest = lax.Precision.HIGHEST
step_scale = 0.3


def rms_norm(values, gain):
    return values * lax.rsqrt(jnp.mean(values * values, axis=-1, keepdims=True) + 1e-06) * gain


def gated_gelu(gate_act, up_act):
    return jax.nn.gelu(gate_act, approximate=True) * up_act


def product(left_side, right_side):
    return jnp.dot(left_side, right_side, preferred_element_type=jnp.float32)


def left_inner(left_side, right_side):
    return lax.dot_general(
        left_side, right_side, (((0,), (0,)), ((), ())), preferred_element_type=jnp.float32
    )


def right_inner(left_side, right_side):
    return lax.dot_general(
        left_side, right_side, (((1,), (1,)), ((), ())), preferred_element_type=jnp.float32
    )


def slot_lanes(values, slot):
    lane = lax.broadcasted_iota(jnp.int32, values.shape, 1)
    return jnp.where((lane >= slot * HD) & (lane < (slot + 1) * HD), values, jnp.zeros_like(values))


def attend_kernel(seq_len, slots, qkv_ref, seg_col_ref, seg_row_ref, vec_ref, out_ref, probs_ref, tilt_ref):
    step = pl.program_id(0)
    steps = seq_len // BLOCK
    lanes = slots * HD

    @pl.when(step == 0)
    def _():
        for slot in range(slots):
            spread = jnp.broadcast_to(vec_ref[slot : slot + 1, :], (BLOCK, 2 * seq_len))
            tilt_ref[slot] = pltpu.roll(
                spread, 2 * seq_len - BLOCK + 1, 1, stride=1, stride_axis=0
            )

    same_doc = seg_col_ref[...] == seg_row_ref[...]
    rows = pl.ds(pl.multiple_of(step * BLOCK, BLOCK), BLOCK)
    window = pl.ds(pl.multiple_of((steps - 1 - step) * BLOCK, BLOCK), seq_len)
    queries = qkv_ref[rows, 0:lanes]
    keys = qkv_ref[:, lanes : 2 * lanes]
    values = qkv_ref[:, 2 * lanes : 3 * lanes]
    mixed = jnp.zeros((BLOCK, lanes), jnp.float32)
    for slot in range(slots):
        scores = right_inner(slot_lanes(queries, slot), keys) + tilt_ref[slot, :, window]
        scores = jnp.where(same_doc, scores, -1e30)
        peak = jnp.max(scores, axis=-1, keepdims=True)
        raised = jnp.exp(scores - peak)
        probs = raised * (1.0 / jnp.sum(raised, axis=-1, keepdims=True))
        probs_ref[slot] = probs
        mixed = mixed + slot_lanes(product(probs.astype(jnp.bfloat16), values), slot)
    out_ref[...] = mixed.astype(jnp.bfloat16)


def attend(qkv, seg_col, seg_row, vector):
    seq_len = qkv.shape[0]
    slots = vector.shape[0]
    lanes = slots * HD
    return pl.pallas_call(
        functools.partial(attend_kernel, seq_len, slots),
        grid=(seq_len // BLOCK,),
        in_specs=[
            pl.BlockSpec((seq_len, 3 * lanes), lambda i: (0, 0)),
            pl.BlockSpec((BLOCK, 1), lambda i: (i, 0)),
            pl.BlockSpec((1, seq_len), lambda i: (0, 0)),
            pl.BlockSpec((slots, 2 * seq_len), lambda i: (0, 0)),
        ],
        out_specs=[
            pl.BlockSpec((BLOCK, lanes), lambda i: (i, 0)),
            pl.BlockSpec((slots, BLOCK, seq_len), lambda i: (0, i, 0)),
        ],
        out_shape=[
            jax.ShapeDtypeStruct((seq_len, lanes), jnp.bfloat16),
            jax.ShapeDtypeStruct((slots, seq_len, seq_len), jnp.float32),
        ],
        scratch_shapes=[pltpu.VMEM((slots, BLOCK, 2 * seq_len), jnp.float32)],
        compiler_params=pltpu.CompilerParams(vmem_limit_bytes=32 << 20),
        cost_estimate=pl.CostEstimate(
            flops=8 * slots * seq_len * seq_len * HD,
            bytes_accessed=4 * slots * seq_len * seq_len,
            transcendentals=slots * seq_len * seq_len,
        ),
        name="attend",
    )(qkv, seg_col, seg_row, vector)


def attend_back_kernel(
    seq_len, slots, qkv_ref, grad_ref, probs_ref, dqkv_ref, dvec_ref, diag_ref, dk_ref, dv_ref
):
    step = pl.program_id(0)
    steps = seq_len // BLOCK
    lanes = slots * HD

    @pl.when(step == 0)
    def _():
        diag_ref[...] = jnp.zeros_like(diag_ref)
        dk_ref[...] = jnp.zeros_like(dk_ref)
        dv_ref[...] = jnp.zeros_like(dv_ref)

    rows = pl.ds(pl.multiple_of(step * BLOCK, BLOCK), BLOCK)
    window = pl.ds(pl.multiple_of((steps - 1 - step) * BLOCK, BLOCK), seq_len)
    queries = qkv_ref[rows, 0:lanes]
    keys = qkv_ref[:, lanes : 2 * lanes]
    values = qkv_ref[:, 2 * lanes : 3 * lanes]
    grad = grad_ref[...]
    d_query = jnp.zeros((BLOCK, lanes), jnp.float32)
    for slot in range(slots):
        probs = probs_ref[slot]
        slot_grad = slot_lanes(grad, slot)
        d_probs = right_inner(slot_grad, values)
        delta = jnp.sum(probs * d_probs, axis=-1, keepdims=True)
        d_scores = (probs * (d_probs - delta)).astype(jnp.bfloat16)
        d_query = d_query + slot_lanes(product(d_scores, keys), slot)
        dk_ref[...] += left_inner(slot_lanes(queries, slot), d_scores)
        dv_ref[...] += left_inner(slot_grad, probs.astype(jnp.bfloat16))
        diag_ref[slot, :, window] += d_scores.astype(jnp.float32)
    dqkv_ref[rows, 0:lanes] = d_query.astype(jnp.bfloat16)

    @pl.when(step == steps - 1)
    def _():
        dqkv_ref[:, lanes : 2 * lanes] = dk_ref[...].T.astype(jnp.bfloat16)
        dqkv_ref[:, 2 * lanes : 3 * lanes] = dv_ref[...].T.astype(jnp.bfloat16)
        for slot in range(slots):
            level = diag_ref[slot]
            half = BLOCK // 2
            while half >= 1:
                level = pltpu.roll(level[:half], half, 1) + level[half:]
                half //= 2
            dvec_ref[slot : slot + 1, :] = level


def attend_back(qkv, grad, probs):
    seq_len = qkv.shape[0]
    slots = probs.shape[0]
    lanes = slots * HD
    return pl.pallas_call(
        functools.partial(attend_back_kernel, seq_len, slots),
        grid=(seq_len // BLOCK,),
        in_specs=[
            pl.BlockSpec((seq_len, 3 * lanes), lambda i: (0, 0)),
            pl.BlockSpec((BLOCK, lanes), lambda i: (i, 0)),
            pl.BlockSpec((slots, BLOCK, seq_len), lambda i: (0, i, 0)),
        ],
        out_specs=[
            pl.BlockSpec((seq_len, 3 * lanes), lambda i: (0, 0)),
            pl.BlockSpec((slots, 2 * seq_len), lambda i: (0, 0)),
        ],
        out_shape=[
            jax.ShapeDtypeStruct((seq_len, 3 * lanes), jnp.bfloat16),
            jax.ShapeDtypeStruct((slots, 2 * seq_len), jnp.float32),
        ],
        scratch_shapes=[
            pltpu.VMEM((slots, BLOCK, 2 * seq_len), jnp.float32),
            pltpu.VMEM((lanes, seq_len), jnp.float32),
            pltpu.VMEM((lanes, seq_len), jnp.float32),
        ],
        compiler_params=pltpu.CompilerParams(vmem_limit_bytes=32 << 20),
        cost_estimate=pl.CostEstimate(
            flops=16 * slots * seq_len * seq_len * HD,
            bytes_accessed=4 * slots * seq_len * seq_len,
            transcendentals=0,
        ),
        name="attend_back",
    )(qkv, grad, probs)


def to_owners(rows_of_slots):
    count = lax.axis_size("mp")
    seq_len, lanes = rows_of_slots.shape
    pieces = rows_of_slots.reshape(count, seq_len // count, lanes)
    pieces = lax.all_to_all(pieces, "mp", split_axis=0, concat_axis=0)
    return pieces.transpose(1, 0, 2).reshape(seq_len // count, count * lanes)


def to_slots(own_rows):
    count = lax.axis_size("mp")
    local_len, width = own_rows.shape
    pieces = own_rows.reshape(local_len, count, width // count).transpose(1, 0, 2)
    pieces = lax.all_to_all(pieces, "mp", split_axis=0, concat_axis=0)
    return pieces.reshape(count * local_len, width // count)


def local(
    layer_in,
    segment_ids,
    bucket_table,
    attn_gain,
    query_weight,
    key_weight,
    value_weight,
    out_weight,
    rel_bias,
    ff_gain,
    gate_weight,
    up_weight,
    down_weight,
    cotangent,
):
    _, local_len, model_width = layer_in.shape
    seq_len = segment_ids.shape[1]
    lane_width = query_weight.shape[1]
    slots_here = lane_width // HD
    ff_width = gate_weight.shape[1]
    tensor_index = lax.axis_index("mp")
    tensor_count = lax.axis_size("mp")
    data_index = lax.axis_index("dp")
    data_count = lax.axis_size("dp")
    layer_in = layer_in[0]
    cotangent = cotangent[0]
    slot_ids = tensor_index * slots_here + jnp.arange(slots_here)
    slot_valid = ((slot_ids < 5) | (slot_ids == 6)).astype(jnp.float32)
    lane_mask = jnp.repeat(slot_valid, HD)
    qkv_low = (
        jnp.concatenate([query_weight, key_weight, value_weight], axis=1) * jnp.tile(lane_mask, 3)
    ).astype(jnp.bfloat16)
    proj_low = (out_weight * lane_mask[:, None]).astype(jnp.bfloat16)
    gate_up_low = jnp.concatenate([gate_weight, up_weight], axis=1).astype(jnp.bfloat16)
    down_low = down_weight.astype(jnp.bfloat16)
    onehot = (bucket_table[:, None] == jnp.arange(BUCKETS)[None, :]).astype(jnp.float32)
    onehot = jnp.pad(onehot, ((0, 1), (0, 0)))
    vector = lax.dot_general(
        rel_bias,
        onehot,
        (((0,), (1,)), ((), ())),
        precision=highest,
        preferred_element_type=jnp.float32,
    )
    residual_in = layer_in.astype(jnp.float32)
    normed_local = rms_norm(residual_in, attn_gain).astype(jnp.bfloat16)
    flat_norm = lax.all_gather(normed_local, "mp", axis=0, tiled=True)
    proj_all = gather_proj(proj_low)
    qkv = product(flat_norm, qkv_low).astype(jnp.bfloat16)
    attended, probs = attend(qkv, segment_ids.reshape(seq_len, 1), segment_ids, vector)
    own_attended = to_owners(attended)
    middle = residual_in + product(own_attended, proj_all)
    normed_ff_local = rms_norm(middle, ff_gain).astype(jnp.bfloat16)
    flat_ff = lax.all_gather(normed_ff_local, "mp", axis=0, tiled=True)
    flat_cot = lax.all_gather(cotangent, "mp", axis=0, tiled=True)
    gate_up = product(flat_ff, gate_up_low)
    gate_act = gate_up[:, :ff_width]
    up_act = gate_up[:, ff_width:]
    hidden = gated_gelu(gate_act, up_act).astype(jnp.bfloat16)
    ff_terms = product(hidden, down_low)
    ff_branch = lax.psum_scatter(
        ff_terms.astype(jnp.bfloat16), "mp", scatter_dimension=0, tiled=True
    ).astype(jnp.float32)
    layer_out = (middle + ff_branch).astype(jnp.bfloat16)
    d_hidden = right_inner(flat_cot, down_low)
    gate_pull = jax.vjp(gated_gelu, gate_act, up_act)[1]
    d_gate, d_up = gate_pull(d_hidden)
    d_gate_up = jnp.concatenate([d_gate, d_up], axis=1).astype(jnp.bfloat16)
    d_down_w = left_inner(hidden, flat_cot)
    d_gate_up_w = left_inner(flat_ff, d_gate_up)
    dn_ff_terms = right_inner(d_gate_up, gate_up_low)
    dn_ff = lax.psum_scatter(
        dn_ff_terms.astype(jnp.bfloat16), "mp", scatter_dimension=0, tiled=True
    ).astype(jnp.float32)
    d_gate_w = lax.psum(d_gate_up_w[:, :ff_width].astype(jnp.bfloat16), "dp").astype(jnp.float32)
    d_up_w = lax.psum(d_gate_up_w[:, ff_width:].astype(jnp.bfloat16), "dp").astype(jnp.float32)
    d_down_w = lax.psum(d_down_w.astype(jnp.bfloat16), "dp").astype(jnp.float32)
    ff_norm_pull = jax.vjp(rms_norm, middle, ff_gain)[1]
    d_middle_norm, d_ff_gain = ff_norm_pull(dn_ff)
    d_middle = cotangent.astype(jnp.float32) + d_middle_norm
    d_attn_local = d_middle.astype(jnp.bfloat16)
    d_attended = to_slots(right_inner(d_attn_local, proj_all).astype(jnp.bfloat16))
    d_out_w = left_inner(own_attended, d_attn_local).astype(jnp.bfloat16)
    d_out_w = lax.psum_scatter(d_out_w, "mp", scatter_dimension=0, tiled=True)
    flat_d_qkv, d_vector = attend_back(qkv, d_attended, probs)
    dn_attn_terms = right_inner(flat_d_qkv, qkv_low)
    dn_attn = lax.psum_scatter(
        dn_attn_terms.astype(jnp.bfloat16), "mp", scatter_dimension=0, tiled=True
    ).astype(jnp.float32)
    attn_norm_pull = jax.vjp(rms_norm, residual_in, attn_gain)[1]
    d_input_norm, d_attn_gain = attn_norm_pull(dn_attn)
    input_grad = (d_middle + d_input_norm).astype(jnp.bfloat16)
    d_qkv_w = left_inner(flat_norm, flat_d_qkv).astype(jnp.bfloat16)
    d_rel = lax.dot_general(
        onehot,
        d_vector,
        (((0,), (1,)), ((), ())),
        precision=highest,
        preferred_element_type=jnp.float32,
    )
    d_qkv_w, d_out_w = lax.psum((d_qkv_w, d_out_w), "dp")
    d_qkv_w = d_qkv_w.astype(jnp.float32)
    d_out_w = d_out_w.astype(jnp.float32)
    small = jnp.concatenate([d_attn_gain, d_ff_gain, d_rel.reshape(-1)])
    small = lax.psum(small, "dp")
    d_rel = small[2 * model_width :].reshape(BUCKETS, slots_here)
    weights = (
        query_weight,
        key_weight,
        value_weight,
        rel_bias,
        gate_weight,
        up_weight,
        out_weight,
        down_weight,
    )
    grads = (
        d_qkv_w[:, :lane_width],
        d_qkv_w[:, lane_width : 2 * lane_width],
        d_qkv_w[:, 2 * lane_width :],
        d_rel,
        d_gate_w,
        d_up_w,
        d_out_w,
        d_down_w,
    )
    split_rows = (False, False, False, False, False, False, True, True)
    whole_sums = []
    shared_sums = []
    weight_squares = []
    for grad, weight, rows_are_split in zip(grads, weights, split_rows):
        squares = grad * grad + 1e-30
        shared_axis = 0 if rows_are_split else 1
        shared_sums.append(jnp.sum(squares, axis=shared_axis))
        whole_sums.append(jnp.sum(squares, axis=1 - shared_axis))
        weight_squares.append(jnp.sum(weight * weight))
    parts = shared_sums + [small[: 2 * model_width], jnp.stack(weight_squares)]
    sums = lax.psum(jnp.concatenate(parts), "mp")
    split = []
    offset = 0
    for part in parts:
        split.append(sums[offset : offset + part.shape[0]])
        offset = offset + part.shape[0]
    gain_sums = split[len(weights)]
    weight_totals = split[len(weights) + 1]
    new_weights = []
    row_moments = []
    col_moments = []
    for position in range(len(weights)):
        grad = grads[position]
        weight = weights[position]
        rows_here, cols_here = grad.shape
        shared = split[position]
        if split_rows[position]:
            rows_here = rows_here * tensor_count
            row_moment = whole_sums[position] / cols_here
            col_moment = shared / rows_here
        else:
            cols_here = cols_here * tensor_count
            row_moment = shared / cols_here
            col_moment = whole_sums[position] / rows_here
        level = jnp.sum(shared) / (rows_here * cols_here)
        step_rate = step_scale * jnp.sqrt(weight_totals[position] / (rows_here * cols_here))
        row_factor = lax.rsqrt(row_moment / level) * step_rate
        col_factor = lax.rsqrt(col_moment)
        new_weights.append(weight - grad * row_factor[:, None] * col_factor[None, :])
        row_moments.append(row_moment)
        col_moments.append(col_moment)

    def gain_step(gain, grad):
        moment = grad * grad + 1e-30
        rate = step_scale * jnp.sqrt(jnp.mean(gain * gain))
        return gain - rate * grad * lax.rsqrt(jnp.mean(moment)), moment

    new_attn_gain, attn_gain_moment = gain_step(attn_gain, gain_sums[:model_width])
    new_ff_gain, ff_gain_moment = gain_step(ff_gain, gain_sums[model_width:])

    def matrix(position):
        return (new_weights[position], row_moments[position], col_moments[position])

    return (
        layer_out[None],
        input_grad[None],
        new_attn_gain,
        attn_gain_moment,
        *matrix(0),
        *matrix(1),
        *matrix(2),
        *matrix(6),
        *matrix(3),
        new_ff_gain,
        ff_gain_moment,
        *matrix(4),
        *matrix(5),
        *matrix(7),
    )


def gather_proj(proj_low):
    data_count = lax.axis_size("dp")
    rows = proj_low.shape[0] // data_count
    part = lax.dynamic_slice_in_dim(proj_low, lax.axis_index("dp") * rows, rows, 0)
    return lax.all_gather(part, ("mp", "dp"), axis=0, tiled=True)


def solution(mesh):
    return jax.shard_map(
        local,
        mesh=mesh,
        in_specs=(
            P("dp", "mp", None),
            P("dp", None),
            P(),
            P(),
            P(None, "mp"),
            P(None, "mp"),
            P(None, "mp"),
            P("mp", None),
            P(None, "mp"),
            P(),
            P(None, "mp"),
            P(None, "mp"),
            P("mp", None),
            P("dp", "mp", None),
        ),
        out_specs=(
            P("dp", "mp", None),
            P("dp", "mp", None),
            P(),
            P(),
            P(None, "mp"),
            P(),
            P("mp"),
            P(None, "mp"),
            P(),
            P("mp"),
            P(None, "mp"),
            P(),
            P("mp"),
            P("mp", None),
            P("mp"),
            P(),
            P(None, "mp"),
            P(),
            P("mp"),
            P(),
            P(),
            P(None, "mp"),
            P(),
            P("mp"),
            P(None, "mp"),
            P(),
            P("mp"),
            P("mp", None),
            P("mp"),
            P(),
        ),
        check_vma=False,
    )
```

```python
import functools

import jax
import jax.numpy as jnp
from jax import lax
from jax.experimental import pallas as pl
from jax.experimental.pallas import tpu as pltpu
from jax.sharding import PartitionSpec as P

HD = 64
BUCKETS = 32
BLOCK = 128


highest = lax.Precision.HIGHEST
step_scale = 0.3


def rms_norm(values, gain):
    return values * lax.rsqrt(jnp.mean(values * values, axis=-1, keepdims=True) + 1e-06) * gain


def gated_gelu(gate_act, up_act):
    return jax.nn.gelu(gate_act, approximate=True) * up_act


def product(left_side, right_side):
    return jnp.dot(left_side, right_side, preferred_element_type=jnp.float32)


def left_inner(left_side, right_side):
    return lax.dot_general(
        left_side, right_side, (((0,), (0,)), ((), ())), preferred_element_type=jnp.float32
    )


def right_inner(left_side, right_side):
    return lax.dot_general(
        left_side, right_side, (((1,), (1,)), ((), ())), preferred_element_type=jnp.float32
    )


def slot_lanes(values, slot):
    lane = lax.broadcasted_iota(jnp.int32, values.shape, 1)
    return jnp.where((lane >= slot * HD) & (lane < (slot + 1) * HD), values, jnp.zeros_like(values))


def attend_kernel(seq_len, slots, qkv_ref, seg_col_ref, seg_row_ref, vec_ref, out_ref, probs_ref, tilt_ref):
    step = pl.program_id(0)
    steps = seq_len // BLOCK
    lanes = slots * HD

    @pl.when(step == 0)
    def _():
        for slot in range(slots):
            spread = jnp.broadcast_to(vec_ref[slot : slot + 1, :], (BLOCK, 2 * seq_len))
            tilt_ref[slot] = pltpu.roll(
                spread, 2 * seq_len - BLOCK + 1, 1, stride=1, stride_axis=0
            )

    same_doc = seg_col_ref[...] == seg_row_ref[...]
    rows = pl.ds(pl.multiple_of(step * BLOCK, BLOCK), BLOCK)
    window = pl.ds(pl.multiple_of((steps - 1 - step) * BLOCK, BLOCK), seq_len)
    queries = qkv_ref[rows, 0:lanes]
    keys = qkv_ref[:, lanes : 2 * lanes]
    values = qkv_ref[:, 2 * lanes : 3 * lanes]
    mixed = jnp.zeros((BLOCK, lanes), jnp.float32)
    for slot in range(slots):
        scores = right_inner(slot_lanes(queries, slot), keys) + tilt_ref[slot, :, window]
        scores = jnp.where(same_doc, scores, -1e30)
        peak = jnp.max(scores, axis=-1, keepdims=True)
        raised = jnp.exp(scores - peak)
        probs = raised * (1.0 / jnp.sum(raised, axis=-1, keepdims=True))
        probs_ref[slot] = probs
        mixed = mixed + slot_lanes(product(probs.astype(jnp.bfloat16), values), slot)
    out_ref[...] = mixed.astype(jnp.bfloat16)


def attend(qkv, seg_col, seg_row, vector):
    seq_len = qkv.shape[0]
    slots = vector.shape[0]
    lanes = slots * HD
    return pl.pallas_call(
        functools.partial(attend_kernel, seq_len, slots),
        grid=(seq_len // BLOCK,),
        in_specs=[
            pl.BlockSpec((seq_len, 3 * lanes), lambda i: (0, 0)),
            pl.BlockSpec((BLOCK, 1), lambda i: (i, 0)),
            pl.BlockSpec((1, seq_len), lambda i: (0, 0)),
            pl.BlockSpec((slots, 2 * seq_len), lambda i: (0, 0)),
        ],
        out_specs=[
            pl.BlockSpec((BLOCK, lanes), lambda i: (i, 0)),
            pl.BlockSpec((slots, BLOCK, seq_len), lambda i: (0, i, 0)),
        ],
        out_shape=[
            jax.ShapeDtypeStruct((seq_len, lanes), jnp.bfloat16),
            jax.ShapeDtypeStruct((slots, seq_len, seq_len), jnp.float32),
        ],
        scratch_shapes=[pltpu.VMEM((slots, BLOCK, 2 * seq_len), jnp.float32)],
        compiler_params=pltpu.CompilerParams(vmem_limit_bytes=32 << 20),
        cost_estimate=pl.CostEstimate(
            flops=8 * slots * seq_len * seq_len * HD,
            bytes_accessed=4 * slots * seq_len * seq_len,
            transcendentals=slots * seq_len * seq_len,
        ),
        name="attend",
    )(qkv, seg_col, seg_row, vector)


def attend_back_kernel(
    seq_len, slots, qkv_ref, grad_ref, probs_ref, dqkv_ref, dvec_ref, diag_ref, dk_ref, dv_ref
):
    step = pl.program_id(0)
    steps = seq_len // BLOCK
    lanes = slots * HD

    @pl.when(step == 0)
    def _():
        diag_ref[...] = jnp.zeros_like(diag_ref)
        dk_ref[...] = jnp.zeros_like(dk_ref)
        dv_ref[...] = jnp.zeros_like(dv_ref)

    rows = pl.ds(pl.multiple_of(step * BLOCK, BLOCK), BLOCK)
    window = pl.ds(pl.multiple_of((steps - 1 - step) * BLOCK, BLOCK), seq_len)
    queries = qkv_ref[rows, 0:lanes]
    keys = qkv_ref[:, lanes : 2 * lanes]
    values = qkv_ref[:, 2 * lanes : 3 * lanes]
    grad = grad_ref[...]
    d_query = jnp.zeros((BLOCK, lanes), jnp.float32)
    for slot in range(slots):
        probs = probs_ref[slot]
        slot_grad = slot_lanes(grad, slot)
        d_probs = right_inner(slot_grad, values)
        delta = jnp.sum(probs * d_probs, axis=-1, keepdims=True)
        d_scores = (probs * (d_probs - delta)).astype(jnp.bfloat16)
        d_query = d_query + slot_lanes(product(d_scores, keys), slot)
        dk_ref[...] += left_inner(slot_lanes(queries, slot), d_scores)
        dv_ref[...] += left_inner(slot_grad, probs.astype(jnp.bfloat16))
        diag_ref[slot, :, window] += d_scores.astype(jnp.float32)
    dqkv_ref[rows, 0:lanes] = d_query.astype(jnp.bfloat16)

    @pl.when(step == steps - 1)
    def _():
        dqkv_ref[:, lanes : 2 * lanes] = dk_ref[...].T.astype(jnp.bfloat16)
        dqkv_ref[:, 2 * lanes : 3 * lanes] = dv_ref[...].T.astype(jnp.bfloat16)
        for slot in range(slots):
            level = diag_ref[slot]
            half = BLOCK // 2
            while half >= 1:
                level = pltpu.roll(level[:half], half, 1) + level[half:]
                half //= 2
            dvec_ref[slot : slot + 1, :] = level


def attend_back(qkv, grad, probs):
    seq_len = qkv.shape[0]
    slots = probs.shape[0]
    lanes = slots * HD
    return pl.pallas_call(
        functools.partial(attend_back_kernel, seq_len, slots),
        grid=(seq_len // BLOCK,),
        in_specs=[
            pl.BlockSpec((seq_len, 3 * lanes), lambda i: (0, 0)),
            pl.BlockSpec((BLOCK, lanes), lambda i: (i, 0)),
            pl.BlockSpec((slots, BLOCK, seq_len), lambda i: (0, i, 0)),
        ],
        out_specs=[
            pl.BlockSpec((seq_len, 3 * lanes), lambda i: (0, 0)),
            pl.BlockSpec((slots, 2 * seq_len), lambda i: (0, 0)),
        ],
        out_shape=[
            jax.ShapeDtypeStruct((seq_len, 3 * lanes), jnp.bfloat16),
            jax.ShapeDtypeStruct((slots, 2 * seq_len), jnp.float32),
        ],
        scratch_shapes=[
            pltpu.VMEM((slots, BLOCK, 2 * seq_len), jnp.float32),
            pltpu.VMEM((lanes, seq_len), jnp.float32),
            pltpu.VMEM((lanes, seq_len), jnp.float32),
        ],
        compiler_params=pltpu.CompilerParams(vmem_limit_bytes=32 << 20),
        cost_estimate=pl.CostEstimate(
            flops=16 * slots * seq_len * seq_len * HD,
            bytes_accessed=4 * slots * seq_len * seq_len,
            transcendentals=0,
        ),
        name="attend_back",
    )(qkv, grad, probs)


class Butterfly:
    def __init__(self, order, base):
        self.order = order
        self.me = lax.axis_index("dp")
        self.line = lax.axis_index("mp")
        self.base = base
        self.offsets = []
        total = 0
        for s in range(len(order)):
            self.offsets.append(total)
            total += 1 << (len(order) - 1 - s)
        self.count = total

    def bit(self, b):
        return (self.me // b) % 2

    def partner(self, s):
        b = self.order[s]
        return (self.me + b * (1 - 2 * self.bit(b)), self.line)

    def pieces(self, s):
        b = self.order[s]
        fixed = sum(k * self.bit(k) for k in self.order[:s])
        free = self.order[s + 1 :]
        found = []
        for j in range(1 << len(free)):
            rest = sum(k for i, k in enumerate(free) if (j >> i) & 1)
            found.append((fixed + b * self.bit(b) + rest, fixed + b * (1 - self.bit(b)) + rest, j))
        return found

    def copy(self, src, dst, sems, slot, s):
        return pltpu.make_async_remote_copy(
            src_ref=src,
            dst_ref=dst,
            send_sem=sems[0].at[self.base + slot],
            recv_sem=sems[1].at[self.base + slot],
            device_id=self.partner(s),
            device_id_type=pl.DeviceIdType.MESH,
        )

    def halve(self, s, source, landing, sems):
        at = self.offsets[s]
        return [
            self.copy(source.at[theirs], landing.at[at + j], sems, at + j, s)
            for _, theirs, j in self.pieces(s)
        ]

    def add(self, s, kept, landing, copies):
        at = self.offsets[s]
        for (mine, _, j), copy in zip(self.pieces(s), copies):
            copy.wait_recv()
            kept[mine] = (
                kept[mine].astype(jnp.float32) + landing[at + j].astype(jnp.float32)
            ).astype(jnp.bfloat16)

    def double(self, s, whole, sems, first=None):
        at = self.offsets[s]
        return [
            self.copy(whole.at[mine] if first is None else first, whole.at[mine], sems, at + j, s)
            for mine, _, j in self.pieces(s)
        ]


def orders(data_count):
    bits = [1 << i for i in range(data_count.bit_length() - 1)]
    return (bits, bits[:1] + bits[:0:-1])


def greet(peers):
    barrier = pltpu.get_barrier_semaphore()
    for peer in peers:
        pl.semaphore_signal(barrier, inc=1, device_id=peer, device_id_type=pl.DeviceIdType.MESH)
    pl.semaphore_wait(barrier, len(peers))


def sum_weights_kernel(data_count, count, layout, *refs):
    n = len(layout)
    sources, wholes = refs[:n], refs[n : 2 * n]
    kept, landings = refs[2 * n : 3 * n], refs[3 * n : 4 * n]
    cross, final, load_sem, keep_sem, down_send, down_recv, up_send, up_recv, cross_send, cross_recv = refs[
        4 * n :
    ]
    me = lax.axis_index("dp")
    place = lax.axis_index("mp")
    ways = orders(data_count)
    span = data_count - 1
    flies = [Butterfly(ways[way], i * span) for i, (way, _) in enumerate(layout)]
    stages = len(ways[0])
    down = (down_send, down_recv)
    up = (up_send, up_recv)
    loads = []
    for i, fly in enumerate(flies):
        for mine, _, j in fly.pieces(0):
            load = pltpu.make_async_copy(
                sources[i].at[mine], kept[i].at[mine], load_sem.at[i * data_count + j]
            )
            load.start()
            loads.append(load)
    others = [(place + k) % count for k in range(1, count)]
    greet([flies[0].partner(s) for s in range(stages)] + [(me, other) for other in others])

    sent = []

    def start(copies):
        for copy in copies:
            copy.start()
        sent.extend(copies)
        return copies

    flights = [start(fly.halve(0, sources[i], landings[i], down)) for i, fly in enumerate(flies)]
    for load in loads:
        load.wait()
    for s in range(stages):
        for i, fly in enumerate(flies):
            fly.add(s, kept[i], landings[i], flights[i])
            if s + 1 < stages:
                flights[i] = start(fly.halve(s + 1, kept[i], landings[i], down))
                continue
            if layout[i][1]:
                crossing = []
                for k, other in enumerate(others):
                    crossing.append(
                        pltpu.make_async_remote_copy(
                            src_ref=kept[i].at[me, other],
                            dst_ref=cross.at[count - 2 - k],
                            send_sem=cross_send.at[k],
                            recv_sem=cross_recv.at[count - 2 - k],
                            device_id=(me, other),
                            device_id_type=pl.DeviceIdType.MESH,
                        )
                    )
                start(crossing)
                total = kept[i][me, place].astype(jnp.float32)
                for k in range(count - 1):
                    pltpu.make_async_remote_copy(
                        src_ref=cross.at[k],
                        dst_ref=cross.at[k],
                        send_sem=cross_send.at[k],
                        recv_sem=cross_recv.at[k],
                        device_id=(me, others[0]),
                        device_id_type=pl.DeviceIdType.MESH,
                    ).wait_recv()
                    total = total + cross[k].astype(jnp.float32)
                final[...] = total.astype(jnp.bfloat16)
                mine = final
            else:
                mine = kept[i].at[me]
            keep = pltpu.make_async_copy(mine, wholes[i].at[me], keep_sem.at[i])
            keep.start()
            flights[i] = (keep, start(fly.double(s, wholes[i], up, mine)))
    keeps = [keep for keep, _ in flights]
    flights = [copies for _, copies in flights]
    for keep in keeps:
        keep.wait()
    for s in reversed(range(stages)):
        for i, fly in enumerate(flies):
            for copy in flights[i]:
                copy.wait_recv()
            if s > 0:
                flights[i] = start(fly.double(s - 1, wholes[i], up))
    for copy in sent:
        copy.wait_send()


def sum_weights(arrays, layout):
    count = lax.axis_size("mp")
    data_count = arrays[0].shape[0]
    anywhere = pl.BlockSpec(memory_space=pl.ANY)
    dma = pltpu.SemaphoreType.DMA
    low = jnp.bfloat16
    shapes = [a.shape[1:] for a in arrays]
    kept_shapes = [(s[1:] if crosses else s) for s, (_, crosses) in zip(shapes, layout)]
    crossing = [s for s, (_, crosses) in zip(kept_shapes, layout) if crosses][0]
    span = data_count - 1
    n = len(arrays)
    moved = 4 * sum(a.size for a in arrays)
    return pl.pallas_call(
        functools.partial(sum_weights_kernel, data_count, count, layout),
        out_shape=[jax.ShapeDtypeStruct((data_count, *s), low) for s in kept_shapes],
        in_specs=[anywhere] * n,
        out_specs=[anywhere] * n,
        scratch_shapes=[pltpu.VMEM((data_count, *s), low) for s in shapes]
        + [pltpu.VMEM((span, *s), low) for s in shapes]
        + [
            pltpu.VMEM((count - 1, *crossing), low),
            pltpu.VMEM(crossing, low),
            dma((n * data_count,)),
            dma((n,)),
            dma((n * span,)),
            dma((n * span,)),
            dma((n * span,)),
            dma((n * span,)),
            dma((count - 1,)),
            dma((count - 1,)),
        ],
        compiler_params=pltpu.CompilerParams(
            collective_id=2, has_side_effects=True, vmem_limit_bytes=48 << 20
        ),
        cost_estimate=pl.CostEstimate(flops=moved, bytes_accessed=moved, transcendentals=0),
        name="sum_weights",
    )(*arrays)


def gather_proj_kernel(data_count, count, own_ref, all_ref, load_sem, cross_send, cross_recv, side_send, side_recv):
    me = lax.axis_index("dp")
    place = lax.axis_index("mp")
    others = [(place + k) % count for k in range(1, count)]
    peers = [(me + k) % data_count for k in range(1, data_count)]
    load = pltpu.make_async_copy(own_ref, all_ref.at[place], load_sem)
    load.start()
    greet([(me, other) for other in others] + [(peer, place) for peer in peers])
    sent = []
    for k, other in enumerate(others):
        copy = pltpu.make_async_remote_copy(
            src_ref=own_ref.at[me],
            dst_ref=all_ref.at[place, me],
            send_sem=cross_send.at[k],
            recv_sem=cross_recv.at[count - 2 - k],
            device_id=(me, other),
            device_id_type=pl.DeviceIdType.MESH,
        )
        copy.start()
        sent.append(copy)
    arrivals = []
    for k, other in enumerate(others):
        pltpu.make_async_remote_copy(
            src_ref=own_ref.at[me],
            dst_ref=all_ref.at[other, me],
            send_sem=cross_send.at[k],
            recv_sem=cross_recv.at[k],
            device_id=(me, other),
            device_id_type=pl.DeviceIdType.MESH,
        ).wait_recv()
        for j, peer in enumerate(peers):
            slot = k * (data_count - 1)
            copy = pltpu.make_async_remote_copy(
                src_ref=all_ref.at[other, me],
                dst_ref=all_ref.at[other, me],
                send_sem=side_send.at[slot + j],
                recv_sem=side_recv.at[slot + data_count - 2 - j],
                device_id=(peer, place),
                device_id_type=pl.DeviceIdType.MESH,
            )
            copy.start()
            sent.append(copy)
            arrivals.append(
                pltpu.make_async_remote_copy(
                    src_ref=all_ref.at[other, peer],
                    dst_ref=all_ref.at[other, peer],
                    send_sem=side_send.at[slot + j],
                    recv_sem=side_recv.at[slot + j],
                    device_id=(peer, place),
                    device_id_type=pl.DeviceIdType.MESH,
                )
            )
    for arrival in arrivals:
        arrival.wait_recv()
    for copy in sent:
        copy.wait_send()
    load.wait()


def gather_proj(proj_low):
    count = lax.axis_size("mp")
    data_count = lax.axis_size("dp")
    lanes, width = proj_low.shape
    part = lanes // data_count
    anywhere = pl.BlockSpec(memory_space=pl.ANY)
    dma = pltpu.SemaphoreType.DMA
    gathered = pl.pallas_call(
        functools.partial(gather_proj_kernel, data_count, count),
        out_shape=jax.ShapeDtypeStruct((count, data_count, part, width), proj_low.dtype),
        in_specs=[anywhere],
        out_specs=anywhere,
        scratch_shapes=[
            dma,
            dma((count - 1,)),
            dma((count - 1,)),
            dma(((count - 1) * (data_count - 1),)),
            dma(((count - 1) * (data_count - 1),)),
        ],
        compiler_params=pltpu.CompilerParams(collective_id=0, has_side_effects=True),
        cost_estimate=pl.CostEstimate(flops=0, bytes_accessed=50 << 20, transcendentals=0),
        name="gather_proj",
    )(proj_low.reshape(data_count, part, width))
    return gathered.reshape(count * lanes, width)


def turn_order(count):
    return [sorted(range(count), key=lambda b: (abs(b - place), b < place)) for place in range(count)]


def look_up(table, row, column):
    found = jnp.int32(0)
    for r, entries in enumerate(table):
        for c, entry in enumerate(entries):
            found = jnp.where((row == r) & (column == c), jnp.int32(entry), found)
    return found


def feed_forward_kernel(
    count,
    parts,
    normed_hbm,
    cot_hbm,
    gate_up_hbm,
    down_hbm,
    out_hbm,
    dn_ref,
    d_gate_hbm,
    d_up_hbm,
    d_down_hbm,
    normed,
    cot,
    gate_up,
    down,
    hidden,
    d_gate_up,
    outgoing,
    incoming,
    stage,
    d_wide,
    d_tall,
    load_sem,
    stage_sem,
    gather_send,
    gather_recv,
    sum_send,
    sum_recv,
):
    place = lax.axis_index("mp")
    row = lax.axis_index("dp")
    block_len, width = dn_ref.shape
    units = down.shape[0]
    part_len = block_len // parts
    last = count - 1
    has_left = place > 0
    has_right = place < last

    loads = [
        pltpu.make_async_copy(normed_hbm, normed.at[place], load_sem.at[0]),
        pltpu.make_async_copy(gate_up_hbm, gate_up, load_sem.at[1]),
        pltpu.make_async_copy(down_hbm, down, load_sem.at[2]),
        pltpu.make_async_copy(cot_hbm, cot, load_sem.at[3]),
    ]
    for load in loads:
        load.start()

    barrier = pltpu.get_barrier_semaphore()
    for side, there in ((-1, has_left), (1, has_right)):

        @pl.when(there)
        def _():
            pl.semaphore_signal(
                barrier, inc=1, device_id=(row, place + side), device_id_type=pl.DeviceIdType.MESH
            )

    pl.semaphore_wait(barrier, has_left.astype(jnp.int32) + has_right.astype(jnp.int32))

    def pass_block(block, side, slot):
        return pltpu.make_async_remote_copy(
            src_ref=normed.at[block],
            dst_ref=normed.at[block],
            send_sem=gather_send.at[slot],
            recv_sem=gather_recv.at[block],
            device_id=(row, place + side),
            device_id_type=pl.DeviceIdType.MESH,
        )

    def rows_of(part):
        return pl.ds(pl.multiple_of(part * part_len, part_len), part_len)

    def pass_sum(block, part, side, slot):
        return pltpu.make_async_remote_copy(
            src_ref=outgoing.at[block, rows_of(part)],
            dst_ref=incoming.at[slot, rows_of(part)],
            send_sem=sum_send.at[block, part],
            recv_sem=sum_recv.at[slot, part],
            device_id=(row, place + side),
            device_id_type=pl.DeviceIdType.MESH,
        )

    def landing(block, side):
        return jnp.where((side == -1) & (place + side == block), count, block)

    loads[0].wait()
    for side, there in ((-1, has_left), (1, has_right)):

        @pl.when(there)
        def _():
            pass_block(place, side, count + (side + 1) // 2).start()

    for load in loads[1:]:
        load.wait()

    def store_out(turn, block):
        return pltpu.make_async_copy(stage.at[turn % 2], out_hbm.at[block], stage_sem.at[turn % 2])

    table = turn_order(count)
    root = 0.7978845608028654

    def turn_body(turn, carry):
        block = look_up(table, place, turn)
        distance = jnp.abs(block - place)

        @pl.when((distance > 0) & ((block > place) | (place + distance > last)))
        def _():
            for side in (1, -1):
                other = place + side * distance

                @pl.when((other >= 0) & (other <= last))
                def _():
                    pass_block(other, 0, other).wait_recv()

                    @pl.when((place - side >= 0) & (place - side <= last))
                    def _():
                        pass_block(other, -side, other).start()

        acts = product(normed[block], gate_up[...])
        gate_act = acts[:, :units]
        up_act = acts[:, units:]
        squared = gate_act * gate_act
        bend = jnp.tanh(root * gate_act * (1.0 + 0.044715 * squared))
        half = 0.5 * (1.0 + bend)
        gelu = gate_act * half
        hidden[block] = (gelu * up_act).astype(jnp.bfloat16)
        d_hidden = right_inner(cot[block], down[...])
        slope = half + 0.5 * gate_act * (1.0 - bend * bend) * (root * (1.0 + 0.134145 * squared))
        d_gate_up[block, :, :units] = (d_hidden * up_act * slope).astype(jnp.bfloat16)
        d_gate_up[block, :, units:] = (d_hidden * gelu).astype(jnp.bfloat16)
        term = right_inner(d_gate_up[block], gate_up[...])

        @pl.when(block == place)
        def _():
            dn_ref[...] = term

        @pl.when(block != place)
        def _():
            outgoing[block] = term.astype(jnp.bfloat16)

        for side, is_end in ((1, place == 0), (-1, place == last)):

            @pl.when(is_end & (block != place))
            def _():
                for part in range(parts):
                    pass_sum(block, part, side, landing(block, side)).start()

        @pl.when(turn >= 2)
        def _():
            store_out(turn, block).wait()

        stage[turn % 2] = product(hidden[block], down[...]).astype(jnp.bfloat16)
        store_out(turn, block).start()
        return carry

    lax.fori_loop(0, count, turn_body, 0)

    def relay(key):
        def relay_part(part, carry):
            for side, block in ((1, key), (-1, last - key)):
                through = (block > place) & has_left if side == 1 else (block < place) & has_right

                @pl.when(through)
                def _():
                    pass_sum(block, part, side, block).wait_recv()
                    rows = rows_of(part)
                    outgoing[block, rows] = (
                        outgoing[block, rows].astype(jnp.float32)
                        + incoming[block, rows].astype(jnp.float32)
                    ).astype(jnp.bfloat16)
                    pass_sum(block, part, side, landing(block, side)).start()

            return carry

        lax.fori_loop(0, parts, relay_part, 0)

    def flat(ref):
        return ref[...].reshape(count * block_len, ref.shape[2])

    d_wide[:, width:] = jnp.zeros((2, d_wide.shape[1] - width, units), jnp.bfloat16)
    d_tall[...] = left_inner(flat(hidden), flat(cot)).astype(jnp.bfloat16)
    save_down = pltpu.make_async_copy(d_tall, d_down_hbm, load_sem.at[2])
    save_down.start()
    for key in range(1, last):
        relay(key)
    d_wide[0, :width] = left_inner(
        flat(normed), d_gate_up[:, :, :units].reshape(count * block_len, units)
    ).astype(jnp.bfloat16)
    save_gate = pltpu.make_async_copy(d_wide.at[0], d_gate_hbm, load_sem.at[0])
    save_gate.start()
    relay(last)
    d_wide[1, :width] = left_inner(
        flat(normed), d_gate_up[:, :, units:].reshape(count * block_len, units)
    ).astype(jnp.bfloat16)
    save_up = pltpu.make_async_copy(d_wide.at[1], d_up_hbm, load_sem.at[1])
    save_up.start()

    for side, there in ((1, has_left), (-1, has_right)):

        @pl.when(there)
        def _():
            slot = place if side == 1 else count

            def add_part(part, carry):
                pass_sum(place, part, side, slot).wait_recv()
                rows = rows_of(part)
                dn_ref[rows] += incoming[slot, rows].astype(jnp.float32)
                return carry

            lax.fori_loop(0, parts, add_part, 0)

    for side, there in ((-1, has_left), (1, has_right)):

        @pl.when(there)
        def _():
            pass_block(place, side, count + (side + 1) // 2).wait_send()

    for block in range(count):

        @pl.when((block != place) & has_left & has_right)
        def _():
            pass_block(block, 1, block).wait_send()

        @pl.when(block != place)
        def _():
            for part in range(parts):
                pass_sum(block, part, 1, block).wait_send()

    for turn in (count - 2, count - 1):
        store_out(turn, 0).wait()
    for save in (save_down, save_gate, save_up):
        save.wait()


def feed_forward(normed, cot_all, gate_up, down, padded):
    count = lax.axis_size("mp")
    block_len, width = normed.shape
    units = down.shape[0]
    parts = 4
    low = jnp.bfloat16
    anywhere = pl.BlockSpec(memory_space=pl.ANY)
    dma = pltpu.SemaphoreType.DMA
    tokens = count * block_len
    out_terms, dn, d_gate, d_up, d_down = pl.pallas_call(
        functools.partial(feed_forward_kernel, count, parts),
        out_shape=[
            jax.ShapeDtypeStruct((count, block_len, width), low),
            jax.ShapeDtypeStruct((block_len, width), jnp.float32),
            jax.ShapeDtypeStruct((padded, units), low),
            jax.ShapeDtypeStruct((padded, units), low),
            jax.ShapeDtypeStruct((units, width), low),
        ],
        in_specs=[anywhere] * 4,
        out_specs=[anywhere, pl.BlockSpec(memory_space=pltpu.VMEM), anywhere, anywhere, anywhere],
        scratch_shapes=[
            pltpu.VMEM((count, block_len, width), low),
            pltpu.VMEM((count, block_len, width), low),
            pltpu.VMEM((width, 2 * units), low),
            pltpu.VMEM((units, width), low),
            pltpu.VMEM((count, block_len, units), low),
            pltpu.VMEM((count, block_len, 2 * units), low),
            pltpu.VMEM((count, block_len, width), low),
            pltpu.VMEM((count + 1, block_len, width), low),
            pltpu.VMEM((2, block_len, width), low),
            pltpu.VMEM((2, padded, units), low),
            pltpu.VMEM((units, width), low),
            dma((4,)),
            dma((2,)),
            dma((count + 2,)),
            dma((count,)),
            dma((count, parts)),
            dma((count + 1, parts)),
        ],
        compiler_params=pltpu.CompilerParams(
            collective_id=1, has_side_effects=True, vmem_limit_bytes=60 << 20
        ),
        cost_estimate=pl.CostEstimate(
            flops=18 * tokens * width * units,
            bytes_accessed=12 * width * units + 6 * tokens * width,
            transcendentals=tokens * units,
        ),
        name="feed_forward",
    )(normed, cot_all.reshape(count, block_len, width), gate_up, down)
    return out_terms.reshape(count * block_len, width), dn, d_gate, d_up, d_down


def to_owners(rows_of_slots):
    count = lax.axis_size("mp")
    seq_len, lanes = rows_of_slots.shape
    pieces = rows_of_slots.reshape(count, seq_len // count, lanes)
    pieces = lax.all_to_all(pieces, "mp", split_axis=0, concat_axis=0)
    return pieces.transpose(1, 0, 2).reshape(seq_len // count, count * lanes)


def to_slots(own_rows):
    count = lax.axis_size("mp")
    local_len, width = own_rows.shape
    pieces = own_rows.reshape(local_len, count, width // count).transpose(1, 0, 2)
    pieces = lax.all_to_all(pieces, "mp", split_axis=0, concat_axis=0)
    return pieces.reshape(count * local_len, width // count)


def local(
    layer_in,
    segment_ids,
    bucket_table,
    attn_gain,
    query_weight,
    key_weight,
    value_weight,
    out_weight,
    rel_bias,
    ff_gain,
    gate_weight,
    up_weight,
    down_weight,
    cotangent,
):
    _, local_len, model_width = layer_in.shape
    seq_len = segment_ids.shape[1]
    lane_width = query_weight.shape[1]
    slots_here = lane_width // HD
    ff_width = gate_weight.shape[1]
    tensor_index = lax.axis_index("mp")
    tensor_count = lax.axis_size("mp")
    data_index = lax.axis_index("dp")
    data_count = lax.axis_size("dp")
    layer_in = layer_in[0]
    cotangent = cotangent[0]
    slot_ids = tensor_index * slots_here + jnp.arange(slots_here)
    slot_valid = ((slot_ids < 5) | (slot_ids == 6)).astype(jnp.float32)
    lane_mask = jnp.repeat(slot_valid, HD)
    qkv_low = (
        jnp.concatenate([query_weight, key_weight, value_weight], axis=1) * jnp.tile(lane_mask, 3)
    ).astype(jnp.bfloat16)
    proj_low = (out_weight * lane_mask[:, None]).astype(jnp.bfloat16)
    gate_up_low = jnp.concatenate([gate_weight, up_weight], axis=1).astype(jnp.bfloat16)
    down_low = down_weight.astype(jnp.bfloat16)
    onehot = (bucket_table[:, None] == jnp.arange(BUCKETS)[None, :]).astype(jnp.float32)
    onehot = jnp.pad(onehot, ((0, 1), (0, 0)))
    vector = lax.dot_general(
        rel_bias,
        onehot,
        (((0,), (1,)), ((), ())),
        precision=highest,
        preferred_element_type=jnp.float32,
    )
    residual_in = layer_in.astype(jnp.float32)
    normed_local = rms_norm(residual_in, attn_gain).astype(jnp.bfloat16)
    flat_norm = lax.all_gather(normed_local, "mp", axis=0, tiled=True)
    proj_all = gather_proj(proj_low)
    flat_norm, late_cot, proj_all, qkv_low, gate_up_low, down_low, vector = lax.optimization_barrier(
        (flat_norm, cotangent, proj_all, qkv_low, gate_up_low, down_low, vector)
    )
    flat_cot = lax.all_gather(late_cot, "mp", axis=0, tiled=True)
    qkv = product(flat_norm, qkv_low).astype(jnp.bfloat16)
    attended, probs = attend(qkv, segment_ids.reshape(seq_len, 1), segment_ids, vector)
    own_attended = to_owners(attended)
    middle = residual_in + product(own_attended, proj_all)
    normed_ff_local = rms_norm(middle, ff_gain).astype(jnp.bfloat16)
    pad_to = 16 * data_count
    padded = (model_width + pad_to - 1) // pad_to * pad_to
    out_terms, dn_ff, d_gate_w, d_up_w, d_down_w = feed_forward(
        normed_ff_local, flat_cot, gate_up_low, down_low, padded
    )
    ff_norm_pull = jax.vjp(rms_norm, middle, ff_gain)[1]
    d_middle_norm, d_ff_gain = ff_norm_pull(dn_ff)
    d_middle = cotangent.astype(jnp.float32) + d_middle_norm
    d_attn_local = d_middle.astype(jnp.bfloat16)
    d_attended = to_slots(right_inner(d_attn_local, proj_all).astype(jnp.bfloat16))
    flat_d_qkv, d_vector = attend_back(qkv, d_attended, probs)
    dn_attn_terms = right_inner(flat_d_qkv, qkv_low).astype(jnp.bfloat16)
    out_terms, dn_attn_terms = lax.optimization_barrier((out_terms, dn_attn_terms))
    dn_attn = lax.psum_scatter(dn_attn_terms, "mp", scatter_dimension=0, tiled=True)
    ff_branch = lax.psum_scatter(out_terms, "mp", scatter_dimension=0, tiled=True)
    layer_out = (middle + ff_branch.astype(jnp.float32)).astype(jnp.bfloat16)
    d_qkv_w = left_inner(flat_norm, flat_d_qkv).astype(jnp.bfloat16)
    d_qkv_w = jnp.pad(d_qkv_w, ((0, padded - model_width), (0, 0)))
    d_out_w = left_inner(own_attended, d_attn_local).astype(jnp.bfloat16)
    d_out_w = d_out_w.reshape(tensor_count, data_count, -1, model_width).transpose(1, 0, 2, 3)
    wide = (data_count, padded // data_count)
    d_gate_w, d_up_w, d_down_w, d_qkv_w, d_out_w = sum_weights(
        (
            d_gate_w.reshape(*wide, ff_width),
            d_up_w.reshape(*wide, ff_width),
            d_down_w.reshape(data_count, ff_width // data_count, model_width),
            d_qkv_w.reshape(*wide, 3 * lane_width),
            d_out_w,
        ),
        ((0, False), (1, False), (0, False), (1, False), (1, True)),
    )

    def region(pieces):
        flat = pieces.reshape(-1, pieces.shape[2])
        return (flat[:model_width] if flat.shape[0] == padded else flat).astype(jnp.float32)

    d_gate_w, d_up_w, d_down_w, d_qkv_w, d_out_w = (
        region(pieces) for pieces in (d_gate_w, d_up_w, d_down_w, d_qkv_w, d_out_w)
    )
    attn_norm_pull = jax.vjp(rms_norm, residual_in, attn_gain)[1]
    d_input_norm, d_attn_gain = attn_norm_pull(dn_attn.astype(jnp.float32))
    input_grad = (d_middle + d_input_norm).astype(jnp.bfloat16)
    d_rel = lax.dot_general(
        onehot,
        d_vector,
        (((0,), (1,)), ((), ())),
        precision=highest,
        preferred_element_type=jnp.float32,
    )
    small = jnp.concatenate([d_attn_gain, d_ff_gain, d_rel.reshape(-1)])
    small = lax.psum(small, "dp")
    d_rel = small[2 * model_width :].reshape(BUCKETS, slots_here)
    weights = (
        query_weight,
        key_weight,
        value_weight,
        rel_bias,
        gate_weight,
        up_weight,
        out_weight,
        down_weight,
    )
    grads = (
        d_qkv_w[:, :lane_width],
        d_qkv_w[:, lane_width : 2 * lane_width],
        d_qkv_w[:, 2 * lane_width :],
        d_rel,
        d_gate_w,
        d_up_w,
        d_out_w,
        d_down_w,
    )
    split_rows = (False, False, False, False, False, False, True, True)
    whole_sums = []
    shared_sums = []
    weight_squares = []
    for grad, weight, rows_are_split in zip(grads, weights, split_rows):
        squares = grad * grad + 1e-30
        shared_axis = 0 if rows_are_split else 1
        shared_sums.append(jnp.sum(squares, axis=shared_axis))
        whole_sums.append(jnp.sum(squares, axis=1 - shared_axis))
        weight_squares.append(jnp.sum(weight * weight))
    parts = shared_sums + [small[: 2 * model_width], jnp.stack(weight_squares)]
    sums = lax.psum(jnp.concatenate(parts), "mp")
    split = []
    offset = 0
    for part in parts:
        split.append(sums[offset : offset + part.shape[0]])
        offset = offset + part.shape[0]
    gain_sums = split[len(weights)]
    weight_totals = split[len(weights) + 1]
    new_weights = []
    row_moments = []
    col_moments = []
    for position in range(len(weights)):
        grad = grads[position]
        weight = weights[position]
        rows_here, cols_here = grad.shape
        shared = split[position]
        if split_rows[position]:
            rows_here = rows_here * tensor_count
            row_moment = whole_sums[position] / cols_here
            col_moment = shared / rows_here
        else:
            cols_here = cols_here * tensor_count
            row_moment = shared / cols_here
            col_moment = whole_sums[position] / rows_here
        level = jnp.sum(shared) / (rows_here * cols_here)
        step_rate = step_scale * jnp.sqrt(weight_totals[position] / (rows_here * cols_here))
        row_factor = lax.rsqrt(row_moment / level) * step_rate
        col_factor = lax.rsqrt(col_moment)
        new_weights.append(weight - grad * row_factor[:, None] * col_factor[None, :])
        row_moments.append(row_moment)
        col_moments.append(col_moment)

    def gain_step(gain, grad):
        moment = grad * grad + 1e-30
        rate = step_scale * jnp.sqrt(jnp.mean(gain * gain))
        return gain - rate * grad * lax.rsqrt(jnp.mean(moment)), moment

    new_attn_gain, attn_gain_moment = gain_step(attn_gain, gain_sums[:model_width])
    new_ff_gain, ff_gain_moment = gain_step(ff_gain, gain_sums[model_width:])

    def matrix(position):
        return (new_weights[position], row_moments[position], col_moments[position])

    return (
        layer_out[None],
        input_grad[None],
        new_attn_gain,
        attn_gain_moment,
        *matrix(0),
        *matrix(1),
        *matrix(2),
        *matrix(6),
        *matrix(3),
        new_ff_gain,
        ff_gain_moment,
        *matrix(4),
        *matrix(5),
        *matrix(7),
    )


def solution(mesh):
    return jax.shard_map(
        local,
        mesh=mesh,
        in_specs=(
            P("dp", "mp", None),
            P("dp", None),
            P(),
            P(),
            P(None, "mp"),
            P(None, "mp"),
            P(None, "mp"),
            P("mp", None),
            P(None, "mp"),
            P(),
            P(None, "mp"),
            P(None, "mp"),
            P("mp", None),
            P("dp", "mp", None),
        ),
        out_specs=(
            P("dp", "mp", None),
            P("dp", "mp", None),
            P(),
            P(),
            P(None, "mp"),
            P(),
            P("mp"),
            P(None, "mp"),
            P(),
            P("mp"),
            P(None, "mp"),
            P(),
            P("mp"),
            P("mp", None),
            P("mp"),
            P(),
            P(None, "mp"),
            P(),
            P("mp"),
            P(),
            P(),
            P(None, "mp"),
            P(),
            P("mp"),
            P(None, "mp"),
            P(),
            P("mp"),
            P("mp", None),
            P("mp"),
            P(),
        ),
        check_vma=False,
    )
```

```python
import functools

import jax
import jax.numpy as jnp
from jax import lax
from jax.experimental import pallas as pl
from jax.experimental.pallas import tpu as pltpu
from jax.sharding import PartitionSpec as P

HD = 64
BUCKETS = 32
BLOCK = 128


highest = lax.Precision.HIGHEST
step_scale = 0.3


def rms_norm(values, gain):
    return values * lax.rsqrt(jnp.mean(values * values, axis=-1, keepdims=True) + 1e-06) * gain


def norm_back(values, gain, grad):
    scale = lax.rsqrt(jnp.mean(values * values, axis=-1, keepdims=True) + 1e-06)
    unit = values * scale
    pull = grad * gain
    return scale * (pull - unit * jnp.mean(pull * unit, axis=-1, keepdims=True))


def product(left_side, right_side):
    return jnp.dot(left_side, right_side, preferred_element_type=jnp.float32)


def left_inner(left_side, right_side):
    return lax.dot_general(
        left_side, right_side, (((0,), (0,)), ((), ())), preferred_element_type=jnp.float32
    )


def right_inner(left_side, right_side):
    return lax.dot_general(
        left_side, right_side, (((1,), (1,)), ((), ())), preferred_element_type=jnp.float32
    )


def slot_lanes(values, slot):
    lane = lax.broadcasted_iota(jnp.int32, values.shape, 1)
    return jnp.where((lane >= slot * HD) & (lane < (slot + 1) * HD), values, jnp.zeros_like(values))


def attend_kernel(seq_len, slots, qkv_ref, seg_col_ref, seg_row_ref, vec_ref, out_ref, probs_ref, tilt_ref):
    step = pl.program_id(0)
    steps = seq_len // BLOCK
    lanes = slots * HD

    @pl.when(step == 0)
    def _():
        for slot in range(slots):
            spread = jnp.broadcast_to(vec_ref[slot : slot + 1, :], (BLOCK, 2 * seq_len))
            tilt_ref[slot] = pltpu.roll(
                spread, 2 * seq_len - BLOCK + 1, 1, stride=1, stride_axis=0
            )

    same_doc = seg_col_ref[...] == seg_row_ref[...]
    rows = pl.ds(pl.multiple_of(step * BLOCK, BLOCK), BLOCK)
    window = pl.ds(pl.multiple_of((steps - 1 - step) * BLOCK, BLOCK), seq_len)
    queries = qkv_ref[rows, 0:lanes]
    keys = qkv_ref[:, lanes : 2 * lanes]
    values = qkv_ref[:, 2 * lanes : 3 * lanes]
    mixed = jnp.zeros((BLOCK, lanes), jnp.float32)
    for slot in range(slots):
        scores = right_inner(slot_lanes(queries, slot), keys) + tilt_ref[slot, :, window]
        scores = jnp.where(same_doc, scores, -1e30)
        peak = jnp.max(scores, axis=-1, keepdims=True)
        raised = jnp.exp(scores - peak)
        probs = raised * (1.0 / jnp.sum(raised, axis=-1, keepdims=True))
        probs_ref[slot] = probs
        mixed = mixed + slot_lanes(product(probs.astype(jnp.bfloat16), values), slot)
    out_ref[...] = mixed.astype(jnp.bfloat16)


def attend(qkv, seg_col, seg_row, vector):
    seq_len = qkv.shape[0]
    slots = vector.shape[0]
    lanes = slots * HD
    return pl.pallas_call(
        functools.partial(attend_kernel, seq_len, slots),
        grid=(seq_len // BLOCK,),
        in_specs=[
            pl.BlockSpec((seq_len, 3 * lanes), lambda i: (0, 0)),
            pl.BlockSpec((BLOCK, 1), lambda i: (i, 0)),
            pl.BlockSpec((1, seq_len), lambda i: (0, 0)),
            pl.BlockSpec((slots, 2 * seq_len), lambda i: (0, 0)),
        ],
        out_specs=[
            pl.BlockSpec((BLOCK, lanes), lambda i: (i, 0)),
            pl.BlockSpec((slots, BLOCK, seq_len), lambda i: (0, i, 0)),
        ],
        out_shape=[
            jax.ShapeDtypeStruct((seq_len, lanes), jnp.bfloat16),
            jax.ShapeDtypeStruct((slots, seq_len, seq_len), jnp.float32),
        ],
        scratch_shapes=[pltpu.VMEM((slots, BLOCK, 2 * seq_len), jnp.float32)],
        compiler_params=pltpu.CompilerParams(vmem_limit_bytes=58 << 20),
        cost_estimate=pl.CostEstimate(
            flops=8 * slots * seq_len * seq_len * HD,
            bytes_accessed=4 * slots * seq_len * seq_len,
            transcendentals=slots * seq_len * seq_len,
        ),
        name="attend",
    )(qkv, seg_col, seg_row, vector)


class Butterfly:
    def __init__(self, order, base):
        self.order = order
        self.me = lax.axis_index("dp")
        self.line = lax.axis_index("mp")
        self.base = base
        self.offsets = []
        total = 0
        for s in range(len(order)):
            self.offsets.append(total)
            total += 1 << (len(order) - 1 - s)

    def bit(self, b):
        return (self.me // b) % 2

    def partner(self, s):
        b = self.order[s]
        return (self.me + b * (1 - 2 * self.bit(b)), self.line)

    def width(self, s):
        return 1 << (len(self.order) - 1 - s)

    def piece(self, s, j, mine):
        b = self.order[s]
        found = sum(k * self.bit(k) for k in self.order[:s])
        found = found + b * (self.bit(b) if mine else 1 - self.bit(b))
        for i, k in enumerate(self.order[s + 1 :]):
            found = found + k * ((j // (1 << i)) % 2)
        return found

    def copy(self, src, dst, sems, slot, s):
        return pltpu.make_async_remote_copy(
            src_ref=src,
            dst_ref=dst,
            send_sem=sems[0].at[self.base + slot],
            recv_sem=sems[1].at[self.base + slot],
            device_id=self.partner(s),
            device_id_type=pl.DeviceIdType.MESH,
        )

    def halve(self, s, source, landing, sems):
        at = self.offsets[s]
        return [
            self.copy(source(self.piece(s, j, False)), landing.at[at + j], sems, at + j, s)
            for j in range(self.width(s))
        ]

    def add(self, s, kept, landing, copies):
        at = self.offsets[s]
        for j, copy in enumerate(copies):
            copy.wait_recv()
            mine = kept(self.piece(s, j, True))
            mine[...] = (mine[...].astype(jnp.float32) + landing[at + j].astype(jnp.float32)).astype(
                jnp.bfloat16
            )

    def double(self, s, whole, sems, first=None):
        at = self.offsets[s]
        copies = []
        for j in range(self.width(s)):
            view = whole(self.piece(s, j, True))
            copies.append(self.copy(view if first is None else first, view, sems, at + j, s))
        return copies


def orders(data_count):
    bits = [1 << i for i in range(data_count.bit_length() - 1)]
    return (bits, bits[:1] + bits[:0:-1])


def greet(peers):
    barrier = pltpu.get_barrier_semaphore()
    for peer in peers:
        pl.semaphore_signal(barrier, inc=1, device_id=peer, device_id_type=pl.DeviceIdType.MESH)
    pl.semaphore_wait(barrier, len(peers))


def row_pieces(ref, data_count, at=0, lanes=None):
    rows = ref.shape[0] // data_count
    columns = pl.ds(at, ref.shape[1] if lanes is None else lanes)
    return lambda q: ref.at[pl.ds(pl.multiple_of(q * rows, rows), rows), columns]


def total(values, axis):
    return jnp.sum(values, axis=axis, keepdims=True)


def sum_weights_kernel(data_count, count, model_width, parts, *refs):
    ff_hbm, qkv_hbm, out_hbm, qkv_low, gate_up_low, squares_ref = refs[:6]
    wholes, (shared_ref, own_ref, tall_ref) = refs[6:11], refs[11:14]
    kept, landings, full = refs[14:16], refs[16:18], refs[18:23]
    (
        cross,
        qkv_w,
        gate_up_w,
        tall,
        cols,
        gathered,
        load_sem,
        save_sem,
        down_send,
        down_recv,
        up_send,
        up_recv,
        cross_send,
        cross_recv,
        share_send,
        share_recv,
    ) = refs[23:]
    me = lax.axis_index("dp")
    place = lax.axis_index("mp")
    span = data_count - 1
    ways = orders(data_count)
    stages = len(ways[0])
    down, up = (down_send, down_recv), (up_send, up_recv)
    padded, units = full[0].shape
    lanes = full[4].shape[1]
    height = padded // data_count
    f32 = jnp.float32

    whole = [row_pieces(ref, data_count) for ref in full]
    saved = [row_pieces(wholes[i], data_count, at, wide) for i, at, wide, _ in parts]
    source = [row_pieces(ref, data_count) for ref in (qkv_hbm, out_hbm)]
    keep = [row_pieces(ref, data_count) for ref in kept]
    halvers = [Butterfly(ways[1 - i], i * span) for i in range(2)]
    doublers = [Butterfly(ways[way], k * span) for k, (_, _, _, way) in enumerate(parts)]
    views = [row_pieces(full[i], data_count, at, wide) for i, at, wide, _ in parts]

    loads = []

    def load(src, dst):
        copy = pltpu.make_async_copy(src, dst, load_sem.at[len(loads)])
        copy.start()
        loads.append(copy)

    first = doublers[0]
    for j in range(first.width(0)):
        q = first.piece(0, j, True)
        for i in range(3):
            load(row_pieces(ff_hbm.at[i], data_count)(q), whole[i](q))
    for i, fly in enumerate(halvers):
        for j in range(fly.width(0)):
            q = fly.piece(0, j, True)
            load(source[i](q), keep[i](q))
    load(qkv_low, qkv_w)
    load(gate_up_low, gate_up_w)
    others = [(place + k) % count for k in range(1, count)]
    greet([halvers[0].partner(s) for s in range(stages)] + [(me, other) for other in others])

    sent = []

    def start(copies):
        for copy in copies:
            copy.start()
        sent.extend(copies)
        return copies

    halves = [start(fly.halve(0, source[i], landings[i], down)) for i, fly in enumerate(halvers)]
    tall[...] = jnp.zeros_like(tall)
    cols[...] = jnp.zeros_like(cols)
    for copy in loads:
        copy.wait()

    doubles = {}

    def spread(s, arrays):
        for k, (i, _, _, _) in enumerate(parts):
            if i in arrays:
                doubles[k] = start(doublers[k].double(s, views[k], up))

    spread(0, (0, 1, 2))

    def note(k, q):
        i, start_lane, wide, _ = parts[k]
        rows = pl.ds(pl.multiple_of(q * height, height), height)
        grad = views[k](q)[...].astype(f32)
        if i == 3:
            at = lax.broadcasted_iota(jnp.int32, grad.shape, 0) + q * height
            grad = jnp.where(at < model_width, grad, 0.0)
        squares = grad * grad
        cols[i : i + 1, start_lane : start_lane + wide] += total(squares, 0)
        if i < 2:
            tall[rows, 3 + i : 4 + i] = total(squares, 1)
            weight = gate_up_w[rows, i * units : (i + 1) * units].astype(f32)
            tall[rows, 6:7] += total(grad * weight, 1)
        elif i == 3:
            for k in range(3):
                tall[rows, k : k + 1] = total(squares[:, k * lanes : (k + 1) * lanes], 1)
            tall[rows, 5:6] = total(grad * qkv_w[rows].astype(f32), 1)
        else:
            lane = 8 if i == 2 else 9
            tall[rows, lane : lane + 1] += total(squares, 1)

    saves = []

    def save(k, q, slot):
        copy = pltpu.make_async_copy(views[k](q), saved[k](q), save_sem.at[k * data_count + slot])
        copy.start()
        saves.append(copy)

    for s in range(stages):
        for i, fly in enumerate(halvers):
            fly.add(s, keep[i], landings[i], halves[i])
            if s + 1 < stages:
                halves[i] = start(fly.halve(s + 1, keep[i], landings[i], down))
    crossing = row_pieces(kept[1], data_count)(me)

    def lanes_of(other):
        return pl.ds(pl.multiple_of(other * lanes, lanes), lanes)

    start(
        [
            pltpu.make_async_remote_copy(
                src_ref=crossing.at[:, lanes_of(other)],
                dst_ref=cross.at[count - 2 - k],
                send_sem=cross_send.at[k],
                recv_sem=cross_recv.at[count - 2 - k],
                device_id=(me, other),
                device_id_type=pl.DeviceIdType.MESH,
            )
            for k, other in enumerate(others)
        ]
    )
    whole[3](me)[...] = keep[0](me)[...]
    spread(stages - 1, (3,))
    summed = crossing[:, lanes_of(place)].astype(f32)
    for k in range(count - 1):
        pltpu.make_async_remote_copy(
            src_ref=cross.at[k],
            dst_ref=cross.at[k],
            send_sem=cross_send.at[k],
            recv_sem=cross_recv.at[k],
            device_id=(me, others[0]),
            device_id_type=pl.DeviceIdType.MESH,
        ).wait_recv()
        summed = summed + cross[k].astype(f32)
    whole[4](me)[...] = summed.astype(jnp.bfloat16)
    spread(stages - 1, (4,))

    def note_pieces(k, s, mine):
        fly = doublers[k]
        for j in range(fly.width(s)):
            save(k, fly.piece(s, j, mine), j if mine else fly.width(s) + j)

        def note_piece(j, carry):
            note(k, fly.piece(s, j, mine))
            return carry

        lax.fori_loop(0, fly.width(s), note_piece, 0)

    early = [k for k, part in enumerate(parts) if part[0] < 3]
    late = [k for k, part in enumerate(parts) if part[0] >= 3]
    for k in early:
        note_pieces(k, 0, True)
    for k in late:
        note(k, me)
        save(k, me, 0)
    for k in early:
        for copy in doubles[k]:
            copy.wait_recv()
        note_pieces(k, 0, False)
    for s in reversed(range(stages)):
        for k in late:
            for copy in doubles[k]:
                copy.wait_recv()
            if s > 0:
                doubles[k] = start(doublers[k].double(s - 1, views[k], up))
        for k in late:
            note_pieces(k, s, False)

    slots_rel = full[3][model_width : model_width + BUCKETS, :128].astype(f32)
    tall[:BUCKETS, 7:8] = total(slots_rel * slots_rel, 1)
    share = gathered.at[place]
    share[...] = tall[...].T[0:16]
    share[10:11, :128] = squares_ref[...]
    shares = start(
        [
            pltpu.make_async_remote_copy(
                src_ref=share,
                dst_ref=share,
                send_sem=share_send.at[k],
                recv_sem=share_recv.at[place],
                device_id=(me, other),
                device_id_type=pl.DeviceIdType.MESH,
            )
            for k, other in enumerate(others)
        ]
    )
    own_ref[...] = jnp.zeros_like(own_ref)
    own_ref[:, : cols.shape[1]] = cols[...]
    for k, other in enumerate(others):
        pltpu.make_async_remote_copy(
            src_ref=gathered.at[other],
            dst_ref=gathered.at[other],
            send_sem=share_send.at[k],
            recv_sem=share_recv.at[other],
            device_id=(me, other),
            device_id_type=pl.DeviceIdType.MESH,
        ).wait_recv()
    summed = gathered[0]
    for k in range(1, count):
        summed = summed + gathered[k]
    shared_ref[...] = summed
    tall_ref[...] = jnp.concatenate([summed, jnp.zeros((112, padded), f32)], axis=0).T
    for copy in saves:
        copy.wait()
    for copy in sent:
        copy.wait_send()


def sum_weights(ff_grads, qkv, out, qkv_low, gate_up_low, squares, model_width):
    count = lax.axis_size("mp")
    data_count = lax.axis_size("dp")
    anywhere = pl.BlockSpec(memory_space=pl.ANY)
    near = pl.BlockSpec(memory_space=pltpu.VMEM)
    dma = pltpu.SemaphoreType.DMA
    low, f32 = jnp.bfloat16, jnp.float32
    span = data_count - 1
    units = ff_grads.shape[2]
    padded, wide = qkv.shape
    height = padded // data_count
    lanes = out.shape[1] // count
    full = [(padded, units)] * 3 + [(padded, wide), (padded, lanes)]
    parts = (*ff_parts(units), (3, 0, wide, 1), (4, 0, lanes, 0))
    n = len(parts)
    return pl.pallas_call(
        functools.partial(sum_weights_kernel, data_count, count, model_width, parts),
        out_shape=[jax.ShapeDtypeStruct(s, low) for s in full]
        + [
            jax.ShapeDtypeStruct((16, padded), f32),
            jax.ShapeDtypeStruct((8, padded), f32),
            jax.ShapeDtypeStruct((padded, 128), f32),
        ],
        in_specs=[anywhere] * 5 + [near],
        out_specs=[anywhere] * 5 + [near] * 3,
        scratch_shapes=[pltpu.VMEM(a.shape, low) for a in (qkv, out)]
        + [pltpu.VMEM((span, height, a.shape[1]), low) for a in (qkv, out)]
        + [pltpu.VMEM(s, low) for s in full]
        + [
            pltpu.VMEM((count - 1, height, lanes), low),
            pltpu.VMEM(qkv_low.shape, low),
            pltpu.VMEM(gate_up_low.shape, low),
            pltpu.VMEM((padded, 128), f32),
            pltpu.VMEM((8, (max(units, wide) + 127) // 128 * 128), f32),
            pltpu.VMEM((count, 16, padded), f32),
            dma((3 * data_count + 5,)),
            dma((n * data_count,)),
            dma((2 * span,)),
            dma((2 * span,)),
            dma((n * span,)),
            dma((n * span,)),
            dma((count - 1,)),
            dma((count - 1,)),
            dma((count - 1,)),
            dma((count,)),
        ],
        compiler_params=pltpu.CompilerParams(
            collective_id=2, has_side_effects=True, vmem_limit_bytes=56 << 20
        ),
        cost_estimate=pl.CostEstimate(
            flops=padded * units, bytes_accessed=200 << 20, transcendentals=0
        ),
        name="sum_weights",
    )(ff_grads, qkv, out, qkv_low, gate_up_low, squares)


def update_kernel(tensor_count, *refs):
    grads, rel_g = refs[:5], refs[5]
    weights, (rel_w, attn_w, ff_w) = refs[6:13], refs[13:16]
    shared_ref, own_ref, tall_ref = refs[16:19]
    news, rel_n = refs[19:26], refs[26]
    along, rel_r = refs[27:34], refs[34]
    across, rel_c = refs[35:42], refs[42]
    attn_n, attn_m, ff_n, ff_m = refs[43:47]
    first = pl.program_id(0) == 0
    f32 = jnp.float32
    width = attn_w.shape[1]
    lanes = weights[3].shape[1]
    slots = rel_w.shape[1]
    tiny = 1e-30

    def step_rate(lane, size):
        return step_scale * jnp.sqrt(shared_ref[10:11, lane : lane + 1] / size)

    qkv = grads[3][...].astype(f32)
    for k, (row, square, own, at) in enumerate(
        (
            (3, 4, 0, 0),
            (4, 5, 1, 0),
            (8, 7, 2, 0),
            (0, 0, 3, 0),
            (1, 1, 3, lanes),
            (2, 2, 3, 2 * lanes),
            (9, 6, 4, 0),
        )
    ):
        here = weights[k].shape[1]
        if own == 3:
            grad = qkv[:, at : at + lanes]
        else:
            grad = grads[own][...].astype(f32)
        cols = here * tensor_count
        size = width * cols
        level = total(shared_ref[row : row + 1, :width], 1) / size + tiny
        rate = step_rate(square, size)
        row_factor = lax.rsqrt((tall_ref[:, row : row + 1] / cols + tiny) / level) * rate
        col_moment = own_ref[own : own + 1, at : at + here] / width + tiny
        news[k][...] = weights[k][...] - grad * row_factor * lax.rsqrt(col_moment)

        @pl.when(first)
        def _():
            along[k][...] = (shared_ref[row : row + 1, :width] / cols + tiny).reshape(width)
            across[k][...] = col_moment.reshape(here)

    @pl.when(first)
    def _():
        rel = rel_g[:, :slots].astype(f32)
        cols = slots * tensor_count
        size = BUCKETS * cols
        row_sums = shared_ref[7:8, :BUCKETS]
        level = total(row_sums, 1) / size + tiny
        row_factor = lax.rsqrt((tall_ref[:BUCKETS, 7:8] / cols + tiny) / level) * step_rate(3, size)
        col_moment = total(rel * rel, 0) / BUCKETS + tiny
        rel_n[...] = rel_w[...] - rel * row_factor * lax.rsqrt(col_moment)
        rel_r[...] = row_sums / cols + tiny
        rel_c[...] = col_moment
        for gain, row, new, moment_out in ((attn_w, 5, attn_n, attn_m), (ff_w, 6, ff_n, ff_m)):
            value = gain[...]
            grad = shared_ref[row : row + 1, :width] / value
            moment = grad * grad + tiny
            rate = step_scale * jnp.sqrt(total(value * value, 1) / width)
            stepped = value - rate * grad * lax.rsqrt(total(moment, 1) / width)
            new[...] = stepped.reshape(width)
            moment_out[...] = moment.reshape(width)


def update(grads, weights, rel_w, attn_w, ff_w, shared, own, tall, chunks=8):
    tensor_count = lax.axis_size("mp")
    width = weights[0].shape[0]
    slots = rel_w.shape[1]
    f32 = jnp.float32

    def blocks(array):
        return pl.BlockSpec((width // chunks, array.shape[1]), lambda i: (i, 0))

    def fixed(rows, cols, at=0):
        return pl.BlockSpec((rows, cols), lambda i: (at, 0))

    def line(size):
        return pl.BlockSpec((size,), lambda i: (0,))

    matrices = [blocks(w) for w in weights]
    rel_spec = fixed(BUCKETS, slots)
    columns = [w.shape[1] for w in weights]
    return pl.pallas_call(
        functools.partial(update_kernel, tensor_count),
        grid=(chunks,),
        in_specs=[
            *[blocks(g) for g in grads],
            fixed(BUCKETS, grads[3].shape[1], width // BUCKETS),
            *matrices,
            rel_spec,
            fixed(1, width),
            fixed(1, width),
            fixed(*shared.shape),
            fixed(*own.shape),
            blocks(tall),
        ],
        out_specs=[*matrices, rel_spec]
        + [line(width)] * 7
        + [fixed(1, BUCKETS)]
        + [line(c) for c in columns]
        + [fixed(1, slots)]
        + [line(width)] * 4,
        out_shape=[jax.ShapeDtypeStruct(w.shape, f32) for w in weights]
        + [jax.ShapeDtypeStruct(rel_w.shape, f32)]
        + [jax.ShapeDtypeStruct((width,), f32)] * 7
        + [jax.ShapeDtypeStruct((1, BUCKETS), f32)]
        + [jax.ShapeDtypeStruct((c,), f32) for c in columns]
        + [jax.ShapeDtypeStruct((1, slots), f32)]
        + [jax.ShapeDtypeStruct((width,), f32)] * 4,
        compiler_params=pltpu.CompilerParams(vmem_limit_bytes=58 << 20),
        cost_estimate=pl.CostEstimate(
            flops=40 * width * columns[0], bytes_accessed=36 * width * columns[0], transcendentals=0
        ),
        name="update",
    )(
        *grads, grads[3], *weights, rel_w,
        attn_w.reshape(1, width), ff_w.reshape(1, width), shared, own, tall,
    )


def gather_proj_kernel(data_count, count, own_ref, all_ref, load_sem, cross_send, cross_recv, side_send, side_recv):
    me = lax.axis_index("dp")
    place = lax.axis_index("mp")
    others = [(place + k) % count for k in range(1, count)]
    peers = [(me + k) % data_count for k in range(1, data_count)]
    load = pltpu.make_async_copy(own_ref, all_ref.at[place], load_sem)
    load.start()
    greet([(me, other) for other in others] + [(peer, place) for peer in peers])
    sent = []
    for k, other in enumerate(others):
        copy = pltpu.make_async_remote_copy(
            src_ref=own_ref.at[me],
            dst_ref=all_ref.at[place, me],
            send_sem=cross_send.at[k],
            recv_sem=cross_recv.at[count - 2 - k],
            device_id=(me, other),
            device_id_type=pl.DeviceIdType.MESH,
        )
        copy.start()
        sent.append(copy)
    arrivals = []
    for k, other in enumerate(others):
        pltpu.make_async_remote_copy(
            src_ref=own_ref.at[me],
            dst_ref=all_ref.at[other, me],
            send_sem=cross_send.at[k],
            recv_sem=cross_recv.at[k],
            device_id=(me, other),
            device_id_type=pl.DeviceIdType.MESH,
        ).wait_recv()
        for j, peer in enumerate(peers):
            slot = k * (data_count - 1)
            copy = pltpu.make_async_remote_copy(
                src_ref=all_ref.at[other, me],
                dst_ref=all_ref.at[other, me],
                send_sem=side_send.at[slot + j],
                recv_sem=side_recv.at[slot + data_count - 2 - j],
                device_id=(peer, place),
                device_id_type=pl.DeviceIdType.MESH,
            )
            copy.start()
            sent.append(copy)
            arrivals.append(
                pltpu.make_async_remote_copy(
                    src_ref=all_ref.at[other, peer],
                    dst_ref=all_ref.at[other, peer],
                    send_sem=side_send.at[slot + j],
                    recv_sem=side_recv.at[slot + j],
                    device_id=(peer, place),
                    device_id_type=pl.DeviceIdType.MESH,
                )
            )
    for arrival in arrivals:
        arrival.wait_recv()
    for copy in sent:
        copy.wait_send()
    load.wait()


def gather_proj(proj_low):
    count = lax.axis_size("mp")
    data_count = lax.axis_size("dp")
    lanes, width = proj_low.shape
    part = lanes // data_count
    anywhere = pl.BlockSpec(memory_space=pl.ANY)
    dma = pltpu.SemaphoreType.DMA
    gathered = pl.pallas_call(
        functools.partial(gather_proj_kernel, data_count, count),
        out_shape=jax.ShapeDtypeStruct((count, data_count, part, width), proj_low.dtype),
        in_specs=[anywhere],
        out_specs=anywhere,
        scratch_shapes=[
            dma,
            dma((count - 1,)),
            dma((count - 1,)),
            dma(((count - 1) * (data_count - 1),)),
            dma(((count - 1) * (data_count - 1),)),
        ],
        compiler_params=pltpu.CompilerParams(collective_id=0, has_side_effects=True),
        cost_estimate=pl.CostEstimate(flops=0, bytes_accessed=50 << 20, transcendentals=0),
        name="gather_proj",
    )(proj_low.reshape(data_count, part, width))
    return gathered.reshape(count * lanes, width)


def turn_order(count):
    return [sorted(range(count), key=lambda b: (abs(b - place), b < place)) for place in range(count)]


def look_up(table, row, column):
    found = jnp.int32(0)
    for r, entries in enumerate(table):
        for c, entry in enumerate(entries):
            found = jnp.where((row == r) & (column == c), jnp.int32(entry), found)
    return found


def feed_forward_kernel(
    data_count,
    count,
    parts,
    normed_hbm,
    cot_hbm,
    gate_up_hbm,
    down_hbm,
    out_hbm,
    dn_ref,
    pieces_hbm,
    normed,
    cot,
    gate_up,
    down,
    hidden,
    d_gate_up,
    outgoing,
    incoming,
    stage,
    grads,
    land_whole,
    land_most,
    land_rest,
    load_sem,
    stage_sem,
    gather_send,
    gather_recv,
    sum_send,
    sum_recv,
    down_send,
    down_recv,
):
    place = lax.axis_index("mp")
    row = lax.axis_index("dp")
    block_len, width = dn_ref.shape
    units = down.shape[1]
    part_len = block_len // parts
    last = count - 1
    has_left = place > 0
    has_right = place < last

    loads = [
        pltpu.make_async_copy(normed_hbm, normed.at[place], load_sem.at[0]),
        pltpu.make_async_copy(gate_up_hbm.at[pl.ds(0, width)], gate_up, load_sem.at[1]),
        pltpu.make_async_copy(down_hbm, down, load_sem.at[2]),
        pltpu.make_async_copy(cot_hbm, cot, load_sem.at[3]),
    ]
    for load in loads:
        load.start()

    ways = orders(data_count)
    span = data_count - 1
    most = land_most.shape[2]
    shares = (
        (0, 0, units, 0, land_whole.at[0]),
        (1, 0, units, 1, land_whole.at[1]),
        (2, 0, most, 0, land_most),
        (2, most, units - most, 1, land_rest),
    )
    flies = [Butterfly(ways[way], k * span) for k, (_, _, _, way, _) in enumerate(shares)]
    stages = len(ways[0])
    sems = (down_send, down_recv)
    views = [row_pieces(grads.at[i], data_count, at, lanes) for i, at, lanes, _, _ in shares]

    barrier = pltpu.get_barrier_semaphore()
    for s in range(stages):
        pl.semaphore_signal(
            barrier, inc=1, device_id=flies[0].partner(s), device_id_type=pl.DeviceIdType.MESH
        )
    for side, there in ((-1, has_left), (1, has_right)):

        @pl.when(there)
        def _():
            pl.semaphore_signal(
                barrier, inc=1, device_id=(row, place + side), device_id_type=pl.DeviceIdType.MESH
            )

    pl.semaphore_wait(barrier, stages + has_left.astype(jnp.int32) + has_right.astype(jnp.int32))

    def pass_block(block, side, slot):
        return pltpu.make_async_remote_copy(
            src_ref=normed.at[block],
            dst_ref=normed.at[block],
            send_sem=gather_send.at[slot],
            recv_sem=gather_recv.at[block],
            device_id=(row, place + side),
            device_id_type=pl.DeviceIdType.MESH,
        )

    def rows_of(part):
        return pl.ds(pl.multiple_of(part * part_len, part_len), part_len)

    def pass_sum(block, part, side, slot):
        return pltpu.make_async_remote_copy(
            src_ref=outgoing.at[block, rows_of(part)],
            dst_ref=incoming.at[slot, rows_of(part)],
            send_sem=sum_send.at[block, part],
            recv_sem=sum_recv.at[slot, part],
            device_id=(row, place + side),
            device_id_type=pl.DeviceIdType.MESH,
        )

    def landing(block, side):
        return jnp.where((side == -1) & (place + side == block), count, block)

    loads[0].wait()
    for side, there in ((-1, has_left), (1, has_right)):

        @pl.when(there)
        def _():
            pass_block(place, side, count + (side + 1) // 2).start()

    for load in loads[1:]:
        load.wait()

    def store_out(turn, block):
        return pltpu.make_async_copy(stage.at[turn % 2], out_hbm.at[block], stage_sem.at[turn % 2])

    table = turn_order(count)
    root = 0.7978845608028654

    def turn_body(turn, carry):
        block = look_up(table, place, turn)
        distance = jnp.abs(block - place)

        @pl.when((distance > 0) & ((block > place) | (place + distance > last)))
        def _():
            for side in (1, -1):
                other = place + side * distance

                @pl.when((other >= 0) & (other <= last))
                def _():
                    pass_block(other, 0, other).wait_recv()

                    @pl.when((place - side >= 0) & (place - side <= last))
                    def _():
                        pass_block(other, -side, other).start()

        acts = product(normed[block], gate_up[...])
        gate_act = acts[:, :units]
        up_act = acts[:, units:]
        squared = gate_act * gate_act
        bend = jnp.tanh(root * gate_act * (1.0 + 0.044715 * squared))
        half = 0.5 * (1.0 + bend)
        gelu = gate_act * half
        hidden[block] = (gelu * up_act).astype(jnp.bfloat16)
        d_hidden = product(cot[block], down[...])
        slope = half + 0.5 * gate_act * (1.0 - bend * bend) * (root * (1.0 + 0.134145 * squared))
        d_gate_up[block, :, :units] = (d_hidden * up_act * slope).astype(jnp.bfloat16)
        d_gate_up[block, :, units:] = (d_hidden * gelu).astype(jnp.bfloat16)
        term = right_inner(d_gate_up[block], gate_up[...])

        @pl.when(block == place)
        def _():
            dn_ref[...] = term

        @pl.when(block != place)
        def _():
            outgoing[block] = term.astype(jnp.bfloat16)

        for side, is_end in ((1, place == 0), (-1, place == last)):

            @pl.when(is_end & (block != place))
            def _():
                for part in range(parts):
                    pass_sum(block, part, side, landing(block, side)).start()

        @pl.when(turn >= 2)
        def _():
            store_out(turn, block).wait()

        stage[turn % 2] = right_inner(hidden[block], down[...]).astype(jnp.bfloat16)
        store_out(turn, block).start()
        return carry

    lax.fori_loop(0, count, turn_body, 0)

    def relay(key):
        def relay_part(part, carry):
            for side, block in ((1, key), (-1, last - key)):
                through = (block > place) & has_left if side == 1 else (block < place) & has_right

                @pl.when(through)
                def _():
                    pass_sum(block, part, side, block).wait_recv()
                    rows = rows_of(part)
                    outgoing[block, rows] = (
                        outgoing[block, rows].astype(jnp.float32)
                        + incoming[block, rows].astype(jnp.float32)
                    ).astype(jnp.bfloat16)
                    pass_sum(block, part, side, landing(block, side)).start()

            return carry

        lax.fori_loop(0, parts, relay_part, 0)

    def flat(ref):
        return ref[...].reshape(count * block_len, ref.shape[2])

    sent = []

    def halve(k, s):
        copies = flies[k].halve(s, views[k], shares[k][4], sems)
        for copy in copies:
            copy.start()
        sent.extend(copies)
        return copies

    def add_halve(k, s, copies):
        flies[k].add(s, views[k], shares[k][4], copies)
        return halve(k, s + 1) if s + 1 < stages else None

    def weigh(i, left, right):
        grads[i, :width] = left_inner(left, right).astype(jnp.bfloat16)

    grads[:, width:] = jnp.zeros((3, grads.shape[1] - width, units), jnp.bfloat16)
    weigh(2, flat(cot), flat(hidden))
    flights = [None, None, halve(2, 0), halve(3, 0)]
    for key in range(1, last):
        relay(key)
    gate_side = d_gate_up[:, :, :units].reshape(count * block_len, units)
    weigh(0, flat(normed), gate_side)
    flights[0] = halve(0, 0)
    for k in (2, 3):
        flights[k] = add_halve(k, 0, flights[k])
    up_side = d_gate_up[:, :, units:].reshape(count * block_len, units)
    weigh(1, flat(normed), up_side)
    flights[1] = halve(1, 0)
    for k in (0, 1):
        flights[k] = add_halve(k, 0, flights[k])
    relay(last)
    for s in range(1, stages - 1):
        for k in (2, 3, 0, 1):
            flights[k] = add_halve(k, s, flights[k])

    for side, there in ((1, has_left), (-1, has_right)):

        @pl.when(there)
        def _():
            slot = place if side == 1 else count

            def add_part(part, carry):
                pass_sum(place, part, side, slot).wait_recv()
                rows = rows_of(part)
                dn_ref[rows] += incoming[slot, rows].astype(jnp.float32)
                return carry

            lax.fori_loop(0, parts, add_part, 0)

    for k in (2, 3, 0, 1):
        add_halve(k, stages - 1, flights[k])
    mine = pl.ds(pl.multiple_of(row * pieces_hbm.shape[1], pieces_hbm.shape[1]), pieces_hbm.shape[1])
    save = pltpu.make_async_copy(grads.at[:, mine], pieces_hbm, load_sem.at[0])
    save.start()
    for copy in sent:
        copy.wait_send()

    for side, there in ((-1, has_left), (1, has_right)):

        @pl.when(there)
        def _():
            pass_block(place, side, count + (side + 1) // 2).wait_send()

    for block in range(count):

        @pl.when((block != place) & has_left & has_right)
        def _():
            pass_block(block, 1, block).wait_send()

        @pl.when(block != place)
        def _():
            for part in range(parts):
                pass_sum(block, part, 1, block).wait_send()

    for turn in (count - 2, count - 1):
        store_out(turn, 0).wait()
    save.wait()


def feed_forward(normed, cot_all, gate_up, down):
    count = lax.axis_size("mp")
    data_count = lax.axis_size("dp")
    block_len, width = normed.shape
    units = down.shape[1]
    padded = gate_up.shape[0]
    parts = 2
    low = jnp.bfloat16
    anywhere = pl.BlockSpec(memory_space=pl.ANY)
    dma = pltpu.SemaphoreType.DMA
    tokens = count * block_len
    height = padded // data_count
    span = data_count - 1
    most = (units // 2 + 127) // 128 * 128
    out_terms, dn, pieces = pl.pallas_call(
        functools.partial(feed_forward_kernel, data_count, count, parts),
        out_shape=[
            jax.ShapeDtypeStruct((count, block_len, width), low),
            jax.ShapeDtypeStruct((block_len, width), jnp.float32),
            jax.ShapeDtypeStruct((3, height, units), low),
        ],
        in_specs=[anywhere] * 4,
        out_specs=[anywhere, pl.BlockSpec(memory_space=pltpu.VMEM), anywhere],
        scratch_shapes=[
            pltpu.VMEM((count, block_len, width), low),
            pltpu.VMEM((count, block_len, width), low),
            pltpu.VMEM((width, 2 * units), low),
            pltpu.VMEM((width, units), low),
            pltpu.VMEM((count, block_len, units), low),
            pltpu.VMEM((count, block_len, 2 * units), low),
            pltpu.VMEM((count, block_len, width), low),
            pltpu.VMEM((count + 1, block_len, width), low),
            pltpu.VMEM((2, block_len, width), low),
            pltpu.VMEM((3, padded, units), low),
            pltpu.VMEM((2, span, height, units), low),
            pltpu.VMEM((span, height, most), low),
            pltpu.VMEM((span, height, units - most), low),
            dma((4,)),
            dma((2,)),
            dma((count + 2,)),
            dma((count,)),
            dma((count, parts)),
            dma((count + 1, parts)),
            dma((4 * span,)),
            dma((4 * span,)),
        ],
        compiler_params=pltpu.CompilerParams(
            collective_id=1, has_side_effects=True, vmem_limit_bytes=60 << 20
        ),
        cost_estimate=pl.CostEstimate(
            flops=18 * tokens * width * units,
            bytes_accessed=12 * width * units + 6 * tokens * width,
            transcendentals=tokens * units,
        ),
        name="feed_forward",
    )(normed, cot_all.reshape(count, block_len, width), gate_up, down)
    return out_terms.reshape(tokens, width), dn, pieces


def ff_parts(units):
    most = (units // 2 + 127) // 128 * 128
    return ((0, 0, units, 0), (1, 0, units, 1), (2, 0, most, 0), (2, most, units - most, 1))


def attend_back_kernel(
    data_count,
    count,
    slots,
    dn_hbm,
    middle_hbm,
    cot_hbm,
    gain_ref,
    proj_hbm,
    own_hbm,
    qkv_hbm,
    probs_hbm,
    norm_hbm,
    qkv_low_hbm,
    onehot_hbm,
    ff_hbm,
    d_middle_hbm,
    terms_hbm,
    d_qkv_w_hbm,
    d_out_w_hbm,
    spread_hbm,
    dn,
    middle,
    cot,
    proj,
    own,
    qkv,
    probs,
    norm,
    qkv_low,
    onehot,
    d_own,
    grad,
    diag,
    dk,
    dv,
    d_qkv,
    terms,
    d_qkv_w,
    d_out_w,
    load_sem,
    probs_sem,
    cross_send,
    cross_recv,
    up_send,
    up_recv,
):
    place = lax.axis_index("mp")
    me = lax.axis_index("dp")
    block_len, width = dn.shape
    seq_len = qkv.shape[0]
    lanes = slots * HD
    padded = d_qkv_w.shape[0]
    steps = seq_len // BLOCK
    f32 = jnp.float32
    low = jnp.bfloat16

    loads = []

    def load(src, dst):
        copy = pltpu.make_async_copy(src, dst, load_sem.at[len(loads)])
        copy.start()
        loads.append(copy)

    load(dn_hbm, dn)
    load(middle_hbm, middle)
    load(cot_hbm, cot)
    load(proj_hbm, proj)
    load(own_hbm, own)
    load(qkv_hbm, qkv)
    load(norm_hbm, norm)
    load(qkv_low_hbm, qkv_low)
    load(onehot_hbm, onehot)
    height = padded // data_count
    mine = pl.ds(pl.multiple_of(me * height, height), height)
    load(ff_hbm, spread_hbm.at[:, mine])

    ways = orders(data_count)
    stages = len(ways[0])
    parts = ff_parts(spread_hbm.shape[2])
    span = data_count - 1
    flies = [Butterfly(ways[way], k * span) for k, (_, _, _, way) in enumerate(parts)]
    views = [row_pieces(spread_hbm.at[i], data_count, at, wide) for i, at, wide, _ in parts]
    others = [(place + k) % count for k in range(1, count)]
    greet([flies[0].partner(s) for s in range(1, stages)] + [(me, other) for other in others])
    sent = []

    def start(copies):
        for copy in copies:
            copy.start()
        sent.extend(copies)
        return copies

    flights = [
        start(
            fly.double(
                stages - 1, view, (up_send, up_recv), ff_hbm.at[i, :, pl.ds(at, wide)]
            )
        )
        for fly, view, (i, at, wide, _) in zip(flies, views, parts)
    ]

    table = turn_order(count)

    def fetch(t):
        per = block_len // BLOCK
        block = look_up(table, place, t // per) * per + t % per
        rows = pl.ds(pl.multiple_of(block * BLOCK, BLOCK), BLOCK)
        return block, pltpu.make_async_copy(
            probs_hbm.at[:, rows], probs.at[t % 2], probs_sem.at[t % 2]
        )

    fetch(0)[1].start()
    diag[...] = jnp.zeros_like(diag)
    dk[...] = jnp.zeros_like(dk)
    dv[...] = jnp.zeros_like(dv)
    for copy in loads[:3]:
        copy.wait()
    d_middle = cot[...].astype(f32) + norm_back(middle[...], gain_ref[...], dn[...])
    middle[...] = d_middle
    save_middle = pltpu.make_async_copy(middle, d_middle_hbm, load_sem.at[0])
    save_middle.start()
    cot[...] = d_middle.astype(low)
    loads[3].wait()
    d_all = right_inner(cot[...], proj[...]).astype(low)

    def own_rows(who):
        return pl.ds(pl.multiple_of(who * block_len, block_len), block_len)

    for k in range(count):
        d_own[k] = d_all[:, k * lanes : (k + 1) * lanes]
    start(
        [
            pltpu.make_async_remote_copy(
                src_ref=d_own.at[other],
                dst_ref=grad.at[own_rows(place)],
                send_sem=cross_send.at[k],
                recv_sem=cross_recv.at[place],
                device_id=(me, other),
                device_id_type=pl.DeviceIdType.MESH,
            )
            for k, other in enumerate(others)
        ]
    )
    grad[own_rows(place)] = d_own[place]
    loads[4].wait()
    d_out_w[width:] = jnp.zeros((padded - width, count * lanes), low)
    d_out_w[:width] = left_inner(cot[...], own[...]).astype(low)
    save_out = pltpu.make_async_copy(d_out_w, d_out_w_hbm, load_sem.at[1])
    save_out.start()
    loads[5].wait()

    def pass_on(s):
        for k, (fly, view) in enumerate(zip(flies, views)):
            for copy in flights[k]:
                copy.wait_recv()
            if s > 1:
                flights[k] = start(fly.double(s - 1, view, (up_send, up_recv)))

    def back_block(t, carry):
        per = block_len // BLOCK

        @pl.when((t > 0) & (t % per == 0))
        def _():
            who = look_up(table, place, t // per)
            pltpu.make_async_remote_copy(
                src_ref=d_own.at[0],
                dst_ref=grad.at[own_rows(who)],
                send_sem=cross_send.at[0],
                recv_sem=cross_recv.at[who],
                device_id=(me, who),
                device_id_type=pl.DeviceIdType.MESH,
            ).wait_recv()

        @pl.when(t + 1 < steps)
        def _():
            fetch(t + 1)[1].start()

        block, arrival = fetch(t)
        arrival.wait()
        rows = pl.ds(pl.multiple_of(block * BLOCK, BLOCK), BLOCK)
        window = pl.ds(pl.multiple_of((steps - 1 - block) * BLOCK, BLOCK), seq_len)
        queries = qkv[rows, 0:lanes]
        keys = qkv[:, lanes : 2 * lanes]
        values = qkv[:, 2 * lanes : 3 * lanes]
        d_query = jnp.zeros((BLOCK, lanes), f32)
        for slot in range(slots):
            weight = probs[t % 2, slot]
            slot_grad = slot_lanes(grad[rows], slot)
            d_probs = right_inner(slot_grad, values)
            delta = jnp.sum(weight * d_probs, axis=-1, keepdims=True)
            d_scores = (weight * (d_probs - delta)).astype(low)
            d_query = d_query + slot_lanes(product(d_scores, keys), slot)
            dk[...] += left_inner(slot_lanes(queries, slot), d_scores)
            dv[...] += left_inner(slot_grad, weight.astype(low))
            diag[slot, :, window] += d_scores.astype(f32)
        d_qkv[rows, 0:lanes] = d_query.astype(low)
        return carry

    loads[9].wait()
    pass_on(stages - 1)
    lax.fori_loop(0, steps, back_block, 0)
    for s in reversed(range(2, stages - 1)):
        pass_on(s)
    d_qkv[:, lanes : 2 * lanes] = dk[...].T.astype(low)
    d_qkv[:, 2 * lanes : 3 * lanes] = dv[...].T.astype(low)
    for copy in loads[6:9]:
        copy.wait()
    terms[...] = right_inner(d_qkv[...], qkv_low[:width]).astype(low)
    save_terms = pltpu.make_async_copy(terms, terms_hbm, load_sem.at[2])
    save_terms.start()
    d_qkv_w[:width] = left_inner(norm[...], d_qkv[...]).astype(low)
    d_qkv_w[width:] = jnp.zeros((padded - width, 3 * lanes), low)
    sums = []
    for slot in range(slots):
        level = diag[slot]
        rest = BLOCK // 2
        while rest >= 1:
            level = pltpu.roll(level[:rest], rest, 1) + level[rest:]
            rest //= 2
        sums.append(level)
    sums = jnp.concatenate(sums + [jnp.zeros((128 - slots, 2 * seq_len), f32)], axis=0)
    d_rel = lax.dot_general(
        onehot[...],
        sums,
        (((1,), (1,)), ((), ())),
        precision=highest,
        preferred_element_type=f32,
    )
    d_qkv_w[width : width + BUCKETS, :128] = d_rel.astype(low)
    save_qkv = pltpu.make_async_copy(d_qkv_w, d_qkv_w_hbm, load_sem.at[3])
    save_qkv.start()
    if stages > 1:
        pass_on(1)
    for copy in sent:
        copy.wait_send()
    for copy in (save_middle, save_out, save_terms, save_qkv):
        copy.wait()


def attend_back(dn, middle, cot, gain, proj_all, own, qkv, probs, norm, qkv_low, onehot, ff_pieces):
    count = lax.axis_size("mp")
    data_count = lax.axis_size("dp")
    seq_len = qkv.shape[0]
    slots = probs.shape[0]
    lanes = slots * HD
    block_len, width = dn.shape
    padded = qkv_low.shape[0]
    _, _, units = ff_pieces.shape
    far = pl.BlockSpec(memory_space=pltpu.HBM)
    near = pl.BlockSpec(memory_space=pltpu.VMEM)
    dma = pltpu.SemaphoreType.DMA
    low, f32 = jnp.bfloat16, jnp.float32
    span = data_count - 1
    scratch = [
        (dn.shape, f32),
        (middle.shape, f32),
        (cot.shape, low),
        (proj_all.shape, low),
        (own.shape, low),
        (qkv.shape, low),
        ((2, slots, BLOCK, seq_len), f32),
        (norm.shape, low),
        (qkv_low.shape, low),
        (onehot.shape, f32),
        ((count, block_len, lanes), low),
        ((seq_len, lanes), low),
        ((slots, BLOCK, 2 * seq_len), f32),
        ((lanes, seq_len), f32),
        ((lanes, seq_len), f32),
        (qkv.shape, low),
        ((seq_len, width), low),
        ((padded, 3 * lanes), low),
        ((padded, count * lanes), low),
    ]
    return pl.pallas_call(
        functools.partial(attend_back_kernel, data_count, count, slots),
        in_specs=[far] * 3 + [near] + [far] * 8,
        out_specs=[far] * 5,
        out_shape=[
            jax.ShapeDtypeStruct((block_len, width), f32),
            jax.ShapeDtypeStruct((seq_len, width), low),
            jax.ShapeDtypeStruct((padded, 3 * lanes), low),
            jax.ShapeDtypeStruct((padded, count * lanes), low),
            jax.ShapeDtypeStruct((3, padded, units), low),
        ],
        scratch_shapes=[pltpu.VMEM(shape, dtype) for shape, dtype in scratch]
        + [
            dma((10,)),
            dma((2,)),
            dma((count - 1,)),
            dma((count,)),
            dma((4 * span,)),
            dma((4 * span,)),
        ],
        compiler_params=pltpu.CompilerParams(
            collective_id=3, has_side_effects=True, vmem_limit_bytes=56 << 20
        ),
        cost_estimate=pl.CostEstimate(
            flops=16 * slots * seq_len * seq_len * HD, bytes_accessed=140 << 20, transcendentals=0
        ),
        name="attend_back",
    )(dn, middle, cot, gain, proj_all, own, qkv, probs, norm, qkv_low, onehot, ff_pieces)


def to_owners(rows_of_slots):
    count = lax.axis_size("mp")
    seq_len, lanes = rows_of_slots.shape
    pieces = rows_of_slots.reshape(count, seq_len // count, lanes)
    pieces = lax.all_to_all(pieces, "mp", split_axis=0, concat_axis=0)
    return pieces.transpose(1, 0, 2).reshape(seq_len // count, count * lanes)


def local(
    layer_in,
    segment_ids,
    bucket_table,
    attn_gain,
    query_weight,
    key_weight,
    value_weight,
    out_weight,
    rel_bias,
    ff_gain,
    gate_weight,
    up_weight,
    down_weight,
    cotangent,
):
    _, local_len, model_width = layer_in.shape
    seq_len = segment_ids.shape[1]
    lane_width = query_weight.shape[1]
    slots_here = lane_width // HD
    ff_width = gate_weight.shape[1]
    tensor_index = lax.axis_index("mp")
    tensor_count = lax.axis_size("mp")
    data_index = lax.axis_index("dp")
    data_count = lax.axis_size("dp")
    layer_in = layer_in[0]
    cotangent = cotangent[0]
    slot_ids = tensor_index * slots_here + jnp.arange(slots_here)
    slot_valid = ((slot_ids < 5) | (slot_ids == 6)).astype(jnp.float32)
    lane_mask = jnp.repeat(slot_valid, HD)
    qkv_low = (
        jnp.concatenate([query_weight, key_weight, value_weight], axis=1) * jnp.tile(lane_mask, 3)
    ).astype(jnp.bfloat16)
    proj_low = (out_weight * lane_mask[:, None]).astype(jnp.bfloat16)
    piece = 16 * data_count
    padded = (model_width + piece - 1) // piece * piece
    extra = padded - model_width
    gate_up_low = jnp.concatenate([gate_weight, up_weight], axis=1).astype(jnp.bfloat16)
    gate_up_low = jnp.pad(gate_up_low, ((0, extra), (0, 0)))
    squares = [
        jnp.sum(w * w)
        for w in (
            query_weight,
            key_weight,
            value_weight,
            rel_bias,
            gate_weight,
            up_weight,
            out_weight,
            down_weight,
        )
    ]
    squares = jnp.pad(jnp.stack(squares), (0, 120)).reshape(1, 128)
    down_turned = down_weight.T
    out_turned = out_weight.T
    down_low = down_turned.astype(jnp.bfloat16)
    onehot = (bucket_table[:, None] == jnp.arange(BUCKETS)[None, :]).astype(jnp.float32)
    onehot = jnp.pad(onehot, ((0, 1), (0, 0)))
    onehot_turned = onehot.T
    qkv_padded = jnp.pad(qkv_low, ((0, extra), (0, 0)))
    vector = lax.dot_general(
        rel_bias,
        onehot,
        (((0,), (1,)), ((), ())),
        precision=highest,
        preferred_element_type=jnp.float32,
    )
    residual_in = layer_in.astype(jnp.float32)
    normed_local = rms_norm(residual_in, attn_gain).astype(jnp.bfloat16)
    flat_norm = lax.all_gather(normed_local, "mp", axis=0, tiled=True)
    proj_all = gather_proj(proj_low)
    (
        flat_norm,
        late_cot,
        proj_all,
        qkv_low,
        gate_up_low,
        down_low,
        vector,
        squares,
        onehot_turned,
        qkv_padded,
    ) = lax.optimization_barrier(
        (
            flat_norm,
            cotangent,
            proj_all,
            qkv_low,
            gate_up_low,
            down_low,
            vector,
            squares,
            onehot_turned,
            qkv_padded,
        )
    )
    flat_cot = lax.all_gather(late_cot, "mp", axis=0, tiled=True)
    qkv = product(flat_norm, qkv_low).astype(jnp.bfloat16)
    attended, probs = attend(qkv, segment_ids.reshape(seq_len, 1), segment_ids, vector)
    own_attended = to_owners(attended)
    middle = residual_in + product(own_attended, proj_all)
    normed_ff_local = rms_norm(middle, ff_gain).astype(jnp.bfloat16)
    out_terms, dn_ff, ff_pieces = feed_forward(normed_ff_local, flat_cot, gate_up_low, down_low)
    d_middle, dn_attn_terms, d_qkv_w, d_out_w, ff_grads = attend_back(
        dn_ff,
        middle,
        cotangent,
        ff_gain.reshape(1, model_width),
        proj_all,
        own_attended,
        qkv,
        probs,
        flat_norm,
        qkv_padded,
        onehot_turned,
        ff_pieces,
    )
    ff_branch = lax.psum_scatter(out_terms, "mp", scatter_dimension=0, tiled=True)
    layer_out = (middle + ff_branch.astype(jnp.float32)).astype(jnp.bfloat16)
    dn_attn = lax.psum_scatter(dn_attn_terms, "mp", scatter_dimension=0, tiled=True)
    *grads, shared, own, tall = sum_weights(
        ff_grads, d_qkv_w, d_out_w, qkv_padded, gate_up_low, squares, model_width
    )
    weights = (
        gate_weight,
        up_weight,
        down_turned,
        query_weight,
        key_weight,
        value_weight,
        out_turned,
    )
    results = update(grads, weights, rel_bias, attn_gain, ff_gain, shared, own, tall)
    news, along, across = results[:8], results[8:16], results[16:24]
    new_attn_gain, attn_gain_moment, new_ff_gain, ff_gain_moment = results[24:]
    gate, up, down, query, key, value, out, rel = zip(news, along, across)
    rel = (rel[0], rel[1].reshape(BUCKETS), rel[2].reshape(slots_here))
    down = (down[0].T, down[2], down[1])
    out = (out[0].T, out[2], out[1])
    input_grad = d_middle + norm_back(residual_in, attn_gain, dn_attn.astype(jnp.float32))
    input_grad = input_grad.astype(jnp.bfloat16)
    return (
        layer_out[None],
        input_grad[None],
        new_attn_gain,
        attn_gain_moment,
        *query,
        *key,
        *value,
        *out,
        *rel,
        new_ff_gain,
        ff_gain_moment,
        *gate,
        *up,
        *down,
    )


def solution(mesh):
    return jax.shard_map(
        local,
        mesh=mesh,
        in_specs=(
            P("dp", "mp", None),
            P("dp", None),
            P(),
            P(),
            P(None, "mp"),
            P(None, "mp"),
            P(None, "mp"),
            P("mp", None),
            P(None, "mp"),
            P(),
            P(None, "mp"),
            P(None, "mp"),
            P("mp", None),
            P("dp", "mp", None),
        ),
        out_specs=(
            P("dp", "mp", None),
            P("dp", "mp", None),
            P(),
            P(),
            P(None, "mp"),
            P(),
            P("mp"),
            P(None, "mp"),
            P(),
            P("mp"),
            P(None, "mp"),
            P(),
            P("mp"),
            P("mp", None),
            P("mp"),
            P(),
            P(None, "mp"),
            P(),
            P("mp"),
            P(),
            P(),
            P(None, "mp"),
            P(),
            P("mp"),
            P(None, "mp"),
            P(),
            P("mp"),
            P("mp", None),
            P("mp"),
            P(),
        ),
        check_vma=False,
    )
```

```python
import functools

import jax
import jax.numpy as jnp
from jax import lax
from jax.experimental import pallas as pl
from jax.experimental.pallas import tpu as pltpu
from jax.sharding import PartitionSpec as P

HD = 64
BUCKETS = 32
BLOCK = 128


highest = lax.Precision.HIGHEST
step_scale = 0.3


def rms_norm(values, gain):
    return values * lax.rsqrt(jnp.mean(values * values, axis=-1, keepdims=True) + 1e-06) * gain


def norm_back(values, gain, grad):
    scale = lax.rsqrt(jnp.mean(values * values, axis=-1, keepdims=True) + 1e-06)
    unit = values * scale
    pull = grad * gain
    return scale * (pull - unit * jnp.mean(pull * unit, axis=-1, keepdims=True))


def product(left_side, right_side):
    return jnp.dot(left_side, right_side, preferred_element_type=jnp.float32)


def left_inner(left_side, right_side):
    return lax.dot_general(
        left_side, right_side, (((0,), (0,)), ((), ())), preferred_element_type=jnp.float32
    )


def right_inner(left_side, right_side):
    return lax.dot_general(
        left_side, right_side, (((1,), (1,)), ((), ())), preferred_element_type=jnp.float32
    )


def slot_lanes(values, slot):
    lane = lax.broadcasted_iota(jnp.int32, values.shape, 1)
    return jnp.where((lane >= slot * HD) & (lane < (slot + 1) * HD), values, jnp.zeros_like(values))


class Butterfly:
    def __init__(self, order, base):
        self.order = order
        self.me = lax.axis_index("dp")
        self.line = lax.axis_index("mp")
        self.base = base
        self.offsets = []
        total = 0
        for s in range(len(order)):
            self.offsets.append(total)
            total += 1 << (len(order) - 1 - s)

    def bit(self, b):
        return (self.me // b) % 2

    def partner(self, s):
        b = self.order[s]
        return (self.me + b * (1 - 2 * self.bit(b)), self.line)

    def width(self, s):
        return 1 << (len(self.order) - 1 - s)

    def piece(self, s, j, mine):
        b = self.order[s]
        found = sum(k * self.bit(k) for k in self.order[:s])
        found = found + b * (self.bit(b) if mine else 1 - self.bit(b))
        for i, k in enumerate(self.order[s + 1 :]):
            found = found + k * ((j // (1 << i)) % 2)
        return found

    def copy(self, src, dst, sems, slot, s):
        return pltpu.make_async_remote_copy(
            src_ref=src,
            dst_ref=dst,
            send_sem=sems[0].at[self.base + slot],
            recv_sem=sems[1].at[self.base + slot],
            device_id=self.partner(s),
            device_id_type=pl.DeviceIdType.MESH,
        )

    def halve(self, s, source, landing, sems):
        at = self.offsets[s]
        return [
            self.copy(source(self.piece(s, j, False)), landing.at[at + j], sems, at + j, s)
            for j in range(self.width(s))
        ]

    def add(self, s, kept, landing, copies):
        at = self.offsets[s]
        for j, copy in enumerate(copies):
            copy.wait_recv()
            mine = kept(self.piece(s, j, True))
            mine[...] = (mine[...].astype(jnp.float32) + landing[at + j].astype(jnp.float32)).astype(
                jnp.bfloat16
            )

    def double(self, s, whole, sems, first=None):
        at = self.offsets[s]
        copies = []
        for j in range(self.width(s)):
            view = whole(self.piece(s, j, True))
            copies.append(self.copy(view if first is None else first, view, sems, at + j, s))
        return copies


def orders(data_count):
    bits = [1 << i for i in range(data_count.bit_length() - 1)]
    return (bits, bits[:1] + bits[:0:-1])


def greet(peers):
    barrier = pltpu.get_barrier_semaphore()
    for peer in peers:
        pl.semaphore_signal(barrier, inc=1, device_id=peer, device_id_type=pl.DeviceIdType.MESH)
    pl.semaphore_wait(barrier, len(peers))


def row_pieces(ref, data_count, at=0, lanes=None):
    rows = ref.shape[0] // data_count
    columns = pl.ds(at, ref.shape[1] if lanes is None else lanes)
    return lambda q: ref.at[pl.ds(pl.multiple_of(q * rows, rows), rows), columns]


def total(values, axis):
    return jnp.sum(values, axis=axis, keepdims=True)


def sum_weights_kernel(data_count, count, model_width, parts, *refs):
    ff_hbm, qkv_hbm, out_hbm, qkv_low, gate_up_low, squares_ref = refs[:6]
    wholes, (shared_ref, own_ref, tall_ref) = refs[6:11], refs[11:14]
    kept, landings, full = refs[14:16], refs[16:18], refs[18:23]
    (
        cross,
        qkv_w,
        gate_up_w,
        tall,
        cols,
        gathered,
        load_sem,
        save_sem,
        down_send,
        down_recv,
        up_send,
        up_recv,
        cross_send,
        cross_recv,
        share_send,
        share_recv,
    ) = refs[23:]
    me = lax.axis_index("dp")
    place = lax.axis_index("mp")
    span = data_count - 1
    ways = orders(data_count)
    stages = len(ways[0])
    down, up = (down_send, down_recv), (up_send, up_recv)
    padded, units = full[0].shape
    lanes = full[4].shape[1]
    height = padded // data_count
    f32 = jnp.float32

    whole = [row_pieces(ref, data_count) for ref in full]
    saved = [row_pieces(wholes[i], data_count, at, wide) for i, at, wide, _ in parts]
    source = [row_pieces(ref, data_count) for ref in (qkv_hbm, out_hbm)]
    keep = [row_pieces(ref, data_count) for ref in kept]
    halvers = [Butterfly(ways[1 - i], i * span) for i in range(2)]
    doublers = [Butterfly(ways[way], k * span) for k, (_, _, _, way) in enumerate(parts)]
    views = [row_pieces(full[i], data_count, at, wide) for i, at, wide, _ in parts]

    loads = []

    def load(src, dst):
        copy = pltpu.make_async_copy(src, dst, load_sem.at[len(loads)])
        copy.start()
        loads.append(copy)

    first = doublers[0]
    for j in range(first.width(0)):
        q = first.piece(0, j, True)
        for i in range(3):
            load(row_pieces(ff_hbm.at[i], data_count)(q), whole[i](q))
    for i, fly in enumerate(halvers):
        for j in range(fly.width(0)):
            q = fly.piece(0, j, True)
            load(source[i](q), keep[i](q))
    load(qkv_low, qkv_w)
    load(gate_up_low, gate_up_w)
    others = [(place + k) % count for k in range(1, count)]
    greet([halvers[0].partner(s) for s in range(stages)] + [(me, other) for other in others])

    sent = []

    def start(copies):
        for copy in copies:
            copy.start()
        sent.extend(copies)
        return copies

    halves = [start(fly.halve(0, source[i], landings[i], down)) for i, fly in enumerate(halvers)]
    tall[...] = jnp.zeros_like(tall)
    cols[...] = jnp.zeros_like(cols)
    for copy in loads:
        copy.wait()

    doubles = {}

    def spread(s, arrays):
        for k, (i, _, _, _) in enumerate(parts):
            if i in arrays:
                doubles[k] = start(doublers[k].double(s, views[k], up))

    spread(0, (0, 1, 2))

    def note(k, q):
        i, start_lane, wide, _ = parts[k]
        rows = pl.ds(pl.multiple_of(q * height, height), height)
        grad = views[k](q)[...].astype(f32)
        if i == 3:
            at = lax.broadcasted_iota(jnp.int32, grad.shape, 0) + q * height
            grad = jnp.where(at < model_width, grad, 0.0)
        squares = grad * grad
        cols[i : i + 1, start_lane : start_lane + wide] += total(squares, 0)
        if i < 2:
            tall[rows, 3 + i : 4 + i] = total(squares, 1)
            weight = gate_up_w[rows, i * units : (i + 1) * units].astype(f32)
            tall[rows, 6:7] += total(grad * weight, 1)
        elif i == 3:
            for k in range(3):
                tall[rows, k : k + 1] = total(squares[:, k * lanes : (k + 1) * lanes], 1)
            tall[rows, 5:6] = total(grad * qkv_w[rows].astype(f32), 1)
        else:
            lane = 8 if i == 2 else 9
            tall[rows, lane : lane + 1] += total(squares, 1)

    saves = []

    def save(k, q, slot):
        copy = pltpu.make_async_copy(views[k](q), saved[k](q), save_sem.at[k * data_count + slot])
        copy.start()
        saves.append(copy)

    for s in range(stages):
        for i, fly in enumerate(halvers):
            fly.add(s, keep[i], landings[i], halves[i])
            if s + 1 < stages:
                halves[i] = start(fly.halve(s + 1, keep[i], landings[i], down))
    crossing = row_pieces(kept[1], data_count)(me)

    def lanes_of(other):
        return pl.ds(pl.multiple_of(other * lanes, lanes), lanes)

    start(
        [
            pltpu.make_async_remote_copy(
                src_ref=crossing.at[:, lanes_of(other)],
                dst_ref=cross.at[count - 2 - k],
                send_sem=cross_send.at[k],
                recv_sem=cross_recv.at[count - 2 - k],
                device_id=(me, other),
                device_id_type=pl.DeviceIdType.MESH,
            )
            for k, other in enumerate(others)
        ]
    )
    whole[3](me)[...] = keep[0](me)[...]
    spread(stages - 1, (3,))
    summed = crossing[:, lanes_of(place)].astype(f32)
    for k in range(count - 1):
        pltpu.make_async_remote_copy(
            src_ref=cross.at[k],
            dst_ref=cross.at[k],
            send_sem=cross_send.at[k],
            recv_sem=cross_recv.at[k],
            device_id=(me, others[0]),
            device_id_type=pl.DeviceIdType.MESH,
        ).wait_recv()
        summed = summed + cross[k].astype(f32)
    whole[4](me)[...] = summed.astype(jnp.bfloat16)
    spread(stages - 1, (4,))

    def note_pieces(k, s, mine):
        fly = doublers[k]
        for j in range(fly.width(s)):
            save(k, fly.piece(s, j, mine), j if mine else fly.width(s) + j)

        def note_piece(j, carry):
            note(k, fly.piece(s, j, mine))
            return carry

        lax.fori_loop(0, fly.width(s), note_piece, 0)

    early = [k for k, part in enumerate(parts) if part[0] < 3]
    late = [k for k, part in enumerate(parts) if part[0] >= 3]
    for k in early:
        note_pieces(k, 0, True)
    for k in late:
        note(k, me)
        save(k, me, 0)
    for k in early:
        for copy in doubles[k]:
            copy.wait_recv()
        note_pieces(k, 0, False)
    for s in reversed(range(stages)):
        for k in late:
            for copy in doubles[k]:
                copy.wait_recv()
            if s > 0:
                doubles[k] = start(doublers[k].double(s - 1, views[k], up))
        for k in late:
            note_pieces(k, s, False)

    slots_rel = full[3][model_width : model_width + BUCKETS, :128].astype(f32)
    tall[:BUCKETS, 7:8] = total(slots_rel * slots_rel, 1)
    share = gathered.at[place]
    share[...] = tall[...].T[0:16]
    share[10:11, :128] = squares_ref[...]
    shares = start(
        [
            pltpu.make_async_remote_copy(
                src_ref=share,
                dst_ref=share,
                send_sem=share_send.at[k],
                recv_sem=share_recv.at[place],
                device_id=(me, other),
                device_id_type=pl.DeviceIdType.MESH,
            )
            for k, other in enumerate(others)
        ]
    )
    own_ref[...] = jnp.zeros_like(own_ref)
    own_ref[:, : cols.shape[1]] = cols[...]
    for k, other in enumerate(others):
        pltpu.make_async_remote_copy(
            src_ref=gathered.at[other],
            dst_ref=gathered.at[other],
            send_sem=share_send.at[k],
            recv_sem=share_recv.at[other],
            device_id=(me, other),
            device_id_type=pl.DeviceIdType.MESH,
        ).wait_recv()
    summed = gathered[0]
    for k in range(1, count):
        summed = summed + gathered[k]
    shared_ref[...] = summed
    tall_ref[...] = jnp.concatenate([summed, jnp.zeros((112, padded), f32)], axis=0).T
    for copy in saves:
        copy.wait()
    for copy in sent:
        copy.wait_send()


def sum_weights(ff_grads, qkv, out, qkv_low, gate_up_low, squares, model_width):
    count = lax.axis_size("mp")
    data_count = lax.axis_size("dp")
    anywhere = pl.BlockSpec(memory_space=pl.ANY)
    near = pl.BlockSpec(memory_space=pltpu.VMEM)
    dma = pltpu.SemaphoreType.DMA
    low, f32 = jnp.bfloat16, jnp.float32
    span = data_count - 1
    units = ff_grads.shape[2]
    padded, wide = qkv.shape
    height = padded // data_count
    lanes = out.shape[1] // count
    full = [(padded, units)] * 3 + [(padded, wide), (padded, lanes)]
    parts = (*ff_parts(units), (3, 0, wide, 1), (4, 0, lanes, 0))
    n = len(parts)
    return pl.pallas_call(
        functools.partial(sum_weights_kernel, data_count, count, model_width, parts),
        out_shape=[jax.ShapeDtypeStruct(s, low) for s in full]
        + [
            jax.ShapeDtypeStruct((16, padded), f32),
            jax.ShapeDtypeStruct((8, padded), f32),
            jax.ShapeDtypeStruct((padded, 128), f32),
        ],
        in_specs=[anywhere] * 5 + [near],
        out_specs=[anywhere] * 5 + [near] * 3,
        scratch_shapes=[pltpu.VMEM(a.shape, low) for a in (qkv, out)]
        + [pltpu.VMEM((span, height, a.shape[1]), low) for a in (qkv, out)]
        + [pltpu.VMEM(s, low) for s in full]
        + [
            pltpu.VMEM((count - 1, height, lanes), low),
            pltpu.VMEM(qkv_low.shape, low),
            pltpu.VMEM(gate_up_low.shape, low),
            pltpu.VMEM((padded, 128), f32),
            pltpu.VMEM((8, (max(units, wide) + 127) // 128 * 128), f32),
            pltpu.VMEM((count, 16, padded), f32),
            dma((3 * data_count + 5,)),
            dma((n * data_count,)),
            dma((2 * span,)),
            dma((2 * span,)),
            dma((n * span,)),
            dma((n * span,)),
            dma((count - 1,)),
            dma((count - 1,)),
            dma((count - 1,)),
            dma((count,)),
        ],
        compiler_params=pltpu.CompilerParams(
            collective_id=2, has_side_effects=True, vmem_limit_bytes=56 << 20
        ),
        cost_estimate=pl.CostEstimate(
            flops=padded * units, bytes_accessed=200 << 20, transcendentals=0
        ),
        name="sum_weights",
    )(ff_grads, qkv, out, qkv_low, gate_up_low, squares)


def update_kernel(tensor_count, *refs):
    grads, rel_g = refs[:5], refs[5]
    weights, (rel_w, attn_w, ff_w) = refs[6:13], refs[13:16]
    shared_ref, own_ref, tall_ref = refs[16:19]
    news, rel_n = refs[19:26], refs[26]
    along, rel_r = refs[27:34], refs[34]
    across, rel_c = refs[35:42], refs[42]
    attn_n, attn_m, ff_n, ff_m = refs[43:47]
    first = pl.program_id(0) == 0
    f32 = jnp.float32
    width = attn_w.shape[1]
    lanes = weights[3].shape[1]
    slots = rel_w.shape[1]
    tiny = 1e-30

    def step_rate(lane, size):
        return step_scale * jnp.sqrt(shared_ref[10:11, lane : lane + 1] / size)

    qkv = grads[3][...].astype(f32)
    for k, (row, square, own, at) in enumerate(
        (
            (3, 4, 0, 0),
            (4, 5, 1, 0),
            (8, 7, 2, 0),
            (0, 0, 3, 0),
            (1, 1, 3, lanes),
            (2, 2, 3, 2 * lanes),
            (9, 6, 4, 0),
        )
    ):
        here = weights[k].shape[1]
        if own == 3:
            grad = qkv[:, at : at + lanes]
        else:
            grad = grads[own][...].astype(f32)
        cols = here * tensor_count
        size = width * cols
        level = total(shared_ref[row : row + 1, :width], 1) / size + tiny
        rate = step_rate(square, size)
        row_factor = lax.rsqrt((tall_ref[:, row : row + 1] / cols + tiny) / level) * rate
        col_moment = own_ref[own : own + 1, at : at + here] / width + tiny
        news[k][...] = weights[k][...] - grad * row_factor * lax.rsqrt(col_moment)

        @pl.when(first)
        def _():
            along[k][...] = (shared_ref[row : row + 1, :width] / cols + tiny).reshape(width)
            across[k][...] = col_moment.reshape(here)

    @pl.when(first)
    def _():
        rel = rel_g[:, :slots].astype(f32)
        cols = slots * tensor_count
        size = BUCKETS * cols
        row_sums = shared_ref[7:8, :BUCKETS]
        level = total(row_sums, 1) / size + tiny
        row_factor = lax.rsqrt((tall_ref[:BUCKETS, 7:8] / cols + tiny) / level) * step_rate(3, size)
        col_moment = total(rel * rel, 0) / BUCKETS + tiny
        rel_n[...] = rel_w[...] - rel * row_factor * lax.rsqrt(col_moment)
        rel_r[...] = row_sums / cols + tiny
        rel_c[...] = col_moment
        for gain, row, new, moment_out in ((attn_w, 5, attn_n, attn_m), (ff_w, 6, ff_n, ff_m)):
            value = gain[...]
            grad = shared_ref[row : row + 1, :width] / value
            moment = grad * grad + tiny
            rate = step_scale * jnp.sqrt(total(value * value, 1) / width)
            stepped = value - rate * grad * lax.rsqrt(total(moment, 1) / width)
            new[...] = stepped.reshape(width)
            moment_out[...] = moment.reshape(width)


def update(grads, weights, rel_w, attn_w, ff_w, shared, own, tall, chunks=8):
    tensor_count = lax.axis_size("mp")
    width = weights[0].shape[0]
    slots = rel_w.shape[1]
    f32 = jnp.float32

    def blocks(array):
        return pl.BlockSpec((width // chunks, array.shape[1]), lambda i: (i, 0))

    def fixed(rows, cols, at=0):
        return pl.BlockSpec((rows, cols), lambda i: (at, 0))

    def line(size):
        return pl.BlockSpec((size,), lambda i: (0,))

    matrices = [blocks(w) for w in weights]
    rel_spec = fixed(BUCKETS, slots)
    columns = [w.shape[1] for w in weights]
    return pl.pallas_call(
        functools.partial(update_kernel, tensor_count),
        grid=(chunks,),
        in_specs=[
            *[blocks(g) for g in grads],
            fixed(BUCKETS, grads[3].shape[1], width // BUCKETS),
            *matrices,
            rel_spec,
            fixed(1, width),
            fixed(1, width),
            fixed(*shared.shape),
            fixed(*own.shape),
            blocks(tall),
        ],
        out_specs=[*matrices, rel_spec]
        + [line(width)] * 7
        + [fixed(1, BUCKETS)]
        + [line(c) for c in columns]
        + [fixed(1, slots)]
        + [line(width)] * 4,
        out_shape=[jax.ShapeDtypeStruct(w.shape, f32) for w in weights]
        + [jax.ShapeDtypeStruct(rel_w.shape, f32)]
        + [jax.ShapeDtypeStruct((width,), f32)] * 7
        + [jax.ShapeDtypeStruct((1, BUCKETS), f32)]
        + [jax.ShapeDtypeStruct((c,), f32) for c in columns]
        + [jax.ShapeDtypeStruct((1, slots), f32)]
        + [jax.ShapeDtypeStruct((width,), f32)] * 4,
        compiler_params=pltpu.CompilerParams(vmem_limit_bytes=58 << 20),
        cost_estimate=pl.CostEstimate(
            flops=40 * width * columns[0], bytes_accessed=36 * width * columns[0], transcendentals=0
        ),
        name="update",
    )(
        *grads, grads[3], *weights, rel_w,
        attn_w.reshape(1, width), ff_w.reshape(1, width), shared, own, tall,
    )


def turn_order(count):
    return [sorted(range(count), key=lambda b: (abs(b - place), b < place)) for place in range(count)]


def look_up(table, row, column):
    found = jnp.int32(0)
    for r, entries in enumerate(table):
        for c, entry in enumerate(entries):
            found = jnp.where((row == r) & (column == c), jnp.int32(entry), found)
    return found


def feed_forward_kernel(
    data_count,
    count,
    parts,
    normed_hbm,
    cot_hbm,
    gate_up_hbm,
    down_hbm,
    out_hbm,
    dn_ref,
    pieces_hbm,
    normed,
    cot,
    gate_up,
    down,
    hidden,
    d_gate_up,
    outgoing,
    incoming,
    stage,
    grads,
    land_whole,
    land_most,
    land_rest,
    load_sem,
    stage_sem,
    gather_send,
    gather_recv,
    sum_send,
    sum_recv,
    down_send,
    down_recv,
):
    place = lax.axis_index("mp")
    row = lax.axis_index("dp")
    block_len, width = dn_ref.shape
    units = down.shape[1]
    part_len = block_len // parts
    last = count - 1
    has_left = place > 0
    has_right = place < last

    loads = [
        pltpu.make_async_copy(normed_hbm, normed.at[place], load_sem.at[0]),
        pltpu.make_async_copy(gate_up_hbm.at[pl.ds(0, width)], gate_up, load_sem.at[1]),
        pltpu.make_async_copy(down_hbm, down, load_sem.at[2]),
        pltpu.make_async_copy(cot_hbm, cot, load_sem.at[3]),
    ]
    for load in loads:
        load.start()

    ways = orders(data_count)
    span = data_count - 1
    most = land_most.shape[2]
    shares = (
        (0, 0, units, 0, land_whole.at[0]),
        (1, 0, units, 1, land_whole.at[1]),
        (2, 0, most, 0, land_most),
        (2, most, units - most, 1, land_rest),
    )
    flies = [Butterfly(ways[way], k * span) for k, (_, _, _, way, _) in enumerate(shares)]
    stages = len(ways[0])
    sems = (down_send, down_recv)
    views = [row_pieces(grads.at[i], data_count, at, lanes) for i, at, lanes, _, _ in shares]

    barrier = pltpu.get_barrier_semaphore()
    for s in range(stages):
        pl.semaphore_signal(
            barrier, inc=1, device_id=flies[0].partner(s), device_id_type=pl.DeviceIdType.MESH
        )
    for side, there in ((-1, has_left), (1, has_right)):

        @pl.when(there)
        def _():
            pl.semaphore_signal(
                barrier, inc=1, device_id=(row, place + side), device_id_type=pl.DeviceIdType.MESH
            )

    pl.semaphore_wait(barrier, stages + has_left.astype(jnp.int32) + has_right.astype(jnp.int32))

    def pass_block(block, side, slot):
        return pltpu.make_async_remote_copy(
            src_ref=normed.at[block],
            dst_ref=normed.at[block],
            send_sem=gather_send.at[slot],
            recv_sem=gather_recv.at[block],
            device_id=(row, place + side),
            device_id_type=pl.DeviceIdType.MESH,
        )

    def rows_of(part):
        return pl.ds(pl.multiple_of(part * part_len, part_len), part_len)

    def pass_sum(block, part, side, slot):
        return pltpu.make_async_remote_copy(
            src_ref=outgoing.at[block, rows_of(part)],
            dst_ref=incoming.at[slot, rows_of(part)],
            send_sem=sum_send.at[block, part],
            recv_sem=sum_recv.at[slot, part],
            device_id=(row, place + side),
            device_id_type=pl.DeviceIdType.MESH,
        )

    def landing(block, side):
        return jnp.where((side == -1) & (place + side == block), count, block)

    loads[0].wait()
    for side, there in ((-1, has_left), (1, has_right)):

        @pl.when(there)
        def _():
            pass_block(place, side, count + (side + 1) // 2).start()

    for load in loads[1:]:
        load.wait()

    def store_out(turn, block):
        return pltpu.make_async_copy(stage.at[turn % 2], out_hbm.at[block], stage_sem.at[turn % 2])

    table = turn_order(count)
    root = 0.7978845608028654

    def turn_body(turn, carry):
        block = look_up(table, place, turn)
        distance = jnp.abs(block - place)

        @pl.when((distance > 0) & ((block > place) | (place + distance > last)))
        def _():
            for side in (1, -1):
                other = place + side * distance

                @pl.when((other >= 0) & (other <= last))
                def _():
                    pass_block(other, 0, other).wait_recv()

                    @pl.when((place - side >= 0) & (place - side <= last))
                    def _():
                        pass_block(other, -side, other).start()

        acts = product(normed[block], gate_up[...])
        gate_act = acts[:, :units]
        up_act = acts[:, units:]
        squared = gate_act * gate_act
        bend = jnp.tanh(root * gate_act * (1.0 + 0.044715 * squared))
        half = 0.5 * (1.0 + bend)
        gelu = gate_act * half
        hidden[block] = (gelu * up_act).astype(jnp.bfloat16)
        d_hidden = product(cot[block], down[...])
        slope = half + 0.5 * gate_act * (1.0 - bend * bend) * (root * (1.0 + 0.134145 * squared))
        d_gate_up[block, :, :units] = (d_hidden * up_act * slope).astype(jnp.bfloat16)
        d_gate_up[block, :, units:] = (d_hidden * gelu).astype(jnp.bfloat16)
        term = right_inner(d_gate_up[block], gate_up[...])

        @pl.when(block == place)
        def _():
            dn_ref[...] = term

        @pl.when(block != place)
        def _():
            outgoing[block] = term.astype(jnp.bfloat16)

        for side, is_end in ((1, place == 0), (-1, place == last)):

            @pl.when(is_end & (block != place))
            def _():
                for part in range(parts):
                    pass_sum(block, part, side, landing(block, side)).start()

        @pl.when(turn >= 2)
        def _():
            store_out(turn, block).wait()

        stage[turn % 2] = right_inner(hidden[block], down[...]).astype(jnp.bfloat16)
        store_out(turn, block).start()
        return carry

    lax.fori_loop(0, count, turn_body, 0)

    def relay(key):
        def relay_part(part, carry):
            for side, block in ((1, key), (-1, last - key)):
                through = (block > place) & has_left if side == 1 else (block < place) & has_right

                @pl.when(through)
                def _():
                    pass_sum(block, part, side, block).wait_recv()
                    rows = rows_of(part)
                    outgoing[block, rows] = (
                        outgoing[block, rows].astype(jnp.float32)
                        + incoming[block, rows].astype(jnp.float32)
                    ).astype(jnp.bfloat16)
                    pass_sum(block, part, side, landing(block, side)).start()

            return carry

        lax.fori_loop(0, parts, relay_part, 0)

    def flat(ref):
        return ref[...].reshape(count * block_len, ref.shape[2])

    sent = []

    def halve(k, s):
        copies = flies[k].halve(s, views[k], shares[k][4], sems)
        for copy in copies:
            copy.start()
        sent.extend(copies)
        return copies

    def add_halve(k, s, copies):
        flies[k].add(s, views[k], shares[k][4], copies)
        return halve(k, s + 1) if s + 1 < stages else None

    def weigh(i, left, right):
        grads[i, :width] = left_inner(left, right).astype(jnp.bfloat16)

    grads[:, width:] = jnp.zeros((3, grads.shape[1] - width, units), jnp.bfloat16)
    weigh(2, flat(cot), flat(hidden))
    flights = [None, None, halve(2, 0), halve(3, 0)]
    for key in range(1, last):
        relay(key)
    gate_side = d_gate_up[:, :, :units].reshape(count * block_len, units)
    weigh(0, flat(normed), gate_side)
    flights[0] = halve(0, 0)
    for k in (2, 3):
        flights[k] = add_halve(k, 0, flights[k])
    up_side = d_gate_up[:, :, units:].reshape(count * block_len, units)
    weigh(1, flat(normed), up_side)
    flights[1] = halve(1, 0)
    for k in (0, 1):
        flights[k] = add_halve(k, 0, flights[k])
    relay(last)
    for s in range(1, stages - 1):
        for k in (2, 3, 0, 1):
            flights[k] = add_halve(k, s, flights[k])

    for side, there in ((1, has_left), (-1, has_right)):

        @pl.when(there)
        def _():
            slot = place if side == 1 else count

            def add_part(part, carry):
                pass_sum(place, part, side, slot).wait_recv()
                rows = rows_of(part)
                dn_ref[rows] += incoming[slot, rows].astype(jnp.float32)
                return carry

            lax.fori_loop(0, parts, add_part, 0)

    for k in (2, 3, 0, 1):
        add_halve(k, stages - 1, flights[k])
    mine = pl.ds(pl.multiple_of(row * pieces_hbm.shape[1], pieces_hbm.shape[1]), pieces_hbm.shape[1])
    save = pltpu.make_async_copy(grads.at[:, mine], pieces_hbm, load_sem.at[0])
    save.start()
    for copy in sent:
        copy.wait_send()

    for side, there in ((-1, has_left), (1, has_right)):

        @pl.when(there)
        def _():
            pass_block(place, side, count + (side + 1) // 2).wait_send()

    for block in range(count):

        @pl.when((block != place) & has_left & has_right)
        def _():
            pass_block(block, 1, block).wait_send()

        @pl.when(block != place)
        def _():
            for part in range(parts):
                pass_sum(block, part, 1, block).wait_send()

    for turn in (count - 2, count - 1):
        store_out(turn, 0).wait()
    save.wait()


def feed_forward(normed, cot_all, gate_up, down):
    count = lax.axis_size("mp")
    data_count = lax.axis_size("dp")
    block_len, width = normed.shape
    units = down.shape[1]
    padded = gate_up.shape[0]
    parts = 2
    low = jnp.bfloat16
    anywhere = pl.BlockSpec(memory_space=pl.ANY)
    dma = pltpu.SemaphoreType.DMA
    tokens = count * block_len
    height = padded // data_count
    span = data_count - 1
    most = (units // 2 + 127) // 128 * 128
    out_terms, dn, pieces = pl.pallas_call(
        functools.partial(feed_forward_kernel, data_count, count, parts),
        out_shape=[
            jax.ShapeDtypeStruct((count, block_len, width), low),
            jax.ShapeDtypeStruct((block_len, width), jnp.float32),
            jax.ShapeDtypeStruct((3, height, units), low),
        ],
        in_specs=[anywhere] * 4,
        out_specs=[anywhere, pl.BlockSpec(memory_space=pltpu.VMEM), anywhere],
        scratch_shapes=[
            pltpu.VMEM((count, block_len, width), low),
            pltpu.VMEM((count, block_len, width), low),
            pltpu.VMEM((width, 2 * units), low),
            pltpu.VMEM((width, units), low),
            pltpu.VMEM((count, block_len, units), low),
            pltpu.VMEM((count, block_len, 2 * units), low),
            pltpu.VMEM((count, block_len, width), low),
            pltpu.VMEM((count + 1, block_len, width), low),
            pltpu.VMEM((2, block_len, width), low),
            pltpu.VMEM((3, padded, units), low),
            pltpu.VMEM((2, span, height, units), low),
            pltpu.VMEM((span, height, most), low),
            pltpu.VMEM((span, height, units - most), low),
            dma((4,)),
            dma((2,)),
            dma((count + 2,)),
            dma((count,)),
            dma((count, parts)),
            dma((count + 1, parts)),
            dma((4 * span,)),
            dma((4 * span,)),
        ],
        compiler_params=pltpu.CompilerParams(
            collective_id=1, has_side_effects=True, vmem_limit_bytes=60 << 20
        ),
        cost_estimate=pl.CostEstimate(
            flops=18 * tokens * width * units,
            bytes_accessed=12 * width * units + 6 * tokens * width,
            transcendentals=tokens * units,
        ),
        name="feed_forward",
    )(normed, cot_all.reshape(count, block_len, width), gate_up, down)
    return out_terms.reshape(tokens, width), dn, pieces


def ff_parts(units):
    most = (units // 2 + 127) // 128 * 128
    return ((0, 0, units, 0), (1, 0, units, 1), (2, 0, most, 0), (2, most, units - most, 1))


def attend_back_kernel(
    data_count,
    count,
    slots,
    dn_hbm,
    middle_hbm,
    cot_hbm,
    gain_ref,
    proj_hbm,
    own_hbm,
    qkv_hbm,
    probs_hbm,
    norm_hbm,
    qkv_low_hbm,
    bucket_ref,
    ff_hbm,
    d_middle_hbm,
    terms_hbm,
    d_qkv_w_hbm,
    d_out_w_hbm,
    spread_hbm,
    dn,
    middle,
    cot,
    proj,
    own,
    qkv,
    probs,
    norm,
    qkv_low,
    d_own,
    grad,
    diag,
    dk,
    dv,
    d_qkv,
    terms,
    d_qkv_w,
    d_out_w,
    load_sem,
    probs_sem,
    cross_send,
    cross_recv,
    up_send,
    up_recv,
):
    place = lax.axis_index("mp")
    me = lax.axis_index("dp")
    block_len, width = dn.shape
    seq_len = qkv.shape[0]
    lanes = slots * HD
    padded = d_qkv_w.shape[0]
    steps = seq_len // BLOCK
    f32 = jnp.float32
    low = jnp.bfloat16

    loads = []

    def load(src, dst):
        copy = pltpu.make_async_copy(src, dst, load_sem.at[len(loads)])
        copy.start()
        loads.append(copy)

    load(dn_hbm, dn)
    load(middle_hbm, middle)
    load(cot_hbm, cot)
    load(proj_hbm, proj)
    load(own_hbm, own)
    load(qkv_hbm, qkv)
    load(norm_hbm, norm)
    load(qkv_low_hbm, qkv_low)
    height = padded // data_count
    mine = pl.ds(pl.multiple_of(me * height, height), height)
    load(ff_hbm, spread_hbm.at[:, mine])

    ways = orders(data_count)
    stages = len(ways[0])
    parts = ff_parts(spread_hbm.shape[2])
    span = data_count - 1
    flies = [Butterfly(ways[way], k * span) for k, (_, _, _, way) in enumerate(parts)]
    views = [row_pieces(spread_hbm.at[i], data_count, at, wide) for i, at, wide, _ in parts]
    others = [(place + k) % count for k in range(1, count)]
    greet([flies[0].partner(s) for s in range(1, stages)] + [(me, other) for other in others])
    sent = []

    def start(copies):
        for copy in copies:
            copy.start()
        sent.extend(copies)
        return copies

    flights = [
        start(
            fly.double(
                stages - 1, view, (up_send, up_recv), ff_hbm.at[i, :, pl.ds(at, wide)]
            )
        )
        for fly, view, (i, at, wide, _) in zip(flies, views, parts)
    ]

    table = turn_order(count)

    def fetch(t):
        per = block_len // BLOCK
        block = look_up(table, place, t // per) * per + t % per
        rows = pl.ds(pl.multiple_of(block * BLOCK, BLOCK), BLOCK)
        return block, pltpu.make_async_copy(
            probs_hbm.at[:, rows], probs.at[t % 2], probs_sem.at[t % 2]
        )

    fetch(0)[1].start()
    diag[...] = jnp.zeros_like(diag)
    dk[...] = jnp.zeros_like(dk)
    dv[...] = jnp.zeros_like(dv)
    for copy in loads[:3]:
        copy.wait()
    d_middle = cot[...].astype(f32) + norm_back(middle[...], gain_ref[...].reshape(1, width), dn[...])
    middle[...] = d_middle
    save_middle = pltpu.make_async_copy(middle, d_middle_hbm, load_sem.at[0])
    save_middle.start()
    cot[...] = d_middle.astype(low)
    loads[3].wait()
    d_all = product(cot[...], proj[:width]).astype(low)

    def own_rows(who):
        return pl.ds(pl.multiple_of(who * block_len, block_len), block_len)

    for k in range(count):
        d_own[k] = d_all[:, k * lanes : (k + 1) * lanes]
    start(
        [
            pltpu.make_async_remote_copy(
                src_ref=d_own.at[other],
                dst_ref=grad.at[own_rows(place)],
                send_sem=cross_send.at[k],
                recv_sem=cross_recv.at[place],
                device_id=(me, other),
                device_id_type=pl.DeviceIdType.MESH,
            )
            for k, other in enumerate(others)
        ]
    )
    grad[own_rows(place)] = d_own[place]
    loads[4].wait()
    d_out_w[width:] = jnp.zeros((padded - width, count * lanes), low)
    d_out_w[:width] = left_inner(cot[...], own[...]).astype(low)
    save_out = pltpu.make_async_copy(d_out_w, d_out_w_hbm, load_sem.at[1])
    save_out.start()
    loads[5].wait()

    def pass_on(s):
        for k, (fly, view) in enumerate(zip(flies, views)):
            for copy in flights[k]:
                copy.wait_recv()
            if s > 1:
                flights[k] = start(fly.double(s - 1, view, (up_send, up_recv)))

    def back_block(t, carry):
        per = block_len // BLOCK

        @pl.when((t > 0) & (t % per == 0))
        def _():
            who = look_up(table, place, t // per)
            pltpu.make_async_remote_copy(
                src_ref=d_own.at[0],
                dst_ref=grad.at[own_rows(who)],
                send_sem=cross_send.at[0],
                recv_sem=cross_recv.at[who],
                device_id=(me, who),
                device_id_type=pl.DeviceIdType.MESH,
            ).wait_recv()

        @pl.when(t + 1 < steps)
        def _():
            fetch(t + 1)[1].start()

        block, arrival = fetch(t)
        arrival.wait()
        rows = pl.ds(pl.multiple_of(block * BLOCK, BLOCK), BLOCK)
        window = pl.ds(pl.multiple_of((steps - 1 - block) * BLOCK, BLOCK), seq_len)
        queries = qkv[rows, 0:lanes]
        keys = qkv[:, lanes : 2 * lanes]
        values = qkv[:, 2 * lanes : 3 * lanes]
        d_query = jnp.zeros((BLOCK, lanes), f32)
        for slot in range(slots):
            weight = probs[t % 2, slot]
            slot_grad = slot_lanes(grad[rows], slot)
            d_probs = right_inner(slot_grad, values)
            delta = jnp.sum(weight * d_probs, axis=-1, keepdims=True)
            d_scores = (weight * (d_probs - delta)).astype(low)
            d_query = d_query + slot_lanes(product(d_scores, keys), slot)
            dk[...] += left_inner(slot_lanes(queries, slot), d_scores)
            dv[...] += left_inner(slot_grad, weight.astype(low))
            diag[slot, :, window] += d_scores.astype(f32)
        d_qkv[rows, 0:lanes] = d_query.astype(low)
        return carry

    loads[8].wait()
    pass_on(stages - 1)
    lax.fori_loop(0, steps, back_block, 0)
    for s in reversed(range(2, stages - 1)):
        pass_on(s)
    d_qkv[:, lanes : 2 * lanes] = dk[...].T.astype(low)
    d_qkv[:, 2 * lanes : 3 * lanes] = dv[...].T.astype(low)
    for copy in loads[6:8]:
        copy.wait()
    terms[...] = right_inner(d_qkv[...], qkv_low[:width]).astype(low)
    save_terms = pltpu.make_async_copy(terms, terms_hbm, load_sem.at[2])
    save_terms.start()
    d_qkv_w[:width] = left_inner(norm[...], d_qkv[...]).astype(low)
    d_qkv_w[width:] = jnp.zeros((padded - width, 3 * lanes), low)
    sums = []
    for slot in range(slots):
        level = diag[slot]
        rest = BLOCK // 2
        while rest >= 1:
            level = pltpu.roll(level[:rest], rest, 1) + level[rest:]
            rest //= 2
        sums.append(level)
    sums = jnp.concatenate(sums + [jnp.zeros((128 - slots, 2 * seq_len), f32)], axis=0)
    d_rel = lax.dot_general(
        onehot_rows(bucket_ref[...]),
        sums,
        (((1,), (1,)), ((), ())),
        precision=highest,
        preferred_element_type=f32,
    )
    d_qkv_w[width : width + BUCKETS, :128] = d_rel.astype(low)
    save_qkv = pltpu.make_async_copy(d_qkv_w, d_qkv_w_hbm, load_sem.at[3])
    save_qkv.start()
    if stages > 1:
        pass_on(1)
    for copy in sent:
        copy.wait_send()
    for copy in (save_middle, save_out, save_terms, save_qkv):
        copy.wait()


def attend_back(dn, middle, cot, gain, proj_all, own, qkv, probs, norm, qkv_low, bucket, ff_pieces):
    count = lax.axis_size("mp")
    data_count = lax.axis_size("dp")
    seq_len = qkv.shape[0]
    slots = probs.shape[0]
    lanes = slots * HD
    block_len, width = dn.shape
    padded = qkv_low.shape[0]
    _, _, units = ff_pieces.shape
    far = pl.BlockSpec(memory_space=pltpu.HBM)
    near = pl.BlockSpec(memory_space=pltpu.VMEM)
    dma = pltpu.SemaphoreType.DMA
    low, f32 = jnp.bfloat16, jnp.float32
    span = data_count - 1
    scratch = [
        (dn.shape, f32),
        (middle.shape, f32),
        (cot.shape, low),
        (proj_all.shape, low),
        (own.shape, low),
        (qkv.shape, low),
        ((2, slots, BLOCK, seq_len), f32),
        (norm.shape, low),
        (qkv_low.shape, low),
        ((count, block_len, lanes), low),
        ((seq_len, lanes), low),
        ((slots, BLOCK, 2 * seq_len), f32),
        ((lanes, seq_len), f32),
        ((lanes, seq_len), f32),
        (qkv.shape, low),
        ((seq_len, width), low),
        ((padded, 3 * lanes), low),
        ((padded, count * lanes), low),
    ]
    return pl.pallas_call(
        functools.partial(attend_back_kernel, data_count, count, slots),
        in_specs=[far] * 3 + [near] + [far] * 6 + [near, far],
        out_specs=[far] * 5,
        out_shape=[
            jax.ShapeDtypeStruct((block_len, width), f32),
            jax.ShapeDtypeStruct((seq_len, width), low),
            jax.ShapeDtypeStruct((padded, 3 * lanes), low),
            jax.ShapeDtypeStruct((padded, count * lanes), low),
            jax.ShapeDtypeStruct((3, padded, units), low),
        ],
        scratch_shapes=[pltpu.VMEM(shape, dtype) for shape, dtype in scratch]
        + [
            dma((10,)),
            dma((2,)),
            dma((count - 1,)),
            dma((count,)),
            dma((4 * span,)),
            dma((4 * span,)),
        ],
        compiler_params=pltpu.CompilerParams(
            collective_id=3, has_side_effects=True, vmem_limit_bytes=56 << 20
        ),
        cost_estimate=pl.CostEstimate(
            flops=16 * slots * seq_len * seq_len * HD, bytes_accessed=140 << 20, transcendentals=0
        ),
        name="attend_back",
    )(dn, middle, cot, gain, proj_all, own, qkv, probs, norm, qkv_low, bucket, ff_pieces)


def onehot_rows(bucket):
    rows = lax.broadcasted_iota(jnp.int32, (BUCKETS, bucket.shape[1]), 0)
    return jnp.where(rows == bucket, 1.0, 0.0)


def front_kernel(
    data_count,
    count,
    slots,
    x_hbm,
    cot_hbm,
    query_hbm,
    key_hbm,
    value_hbm,
    out_hbm,
    gate_hbm,
    up_hbm,
    down_hbm,
    segments_ref,
    bucket_ref,
    rel_ref,
    attn_gain_ref,
    ff_gain_ref,
    norm_far,
    cot_far,
    own_cot_far,
    qkv_far,
    probs_far,
    own_far,
    middle_far,
    normed_far,
    proj_far,
    qkv_low_far,
    gate_up_far,
    down_far,
    squares_ref,
    x_in,
    cot_in,
    x,
    norm,
    cot,
    thin,
    wide,
    gate_low,
    up_low,
    down_low,
    blank,
    proj,
    qkv_low,
    qkv,
    tilt,
    seg_col,
    probs,
    mixed,
    own,
    normed,
    load_sem,
    save_sem,
    probs_sem,
    norm_send,
    norm_recv,
    cot_send,
    cot_recv,
    cross_send,
    cross_recv,
    side_send,
    side_recv,
    mix_send,
    mix_recv,
):
    place = lax.axis_index("mp")
    me = lax.axis_index("dp")
    last = count - 1
    f32, low = jnp.float32, jnp.bfloat16
    block_len, width = x.shape
    seq_len = count * block_len
    lanes = slots * HD
    padded = proj.shape[0]
    height = padded // data_count
    units = gate_low.shape[1]
    mesh_id = pl.DeviceIdType.MESH
    others = [(place + k) % count for k in range(1, count)]
    peers = [(me + k) % data_count for k in range(1, data_count)]

    def load(k, from_ref, to_ref):
        copy = pltpu.make_async_copy(from_ref, to_ref, load_sem.at[k])
        copy.start()
        return copy

    load_x = load(0, x_hbm, x_in)
    load_thin = [
        load(1 + k, ref, thin.at[k])
        for k, ref in enumerate((out_hbm, query_hbm, key_hbm, value_hbm))
    ]
    load_cot = load(5, cot_hbm, cot_in)
    load_gate = load(6, gate_hbm, wide.at[0])
    load_up = load(7, up_hbm, wide.at[1])
    greet([(me, other) for other in others] + [(peer, place) for peer in peers])

    saves = []

    def save(from_ref, to_ref):
        copy = pltpu.make_async_copy(from_ref, to_ref, save_sem.at[len(saves)])
        copy.start()
        saves.append(copy)

    sent = []

    def start(copy):
        copy.start()
        sent.append(copy)

    def pass_block(buffer, sems, block, side, slot):
        return pltpu.make_async_remote_copy(
            src_ref=buffer.at[block],
            dst_ref=buffer.at[block],
            send_sem=sems[0].at[slot],
            recv_sem=sems[1].at[block],
            device_id=(me, place + side),
            device_id_type=mesh_id,
        )

    def inside(block):
        return (block >= 0) & (block <= last)

    norm_sems = (norm_send, norm_recv)
    cot_sems = (cot_send, cot_recv)

    def take(buffer, sems, distance):
        for side in (1, -1):
            other = place + side * distance

            @pl.when(inside(other))
            def _():
                pass_block(buffer, sems, other, side, other).wait_recv()

                @pl.when(inside(place - side))
                def _():
                    pass_block(buffer, sems, other, -side, other).start()

    def send_own(buffer, sems, side):
        return pass_block(buffer, sems, place, side, count + (side + 1) // 2)

    def cot_may_go(distance):
        for side in (1, -1):
            behind = place if side == 1 else last - place

            @pl.when((behind == distance) & inside(place + side))
            def _():
                if distance == 0:
                    send_own(norm, norm_sems, side).wait_send()
                else:
                    far_end = 0 if side == 1 else last
                    pass_block(norm, norm_sems, far_end, side, far_end).wait_send()
                send_own(cot, cot_sems, side).start()

    between = inside(place - 1) & inside(place + 1)

    load_x.wait()
    x[...] = x_in[...].T.astype(f32)
    norm[place] = rms_norm(x[...], attn_gain_ref[...].reshape(1, width)).astype(low)
    for side in (1, -1):

        @pl.when(inside(place + side))
        def _():
            send_own(norm, norm_sems, side).start()

    load_cot.wait()
    cot[place] = cot_in[...].T
    save(cot.at[place], own_cot_far)

    lane = lax.broadcasted_iota(jnp.int32, (1, lanes), 1)
    slot_of = place * slots + lane // HD
    lane_mask = jnp.where((slot_of < 5) | (slot_of == 6), 1.0, 0.0)
    for copy in load_thin:
        copy.wait()

    def lanes_of(who):
        return pl.ds(pl.multiple_of(who * lanes, lanes), lanes)

    def rows_of(who):
        return pl.ds(pl.multiple_of(who * height, height), height)

    proj[width:, lanes_of(place)] = jnp.zeros((padded - width, lanes), low)
    qkv_low[width:] = jnp.zeros((padded - width, 3 * lanes), low)
    blank[...] = jnp.zeros_like(blank)
    column = lax.broadcasted_iota(jnp.int32, (1, 128), 1)
    squares = jnp.zeros((1, 128), f32)

    def square_of(values, at):
        return jnp.where(column == at, total(total(values * values, 1), 0), 0.0)

    masked = (thin[0] * lane_mask).astype(low)
    proj[:width, lanes_of(place)] = masked

    def proj_copy(src, dst, sems, send_slot, recv_slot, device):
        return pltpu.make_async_remote_copy(
            src_ref=src,
            dst_ref=dst,
            send_sem=sems[0].at[send_slot],
            recv_sem=sems[1].at[recv_slot],
            device_id=device,
            device_id_type=mesh_id,
        )

    cross, aside = (cross_send, cross_recv), (side_send, side_recv)
    for k, other in enumerate(others):
        view = proj.at[rows_of(me), lanes_of(place)]
        start(proj_copy(view, view, cross, k, count - 2 - k, (me, other)))
    for k in range(3):
        qkv_low[:width, k * lanes : (k + 1) * lanes] = (thin[1 + k] * lane_mask).astype(low)
        squares = squares + square_of(thin[1 + k], k)
    squares = squares + square_of(thin[0], 6) + square_of(rel_ref[...], 3)
    save(qkv_low, qkv_low_far)

    onehot = onehot_rows(bucket_ref[...])
    vector = lax.dot_general(
        rel_ref[...],
        onehot,
        (((0,), (0,)), ((), ())),
        precision=highest,
        preferred_element_type=f32,
    )
    for slot in range(slots):
        spread = jnp.broadcast_to(vector[slot : slot + 1, :], (BLOCK, 2 * seq_len))
        tilt[slot] = pltpu.roll(spread, 2 * seq_len - BLOCK + 1, 1, stride=1, stride_axis=0)
    seg_row = segments_ref[...].astype(f32)
    seg_col[...] = jnp.broadcast_to(seg_row, (128, seq_len)).T

    arrivals = []
    for k, other in enumerate(others):
        view = proj.at[rows_of(me), lanes_of(other)]
        proj_copy(view, view, cross, k, k, (me, other)).wait_recv()
        at = k * (data_count - 1)
        for j, peer in enumerate(peers):
            start(proj_copy(view, view, aside, at + j, at + data_count - 2 - j, (peer, place)))
            come = proj.at[rows_of(peer), lanes_of(other)]
            arrivals.append(proj_copy(come, come, aside, at + j, at + j, (peer, place)))

    def own_rows(who):
        return pl.ds(pl.multiple_of(who * block_len, block_len), block_len)

    def project(block):
        qkv[own_rows(block)] = product(norm[block], qkv_low[:width]).astype(low)

    def project_at(distance):
        for side in (1, -1):
            other = place + side * distance

            @pl.when(inside(other))
            def _():
                project(other)

    project(place)
    load_gate.wait()
    gate_low[...] = wide[0].astype(low)
    squares = squares + square_of(wide[0], 4)
    load_down = load(6, down_hbm, wide.at[0])
    rows_used = pl.ds(0, width)
    save(gate_low, gate_up_far.at[rows_used, pl.ds(0, units)])
    load_up.wait()
    up_low[...] = wide[1].astype(low)
    squares = squares + square_of(wide[1], 5)
    save(up_low, gate_up_far.at[rows_used, pl.ds(units, units)])
    save(blank, gate_up_far.at[pl.ds(width, padded - width)])
    take(norm, norm_sems, 1)
    cot_may_go(0)
    project_at(1)
    load_down.wait()
    down_low[...] = wide[0].astype(low)
    squares = squares + square_of(wide[0], 7)
    save(down_low, down_far)
    squares_ref[...] = squares
    for distance in range(2, count):
        take(norm, norm_sems, distance)
        cot_may_go(distance - 1)
        project_at(distance)
    save(qkv, qkv_far)
    save(norm, norm_far)

    @pl.when(between)
    def _():
        take(cot, cot_sems, 1)

    steps = seq_len // BLOCK
    per = block_len // BLOCK
    table = [order[::-1] for order in turn_order(count)]

    def store_probs(t, block):
        rows = pl.ds(pl.multiple_of(block * BLOCK, BLOCK), BLOCK)
        return pltpu.make_async_copy(probs.at[t % 2], probs_far.at[:, rows], probs_sem.at[t % 2])

    def mix_copy(owner):
        return pltpu.make_async_remote_copy(
            src_ref=mixed.at[own_rows(owner)],
            dst_ref=own.at[:, lanes_of(place)],
            send_sem=mix_send.at[owner],
            recv_sem=mix_recv.at[place],
            device_id=(me, owner),
            device_id_type=mesh_id,
        )

    def attend_block(t, carry):
        owner = look_up(table, place, t // per)
        block = owner * per + t % per
        rows = pl.ds(pl.multiple_of(block * BLOCK, BLOCK), BLOCK)
        window = pl.ds(pl.multiple_of((steps - 1 - block) * BLOCK, BLOCK), seq_len)
        same_doc = seg_col[rows, 0:1] == seg_row
        queries = qkv[rows, 0:lanes]
        keys = qkv[:, lanes : 2 * lanes]
        values = qkv[:, 2 * lanes : 3 * lanes]
        result = jnp.zeros((BLOCK, lanes), f32)

        @pl.when(t >= 2)
        def _():
            store_probs(t, block).wait()

        for slot in range(slots):
            scores = right_inner(slot_lanes(queries, slot), keys) + tilt[slot, :, window]
            scores = jnp.where(same_doc, scores, -1e30)
            peak = jnp.max(scores, axis=-1, keepdims=True)
            raised = jnp.exp(scores - peak)
            weight = raised * (1.0 / jnp.sum(raised, axis=-1, keepdims=True))
            probs[t % 2, slot] = weight
            result = result + slot_lanes(product(weight.astype(low), values), slot)
        store_probs(t, block).start()
        mixed[rows] = result.astype(low)

        @pl.when((t % per == per - 1) & (owner != place))
        def _():
            mix_copy(owner).start()

        return carry

    lax.fori_loop(0, steps, attend_block, 0)
    own[:, lanes_of(place)] = mixed[own_rows(place)]

    @pl.when(between)
    def _():
        for distance in range(2, count):
            take(cot, cot_sems, distance)

    for arrival in arrivals:
        arrival.wait_recv()
    save(proj, proj_far)
    for k, other in enumerate(others):
        pltpu.make_async_remote_copy(
            src_ref=mixed.at[own_rows(other)],
            dst_ref=own.at[:, lanes_of(other)],
            send_sem=mix_send.at[other],
            recv_sem=mix_recv.at[other],
            device_id=(me, other),
            device_id_type=mesh_id,
        ).wait_recv()
    save(own, own_far)
    x[...] = x[...] + right_inner(own[...], proj[:width])
    save(x, middle_far)
    normed[...] = rms_norm(x[...], ff_gain_ref[...].reshape(1, width)).astype(low)
    save(normed, normed_far)

    @pl.when(jnp.logical_not(between))
    def _():
        for distance in range(1, count):
            take(cot, cot_sems, distance)

    save(cot, cot_far)
    for t in (0, 1):
        store_probs(t, 0).wait()
    for copy in saves:
        copy.wait()
    for copy in sent:
        copy.wait_send()
    for k, other in enumerate(others):
        mix_copy(other).wait_send()
    for buffer, sems in ((norm, norm_sems), (cot, cot_sems)):
        for side in (1, -1):
            behind = place if side == 1 else last - place
            unwaited = behind > 0 if buffer is norm else behind >= 0

            @pl.when(unwaited & inside(place + side))
            def _():
                send_own(buffer, sems, side).wait_send()

        for block in range(1, last) if buffer is norm else range(count):

            @pl.when((block != place) & between)
            def _():
                pass_block(buffer, sems, block, 1, block).wait_send()


def front(x, cot, weights, segments, bucket, rel_bias, attn_gain, ff_gain):
    count = lax.axis_size("mp")
    data_count = lax.axis_size("dp")
    query, key, value, out, gate, up, down = weights
    width, block_len = x.shape
    lanes = query.shape[1]
    slots = lanes // HD
    units = gate.shape[1]
    seq_len = count * block_len
    piece = 16 * data_count
    padded = (width + piece - 1) // piece * piece
    low, f32 = jnp.bfloat16, jnp.float32
    far = pl.BlockSpec(memory_space=pltpu.HBM)
    near = pl.BlockSpec(memory_space=pltpu.VMEM)
    dma = pltpu.SemaphoreType.DMA
    outs = [
        ((count, block_len, width), low),
        ((count, block_len, width), low),
        ((block_len, width), low),
        ((seq_len, 3 * lanes), low),
        ((slots, seq_len, seq_len), f32),
        ((block_len, count * lanes), low),
        ((block_len, width), f32),
        ((block_len, width), low),
        ((padded, count * lanes), low),
        ((padded, 3 * lanes), low),
        ((padded, 2 * units), low),
        ((width, units), low),
        ((1, 128), f32),
    ]
    scratch = [
        ((width, block_len), low),
        ((width, block_len), low),
        ((block_len, width), f32),
        ((count, block_len, width), low),
        ((count, block_len, width), low),
        ((4, width, lanes), f32),
        ((2, width, units), f32),
        ((width, units), low),
        ((width, units), low),
        ((width, units), low),
        ((padded - width, 2 * units), low),
        ((padded, count * lanes), low),
        ((padded, 3 * lanes), low),
        ((seq_len, 3 * lanes), low),
        ((slots, BLOCK, 2 * seq_len), f32),
        ((seq_len, 128), f32),
        ((2, slots, BLOCK, seq_len), f32),
        ((seq_len, lanes), low),
        ((block_len, count * lanes), low),
        ((block_len, width), low),
    ]
    sides = (count - 1) * (data_count - 1)
    return pl.pallas_call(
        functools.partial(front_kernel, data_count, count, slots),
        in_specs=[far] * 9 + [near] * 5,
        out_specs=[far] * 12 + [near],
        out_shape=[jax.ShapeDtypeStruct(shape, dtype) for shape, dtype in outs],
        scratch_shapes=[pltpu.VMEM(shape, dtype) for shape, dtype in scratch]
        + [
            dma((8,)),
            dma((16,)),
            dma((2,)),
            dma((count + 2,)),
            dma((count,)),
            dma((count + 2,)),
            dma((count,)),
            dma((count - 1,)),
            dma((count - 1,)),
            dma((sides,)),
            dma((sides,)),
            dma((count,)),
            dma((count,)),
        ],
        compiler_params=pltpu.CompilerParams(
            collective_id=0, has_side_effects=True, vmem_limit_bytes=60 << 20
        ),
        cost_estimate=pl.CostEstimate(
            flops=8 * slots * seq_len * seq_len * HD,
            bytes_accessed=300 << 20,
            transcendentals=slots * seq_len * seq_len,
        ),
        name="front",
    )(
        x, cot, query, key, value, out, gate, up, down,
        segments, bucket, rel_bias, attn_gain, ff_gain,
    )


def local(
    layer_in,
    segment_ids,
    bucket_table,
    attn_gain,
    query_weight,
    key_weight,
    value_weight,
    out_weight,
    rel_bias,
    ff_gain,
    gate_weight,
    up_weight,
    down_weight,
    cotangent,
):
    model_width = layer_in.shape[2]
    slots_here = rel_bias.shape[1]
    layer_in = layer_in[0]
    down_turned = down_weight.T
    out_turned = out_weight.T
    bucket = jnp.pad(bucket_table, (0, 1)).reshape(1, -1)
    (
        flat_norm,
        flat_cot,
        own_cot,
        qkv,
        probs,
        own_attended,
        middle,
        normed_ff_local,
        proj_all,
        qkv_low,
        gate_up_low,
        down_low,
        squares,
    ) = front(
        layer_in.T,
        cotangent[0].T,
        (query_weight, key_weight, value_weight, out_turned, gate_weight, up_weight, down_turned),
        segment_ids,
        bucket,
        rel_bias,
        attn_gain,
        ff_gain,
    )
    flat_norm = flat_norm.reshape(-1, model_width)
    residual_in = layer_in.astype(jnp.float32)
    out_terms, dn_ff, ff_pieces = feed_forward(normed_ff_local, flat_cot, gate_up_low, down_low)
    d_middle, dn_attn_terms, d_qkv_w, d_out_w, ff_grads = attend_back(
        dn_ff,
        middle,
        own_cot,
        ff_gain,
        proj_all,
        own_attended,
        qkv,
        probs,
        flat_norm,
        qkv_low,
        bucket,
        ff_pieces,
    )
    ff_branch = lax.psum_scatter(out_terms, "mp", scatter_dimension=0, tiled=True)
    layer_out = (middle + ff_branch.astype(jnp.float32)).astype(jnp.bfloat16)
    dn_attn = lax.psum_scatter(dn_attn_terms, "mp", scatter_dimension=0, tiled=True)
    *grads, shared, own, tall = sum_weights(
        ff_grads, d_qkv_w, d_out_w, qkv_low, gate_up_low, squares, model_width
    )
    weights = (
        gate_weight,
        up_weight,
        down_turned,
        query_weight,
        key_weight,
        value_weight,
        out_turned,
    )
    results = update(grads, weights, rel_bias, attn_gain, ff_gain, shared, own, tall)
    news, along, across = results[:8], results[8:16], results[16:24]
    new_attn_gain, attn_gain_moment, new_ff_gain, ff_gain_moment = results[24:]
    gate, up, down, query, key, value, out, rel = zip(news, along, across)
    rel = (rel[0], rel[1].reshape(BUCKETS), rel[2].reshape(slots_here))
    down = (down[0].T, down[2], down[1])
    out = (out[0].T, out[2], out[1])
    input_grad = d_middle + norm_back(residual_in, attn_gain, dn_attn.astype(jnp.float32))
    input_grad = input_grad.astype(jnp.bfloat16)
    return (
        layer_out[None],
        input_grad[None],
        new_attn_gain,
        attn_gain_moment,
        *query,
        *key,
        *value,
        *out,
        *rel,
        new_ff_gain,
        ff_gain_moment,
        *gate,
        *up,
        *down,
    )


def solution(mesh):
    return jax.shard_map(
        local,
        mesh=mesh,
        in_specs=(
            P("dp", "mp", None),
            P("dp", None),
            P(),
            P(),
            P(None, "mp"),
            P(None, "mp"),
            P(None, "mp"),
            P("mp", None),
            P(None, "mp"),
            P(),
            P(None, "mp"),
            P(None, "mp"),
            P("mp", None),
            P("dp", "mp", None),
        ),
        out_specs=(
            P("dp", "mp", None),
            P("dp", "mp", None),
            P(),
            P(),
            P(None, "mp"),
            P(),
            P("mp"),
            P(None, "mp"),
            P(),
            P("mp"),
            P(None, "mp"),
            P(),
            P("mp"),
            P("mp", None),
            P("mp"),
            P(),
            P(None, "mp"),
            P(),
            P("mp"),
            P(),
            P(),
            P(None, "mp"),
            P(),
            P("mp"),
            P(None, "mp"),
            P(),
            P("mp"),
            P("mp", None),
            P("mp"),
            P(),
        ),
        check_vma=False,
    )
```

```python
import functools

import jax
import jax.numpy as jnp
from jax import lax
from jax.experimental import pallas as pl
from jax.experimental.pallas import tpu as pltpu
from jax.sharding import PartitionSpec as P

HD = 64
BUCKETS = 32
BLOCK = 128


highest = lax.Precision.HIGHEST
step_scale = 0.3


def rms_norm(values, gain):
    return values * lax.rsqrt(jnp.mean(values * values, axis=-1, keepdims=True) + 1e-06) * gain


def norm_back(values, gain, grad):
    scale = lax.rsqrt(jnp.mean(values * values, axis=-1, keepdims=True) + 1e-06)
    unit = values * scale
    pull = grad * gain
    return scale * (pull - unit * jnp.mean(pull * unit, axis=-1, keepdims=True))


def product(left_side, right_side):
    return jnp.dot(left_side, right_side, preferred_element_type=jnp.float32)


def left_inner(left_side, right_side):
    return lax.dot_general(
        left_side, right_side, (((0,), (0,)), ((), ())), preferred_element_type=jnp.float32
    )


def right_inner(left_side, right_side):
    return lax.dot_general(
        left_side, right_side, (((1,), (1,)), ((), ())), preferred_element_type=jnp.float32
    )


def slot_lanes(values, slot):
    lane = lax.broadcasted_iota(jnp.int32, values.shape, 1)
    return jnp.where((lane >= slot * HD) & (lane < (slot + 1) * HD), values, jnp.zeros_like(values))


class Butterfly:
    def __init__(self, order, base):
        self.order = order
        self.me = lax.axis_index("dp")
        self.line = lax.axis_index("mp")
        self.base = base
        self.offsets = []
        total = 0
        for s in range(len(order)):
            self.offsets.append(total)
            total += 1 << (len(order) - 1 - s)

    def bit(self, b):
        return (self.me // b) % 2

    def partner(self, s):
        b = self.order[s]
        return (self.me + b * (1 - 2 * self.bit(b)), self.line)

    def width(self, s):
        return 1 << (len(self.order) - 1 - s)

    def piece(self, s, j, mine):
        b = self.order[s]
        found = sum(k * self.bit(k) for k in self.order[:s])
        found = found + b * (self.bit(b) if mine else 1 - self.bit(b))
        for i, k in enumerate(self.order[s + 1 :]):
            found = found + k * ((j // (1 << i)) % 2)
        return found

    def copy(self, src, dst, sems, slot, s):
        return pltpu.make_async_remote_copy(
            src_ref=src,
            dst_ref=dst,
            send_sem=sems[0].at[self.base + slot],
            recv_sem=sems[1].at[self.base + slot],
            device_id=self.partner(s),
            device_id_type=pl.DeviceIdType.MESH,
        )

    def halve(self, s, source, landing, sems):
        at = self.offsets[s]
        return [
            self.copy(source(self.piece(s, j, False)), landing.at[at + j], sems, at + j, s)
            for j in range(self.width(s))
        ]

    def add(self, s, kept, landing, copies):
        at = self.offsets[s]
        for j, copy in enumerate(copies):
            copy.wait_recv()
            mine = kept(self.piece(s, j, True))
            mine[...] = (mine[...].astype(jnp.float32) + landing[at + j].astype(jnp.float32)).astype(
                jnp.bfloat16
            )

    def double(self, s, whole, sems, first=None):
        at = self.offsets[s]
        copies = []
        for j in range(self.width(s)):
            view = whole(self.piece(s, j, True))
            copies.append(self.copy(view if first is None else first, view, sems, at + j, s))
        return copies


def orders(data_count):
    bits = [1 << i for i in range(data_count.bit_length() - 1)]
    return (bits, bits[:1] + bits[:0:-1])


def greet(peers):
    barrier = pltpu.get_barrier_semaphore()
    for peer in peers:
        pl.semaphore_signal(barrier, inc=1, device_id=peer, device_id_type=pl.DeviceIdType.MESH)
    pl.semaphore_wait(barrier, len(peers))


def row_pieces(ref, data_count, at=0, lanes=None):
    rows = ref.shape[0] // data_count
    columns = pl.ds(at, ref.shape[1] if lanes is None else lanes)
    return lambda q: ref.at[pl.ds(pl.multiple_of(q * rows, rows), rows), columns]


def total(values, axis):
    return jnp.sum(values, axis=axis, keepdims=True)


def sum_weights_kernel(data_count, count, model_width, parts, *refs):
    ff_hbm, qkv_hbm, out_hbm, qkv_low, gate_up_low, squares_ref = refs[:6]
    weights_hbm, full, weights = refs[6:13], refs[13:18], refs[18:25]
    shared_ref, own_ref, tall_ref = refs[25:28]
    kept, landings = refs[28:30], refs[30:32]
    (
        cross,
        qkv_w,
        gate_up_w,
        tall,
        cols,
        gathered,
        load_sem,
        down_send,
        down_recv,
        up_send,
        up_recv,
        cross_send,
        cross_recv,
        share_send,
        share_recv,
    ) = refs[32:]
    me = lax.axis_index("dp")
    place = lax.axis_index("mp")
    span = data_count - 1
    ways = orders(data_count)
    stages = len(ways[0])
    down, up = (down_send, down_recv), (up_send, up_recv)
    padded, units = full[0].shape
    lanes = full[4].shape[1]
    height = padded // data_count
    f32 = jnp.float32

    whole = [row_pieces(ref, data_count) for ref in full]
    source = [row_pieces(ref, data_count) for ref in (qkv_hbm, out_hbm)]
    keep = [row_pieces(ref, data_count) for ref in kept]
    halvers = [Butterfly(ways[1 - i], i * span) for i in range(2)]
    doublers = [Butterfly(ways[way], k * span) for k, (_, _, _, way) in enumerate(parts)]
    views = [row_pieces(full[i], data_count, at, wide) for i, at, wide, _ in parts]

    loads = []

    def load(src, dst):
        copy = pltpu.make_async_copy(src, dst, load_sem.at[len(loads)])
        copy.start()
        loads.append(copy)

    early = [k for k, part in enumerate(parts) if part[0] < 3]
    late = [k for k, part in enumerate(parts) if part[0] >= 3]
    begin = {k: stages_left(parts[k], stages) - 1 for k in early}
    for k in early:
        i, at, wide, _ = parts[k]
        for j in range(doublers[k].width(begin[k])):
            q = doublers[k].piece(begin[k], j, True)
            load(row_pieces(ff_hbm.at[i], data_count, at, wide)(q), views[k](q))
    for i, fly in enumerate(halvers):
        for j in range(fly.width(0)):
            q = fly.piece(0, j, True)
            load(source[i](q), keep[i](q))
    load(qkv_low, qkv_w)
    load(gate_up_low, gate_up_w)
    others = [(place + k) % count for k in range(1, count)]
    greet([halvers[0].partner(s) for s in range(stages)] + [(me, other) for other in others])

    sent = []

    def start(copies):
        for copy in copies:
            copy.start()
        sent.extend(copies)
        return copies

    halves = [start(fly.halve(0, source[i], landings[i], down)) for i, fly in enumerate(halvers)]
    tall[...] = jnp.zeros_like(tall)
    cols[...] = jnp.zeros_like(cols)
    for copy in loads:
        copy.wait()
    fetched = []
    for i, (far_weight, near_weight) in enumerate(zip(weights_hbm, weights)):
        copy = pltpu.make_async_copy(far_weight, near_weight, load_sem.at[i])
        copy.start()
        fetched.append(copy)

    doubles = {}

    def spread(s, which):
        for k in which:
            doubles[k] = start(doublers[k].double(s, views[k], up))

    for k in early:
        spread(begin[k], [k])

    def note(k, q):
        i, start_lane, wide, _ = parts[k]
        rows = pl.ds(pl.multiple_of(q * height, height), height)
        grad = views[k](q)[...].astype(f32)
        if i == 3:
            at = lax.broadcasted_iota(jnp.int32, grad.shape, 0) + q * height
            grad = jnp.where(at < model_width, grad, 0.0)
        squares = grad * grad
        cols[i : i + 1, start_lane : start_lane + wide] += total(squares, 0)
        if i < 2:
            tall[rows, 3 + i : 4 + i] = total(squares, 1)
            weight = gate_up_w[rows, i * units : (i + 1) * units].astype(f32)
            tall[rows, 6:7] += total(grad * weight, 1)
        elif i == 3:
            for k in range(3):
                tall[rows, k : k + 1] = total(squares[:, k * lanes : (k + 1) * lanes], 1)
            tall[rows, 5:6] = total(grad * qkv_w[rows].astype(f32), 1)
        else:
            lane = 8 if i == 2 else 9
            tall[rows, lane : lane + 1] += total(squares, 1)

    for s in range(stages):
        for i, fly in enumerate(halvers):
            fly.add(s, keep[i], landings[i], halves[i])
            if s + 1 < stages:
                halves[i] = start(fly.halve(s + 1, keep[i], landings[i], down))
        if s == min(1, stages - 1):
            for k in early:
                if begin[k] > 0:
                    for copy in doubles[k]:
                        copy.wait_recv()
                    spread(0, [k])
    crossing = row_pieces(kept[1], data_count)(me)

    def lanes_of(other):
        return pl.ds(pl.multiple_of(other * lanes, lanes), lanes)

    start(
        [
            pltpu.make_async_remote_copy(
                src_ref=crossing.at[:, lanes_of(other)],
                dst_ref=cross.at[count - 2 - k],
                send_sem=cross_send.at[k],
                recv_sem=cross_recv.at[count - 2 - k],
                device_id=(me, other),
                device_id_type=pl.DeviceIdType.MESH,
            )
            for k, other in enumerate(others)
        ]
    )
    whole[3](me)[...] = keep[0](me)[...]
    spread(stages - 1, late[:1])
    summed = crossing[:, lanes_of(place)].astype(f32)
    for k in range(count - 1):
        pltpu.make_async_remote_copy(
            src_ref=cross.at[k],
            dst_ref=cross.at[k],
            send_sem=cross_send.at[k],
            recv_sem=cross_recv.at[k],
            device_id=(me, others[0]),
            device_id_type=pl.DeviceIdType.MESH,
        ).wait_recv()
        summed = summed + cross[k].astype(f32)
    whole[4](me)[...] = summed.astype(jnp.bfloat16)
    spread(stages - 1, late[1:])

    def note_pieces(k, s, mine):
        fly = doublers[k]

        def note_piece(j, carry):
            note(k, fly.piece(s, j, mine))
            return carry

        lax.fori_loop(0, fly.width(s), note_piece, 0)

    for k in early:
        note_pieces(k, 0, True)
    for k in late:
        note(k, me)
    for k in early:
        for copy in doubles[k]:
            copy.wait_recv()
        note_pieces(k, 0, False)
    for s in reversed(range(stages)):
        for k in late:
            for copy in doubles[k]:
                copy.wait_recv()
            if s > 0:
                doubles[k] = start(doublers[k].double(s - 1, views[k], up))
        for k in late:
            note_pieces(k, s, False)

    slots_rel = full[3][model_width : model_width + BUCKETS, :128].astype(f32)
    tall[:BUCKETS, 7:8] = total(slots_rel * slots_rel, 1)
    share = gathered.at[place]
    flat = tall[...].T[0:16]
    row = lax.broadcasted_iota(jnp.int32, flat.shape, 0)
    spare = jnp.concatenate([squares_ref[...], jnp.zeros((1, padded - 128), f32)], axis=1)
    share[...] = jnp.where(row == 10, spare, flat).astype(jnp.bfloat16)
    shares = start(
        [
            pltpu.make_async_remote_copy(
                src_ref=share,
                dst_ref=share,
                send_sem=share_send.at[k],
                recv_sem=share_recv.at[place],
                device_id=(me, other),
                device_id_type=pl.DeviceIdType.MESH,
            )
            for k, other in enumerate(others)
        ]
    )
    own_ref[...] = jnp.zeros_like(own_ref)
    own_ref[:, : cols.shape[1]] = cols[...]
    for k, other in enumerate(others):
        pltpu.make_async_remote_copy(
            src_ref=gathered.at[other],
            dst_ref=gathered.at[other],
            send_sem=share_send.at[k],
            recv_sem=share_recv.at[other],
            device_id=(me, other),
            device_id_type=pl.DeviceIdType.MESH,
        ).wait_recv()
    summed = gathered[0].astype(f32)
    for k in range(1, count):
        summed = summed + gathered[k].astype(f32)
    shared_ref[...] = summed
    tall_ref[...] = jnp.concatenate([summed, jnp.zeros((112, padded), f32)], axis=0).T
    for copy in fetched:
        copy.wait()
    for copy in sent:
        copy.wait_send()


def sum_weights(ff_grads, qkv, out, qkv_low, gate_up_low, squares, weights, model_width):
    count = lax.axis_size("mp")
    data_count = lax.axis_size("dp")
    far = pl.BlockSpec(memory_space=pltpu.HBM)
    near = pl.BlockSpec(memory_space=pltpu.VMEM)
    dma = pltpu.SemaphoreType.DMA
    low, f32 = jnp.bfloat16, jnp.float32
    span = data_count - 1
    units = ff_grads.shape[2]
    padded, wide = qkv.shape
    height = padded // data_count
    lanes = out.shape[1] // count
    full = [(padded, units)] * 3 + [(padded, wide), (padded, lanes)]
    parts = (*ff_parts(units), (3, 0, wide, 1), (4, 0, lanes, 0))
    n = len(parts)
    return pl.pallas_call(
        functools.partial(sum_weights_kernel, data_count, count, model_width, parts),
        out_shape=[pltpu.VMEM(s, low) for s in full]
        + [pltpu.VMEM(w.shape, f32) for w in weights]
        + [
            jax.ShapeDtypeStruct((16, padded), f32),
            jax.ShapeDtypeStruct((8, padded), f32),
            jax.ShapeDtypeStruct((padded, 128), f32),
        ],
        in_specs=[far] * 5 + [near] + [far] * len(weights),
        out_specs=[near] * (8 + len(weights)),
        scratch_shapes=[pltpu.VMEM(a.shape, low) for a in (qkv, out)]
        + [pltpu.VMEM((span, height, a.shape[1]), low) for a in (qkv, out)]
        + [
            pltpu.VMEM((count - 1, height, lanes), low),
            pltpu.VMEM(qkv_low.shape, low),
            pltpu.VMEM(gate_up_low.shape, low),
            pltpu.VMEM((padded, 128), f32),
            pltpu.VMEM((8, (max(units, wide) + 127) // 128 * 128), f32),
            pltpu.VMEM((count, 16, padded), low),
            dma((3 * data_count + 5,)),
            dma((2 * span,)),
            dma((2 * span,)),
            dma((n * span,)),
            dma((n * span,)),
            dma((count - 1,)),
            dma((count - 1,)),
            dma((count - 1,)),
            dma((count,)),
        ],
        compiler_params=pltpu.CompilerParams(
            collective_id=2, has_side_effects=True, vmem_limit_bytes=22 << 20
        ),
        cost_estimate=pl.CostEstimate(
            flops=padded * units, bytes_accessed=200 << 20, transcendentals=0
        ),
        name="sum_weights",
    )(ff_grads, qkv, out, qkv_low, gate_up_low, squares, *weights)


def update_kernel(tensor_count, *refs):
    grads = refs[:5]
    weights, (rel_w, attn_w, ff_w) = refs[5:12], refs[12:15]
    shared_ref, own_ref, tall_ref = refs[15:18]
    news, rel_n = refs[18:25], refs[25]
    along, rel_r = refs[26:33], refs[33]
    across, rel_c = refs[34:41], refs[41]
    attn_n, attn_m, ff_n, ff_m = refs[42:46]
    first = pl.program_id(0) == 0
    height = news[0].shape[0]
    here_rows = pl.ds(pl.multiple_of(pl.program_id(0) * height, height), height)
    f32 = jnp.float32
    width = attn_w.shape[1]
    lanes = weights[3].shape[1]
    slots = rel_w.shape[0]
    tiny = 1e-30

    def step_rate(lane, size):
        return step_scale * jnp.sqrt(shared_ref[10:11, lane : lane + 1] / size)

    qkv = grads[3][here_rows].astype(f32)
    for k, (row, square, own, at) in enumerate(
        (
            (3, 4, 0, 0),
            (4, 5, 1, 0),
            (8, 7, 2, 0),
            (0, 0, 3, 0),
            (1, 1, 3, lanes),
            (2, 2, 3, 2 * lanes),
            (9, 6, 4, 0),
        )
    ):
        here = weights[k].shape[1]
        if own == 3:
            grad = qkv[:, at : at + lanes]
        else:
            grad = grads[own][here_rows].astype(f32)
        cols = here * tensor_count
        size = width * cols
        level = total(shared_ref[row : row + 1, :width], 1) / size + tiny
        rate = step_rate(square, size)
        row_factor = lax.rsqrt((tall_ref[:, row : row + 1] / cols + tiny) / level) * rate
        col_moment = own_ref[own : own + 1, at : at + here] / width + tiny
        news[k][...] = weights[k][here_rows] - grad * row_factor * lax.rsqrt(col_moment)

        @pl.when(first)
        def _():
            along[k][...] = (shared_ref[row : row + 1, :width] / cols + tiny).reshape(width)
            across[k][...] = col_moment.reshape(here)

    @pl.when(first)
    def _():
        rel = grads[3][width : width + BUCKETS, :128].astype(f32)
        cols = slots * tensor_count
        size = BUCKETS * cols
        row_moment = shared_ref[7:8, :BUCKETS] / cols + tiny
        level = total(row_moment, 1) / BUCKETS
        row_factor = lax.rsqrt(row_moment / level) * step_rate(3, size)
        turned = rel.T[:slots]
        col_moment = total(turned * turned, 1) / BUCKETS + tiny
        rel_n[...] = rel_w[...] - turned * row_factor * lax.rsqrt(col_moment)
        rel_r[...] = row_moment.reshape(BUCKETS)
        rel_c[...] = (total(rel * rel, 0) / BUCKETS + tiny)[:, :slots]
        for gain, row, new, moment_out in ((attn_w, 5, attn_n, attn_m), (ff_w, 6, ff_n, ff_m)):
            value = gain[...]
            grad = shared_ref[row : row + 1, :width] / value
            moment = grad * grad + tiny
            rate = step_scale * jnp.sqrt(total(value * value, 1) / width)
            stepped = value - rate * grad * lax.rsqrt(total(moment, 1) / width)
            new[...] = stepped.reshape(width)
            moment_out[...] = moment.reshape(width)


def update(grads, weights, rel_w, attn_w, ff_w, shared, own, tall, chunks=4):
    tensor_count = lax.axis_size("mp")
    width = weights[0].shape[0]
    slots = rel_w.shape[0]
    f32 = jnp.float32

    def blocks(array):
        return pl.BlockSpec((width // chunks, array.shape[1]), lambda i: (i, 0))

    def fixed(rows, cols, at=0):
        return pl.BlockSpec((rows, cols), lambda i: (at, 0))

    def line(size):
        return pl.BlockSpec((size,), lambda i: (0,))

    matrices = [blocks(w) for w in weights]
    near = pl.BlockSpec(memory_space=pltpu.VMEM)
    rel_spec = fixed(slots, BUCKETS)
    columns = [w.shape[1] for w in weights]
    return pl.pallas_call(
        functools.partial(update_kernel, tensor_count),
        grid=(chunks,),
        in_specs=[
            *[near] * (len(grads) + len(weights)),
            rel_spec,
            fixed(1, width),
            fixed(1, width),
            fixed(*shared.shape),
            fixed(*own.shape),
            blocks(tall),
        ],
        out_specs=[*matrices, rel_spec]
        + [line(width)] * 7
        + [line(BUCKETS)]
        + [line(c) for c in columns]
        + [fixed(1, slots)]
        + [line(width)] * 4,
        out_shape=[jax.ShapeDtypeStruct(w.shape, f32) for w in weights]
        + [jax.ShapeDtypeStruct(rel_w.shape, f32)]
        + [jax.ShapeDtypeStruct((width,), f32)] * 7
        + [jax.ShapeDtypeStruct((BUCKETS,), f32)]
        + [jax.ShapeDtypeStruct((c,), f32) for c in columns]
        + [jax.ShapeDtypeStruct((1, slots), f32)]
        + [jax.ShapeDtypeStruct((width,), f32)] * 4,
        compiler_params=pltpu.CompilerParams(vmem_limit_bytes=16 << 20),
        cost_estimate=pl.CostEstimate(
            flops=40 * width * columns[0], bytes_accessed=36 * width * columns[0], transcendentals=0
        ),
        name="update",
    )(
        *grads, *weights, rel_w,
        attn_w.reshape(1, width), ff_w.reshape(1, width), shared, own, tall,
    )


def turn_order(count):
    return [sorted(range(count), key=lambda b: (abs(b - place), b < place)) for place in range(count)]


def look_up(table, row, column):
    found = jnp.int32(0)
    for r, entries in enumerate(table):
        for c, entry in enumerate(entries):
            found = jnp.where((row == r) & (column == c), jnp.int32(entry), found)
    return found


def feed_forward_kernel(
    data_count,
    count,
    parts,
    normed_hbm,
    cot_hbm,
    gate_up_hbm,
    down_hbm,
    out_hbm,
    dn_ref,
    pieces_hbm,
    normed,
    cot,
    gate_up,
    down,
    hidden,
    d_gate_up,
    outgoing,
    incoming,
    stage,
    grads,
    land_whole,
    land_most,
    land_rest,
    load_sem,
    stage_sem,
    gather_send,
    gather_recv,
    sum_send,
    sum_recv,
    down_send,
    down_recv,
):
    place = lax.axis_index("mp")
    row = lax.axis_index("dp")
    block_len, width = dn_ref.shape
    units = down.shape[1]
    part_len = block_len // parts
    last = count - 1
    has_left = place > 0
    has_right = place < last

    loads = [
        pltpu.make_async_copy(normed_hbm, normed.at[place], load_sem.at[0]),
        pltpu.make_async_copy(gate_up_hbm.at[pl.ds(0, width)], gate_up, load_sem.at[1]),
        pltpu.make_async_copy(down_hbm, down, load_sem.at[2]),
        pltpu.make_async_copy(cot_hbm, cot, load_sem.at[3]),
    ]
    for load in loads:
        load.start()

    ways = orders(data_count)
    span = data_count - 1
    most = land_most.shape[2]
    shares = (
        (0, 0, units, 0, land_whole.at[0]),
        (1, 0, units, 1, land_whole.at[1]),
        (2, 0, most, 0, land_most),
        (2, most, units - most, 1, land_rest),
    )
    flies = [Butterfly(ways[way], k * span) for k, (_, _, _, way, _) in enumerate(shares)]
    stages = len(ways[0])
    sems = (down_send, down_recv)
    views = [row_pieces(grads.at[i], data_count, at, lanes) for i, at, lanes, _, _ in shares]

    barrier = pltpu.get_barrier_semaphore()
    for s in range(stages):
        pl.semaphore_signal(
            barrier, inc=1, device_id=flies[0].partner(s), device_id_type=pl.DeviceIdType.MESH
        )
    for side, there in ((-1, has_left), (1, has_right)):

        @pl.when(there)
        def _():
            pl.semaphore_signal(
                barrier, inc=1, device_id=(row, place + side), device_id_type=pl.DeviceIdType.MESH
            )

    pl.semaphore_wait(barrier, stages + has_left.astype(jnp.int32) + has_right.astype(jnp.int32))

    def pass_block(block, side, slot):
        return pltpu.make_async_remote_copy(
            src_ref=normed.at[block],
            dst_ref=normed.at[block],
            send_sem=gather_send.at[slot],
            recv_sem=gather_recv.at[block],
            device_id=(row, place + side),
            device_id_type=pl.DeviceIdType.MESH,
        )

    def rows_of(part):
        return pl.ds(pl.multiple_of(part * part_len, part_len), part_len)

    def pass_sum(block, part, side, slot):
        return pltpu.make_async_remote_copy(
            src_ref=outgoing.at[block, rows_of(part)],
            dst_ref=incoming.at[slot, rows_of(part)],
            send_sem=sum_send.at[block, part],
            recv_sem=sum_recv.at[slot, part],
            device_id=(row, place + side),
            device_id_type=pl.DeviceIdType.MESH,
        )

    def landing(block, side):
        return jnp.where((side == -1) & (place + side == block), count, block)

    loads[0].wait()
    for side, there in ((-1, has_left), (1, has_right)):

        @pl.when(there)
        def _():
            pass_block(place, side, count + (side + 1) // 2).start()

    for load in loads[1:]:
        load.wait()

    def store_out(turn, block):
        return pltpu.make_async_copy(stage.at[turn % 2], out_hbm.at[block], stage_sem.at[turn % 2])

    table = turn_order(count)
    root = 0.7978845608028654

    def turn_body(turn, carry):
        block = look_up(table, place, turn)
        distance = jnp.abs(block - place)

        @pl.when((distance > 0) & ((block > place) | (place + distance > last)))
        def _():
            for side in (1, -1):
                other = place + side * distance

                @pl.when((other >= 0) & (other <= last))
                def _():
                    pass_block(other, 0, other).wait_recv()

                    @pl.when((place - side >= 0) & (place - side <= last))
                    def _():
                        pass_block(other, -side, other).start()

        acts = product(normed[block], gate_up[...])
        gate_act = acts[:, :units]
        up_act = acts[:, units:]
        squared = gate_act * gate_act
        bend = jnp.tanh(root * gate_act * (1.0 + 0.044715 * squared))
        half = 0.5 * (1.0 + bend)
        gelu = gate_act * half
        hidden[block] = (gelu * up_act).astype(jnp.bfloat16)
        d_hidden = product(cot[block], down[...])
        slope = half + 0.5 * gate_act * (1.0 - bend * bend) * (root * (1.0 + 0.134145 * squared))
        d_gate_up[block, :, :units] = (d_hidden * up_act * slope).astype(jnp.bfloat16)
        d_gate_up[block, :, units:] = (d_hidden * gelu).astype(jnp.bfloat16)
        term = right_inner(d_gate_up[block], gate_up[...])

        @pl.when(block == place)
        def _():
            dn_ref[...] = term

        @pl.when(block != place)
        def _():
            outgoing[block] = term.astype(jnp.bfloat16)

        for side, is_end in ((1, place == 0), (-1, place == last)):

            @pl.when(is_end & (block != place))
            def _():
                for part in range(parts):
                    pass_sum(block, part, side, landing(block, side)).start()

        @pl.when(turn >= 2)
        def _():
            store_out(turn, block).wait()

        stage[turn % 2] = right_inner(hidden[block], down[...]).astype(jnp.bfloat16)
        store_out(turn, block).start()
        return carry

    lax.fori_loop(0, count, turn_body, 0)

    def relay_side(key, side):
        owner = key if side == 1 else last - key
        through = (owner > place) & has_left if side == 1 else (owner < place) & has_right

        @pl.when(through)
        def _():
            def relay_part(part, carry):
                pass_sum(owner, part, side, owner).wait_recv()
                rows = rows_of(part)
                outgoing[owner, rows] = (
                    outgoing[owner, rows].astype(jnp.float32)
                    + incoming[owner, rows].astype(jnp.float32)
                ).astype(jnp.bfloat16)
                pass_sum(owner, part, side, landing(owner, side)).start()
                return carry

            lax.fori_loop(0, parts, relay_part, 0)

    def relay(key, between=None):
        for turn in (0, 1):
            for side in (1, -1):
                sooner = 2 * place <= last if side == 1 else 2 * place > last

                @pl.when(sooner if turn == 0 else jnp.logical_not(sooner))
                def _():
                    relay_side(key, side)

            if turn == 0 and between is not None:
                between()

    def flat(ref):
        return ref[...].reshape(count * block_len, ref.shape[2])

    sent = []

    def halve(k, s):
        copies = flies[k].halve(s, views[k], shares[k][4], sems)
        for copy in copies:
            copy.start()
        sent.extend(copies)
        return copies

    def add_halve(k, s, copies):
        flies[k].add(s, views[k], shares[k][4], copies)
        return halve(k, s + 1) if s + 1 < stages else None

    def weigh(i, left, right):
        grads[i, :width] = left_inner(left, right).astype(jnp.bfloat16)

    grads[:, width:] = jnp.zeros((3, grads.shape[1] - width, units), jnp.bfloat16)
    weigh(2, flat(cot), flat(hidden))
    flights = [None, None, halve(2, 0), halve(3, 0)]
    for key in range(1, last):
        relay(key)
    gate_side = d_gate_up[:, :, :units].reshape(count * block_len, units)
    weigh(0, flat(normed), gate_side)
    flights[0] = halve(0, 0)
    for k in (2, 3):
        flights[k] = add_halve(k, 0, flights[k])
    up_side = d_gate_up[:, :, units:].reshape(count * block_len, units)
    weigh(1, flat(normed), up_side)
    flights[1] = halve(1, 0)
    for k in (0, 1):
        flights[k] = add_halve(k, 0, flights[k])

    def halve_on():
        for s in range(1, stages - 1):
            for k in (2, 3, 0, 1):
                flights[k] = add_halve(k, s, flights[k])

    relay(last, halve_on)

    for side, there in ((1, has_left), (-1, has_right)):

        @pl.when(there)
        def _():
            slot = place if side == 1 else count

            def add_part(part, carry):
                pass_sum(place, part, side, slot).wait_recv()
                rows = rows_of(part)
                dn_ref[rows] += incoming[slot, rows].astype(jnp.float32)
                return carry

            lax.fori_loop(0, parts, add_part, 0)

    for k in (2, 3, 0, 1):
        add_halve(k, stages - 1, flights[k])
    mine = pl.ds(pl.multiple_of(row * pieces_hbm.shape[1], pieces_hbm.shape[1]), pieces_hbm.shape[1])
    save = pltpu.make_async_copy(grads.at[:, mine], pieces_hbm, load_sem.at[0])
    save.start()
    for copy in sent:
        copy.wait_send()

    for side, there in ((-1, has_left), (1, has_right)):

        @pl.when(there)
        def _():
            pass_block(place, side, count + (side + 1) // 2).wait_send()

    for block in range(count):

        @pl.when((block != place) & has_left & has_right)
        def _():
            pass_block(block, 1, block).wait_send()

        @pl.when(block != place)
        def _():
            for part in range(parts):
                pass_sum(block, part, 1, block).wait_send()

    for turn in (count - 2, count - 1):
        store_out(turn, 0).wait()
    save.wait()


def feed_forward(normed, cot_all, gate_up, down):
    count = lax.axis_size("mp")
    data_count = lax.axis_size("dp")
    block_len, width = normed.shape
    units = down.shape[1]
    padded = gate_up.shape[0]
    parts = 2
    low = jnp.bfloat16
    anywhere = pl.BlockSpec(memory_space=pl.ANY)
    dma = pltpu.SemaphoreType.DMA
    tokens = count * block_len
    height = padded // data_count
    span = data_count - 1
    most = (units // 2 + 127) // 128 * 128
    out_terms, dn, pieces = pl.pallas_call(
        functools.partial(feed_forward_kernel, data_count, count, parts),
        out_shape=[
            jax.ShapeDtypeStruct((count, block_len, width), low),
            jax.ShapeDtypeStruct((block_len, width), jnp.float32),
            jax.ShapeDtypeStruct((3, height, units), low),
        ],
        in_specs=[anywhere] * 4,
        out_specs=[anywhere, pl.BlockSpec(memory_space=pltpu.VMEM), anywhere],
        scratch_shapes=[
            pltpu.VMEM((count, block_len, width), low),
            pltpu.VMEM((count, block_len, width), low),
            pltpu.VMEM((width, 2 * units), low),
            pltpu.VMEM((width, units), low),
            pltpu.VMEM((count, block_len, units), low),
            pltpu.VMEM((count, block_len, 2 * units), low),
            pltpu.VMEM((count, block_len, width), low),
            pltpu.VMEM((count + 1, block_len, width), low),
            pltpu.VMEM((2, block_len, width), low),
            pltpu.VMEM((3, padded, units), low),
            pltpu.VMEM((2, span, height, units), low),
            pltpu.VMEM((span, height, most), low),
            pltpu.VMEM((span, height, units - most), low),
            dma((4,)),
            dma((2,)),
            dma((count + 2,)),
            dma((count,)),
            dma((count, parts)),
            dma((count + 1, parts)),
            dma((4 * span,)),
            dma((4 * span,)),
        ],
        compiler_params=pltpu.CompilerParams(
            collective_id=1, has_side_effects=True, vmem_limit_bytes=60 << 20
        ),
        cost_estimate=pl.CostEstimate(
            flops=18 * tokens * width * units,
            bytes_accessed=12 * width * units + 6 * tokens * width,
            transcendentals=tokens * units,
        ),
        name="feed_forward",
    )(normed, cot_all.reshape(count, block_len, width), gate_up, down)
    return out_terms.reshape(tokens, width), dn, pieces


def ff_parts(units):
    most = (units // 2 + 127) // 128 * 128
    return ((0, 0, units, 0), (1, 0, units, 1), (2, 0, most, 0), (2, most, units - most, 1))


def stages_left(part, stages):
    return min(2 if part[0] == 2 else 1, stages - 1)


def attend_back_kernel(
    data_count,
    count,
    slots,
    dn_hbm,
    middle_hbm,
    cot_hbm,
    gain_ref,
    proj_hbm,
    own_hbm,
    qkv_hbm,
    probs_hbm,
    norm_hbm,
    qkv_low_hbm,
    bucket_ref,
    ff_hbm,
    d_middle_hbm,
    terms_hbm,
    d_qkv_w_hbm,
    d_out_w_hbm,
    spread_hbm,
    dn,
    middle,
    cot,
    proj,
    own,
    qkv,
    probs,
    norm,
    qkv_low,
    d_own,
    grad,
    diag,
    dk,
    dv,
    d_qkv,
    terms,
    d_qkv_w,
    d_out_w,
    line,
    load_sem,
    probs_sem,
    cross_send,
    cross_recv,
    up_send,
    up_recv,
):
    place = lax.axis_index("mp")
    me = lax.axis_index("dp")
    block_len, width = dn.shape
    seq_len = qkv.shape[0]
    lanes = slots * HD
    padded = d_qkv_w.shape[0]
    steps = seq_len // BLOCK
    f32 = jnp.float32
    low = jnp.bfloat16

    loads = []

    def load(src, dst):
        copy = pltpu.make_async_copy(src, dst, load_sem.at[len(loads)])
        copy.start()
        loads.append(copy)

    load(dn_hbm, dn)
    load(middle_hbm, middle)
    load(cot_hbm, cot)
    load(proj_hbm, proj)
    load(own_hbm, own)
    load(qkv_hbm, qkv)
    load(norm_hbm, norm)
    load(qkv_low_hbm, qkv_low)
    height = padded // data_count
    mine = pl.ds(pl.multiple_of(me * height, height), height)
    load(ff_hbm, spread_hbm.at[:, mine])

    ways = orders(data_count)
    stages = len(ways[0])
    parts = ff_parts(spread_hbm.shape[2])
    span = data_count - 1
    flies = [Butterfly(ways[way], k * span) for k, (_, _, _, way) in enumerate(parts)]
    views = [row_pieces(spread_hbm.at[i], data_count, at, wide) for i, at, wide, _ in parts]
    others = [(place + k) % count for k in range(1, count)]
    greet([flies[0].partner(s) for s in range(1, stages)] + [(me, other) for other in others])
    sent = []

    def start(copies):
        for copy in copies:
            copy.start()
        sent.extend(copies)
        return copies

    flights = [
        start(
            fly.double(
                stages - 1, view, (up_send, up_recv), ff_hbm.at[i, :, pl.ds(at, wide)]
            )
        )
        for fly, view, (i, at, wide, _) in zip(flies, views, parts)
    ]

    table = turn_order(count)

    def fetch(t):
        per = block_len // BLOCK
        block = look_up(table, place, t // per) * per + t % per
        rows = pl.ds(pl.multiple_of(block * BLOCK, BLOCK), BLOCK)
        return block, pltpu.make_async_copy(
            probs_hbm.at[:, rows], probs.at[t % 2], probs_sem.at[t % 2]
        )

    fetch(0)[1].start()
    diag[...] = jnp.zeros_like(diag)
    dk[...] = jnp.zeros_like(dk)
    dv[...] = jnp.zeros_like(dv)
    for copy in loads[:3]:
        copy.wait()
    d_middle = cot[...].astype(f32) + norm_back(middle[...], gain_ref[...].reshape(1, width), dn[...])
    middle[...] = d_middle
    save_middle = pltpu.make_async_copy(middle, d_middle_hbm, load_sem.at[0])
    save_middle.start()
    cot[...] = d_middle.astype(low)
    loads[3].wait()
    d_all = product(cot[...], proj[:width]).astype(low)

    def own_rows(who):
        return pl.ds(pl.multiple_of(who * block_len, block_len), block_len)

    for k in range(count):
        d_own[k] = d_all[:, k * lanes : (k + 1) * lanes]
    start(
        [
            pltpu.make_async_remote_copy(
                src_ref=d_own.at[other],
                dst_ref=grad.at[own_rows(place)],
                send_sem=cross_send.at[k],
                recv_sem=cross_recv.at[place],
                device_id=(me, other),
                device_id_type=pl.DeviceIdType.MESH,
            )
            for k, other in enumerate(others)
        ]
    )
    grad[own_rows(place)] = d_own[place]
    loads[4].wait()
    d_out_w[width:] = jnp.zeros((padded - width, count * lanes), low)
    d_out_w[:width] = left_inner(cot[...], own[...]).astype(low)
    save_out = pltpu.make_async_copy(d_out_w, d_out_w_hbm, load_sem.at[1])
    save_out.start()
    loads[5].wait()

    def pass_on(s):
        for k, (fly, view) in enumerate(zip(flies, views)):
            for copy in flights[k]:
                copy.wait_recv()
            flights[k] = []
            if s > 1 and s - 1 >= stages_left(parts[k], stages):
                flights[k] = start(fly.double(s - 1, view, (up_send, up_recv)))

    def back_block(t, carry):
        per = block_len // BLOCK

        @pl.when((t > 0) & (t % per == 0))
        def _():
            who = look_up(table, place, t // per)
            pltpu.make_async_remote_copy(
                src_ref=d_own.at[0],
                dst_ref=grad.at[own_rows(who)],
                send_sem=cross_send.at[0],
                recv_sem=cross_recv.at[who],
                device_id=(me, who),
                device_id_type=pl.DeviceIdType.MESH,
            ).wait_recv()

        @pl.when(t + 1 < steps)
        def _():
            fetch(t + 1)[1].start()

        block, arrival = fetch(t)
        arrival.wait()
        rows = pl.ds(pl.multiple_of(block * BLOCK, BLOCK), BLOCK)
        window = pl.ds(pl.multiple_of((steps - 1 - block) * BLOCK, BLOCK), seq_len)
        queries = qkv[rows, 0:lanes]
        keys = qkv[:, lanes : 2 * lanes]
        values = qkv[:, 2 * lanes : 3 * lanes]
        d_query = jnp.zeros((BLOCK, lanes), f32)
        for slot in range(slots):
            weight = probs[t % 2, slot]
            slot_grad = slot_lanes(grad[rows], slot)
            d_probs = right_inner(slot_grad, values)
            delta = jnp.sum(weight * d_probs, axis=-1, keepdims=True)
            d_scores = (weight * (d_probs - delta)).astype(low)
            d_query = d_query + slot_lanes(product(d_scores, keys), slot)
            dk[...] += left_inner(slot_lanes(queries, slot), d_scores)
            dv[...] += left_inner(slot_grad, weight.astype(low))
            diag[slot, :, window] += d_scores.astype(f32)
        d_qkv[rows, 0:lanes] = d_query.astype(low)
        return carry

    loads[8].wait()
    pass_on(stages - 1)
    lax.fori_loop(0, steps, back_block, 0)
    for s in reversed(range(2, stages - 1)):
        pass_on(s)
    d_qkv[:, lanes : 2 * lanes] = dk[...].T.astype(low)
    d_qkv[:, 2 * lanes : 3 * lanes] = dv[...].T.astype(low)
    for copy in loads[6:8]:
        copy.wait()
    terms[...] = right_inner(d_qkv[...], qkv_low[:width]).astype(low)
    save_terms = pltpu.make_async_copy(terms, terms_hbm, load_sem.at[2])
    save_terms.start()
    d_qkv_w[:width] = left_inner(norm[...], d_qkv[...]).astype(low)
    d_qkv_w[width:] = jnp.zeros((padded - width, 3 * lanes), low)
    sums = []
    for slot in range(slots):
        level = diag[slot]
        rest = BLOCK // 2
        while rest >= 1:
            level = pltpu.roll(level[:rest], rest, 1) + level[rest:]
            rest //= 2
        sums.append(level)
    sums = jnp.concatenate(sums + [jnp.zeros((128 - slots, 2 * seq_len), f32)], axis=0)
    d_rel = lax.dot_general(
        onehot_rows(bucket_ref, line),
        sums,
        (((1,), (1,)), ((), ())),
        precision=highest,
        preferred_element_type=f32,
    )
    d_qkv_w[width : width + BUCKETS, :128] = d_rel.astype(low)
    save_qkv = pltpu.make_async_copy(d_qkv_w, d_qkv_w_hbm, load_sem.at[3])
    save_qkv.start()
    if stages > 1:
        pass_on(1)
    for copy in sent:
        copy.wait_send()
    for copy in (save_middle, save_out, save_terms, save_qkv):
        copy.wait()


def attend_back(dn, middle, cot, gain, proj_all, own, qkv, probs, norm, qkv_low, bucket, ff_pieces):
    count = lax.axis_size("mp")
    data_count = lax.axis_size("dp")
    seq_len = qkv.shape[0]
    slots = probs.shape[0]
    lanes = slots * HD
    block_len, width = dn.shape
    padded = qkv_low.shape[0]
    _, _, units = ff_pieces.shape
    far = pl.BlockSpec(memory_space=pltpu.HBM)
    near = pl.BlockSpec(memory_space=pltpu.VMEM)
    dma = pltpu.SemaphoreType.DMA
    low, f32 = jnp.bfloat16, jnp.float32
    span = data_count - 1
    scratch = [
        (dn.shape, f32),
        (middle.shape, f32),
        (cot.shape, low),
        (proj_all.shape, low),
        (own.shape, low),
        (qkv.shape, low),
        ((2, slots, BLOCK, seq_len), f32),
        (norm.shape, low),
        (qkv_low.shape, low),
        ((count, block_len, lanes), low),
        ((seq_len, lanes), low),
        ((slots, BLOCK, 2 * seq_len), f32),
        ((lanes, seq_len), f32),
        ((lanes, seq_len), f32),
        (qkv.shape, low),
        ((seq_len, width), low),
        ((padded, 3 * lanes), low),
        ((padded, count * lanes), low),
    ]
    return pl.pallas_call(
        functools.partial(attend_back_kernel, data_count, count, slots),
        in_specs=[far] * 3 + [near] + [far] * 6 + [near, far],
        out_specs=[far] * 5,
        out_shape=[
            jax.ShapeDtypeStruct((block_len, width), f32),
            jax.ShapeDtypeStruct((seq_len, width), low),
            jax.ShapeDtypeStruct((padded, 3 * lanes), low),
            jax.ShapeDtypeStruct((padded, count * lanes), low),
            jax.ShapeDtypeStruct((3, padded, units), low),
        ],
        scratch_shapes=[pltpu.VMEM(shape, dtype) for shape, dtype in scratch]
        + [
            pltpu.VMEM((1, 2 * seq_len), jnp.int32),
            dma((10,)),
            dma((2,)),
            dma((count - 1,)),
            dma((count,)),
            dma((4 * span,)),
            dma((4 * span,)),
        ],
        compiler_params=pltpu.CompilerParams(
            collective_id=3, has_side_effects=True, vmem_limit_bytes=56 << 20
        ),
        cost_estimate=pl.CostEstimate(
            flops=16 * slots * seq_len * seq_len * HD, bytes_accessed=140 << 20, transcendentals=0
        ),
        name="attend_back",
    )(dn, middle, cot, gain, proj_all, own, qkv, probs, norm, qkv_low, bucket, ff_pieces)


def onehot_rows(bucket_ref, line_ref):
    offsets = bucket_ref.shape[0]
    line_ref[...] = jnp.full(line_ref.shape, -1, jnp.int32)
    line_ref[:, :offsets] = bucket_ref[...].reshape(1, offsets)
    rows = lax.broadcasted_iota(jnp.int32, (BUCKETS, line_ref.shape[1]), 0)
    return jnp.where(rows == line_ref[...], 1.0, 0.0)


def front_kernel(
    data_count,
    count,
    slots,
    x_hbm,
    cot_hbm,
    query_hbm,
    key_hbm,
    value_hbm,
    out_hbm,
    gate_hbm,
    up_hbm,
    down_hbm,
    segments_ref,
    bucket_ref,
    rel_ref,
    attn_gain_ref,
    ff_gain_ref,
    norm_far,
    cot_far,
    own_cot_far,
    qkv_far,
    probs_far,
    own_far,
    middle_far,
    normed_far,
    proj_far,
    qkv_low_far,
    gate_up_far,
    down_far,
    squares_ref,
    x_in,
    cot_in,
    x,
    norm,
    cot,
    thin,
    wide,
    gate_low,
    up_low,
    down_low,
    blank,
    proj,
    qkv_low,
    qkv,
    tilt,
    seg_col,
    probs,
    mixed,
    own,
    normed,
    line,
    load_sem,
    save_sem,
    probs_sem,
    norm_send,
    norm_recv,
    cot_send,
    cot_recv,
    cross_send,
    cross_recv,
    side_send,
    side_recv,
    mix_send,
    mix_recv,
):
    place = lax.axis_index("mp")
    me = lax.axis_index("dp")
    last = count - 1
    f32, low = jnp.float32, jnp.bfloat16
    block_len, width = x.shape
    seq_len = count * block_len
    lanes = slots * HD
    padded = proj.shape[0]
    height = padded // data_count
    units = gate_low.shape[1]
    mesh_id = pl.DeviceIdType.MESH
    others = [(place + k) % count for k in range(1, count)]
    peers = [(me + k) % data_count for k in range(1, data_count)]

    def load(k, from_ref, to_ref):
        copy = pltpu.make_async_copy(from_ref, to_ref, load_sem.at[k])
        copy.start()
        return copy

    load_x = load(0, x_hbm, x_in)
    load_thin = [
        load(1 + k, ref, thin.at[k])
        for k, ref in enumerate((out_hbm, query_hbm, key_hbm, value_hbm))
    ]
    load_cot = load(5, cot_hbm, cot_in)
    load_gate = load(6, gate_hbm, wide.at[0])
    load_up = load(7, up_hbm, wide.at[1])
    greet([(me, other) for other in others] + [(peer, place) for peer in peers])

    saves = []

    def save(from_ref, to_ref):
        copy = pltpu.make_async_copy(from_ref, to_ref, save_sem.at[len(saves)])
        copy.start()
        saves.append(copy)

    sent = []

    def start(copy):
        copy.start()
        sent.append(copy)

    def pass_block(buffer, sems, block, side, slot):
        return pltpu.make_async_remote_copy(
            src_ref=buffer.at[block],
            dst_ref=buffer.at[block],
            send_sem=sems[0].at[slot],
            recv_sem=sems[1].at[block],
            device_id=(me, place + side),
            device_id_type=mesh_id,
        )

    def inside(block):
        return (block >= 0) & (block <= last)

    norm_sems = (norm_send, norm_recv)
    cot_sems = (cot_send, cot_recv)

    def take(buffer, sems, distance):
        for side in (1, -1):
            other = place + side * distance

            @pl.when(inside(other))
            def _():
                pass_block(buffer, sems, other, side, other).wait_recv()

                @pl.when(inside(place - side))
                def _():
                    pass_block(buffer, sems, other, -side, other).start()

    def send_own(buffer, sems, side):
        return pass_block(buffer, sems, place, side, count + (side + 1) // 2)

    def cot_may_go(distance):
        for side in (1, -1):
            behind = place if side == 1 else last - place

            @pl.when((behind == distance) & inside(place + side))
            def _():
                if distance == 0:
                    send_own(norm, norm_sems, side).wait_send()
                else:
                    far_end = 0 if side == 1 else last
                    pass_block(norm, norm_sems, far_end, side, far_end).wait_send()
                send_own(cot, cot_sems, side).start()

    between = inside(place - 1) & inside(place + 1)

    load_x.wait()
    x[...] = x_in[...].T.astype(f32)
    norm[place] = rms_norm(x[...], attn_gain_ref[...].reshape(1, width)).astype(low)
    for side in (1, -1):

        @pl.when(inside(place + side))
        def _():
            send_own(norm, norm_sems, side).start()

    load_cot.wait()
    cot[place] = cot_in[...].T
    save(cot.at[place], own_cot_far)

    lane = lax.broadcasted_iota(jnp.int32, (1, lanes), 1)
    slot_of = place * slots + lane // HD
    lane_mask = jnp.where((slot_of < 5) | (slot_of == 6), 1.0, 0.0)
    for copy in load_thin:
        copy.wait()

    def lanes_of(who):
        return pl.ds(pl.multiple_of(who * lanes, lanes), lanes)

    def rows_of(who):
        return pl.ds(pl.multiple_of(who * height, height), height)

    proj[width:, lanes_of(place)] = jnp.zeros((padded - width, lanes), low)
    qkv_low[width:] = jnp.zeros((padded - width, 3 * lanes), low)
    blank[...] = jnp.zeros_like(blank)
    column = lax.broadcasted_iota(jnp.int32, (1, 128), 1)
    squares = jnp.zeros((1, 128), f32)

    def square_of(values, at):
        return jnp.where(column == at, total(total(values * values, 1), 0), 0.0)

    masked = (thin[0] * lane_mask).astype(low)
    proj[:width, lanes_of(place)] = masked

    def proj_copy(src, dst, sems, send_slot, recv_slot, device):
        return pltpu.make_async_remote_copy(
            src_ref=src,
            dst_ref=dst,
            send_sem=sems[0].at[send_slot],
            recv_sem=sems[1].at[recv_slot],
            device_id=device,
            device_id_type=mesh_id,
        )

    cross, aside = (cross_send, cross_recv), (side_send, side_recv)
    for k, other in enumerate(others):
        view = proj.at[rows_of(me), lanes_of(place)]
        start(proj_copy(view, view, cross, k, count - 2 - k, (me, other)))
    for k in range(3):
        qkv_low[:width, k * lanes : (k + 1) * lanes] = (thin[1 + k] * lane_mask).astype(low)
        squares = squares + square_of(thin[1 + k], k)
    squares = squares + square_of(thin[0], 6) + square_of(rel_ref[...], 3)
    save(qkv_low, qkv_low_far)

    onehot = onehot_rows(bucket_ref, line)
    vector = lax.dot_general(
        rel_ref[...],
        onehot,
        (((1,), (0,)), ((), ())),
        precision=highest,
        preferred_element_type=f32,
    )
    for slot in range(slots):
        spread = jnp.broadcast_to(vector[slot : slot + 1, :], (BLOCK, 2 * seq_len))
        tilt[slot] = pltpu.roll(spread, 2 * seq_len - BLOCK + 1, 1, stride=1, stride_axis=0)
    seg_row = segments_ref[...].astype(f32)
    seg_col[...] = jnp.broadcast_to(seg_row, (128, seq_len)).T

    arrivals = []
    for k, other in enumerate(others):
        view = proj.at[rows_of(me), lanes_of(other)]
        proj_copy(view, view, cross, k, k, (me, other)).wait_recv()
        at = k * (data_count - 1)
        for j, peer in enumerate(peers):
            start(proj_copy(view, view, aside, at + j, at + data_count - 2 - j, (peer, place)))
            come = proj.at[rows_of(peer), lanes_of(other)]
            arrivals.append(proj_copy(come, come, aside, at + j, at + j, (peer, place)))

    def own_rows(who):
        return pl.ds(pl.multiple_of(who * block_len, block_len), block_len)

    def project(block):
        qkv[own_rows(block)] = product(norm[block], qkv_low[:width]).astype(low)

    def project_at(distance):
        for side in (1, -1):
            other = place + side * distance

            @pl.when(inside(other))
            def _():
                project(other)

    project(place)
    load_gate.wait()
    gate_low[...] = wide[0].astype(low)
    squares = squares + square_of(wide[0], 4)
    load_down = load(6, down_hbm, wide.at[0])
    rows_used = pl.ds(0, width)
    save(gate_low, gate_up_far.at[rows_used, pl.ds(0, units)])
    load_up.wait()
    up_low[...] = wide[1].astype(low)
    squares = squares + square_of(wide[1], 5)
    save(up_low, gate_up_far.at[rows_used, pl.ds(units, units)])
    save(blank, gate_up_far.at[pl.ds(width, padded - width)])
    take(norm, norm_sems, 1)
    cot_may_go(0)
    project_at(1)
    load_down.wait()
    down_low[...] = wide[0].astype(low)
    squares = squares + square_of(wide[0], 7)
    save(down_low, down_far)
    squares_ref[...] = squares
    for distance in range(2, count):
        take(norm, norm_sems, distance)
        cot_may_go(distance - 1)
        project_at(distance)
    save(qkv, qkv_far)
    save(norm, norm_far)

    @pl.when(between)
    def _():
        take(cot, cot_sems, 1)

    steps = seq_len // BLOCK
    per = block_len // BLOCK
    table = [order[::-1] for order in turn_order(count)]

    def store_probs(t, block):
        rows = pl.ds(pl.multiple_of(block * BLOCK, BLOCK), BLOCK)
        return pltpu.make_async_copy(probs.at[t % 2], probs_far.at[:, rows], probs_sem.at[t % 2])

    def mix_copy(owner):
        return pltpu.make_async_remote_copy(
            src_ref=mixed.at[own_rows(owner)],
            dst_ref=own.at[:, lanes_of(place)],
            send_sem=mix_send.at[owner],
            recv_sem=mix_recv.at[place],
            device_id=(me, owner),
            device_id_type=mesh_id,
        )

    def attend_block(t, carry):
        owner = look_up(table, place, t // per)
        block = owner * per + t % per
        rows = pl.ds(pl.multiple_of(block * BLOCK, BLOCK), BLOCK)
        window = pl.ds(pl.multiple_of((steps - 1 - block) * BLOCK, BLOCK), seq_len)
        same_doc = seg_col[rows, 0:1] == seg_row
        queries = qkv[rows, 0:lanes]
        keys = qkv[:, lanes : 2 * lanes]
        values = qkv[:, 2 * lanes : 3 * lanes]
        result = jnp.zeros((BLOCK, lanes), f32)

        @pl.when(t >= 2)
        def _():
            store_probs(t, block).wait()

        for slot in range(slots):
            scores = right_inner(slot_lanes(queries, slot), keys) + tilt[slot, :, window]
            scores = jnp.where(same_doc, scores, -1e30)
            peak = jnp.max(scores, axis=-1, keepdims=True)
            raised = jnp.exp(scores - peak)
            weight = raised * (1.0 / jnp.sum(raised, axis=-1, keepdims=True))
            probs[t % 2, slot] = weight
            result = result + slot_lanes(product(weight.astype(low), values), slot)
        store_probs(t, block).start()
        mixed[rows] = result.astype(low)

        @pl.when((t % per == per - 1) & (owner != place))
        def _():
            mix_copy(owner).start()

        return carry

    lax.fori_loop(0, steps, attend_block, 0)
    own[:, lanes_of(place)] = mixed[own_rows(place)]

    @pl.when(between)
    def _():
        for distance in range(2, count):
            take(cot, cot_sems, distance)

    for arrival in arrivals:
        arrival.wait_recv()
    save(proj, proj_far)
    for k, other in enumerate(others):
        pltpu.make_async_remote_copy(
            src_ref=mixed.at[own_rows(other)],
            dst_ref=own.at[:, lanes_of(other)],
            send_sem=mix_send.at[other],
            recv_sem=mix_recv.at[other],
            device_id=(me, other),
            device_id_type=mesh_id,
        ).wait_recv()
    save(own, own_far)
    x[...] = x[...] + right_inner(own[...], proj[:width])
    save(x, middle_far)
    normed[...] = rms_norm(x[...], ff_gain_ref[...].reshape(1, width)).astype(low)
    save(normed, normed_far)

    @pl.when(jnp.logical_not(between))
    def _():
        for distance in range(1, count):
            take(cot, cot_sems, distance)

    save(cot, cot_far)
    for t in (0, 1):
        store_probs(t, 0).wait()
    for copy in saves:
        copy.wait()
    for copy in sent:
        copy.wait_send()
    for k, other in enumerate(others):
        mix_copy(other).wait_send()
    for buffer, sems in ((norm, norm_sems), (cot, cot_sems)):
        for side in (1, -1):
            behind = place if side == 1 else last - place
            unwaited = behind > 0 if buffer is norm else behind >= 0

            @pl.when(unwaited & inside(place + side))
            def _():
                send_own(buffer, sems, side).wait_send()

        for block in range(1, last) if buffer is norm else range(count):

            @pl.when((block != place) & between)
            def _():
                pass_block(buffer, sems, block, 1, block).wait_send()


def front(x, cot, weights, segments, bucket, rel_bias, attn_gain, ff_gain):
    count = lax.axis_size("mp")
    data_count = lax.axis_size("dp")
    query, key, value, out, gate, up, down = weights
    width, block_len = x.shape
    lanes = query.shape[1]
    slots = lanes // HD
    units = gate.shape[1]
    seq_len = count * block_len
    piece = 16 * data_count
    padded = (width + piece - 1) // piece * piece
    low, f32 = jnp.bfloat16, jnp.float32
    far = pl.BlockSpec(memory_space=pltpu.HBM)
    near = pl.BlockSpec(memory_space=pltpu.VMEM)
    dma = pltpu.SemaphoreType.DMA
    outs = [
        ((count, block_len, width), low),
        ((count, block_len, width), low),
        ((block_len, width), low),
        ((seq_len, 3 * lanes), low),
        ((slots, seq_len, seq_len), f32),
        ((block_len, count * lanes), low),
        ((block_len, width), f32),
        ((block_len, width), low),
        ((padded, count * lanes), low),
        ((padded, 3 * lanes), low),
        ((padded, 2 * units), low),
        ((width, units), low),
        ((1, 128), f32),
    ]
    scratch = [
        ((width, block_len), low),
        ((width, block_len), low),
        ((block_len, width), f32),
        ((count, block_len, width), low),
        ((count, block_len, width), low),
        ((4, width, lanes), f32),
        ((2, width, units), f32),
        ((width, units), low),
        ((width, units), low),
        ((width, units), low),
        ((padded - width, 2 * units), low),
        ((padded, count * lanes), low),
        ((padded, 3 * lanes), low),
        ((seq_len, 3 * lanes), low),
        ((slots, BLOCK, 2 * seq_len), f32),
        ((seq_len, 128), f32),
        ((2, slots, BLOCK, seq_len), f32),
        ((seq_len, lanes), low),
        ((block_len, count * lanes), low),
        ((block_len, width), low),
    ]
    sides = (count - 1) * (data_count - 1)
    return pl.pallas_call(
        functools.partial(front_kernel, data_count, count, slots),
        in_specs=[far] * 9 + [near] * 5,
        out_specs=[far] * 12 + [near],
        out_shape=[jax.ShapeDtypeStruct(shape, dtype) for shape, dtype in outs],
        scratch_shapes=[pltpu.VMEM(shape, dtype) for shape, dtype in scratch]
        + [
            pltpu.VMEM((1, 2 * seq_len), jnp.int32),
            dma((8,)),
            dma((16,)),
            dma((2,)),
            dma((count + 2,)),
            dma((count,)),
            dma((count + 2,)),
            dma((count,)),
            dma((count - 1,)),
            dma((count - 1,)),
            dma((sides,)),
            dma((sides,)),
            dma((count,)),
            dma((count,)),
        ],
        compiler_params=pltpu.CompilerParams(
            collective_id=0, has_side_effects=True, vmem_limit_bytes=60 << 20
        ),
        cost_estimate=pl.CostEstimate(
            flops=8 * slots * seq_len * seq_len * HD,
            bytes_accessed=300 << 20,
            transcendentals=slots * seq_len * seq_len,
        ),
        name="front",
    )(
        x, cot, query, key, value, out, gate, up, down,
        segments, bucket, rel_bias, attn_gain, ff_gain,
    )


def local(
    layer_in,
    segment_ids,
    bucket_table,
    attn_gain,
    query_weight,
    key_weight,
    value_weight,
    out_weight,
    rel_bias,
    ff_gain,
    gate_weight,
    up_weight,
    down_weight,
    cotangent,
):
    model_width = layer_in.shape[2]
    slots_here = rel_bias.shape[1]
    layer_in = layer_in[0]
    down_turned = down_weight.T
    out_turned = out_weight.T
    rel_turned = rel_bias.T
    (
        flat_norm,
        flat_cot,
        own_cot,
        qkv,
        probs,
        own_attended,
        middle,
        normed_ff_local,
        proj_all,
        qkv_low,
        gate_up_low,
        down_low,
        squares,
    ) = front(
        layer_in.T,
        cotangent[0].T,
        (query_weight, key_weight, value_weight, out_turned, gate_weight, up_weight, down_turned),
        segment_ids,
        bucket_table,
        rel_turned,
        attn_gain,
        ff_gain,
    )
    flat_norm = flat_norm.reshape(-1, model_width)
    residual_in = layer_in.astype(jnp.float32)
    out_terms, dn_ff, ff_pieces = feed_forward(normed_ff_local, flat_cot, gate_up_low, down_low)
    d_middle, dn_attn_terms, d_qkv_w, d_out_w, ff_grads = attend_back(
        dn_ff,
        middle,
        own_cot,
        ff_gain,
        proj_all,
        own_attended,
        qkv,
        probs,
        flat_norm,
        qkv_low,
        bucket_table,
        ff_pieces,
    )
    ff_branch = lax.psum_scatter(out_terms, "mp", scatter_dimension=0, tiled=True)
    layer_out = (middle + ff_branch.astype(jnp.float32)).astype(jnp.bfloat16)
    dn_attn = lax.psum_scatter(dn_attn_terms, "mp", scatter_dimension=0, tiled=True)
    weights = (
        gate_weight,
        up_weight,
        down_turned,
        query_weight,
        key_weight,
        value_weight,
        out_turned,
    )
    *held, shared, own, tall = sum_weights(
        ff_grads, d_qkv_w, d_out_w, qkv_low, gate_up_low, squares, weights, model_width
    )
    results = update(held[:5], held[5:], rel_turned, attn_gain, ff_gain, shared, own, tall)
    news, along, across = results[:8], results[8:16], results[16:24]
    new_attn_gain, attn_gain_moment, new_ff_gain, ff_gain_moment = results[24:]
    gate, up, down, query, key, value, out, rel = zip(news, along, across)
    rel = (rel[0].T, rel[1], rel[2].reshape(slots_here))
    down = (down[0].T, down[2], down[1])
    out = (out[0].T, out[2], out[1])
    input_grad = d_middle + norm_back(residual_in, attn_gain, dn_attn.astype(jnp.float32))
    input_grad = input_grad.astype(jnp.bfloat16)
    return (
        layer_out[None],
        input_grad[None],
        new_attn_gain,
        attn_gain_moment,
        *query,
        *key,
        *value,
        *out,
        *rel,
        new_ff_gain,
        ff_gain_moment,
        *gate,
        *up,
        *down,
    )


def solution(mesh):
    return jax.shard_map(
        local,
        mesh=mesh,
        in_specs=(
            P("dp", "mp", None),
            P("dp", None),
            P(),
            P(),
            P(None, "mp"),
            P(None, "mp"),
            P(None, "mp"),
            P("mp", None),
            P(None, "mp"),
            P(),
            P(None, "mp"),
            P(None, "mp"),
            P("mp", None),
            P("dp", "mp", None),
        ),
        out_specs=(
            P("dp", "mp", None),
            P("dp", "mp", None),
            P(),
            P(),
            P(None, "mp"),
            P(),
            P("mp"),
            P(None, "mp"),
            P(),
            P("mp"),
            P(None, "mp"),
            P(),
            P("mp"),
            P("mp", None),
            P("mp"),
            P(),
            P(None, "mp"),
            P(),
            P("mp"),
            P(),
            P(),
            P(None, "mp"),
            P(),
            P("mp"),
            P(None, "mp"),
            P(),
            P("mp"),
            P("mp", None),
            P("mp"),
            P(),
        ),
        check_vma=False,
    )
```

```python
import functools

import jax
import jax.numpy as jnp
from jax import lax
from jax.experimental import pallas as pl
from jax.experimental.pallas import tpu as pltpu
from jax.sharding import PartitionSpec as P

HD = 64
BUCKETS = 32
BLOCK = 128


highest = lax.Precision.HIGHEST
step_scale = 0.3


def rms_norm(values, gain):
    return values * lax.rsqrt(jnp.mean(values * values, axis=-1, keepdims=True) + 1e-06) * gain


def norm_back(values, gain, grad):
    scale = lax.rsqrt(jnp.mean(values * values, axis=-1, keepdims=True) + 1e-06)
    unit = values * scale
    pull = grad * gain
    return scale * (pull - unit * jnp.mean(pull * unit, axis=-1, keepdims=True))


def product(left_side, right_side):
    return jnp.dot(left_side, right_side, preferred_element_type=jnp.float32)


def left_inner(left_side, right_side):
    return lax.dot_general(
        left_side, right_side, (((0,), (0,)), ((), ())), preferred_element_type=jnp.float32
    )


def right_inner(left_side, right_side):
    return lax.dot_general(
        left_side, right_side, (((1,), (1,)), ((), ())), preferred_element_type=jnp.float32
    )


def slot_lanes(values, slot):
    lane = lax.broadcasted_iota(jnp.int32, values.shape, 1)
    return jnp.where((lane >= slot * HD) & (lane < (slot + 1) * HD), values, jnp.zeros_like(values))


class Butterfly:
    def __init__(self, order, base):
        self.order = order
        self.me = lax.axis_index("dp")
        self.line = lax.axis_index("mp")
        self.base = base
        self.offsets = []
        total = 0
        for s in range(len(order)):
            self.offsets.append(total)
            total += 1 << (len(order) - 1 - s)

    def bit(self, b):
        return (self.me // b) % 2

    def partner(self, s):
        b = self.order[s]
        return (self.me + b * (1 - 2 * self.bit(b)), self.line)

    def width(self, s):
        return 1 << (len(self.order) - 1 - s)

    def piece(self, s, j, mine):
        b = self.order[s]
        found = sum(k * self.bit(k) for k in self.order[:s])
        found = found + b * (self.bit(b) if mine else 1 - self.bit(b))
        for i, k in enumerate(self.order[s + 1 :]):
            found = found + k * ((j // (1 << i)) % 2)
        return found

    def copy(self, src, dst, sems, slot, s):
        return pltpu.make_async_remote_copy(
            src_ref=src,
            dst_ref=dst,
            send_sem=sems[0].at[self.base + slot],
            recv_sem=sems[1].at[self.base + slot],
            device_id=self.partner(s),
            device_id_type=pl.DeviceIdType.MESH,
        )

    def halve(self, s, source, landing, sems):
        at = self.offsets[s]
        return [
            self.copy(source(self.piece(s, j, False)), landing.at[at + j], sems, at + j, s)
            for j in range(self.width(s))
        ]

    def add(self, s, kept, landing, copies):
        at = self.offsets[s]
        for j, copy in enumerate(copies):
            copy.wait_recv()
            mine = kept(self.piece(s, j, True))
            mine[...] = (mine[...].astype(jnp.float32) + landing[at + j].astype(jnp.float32)).astype(
                jnp.bfloat16
            )

    def double(self, s, whole, sems, first=None):
        at = self.offsets[s]
        copies = []
        for j in range(self.width(s)):
            view = whole(self.piece(s, j, True))
            copies.append(self.copy(view if first is None else first, view, sems, at + j, s))
        return copies


def orders(data_count):
    bits = [1 << i for i in range(data_count.bit_length() - 1)]
    return (bits, bits[:1] + bits[:0:-1])


def greet(peers):
    barrier = pltpu.get_barrier_semaphore()
    for peer in peers:
        pl.semaphore_signal(barrier, inc=1, device_id=peer, device_id_type=pl.DeviceIdType.MESH)
    pl.semaphore_wait(barrier, len(peers))


def row_pieces(ref, data_count, at=0, lanes=None):
    rows = ref.shape[0] // data_count
    columns = pl.ds(at, ref.shape[1] if lanes is None else lanes)
    return lambda q: ref.at[pl.ds(pl.multiple_of(q * rows, rows), rows), columns]


def total(values, axis):
    return jnp.sum(values, axis=axis, keepdims=True)


def sum_weights_kernel(data_count, count, model_width, parts, *refs):
    ff_hbm, qkv_hbm, out_hbm, qkv_low, gate_up_low, squares_ref = refs[:6]
    weights_hbm, full, weights = refs[6:13], refs[13:18], refs[18:25]
    shared_ref, own_ref, tall_ref = refs[25:28]
    kept, landings = refs[28:30], refs[30:32]
    (
        cross,
        qkv_w,
        gate_up_w,
        tall,
        cols,
        gathered,
        load_sem,
        down_send,
        down_recv,
        up_send,
        up_recv,
        cross_send,
        cross_recv,
        share_send,
        share_recv,
    ) = refs[32:]
    me = lax.axis_index("dp")
    place = lax.axis_index("mp")
    span = data_count - 1
    ways = orders(data_count)
    stages = len(ways[0])
    down, up = (down_send, down_recv), (up_send, up_recv)
    padded, units = full[0].shape
    lanes = full[4].shape[1]
    height = padded // data_count
    f32 = jnp.float32

    whole = [row_pieces(ref, data_count) for ref in full]
    source = [row_pieces(ref, data_count) for ref in (qkv_hbm, out_hbm)]
    keep = [row_pieces(ref, data_count) for ref in kept]
    halvers = [Butterfly(ways[1 - i], i * span) for i in range(2)]
    doublers = [Butterfly(ways[way], k * span) for k, (_, _, _, way) in enumerate(parts)]
    views = [row_pieces(full[i], data_count, at, wide) for i, at, wide, _ in parts]

    loads = []

    def load(src, dst):
        copy = pltpu.make_async_copy(src, dst, load_sem.at[len(loads)])
        copy.start()
        loads.append(copy)

    early = [k for k, part in enumerate(parts) if part[0] < 3]
    late = [k for k, part in enumerate(parts) if part[0] >= 3]
    begin = {k: stages_left(parts[k], stages) - 1 for k in early}
    for k in early:
        i, at, wide, _ = parts[k]
        for j in range(doublers[k].width(begin[k])):
            q = doublers[k].piece(begin[k], j, True)
            load(row_pieces(ff_hbm.at[i], data_count, at, wide)(q), views[k](q))
    for i, fly in enumerate(halvers):
        for j in range(fly.width(0)):
            q = fly.piece(0, j, True)
            load(source[i](q), keep[i](q))
    load(qkv_low, qkv_w)
    load(gate_up_low, gate_up_w)
    others = [(place + k) % count for k in range(1, count)]
    greet([halvers[0].partner(s) for s in range(stages)] + [(me, other) for other in others])

    sent = []

    def start(copies):
        for copy in copies:
            copy.start()
        sent.extend(copies)
        return copies

    halves = [start(fly.halve(0, source[i], landings[i], down)) for i, fly in enumerate(halvers)]
    tall[...] = jnp.zeros_like(tall)
    cols[...] = jnp.zeros_like(cols)
    for copy in loads:
        copy.wait()
    fetched = []
    for i, (far_weight, near_weight) in enumerate(zip(weights_hbm, weights)):
        copy = pltpu.make_async_copy(far_weight, near_weight, load_sem.at[i])
        copy.start()
        fetched.append(copy)

    doubles = {}

    def spread(s, which):
        for k in which:
            doubles[k] = start(doublers[k].double(s, views[k], up))

    for k in early:
        spread(begin[k], [k])

    def note(k, q):
        i, start_lane, wide, _ = parts[k]
        rows = pl.ds(pl.multiple_of(q * height, height), height)
        grad = views[k](q)[...].astype(f32)
        if i == 3:
            at = lax.broadcasted_iota(jnp.int32, grad.shape, 0) + q * height
            grad = jnp.where(at < model_width, grad, 0.0)
        squares = grad * grad
        cols[i : i + 1, start_lane : start_lane + wide] += total(squares, 0)
        if i < 2:
            tall[rows, 3 + i : 4 + i] = total(squares, 1)
            weight = gate_up_w[rows, i * units : (i + 1) * units].astype(f32)
            tall[rows, 6:7] += total(grad * weight, 1)
        elif i == 3:
            for k in range(3):
                tall[rows, k : k + 1] = total(squares[:, k * lanes : (k + 1) * lanes], 1)
            tall[rows, 5:6] = total(grad * qkv_w[rows].astype(f32), 1)
        else:
            lane = 8 if i == 2 else 9
            tall[rows, lane : lane + 1] += total(squares, 1)

    for s in range(stages):
        for i, fly in enumerate(halvers):
            fly.add(s, keep[i], landings[i], halves[i])
            if s + 1 < stages:
                halves[i] = start(fly.halve(s + 1, keep[i], landings[i], down))
        if s == min(1, stages - 1):
            for k in early:
                if begin[k] > 0:
                    for copy in doubles[k]:
                        copy.wait_recv()
                    spread(0, [k])
    crossing = row_pieces(kept[1], data_count)(me)

    def lanes_of(other):
        return pl.ds(pl.multiple_of(other * lanes, lanes), lanes)

    start(
        [
            pltpu.make_async_remote_copy(
                src_ref=crossing.at[:, lanes_of(other)],
                dst_ref=cross.at[count - 2 - k],
                send_sem=cross_send.at[k],
                recv_sem=cross_recv.at[count - 2 - k],
                device_id=(me, other),
                device_id_type=pl.DeviceIdType.MESH,
            )
            for k, other in enumerate(others)
        ]
    )
    whole[3](me)[...] = keep[0](me)[...]
    spread(stages - 1, late[:1])
    summed = crossing[:, lanes_of(place)].astype(f32)
    for k in range(count - 1):
        pltpu.make_async_remote_copy(
            src_ref=cross.at[k],
            dst_ref=cross.at[k],
            send_sem=cross_send.at[k],
            recv_sem=cross_recv.at[k],
            device_id=(me, others[0]),
            device_id_type=pl.DeviceIdType.MESH,
        ).wait_recv()
        summed = summed + cross[k].astype(f32)
    whole[4](me)[...] = summed.astype(jnp.bfloat16)
    spread(stages - 1, late[1:])

    def note_pieces(k, s, mine):
        fly = doublers[k]

        def note_piece(j, carry):
            note(k, fly.piece(s, j, mine))
            return carry

        lax.fori_loop(0, fly.width(s), note_piece, 0)

    for k in early:
        note_pieces(k, 0, True)
    for k in late:
        note(k, me)
    for k in early:
        for copy in doubles[k]:
            copy.wait_recv()
        note_pieces(k, 0, False)
    for s in reversed(range(stages)):
        for k in late:
            for copy in doubles[k]:
                copy.wait_recv()
            if s > 0:
                doubles[k] = start(doublers[k].double(s - 1, views[k], up))
        for k in late:
            note_pieces(k, s, False)

    slots_rel = full[3][model_width : model_width + BUCKETS, :128].astype(f32)
    tall[:BUCKETS, 7:8] = total(slots_rel * slots_rel, 1)
    share = gathered.at[place]
    flat = tall[...].T[0:16]
    row = lax.broadcasted_iota(jnp.int32, flat.shape, 0)
    spare = jnp.concatenate([squares_ref[...], jnp.zeros((1, padded - 128), f32)], axis=1)
    share[...] = jnp.where(row == 10, spare, flat).astype(jnp.bfloat16)
    shares = start(
        [
            pltpu.make_async_remote_copy(
                src_ref=share,
                dst_ref=share,
                send_sem=share_send.at[k],
                recv_sem=share_recv.at[place],
                device_id=(me, other),
                device_id_type=pl.DeviceIdType.MESH,
            )
            for k, other in enumerate(others)
        ]
    )
    own_ref[...] = jnp.zeros_like(own_ref)
    own_ref[:, : cols.shape[1]] = cols[...]
    for k, other in enumerate(others):
        pltpu.make_async_remote_copy(
            src_ref=gathered.at[other],
            dst_ref=gathered.at[other],
            send_sem=share_send.at[k],
            recv_sem=share_recv.at[other],
            device_id=(me, other),
            device_id_type=pl.DeviceIdType.MESH,
        ).wait_recv()
    summed = gathered[0].astype(f32)
    for k in range(1, count):
        summed = summed + gathered[k].astype(f32)
    shared_ref[...] = summed
    tall_ref[...] = jnp.concatenate([summed, jnp.zeros((112, padded), f32)], axis=0).T
    for copy in fetched:
        copy.wait()
    for copy in sent:
        copy.wait_send()


def sum_weights(ff_grads, qkv, out, qkv_low, gate_up_low, squares, weights, model_width):
    count = lax.axis_size("mp")
    data_count = lax.axis_size("dp")
    far = pl.BlockSpec(memory_space=pltpu.HBM)
    near = pl.BlockSpec(memory_space=pltpu.VMEM)
    dma = pltpu.SemaphoreType.DMA
    low, f32 = jnp.bfloat16, jnp.float32
    span = data_count - 1
    units = ff_grads.shape[2]
    padded, wide = qkv.shape
    height = padded // data_count
    lanes = out.shape[1] // count
    full = [(padded, units)] * 3 + [(padded, wide), (padded, lanes)]
    parts = (*ff_parts(units), (3, 0, wide, 1), (4, 0, lanes, 0))
    n = len(parts)
    return pl.pallas_call(
        functools.partial(sum_weights_kernel, data_count, count, model_width, parts),
        out_shape=[pltpu.VMEM(s, low) for s in full]
        + [pltpu.VMEM(w.shape, f32) for w in weights]
        + [
            pltpu.VMEM((16, padded), f32),
            pltpu.VMEM((8, padded), f32),
            pltpu.VMEM((padded, 128), f32),
        ],
        in_specs=[far] * 5 + [near] + [far] * len(weights),
        out_specs=[near] * (8 + len(weights)),
        scratch_shapes=[pltpu.VMEM(a.shape, low) for a in (qkv, out)]
        + [pltpu.VMEM((span, height, a.shape[1]), low) for a in (qkv, out)]
        + [
            pltpu.VMEM((count - 1, height, lanes), low),
            pltpu.VMEM(qkv_low.shape, low),
            pltpu.VMEM(gate_up_low.shape, low),
            pltpu.VMEM((padded, 128), f32),
            pltpu.VMEM((8, (max(units, wide) + 127) // 128 * 128), f32),
            pltpu.VMEM((count, 16, padded), low),
            dma((3 * data_count + 5,)),
            dma((2 * span,)),
            dma((2 * span,)),
            dma((n * span,)),
            dma((n * span,)),
            dma((count - 1,)),
            dma((count - 1,)),
            dma((count - 1,)),
            dma((count,)),
        ],
        compiler_params=pltpu.CompilerParams(
            collective_id=2, has_side_effects=True, vmem_limit_bytes=30 << 20
        ),
        cost_estimate=pl.CostEstimate(
            flops=padded * units, bytes_accessed=200 << 20, transcendentals=0
        ),
        name="sum_weights",
    )(ff_grads, qkv, out, qkv_low, gate_up_low, squares, *weights)


def update_kernel(tensor_count, *refs):
    grads = refs[:5]
    weights, (rel_w, attn_w, ff_w) = refs[5:12], refs[12:15]
    shared_ref, own_ref, tall_ref = refs[15:18]
    news, rel_n = refs[18:25], refs[25]
    along, rel_r = refs[26:33], refs[33]
    across, rel_c = refs[34:41], refs[41]
    attn_n, attn_m, ff_n, ff_m = refs[42:46]
    first = pl.program_id(0) == 0
    height = news[0].shape[0]
    here_rows = pl.ds(pl.multiple_of(pl.program_id(0) * height, height), height)
    f32 = jnp.float32
    width = attn_w.shape[1]
    lanes = weights[3].shape[1]
    slots = rel_w.shape[0]
    tiny = 1e-30

    def step_rate(lane, size):
        return step_scale * jnp.sqrt(shared_ref[10:11, lane : lane + 1] / size)

    qkv = grads[3][here_rows].astype(f32)
    for k, (row, square, own, at) in enumerate(
        (
            (3, 4, 0, 0),
            (4, 5, 1, 0),
            (8, 7, 2, 0),
            (0, 0, 3, 0),
            (1, 1, 3, lanes),
            (2, 2, 3, 2 * lanes),
            (9, 6, 4, 0),
        )
    ):
        here = weights[k].shape[1]
        if own == 3:
            grad = qkv[:, at : at + lanes]
        else:
            grad = grads[own][here_rows].astype(f32)
        cols = here * tensor_count
        size = width * cols
        level = total(shared_ref[row : row + 1, :width], 1) / size + tiny
        rate = step_rate(square, size)
        row_factor = lax.rsqrt((tall_ref[here_rows, row : row + 1] / cols + tiny) / level) * rate
        col_moment = own_ref[own : own + 1, at : at + here] / width + tiny
        news[k][...] = weights[k][here_rows] - grad * row_factor * lax.rsqrt(col_moment)

        @pl.when(first)
        def _():
            along[k][...] = (shared_ref[row : row + 1, :width] / cols + tiny).reshape(width)
            across[k][...] = col_moment.reshape(here)

    @pl.when(first)
    def _():
        rel = grads[3][width : width + BUCKETS, :128].astype(f32)
        cols = slots * tensor_count
        size = BUCKETS * cols
        row_moment = shared_ref[7:8, :BUCKETS] / cols + tiny
        level = total(row_moment, 1) / BUCKETS
        row_factor = lax.rsqrt(row_moment / level) * step_rate(3, size)
        turned = rel.T[:slots]
        col_moment = total(turned * turned, 1) / BUCKETS + tiny
        rel_n[...] = rel_w[...] - turned * row_factor * lax.rsqrt(col_moment)
        rel_r[...] = row_moment.reshape(BUCKETS)
        rel_c[...] = (total(rel * rel, 0) / BUCKETS + tiny)[:, :slots]
        for gain, row, new, moment_out in ((attn_w, 5, attn_n, attn_m), (ff_w, 6, ff_n, ff_m)):
            value = gain[...]
            grad = shared_ref[row : row + 1, :width] / value
            moment = grad * grad + tiny
            rate = step_scale * jnp.sqrt(total(value * value, 1) / width)
            stepped = value - rate * grad * lax.rsqrt(total(moment, 1) / width)
            new[...] = stepped.reshape(width)
            moment_out[...] = moment.reshape(width)


def update(grads, weights, rel_w, attn_w, ff_w, shared, own, tall, chunks=4):
    tensor_count = lax.axis_size("mp")
    width = weights[0].shape[0]
    slots = rel_w.shape[0]
    f32 = jnp.float32

    def blocks(array):
        return pl.BlockSpec((width // chunks, array.shape[1]), lambda i: (i, 0))

    def fixed(rows, cols, at=0):
        return pl.BlockSpec((rows, cols), lambda i: (at, 0))

    def line(size):
        return pl.BlockSpec((size,), lambda i: (0,))

    matrices = [blocks(w) for w in weights]
    near = pl.BlockSpec(memory_space=pltpu.VMEM)
    rel_spec = fixed(slots, BUCKETS)
    columns = [w.shape[1] for w in weights]
    return pl.pallas_call(
        functools.partial(update_kernel, tensor_count),
        grid=(chunks,),
        in_specs=[
            *[near] * (len(grads) + len(weights)),
            rel_spec,
            fixed(1, width),
            fixed(1, width),
            near,
            near,
            near,
        ],
        out_specs=[*matrices, rel_spec]
        + [line(width)] * 7
        + [line(BUCKETS)]
        + [line(c) for c in columns]
        + [fixed(1, slots)]
        + [line(width)] * 4,
        out_shape=[jax.ShapeDtypeStruct(w.shape, f32) for w in weights]
        + [jax.ShapeDtypeStruct(rel_w.shape, f32)]
        + [jax.ShapeDtypeStruct((width,), f32)] * 7
        + [jax.ShapeDtypeStruct((BUCKETS,), f32)]
        + [jax.ShapeDtypeStruct((c,), f32) for c in columns]
        + [jax.ShapeDtypeStruct((1, slots), f32)]
        + [jax.ShapeDtypeStruct((width,), f32)] * 4,
        compiler_params=pltpu.CompilerParams(vmem_limit_bytes=16 << 20),
        cost_estimate=pl.CostEstimate(
            flops=40 * width * columns[0], bytes_accessed=36 * width * columns[0], transcendentals=0
        ),
        name="update",
    )(
        *grads, *weights, rel_w,
        attn_w.reshape(1, width), ff_w.reshape(1, width), shared, own, tall,
    )


def finish_kernel(middle_ref, ff_ref, d_middle_ref, dn_ref, x_ref, gain_ref, out_ref, grad_ref):
    f32, low = jnp.float32, jnp.bfloat16
    width = middle_ref.shape[1]
    out_ref[...] = (middle_ref[...] + ff_ref[...].astype(f32)).astype(low).T
    x = x_ref[...].T.astype(f32)
    back = norm_back(x, gain_ref[...].reshape(1, width), dn_ref[...].astype(f32))
    grad_ref[...] = (d_middle_ref[...] + back).astype(low).T


def finish(middle, ff, d_middle, dn, x, gain):
    positions, width = middle.shape
    rows = pl.BlockSpec((BLOCK, width), lambda i: (i, 0))
    columns = pl.BlockSpec((width, BLOCK), lambda i: (0, i))
    return pl.pallas_call(
        finish_kernel,
        grid=(positions // BLOCK,),
        in_specs=[rows] * 4 + [columns, pl.BlockSpec((width,), lambda i: (0,))],
        out_specs=[columns] * 2,
        out_shape=[jax.ShapeDtypeStruct((width, positions), jnp.bfloat16)] * 2,
        compiler_params=pltpu.CompilerParams(vmem_limit_bytes=58 << 20),
        cost_estimate=pl.CostEstimate(
            flops=20 * positions * width, bytes_accessed=18 * positions * width, transcendentals=0
        ),
        name="finish",
    )(middle, ff, d_middle, dn, x, gain)


def turn_order(count):
    return [sorted(range(count), key=lambda b: (abs(b - place), b < place)) for place in range(count)]


def look_up(table, row, column):
    found = jnp.int32(0)
    for r, entries in enumerate(table):
        for c, entry in enumerate(entries):
            found = jnp.where((row == r) & (column == c), jnp.int32(entry), found)
    return found


def feed_forward_kernel(
    data_count,
    count,
    parts,
    normed_hbm,
    cot_hbm,
    gate_up_hbm,
    down_hbm,
    out_hbm,
    dn_ref,
    pieces_hbm,
    normed,
    cot,
    gate_up,
    down,
    hidden,
    d_gate_up,
    outgoing,
    incoming,
    stage,
    grads,
    land_whole,
    land_most,
    land_rest,
    load_sem,
    stage_sem,
    gather_send,
    gather_recv,
    sum_send,
    sum_recv,
    down_send,
    down_recv,
):
    place = lax.axis_index("mp")
    row = lax.axis_index("dp")
    block_len, width = dn_ref.shape
    units = down.shape[1]
    part_len = block_len // parts
    last = count - 1
    has_left = place > 0
    has_right = place < last

    loads = [
        pltpu.make_async_copy(normed_hbm, normed.at[place], load_sem.at[0]),
        pltpu.make_async_copy(gate_up_hbm.at[pl.ds(0, width)], gate_up, load_sem.at[1]),
        pltpu.make_async_copy(down_hbm, down, load_sem.at[2]),
        pltpu.make_async_copy(cot_hbm, cot, load_sem.at[3]),
    ]
    for load in loads:
        load.start()

    ways = orders(data_count)
    span = data_count - 1
    most = land_most.shape[2]
    shares = (
        (0, 0, units, 0, land_whole.at[0]),
        (1, 0, units, 1, land_whole.at[1]),
        (2, 0, most, 0, land_most),
        (2, most, units - most, 1, land_rest),
    )
    flies = [Butterfly(ways[way], k * span) for k, (_, _, _, way, _) in enumerate(shares)]
    stages = len(ways[0])
    sems = (down_send, down_recv)
    views = [row_pieces(grads.at[i], data_count, at, lanes) for i, at, lanes, _, _ in shares]

    barrier = pltpu.get_barrier_semaphore()
    for s in range(stages):
        pl.semaphore_signal(
            barrier, inc=1, device_id=flies[0].partner(s), device_id_type=pl.DeviceIdType.MESH
        )
    for side, there in ((-1, has_left), (1, has_right)):

        @pl.when(there)
        def _():
            pl.semaphore_signal(
                barrier, inc=1, device_id=(row, place + side), device_id_type=pl.DeviceIdType.MESH
            )

    pl.semaphore_wait(barrier, stages + has_left.astype(jnp.int32) + has_right.astype(jnp.int32))

    def pass_block(block, side, slot):
        return pltpu.make_async_remote_copy(
            src_ref=normed.at[block],
            dst_ref=normed.at[block],
            send_sem=gather_send.at[slot],
            recv_sem=gather_recv.at[block],
            device_id=(row, place + side),
            device_id_type=pl.DeviceIdType.MESH,
        )

    def rows_of(part):
        return pl.ds(pl.multiple_of(part * part_len, part_len), part_len)

    def pass_sum(block, part, side, slot):
        return pltpu.make_async_remote_copy(
            src_ref=outgoing.at[block, rows_of(part)],
            dst_ref=incoming.at[slot, rows_of(part)],
            send_sem=sum_send.at[block, part],
            recv_sem=sum_recv.at[slot, part],
            device_id=(row, place + side),
            device_id_type=pl.DeviceIdType.MESH,
        )

    def landing(block, side):
        return jnp.where((side == -1) & (place + side == block), count, block)

    loads[0].wait()
    for side, there in ((-1, has_left), (1, has_right)):

        @pl.when(there)
        def _():
            pass_block(place, side, count + (side + 1) // 2).start()

    for load in loads[1:]:
        load.wait()

    def store_out(turn, block):
        return pltpu.make_async_copy(stage.at[turn % 2], out_hbm.at[block], stage_sem.at[turn % 2])

    table = turn_order(count)
    root = 0.7978845608028654

    def turn_body(turn, carry):
        block = look_up(table, place, turn)
        distance = jnp.abs(block - place)

        @pl.when((distance > 0) & ((block > place) | (place + distance > last)))
        def _():
            for side in (1, -1):
                other = place + side * distance

                @pl.when((other >= 0) & (other <= last))
                def _():
                    pass_block(other, 0, other).wait_recv()

                    @pl.when((place - side >= 0) & (place - side <= last))
                    def _():
                        pass_block(other, -side, other).start()

        acts = product(normed[block], gate_up[...])
        gate_act = acts[:, :units]
        up_act = acts[:, units:]
        squared = gate_act * gate_act
        bend = jnp.tanh(root * gate_act * (1.0 + 0.044715 * squared))
        half = 0.5 * (1.0 + bend)
        gelu = gate_act * half
        hidden[block] = (gelu * up_act).astype(jnp.bfloat16)
        d_hidden = product(cot[block], down[...])
        slope = half + 0.5 * gate_act * (1.0 - bend * bend) * (root * (1.0 + 0.134145 * squared))
        d_gate_up[block, :, :units] = (d_hidden * up_act * slope).astype(jnp.bfloat16)
        d_gate_up[block, :, units:] = (d_hidden * gelu).astype(jnp.bfloat16)
        term = right_inner(d_gate_up[block], gate_up[...])

        @pl.when(block == place)
        def _():
            dn_ref[...] = term

        @pl.when(block != place)
        def _():
            outgoing[block] = term.astype(jnp.bfloat16)

        for side, is_end in ((1, place == 0), (-1, place == last)):

            @pl.when(is_end & (block != place))
            def _():
                for part in range(parts):
                    pass_sum(block, part, side, landing(block, side)).start()

        @pl.when(turn >= 2)
        def _():
            store_out(turn, block).wait()

        stage[turn % 2] = right_inner(hidden[block], down[...]).astype(jnp.bfloat16)
        store_out(turn, block).start()
        return carry

    lax.fori_loop(0, count, turn_body, 0)

    def relay_side(key, side):
        owner = key if side == 1 else last - key
        through = (owner > place) & has_left if side == 1 else (owner < place) & has_right

        @pl.when(through)
        def _():
            def relay_part(part, carry):
                pass_sum(owner, part, side, owner).wait_recv()
                rows = rows_of(part)
                outgoing[owner, rows] = (
                    outgoing[owner, rows].astype(jnp.float32)
                    + incoming[owner, rows].astype(jnp.float32)
                ).astype(jnp.bfloat16)
                pass_sum(owner, part, side, landing(owner, side)).start()
                return carry

            lax.fori_loop(0, parts, relay_part, 0)

    def relay(key, between=None):
        for turn in (0, 1):
            for side in (1, -1):
                sooner = 2 * place <= last if side == 1 else 2 * place > last

                @pl.when(sooner if turn == 0 else jnp.logical_not(sooner))
                def _():
                    relay_side(key, side)

            if turn == 0 and between is not None:
                between()

    def flat(ref):
        return ref[...].reshape(count * block_len, ref.shape[2])

    sent = []

    def halve(k, s):
        copies = flies[k].halve(s, views[k], shares[k][4], sems)
        for copy in copies:
            copy.start()
        sent.extend(copies)
        return copies

    def add_halve(k, s, copies):
        flies[k].add(s, views[k], shares[k][4], copies)
        return halve(k, s + 1) if s + 1 < stages else None

    def weigh(i, left, right):
        grads[i, :width] = left_inner(left, right).astype(jnp.bfloat16)

    grads[:, width:] = jnp.zeros((3, grads.shape[1] - width, units), jnp.bfloat16)
    weigh(2, flat(cot), flat(hidden))
    flights = [None, None, halve(2, 0), halve(3, 0)]
    for key in range(1, last):
        relay(key)
    gate_side = d_gate_up[:, :, :units].reshape(count * block_len, units)
    weigh(0, flat(normed), gate_side)
    flights[0] = halve(0, 0)
    for k in (2, 3):
        flights[k] = add_halve(k, 0, flights[k])
    up_side = d_gate_up[:, :, units:].reshape(count * block_len, units)
    weigh(1, flat(normed), up_side)
    flights[1] = halve(1, 0)
    for k in (0, 1):
        flights[k] = add_halve(k, 0, flights[k])

    def halve_on():
        for s in range(1, stages - 1):
            for k in (2, 3, 0, 1):
                flights[k] = add_halve(k, s, flights[k])

    relay(last, halve_on)

    for side, there in ((1, has_left), (-1, has_right)):

        @pl.when(there)
        def _():
            slot = place if side == 1 else count

            def add_part(part, carry):
                pass_sum(place, part, side, slot).wait_recv()
                rows = rows_of(part)
                dn_ref[rows] += incoming[slot, rows].astype(jnp.float32)
                return carry

            lax.fori_loop(0, parts, add_part, 0)

    for k in (2, 3, 0, 1):
        add_halve(k, stages - 1, flights[k])
    mine = pl.ds(pl.multiple_of(row * pieces_hbm.shape[1], pieces_hbm.shape[1]), pieces_hbm.shape[1])
    save = pltpu.make_async_copy(grads.at[:, mine], pieces_hbm, load_sem.at[0])
    save.start()
    for copy in sent:
        copy.wait_send()

    for side, there in ((-1, has_left), (1, has_right)):

        @pl.when(there)
        def _():
            pass_block(place, side, count + (side + 1) // 2).wait_send()

    for block in range(count):

        @pl.when((block != place) & has_left & has_right)
        def _():
            pass_block(block, 1, block).wait_send()

        @pl.when(block != place)
        def _():
            for part in range(parts):
                pass_sum(block, part, 1, block).wait_send()

    for turn in (count - 2, count - 1):
        store_out(turn, 0).wait()
    save.wait()


def feed_forward(normed, cot_all, gate_up, down):
    count = lax.axis_size("mp")
    data_count = lax.axis_size("dp")
    block_len, width = normed.shape
    units = down.shape[1]
    padded = gate_up.shape[0]
    parts = 2
    low = jnp.bfloat16
    anywhere = pl.BlockSpec(memory_space=pl.ANY)
    dma = pltpu.SemaphoreType.DMA
    tokens = count * block_len
    height = padded // data_count
    span = data_count - 1
    most = (units // 2 + 127) // 128 * 128
    out_terms, dn, pieces = pl.pallas_call(
        functools.partial(feed_forward_kernel, data_count, count, parts),
        out_shape=[
            jax.ShapeDtypeStruct((count, block_len, width), low),
            jax.ShapeDtypeStruct((block_len, width), jnp.float32),
            jax.ShapeDtypeStruct((3, height, units), low),
        ],
        in_specs=[anywhere] * 4,
        out_specs=[anywhere, pl.BlockSpec(memory_space=pltpu.VMEM), anywhere],
        scratch_shapes=[
            pltpu.VMEM((count, block_len, width), low),
            pltpu.VMEM((count, block_len, width), low),
            pltpu.VMEM((width, 2 * units), low),
            pltpu.VMEM((width, units), low),
            pltpu.VMEM((count, block_len, units), low),
            pltpu.VMEM((count, block_len, 2 * units), low),
            pltpu.VMEM((count, block_len, width), low),
            pltpu.VMEM((count + 1, block_len, width), low),
            pltpu.VMEM((2, block_len, width), low),
            pltpu.VMEM((3, padded, units), low),
            pltpu.VMEM((2, span, height, units), low),
            pltpu.VMEM((span, height, most), low),
            pltpu.VMEM((span, height, units - most), low),
            dma((4,)),
            dma((2,)),
            dma((count + 2,)),
            dma((count,)),
            dma((count, parts)),
            dma((count + 1, parts)),
            dma((4 * span,)),
            dma((4 * span,)),
        ],
        compiler_params=pltpu.CompilerParams(
            collective_id=1, has_side_effects=True, vmem_limit_bytes=60 << 20
        ),
        cost_estimate=pl.CostEstimate(
            flops=18 * tokens * width * units,
            bytes_accessed=12 * width * units + 6 * tokens * width,
            transcendentals=tokens * units,
        ),
        name="feed_forward",
    )(normed, cot_all.reshape(count, block_len, width), gate_up, down)
    return out_terms.reshape(tokens, width), dn, pieces


def ff_parts(units):
    most = (units // 2 + 127) // 128 * 128
    return ((0, 0, units, 0), (1, 0, units, 1), (2, 0, most, 0), (2, most, units - most, 1))


def stages_left(part, stages):
    return min(2 if part[0] == 2 else 1, stages - 1)


def attend_back_kernel(
    data_count,
    count,
    slots,
    dn_hbm,
    middle_hbm,
    cot_hbm,
    gain_ref,
    proj_hbm,
    own_hbm,
    qkv_hbm,
    probs_hbm,
    norm_hbm,
    qkv_low_hbm,
    bucket_ref,
    ff_hbm,
    d_middle_hbm,
    terms_hbm,
    d_qkv_w_hbm,
    d_out_w_hbm,
    spread_hbm,
    dn,
    middle,
    cot,
    proj,
    own,
    qkv,
    probs,
    norm,
    qkv_low,
    d_own,
    grad,
    diag,
    dk,
    dv,
    d_qkv,
    terms,
    d_qkv_w,
    d_out_w,
    line,
    load_sem,
    probs_sem,
    cross_send,
    cross_recv,
    up_send,
    up_recv,
):
    place = lax.axis_index("mp")
    me = lax.axis_index("dp")
    block_len, width = dn.shape
    seq_len = qkv.shape[0]
    lanes = slots * HD
    padded = d_qkv_w.shape[0]
    steps = seq_len // BLOCK
    f32 = jnp.float32
    low = jnp.bfloat16

    loads = []

    def load(src, dst):
        copy = pltpu.make_async_copy(src, dst, load_sem.at[len(loads)])
        copy.start()
        loads.append(copy)

    load(dn_hbm, dn)
    load(middle_hbm, middle)
    load(cot_hbm, cot)
    load(proj_hbm, proj)
    load(own_hbm, own)
    load(qkv_hbm, qkv)
    load(norm_hbm, norm)
    load(qkv_low_hbm, qkv_low)
    height = padded // data_count
    mine = pl.ds(pl.multiple_of(me * height, height), height)
    load(ff_hbm, spread_hbm.at[:, mine])

    ways = orders(data_count)
    stages = len(ways[0])
    parts = ff_parts(spread_hbm.shape[2])
    span = data_count - 1
    flies = [Butterfly(ways[way], k * span) for k, (_, _, _, way) in enumerate(parts)]
    views = [row_pieces(spread_hbm.at[i], data_count, at, wide) for i, at, wide, _ in parts]
    others = [(place + k) % count for k in range(1, count)]
    greet([flies[0].partner(s) for s in range(1, stages)] + [(me, other) for other in others])
    sent = []

    def start(copies):
        for copy in copies:
            copy.start()
        sent.extend(copies)
        return copies

    flights = [
        start(
            fly.double(
                stages - 1, view, (up_send, up_recv), ff_hbm.at[i, :, pl.ds(at, wide)]
            )
        )
        for fly, view, (i, at, wide, _) in zip(flies, views, parts)
    ]

    table = turn_order(count)

    def fetch(t):
        per = block_len // BLOCK
        block = look_up(table, place, t // per) * per + t % per
        rows = pl.ds(pl.multiple_of(block * BLOCK, BLOCK), BLOCK)
        return block, pltpu.make_async_copy(
            probs_hbm.at[:, rows], probs.at[t % 2], probs_sem.at[t % 2]
        )

    fetch(0)[1].start()
    diag[...] = jnp.zeros_like(diag)
    dk[...] = jnp.zeros_like(dk)
    dv[...] = jnp.zeros_like(dv)
    for copy in loads[:3]:
        copy.wait()
    d_middle = cot[...].astype(f32) + norm_back(middle[...], gain_ref[...].reshape(1, width), dn[...])
    middle[...] = d_middle
    save_middle = pltpu.make_async_copy(middle, d_middle_hbm, load_sem.at[0])
    save_middle.start()
    cot[...] = d_middle.astype(low)
    loads[3].wait()
    d_all = product(cot[...], proj[:width]).astype(low)

    def own_rows(who):
        return pl.ds(pl.multiple_of(who * block_len, block_len), block_len)

    for k in range(count):
        d_own[k] = d_all[:, k * lanes : (k + 1) * lanes]
    start(
        [
            pltpu.make_async_remote_copy(
                src_ref=d_own.at[other],
                dst_ref=grad.at[own_rows(place)],
                send_sem=cross_send.at[k],
                recv_sem=cross_recv.at[place],
                device_id=(me, other),
                device_id_type=pl.DeviceIdType.MESH,
            )
            for k, other in enumerate(others)
        ]
    )
    grad[own_rows(place)] = d_own[place]
    loads[4].wait()
    d_out_w[width:] = jnp.zeros((padded - width, count * lanes), low)
    d_out_w[:width] = left_inner(cot[...], own[...]).astype(low)
    save_out = pltpu.make_async_copy(d_out_w, d_out_w_hbm, load_sem.at[1])
    save_out.start()
    loads[5].wait()

    def pass_on(s):
        for k, (fly, view) in enumerate(zip(flies, views)):
            for copy in flights[k]:
                copy.wait_recv()
            flights[k] = []
            if s > 1 and s - 1 >= stages_left(parts[k], stages):
                flights[k] = start(fly.double(s - 1, view, (up_send, up_recv)))

    def back_block(t, carry):
        per = block_len // BLOCK

        @pl.when((t > 0) & (t % per == 0))
        def _():
            who = look_up(table, place, t // per)
            pltpu.make_async_remote_copy(
                src_ref=d_own.at[0],
                dst_ref=grad.at[own_rows(who)],
                send_sem=cross_send.at[0],
                recv_sem=cross_recv.at[who],
                device_id=(me, who),
                device_id_type=pl.DeviceIdType.MESH,
            ).wait_recv()

        @pl.when(t + 1 < steps)
        def _():
            fetch(t + 1)[1].start()

        block, arrival = fetch(t)
        arrival.wait()
        rows = pl.ds(pl.multiple_of(block * BLOCK, BLOCK), BLOCK)
        window = pl.ds(pl.multiple_of((steps - 1 - block) * BLOCK, BLOCK), seq_len)
        queries = qkv[rows, 0:lanes]
        keys = qkv[:, lanes : 2 * lanes]
        values = qkv[:, 2 * lanes : 3 * lanes]
        d_query = jnp.zeros((BLOCK, lanes), f32)
        for slot in range(slots):
            weight = probs[t % 2, slot]
            slot_grad = slot_lanes(grad[rows], slot)
            d_probs = right_inner(slot_grad, values)
            delta = jnp.sum(weight * d_probs, axis=-1, keepdims=True)
            d_scores = (weight * (d_probs - delta)).astype(low)
            d_query = d_query + slot_lanes(product(d_scores, keys), slot)
            dk[...] += left_inner(slot_lanes(queries, slot), d_scores)
            dv[...] += left_inner(slot_grad, weight.astype(low))
            diag[slot, :, window] += d_scores.astype(f32)
        d_qkv[rows, 0:lanes] = d_query.astype(low)
        return carry

    loads[8].wait()
    pass_on(stages - 1)
    lax.fori_loop(0, steps, back_block, 0)
    for s in reversed(range(2, stages - 1)):
        pass_on(s)
    d_qkv[:, lanes : 2 * lanes] = dk[...].T.astype(low)
    d_qkv[:, 2 * lanes : 3 * lanes] = dv[...].T.astype(low)
    for copy in loads[6:8]:
        copy.wait()
    terms[...] = right_inner(d_qkv[...], qkv_low[:width]).astype(low)
    save_terms = pltpu.make_async_copy(terms, terms_hbm, load_sem.at[2])
    save_terms.start()
    d_qkv_w[:width] = left_inner(norm[...], d_qkv[...]).astype(low)
    d_qkv_w[width:] = jnp.zeros((padded - width, 3 * lanes), low)
    sums = []
    for slot in range(slots):
        level = diag[slot]
        rest = BLOCK // 2
        while rest >= 1:
            level = pltpu.roll(level[:rest], rest, 1) + level[rest:]
            rest //= 2
        sums.append(level)
    sums = jnp.concatenate(sums + [jnp.zeros((128 - slots, 2 * seq_len), f32)], axis=0)
    d_rel = lax.dot_general(
        onehot_rows(bucket_ref, line),
        sums,
        (((1,), (1,)), ((), ())),
        precision=highest,
        preferred_element_type=f32,
    )
    d_qkv_w[width : width + BUCKETS, :128] = d_rel.astype(low)
    save_qkv = pltpu.make_async_copy(d_qkv_w, d_qkv_w_hbm, load_sem.at[3])
    save_qkv.start()
    if stages > 1:
        pass_on(1)
    for copy in sent:
        copy.wait_send()
    for copy in (save_middle, save_out, save_terms, save_qkv):
        copy.wait()


def attend_back(dn, middle, cot, gain, proj_all, own, qkv, probs, norm, qkv_low, bucket, ff_pieces):
    count = lax.axis_size("mp")
    data_count = lax.axis_size("dp")
    seq_len = qkv.shape[0]
    slots = probs.shape[0]
    lanes = slots * HD
    block_len, width = dn.shape
    padded = qkv_low.shape[0]
    _, _, units = ff_pieces.shape
    far = pl.BlockSpec(memory_space=pltpu.HBM)
    near = pl.BlockSpec(memory_space=pltpu.VMEM)
    dma = pltpu.SemaphoreType.DMA
    low, f32 = jnp.bfloat16, jnp.float32
    span = data_count - 1
    scratch = [
        (dn.shape, f32),
        (middle.shape, f32),
        (cot.shape, low),
        (proj_all.shape, low),
        (own.shape, low),
        (qkv.shape, low),
        ((2, slots, BLOCK, seq_len), f32),
        (norm.shape, low),
        (qkv_low.shape, low),
        ((count, block_len, lanes), low),
        ((seq_len, lanes), low),
        ((slots, BLOCK, 2 * seq_len), f32),
        ((lanes, seq_len), f32),
        ((lanes, seq_len), f32),
        (qkv.shape, low),
        ((seq_len, width), low),
        ((padded, 3 * lanes), low),
        ((padded, count * lanes), low),
    ]
    return pl.pallas_call(
        functools.partial(attend_back_kernel, data_count, count, slots),
        in_specs=[far] * 3 + [near] + [far] * 6 + [near, far],
        out_specs=[far] * 5,
        out_shape=[
            jax.ShapeDtypeStruct((block_len, width), f32),
            jax.ShapeDtypeStruct((seq_len, width), low),
            jax.ShapeDtypeStruct((padded, 3 * lanes), low),
            jax.ShapeDtypeStruct((padded, count * lanes), low),
            jax.ShapeDtypeStruct((3, padded, units), low),
        ],
        scratch_shapes=[pltpu.VMEM(shape, dtype) for shape, dtype in scratch]
        + [
            pltpu.VMEM((1, 2 * seq_len), jnp.int32),
            dma((10,)),
            dma((2,)),
            dma((count - 1,)),
            dma((count,)),
            dma((4 * span,)),
            dma((4 * span,)),
        ],
        compiler_params=pltpu.CompilerParams(
            collective_id=3, has_side_effects=True, vmem_limit_bytes=56 << 20
        ),
        cost_estimate=pl.CostEstimate(
            flops=16 * slots * seq_len * seq_len * HD, bytes_accessed=140 << 20, transcendentals=0
        ),
        name="attend_back",
    )(dn, middle, cot, gain, proj_all, own, qkv, probs, norm, qkv_low, bucket, ff_pieces)


def onehot_rows(bucket_ref, line_ref):
    offsets = bucket_ref.shape[0]
    line_ref[...] = jnp.full(line_ref.shape, -1, jnp.int32)
    line_ref[:, :offsets] = bucket_ref[...].reshape(1, offsets)
    rows = lax.broadcasted_iota(jnp.int32, (BUCKETS, line_ref.shape[1]), 0)
    return jnp.where(rows == line_ref[...], 1.0, 0.0)


def front_kernel(
    data_count,
    count,
    slots,
    x_hbm,
    cot_hbm,
    query_hbm,
    key_hbm,
    value_hbm,
    out_hbm,
    gate_hbm,
    up_hbm,
    down_hbm,
    segments_ref,
    bucket_ref,
    rel_ref,
    attn_gain_ref,
    ff_gain_ref,
    norm_far,
    cot_far,
    own_cot_far,
    qkv_far,
    probs_far,
    own_far,
    middle_far,
    normed_far,
    proj_far,
    qkv_low_far,
    gate_up_far,
    down_far,
    squares_ref,
    x_in,
    cot_in,
    x,
    norm,
    cot,
    thin,
    wide,
    gate_low,
    up_low,
    down_low,
    blank,
    proj,
    qkv_low,
    qkv,
    tilt,
    seg_col,
    probs,
    mixed,
    own,
    normed,
    line,
    load_sem,
    save_sem,
    probs_sem,
    norm_send,
    norm_recv,
    cot_send,
    cot_recv,
    cross_send,
    cross_recv,
    side_send,
    side_recv,
    mix_send,
    mix_recv,
):
    place = lax.axis_index("mp")
    me = lax.axis_index("dp")
    last = count - 1
    f32, low = jnp.float32, jnp.bfloat16
    block_len, width = x.shape
    seq_len = count * block_len
    lanes = slots * HD
    padded = proj.shape[0]
    height = padded // data_count
    units = gate_low.shape[1]
    mesh_id = pl.DeviceIdType.MESH
    others = [(place + k) % count for k in range(1, count)]
    peers = [(me + k) % data_count for k in range(1, data_count)]

    def load(k, from_ref, to_ref):
        copy = pltpu.make_async_copy(from_ref, to_ref, load_sem.at[k])
        copy.start()
        return copy

    load_x = load(0, x_hbm, x_in)
    load_thin = [
        load(1 + k, ref, thin.at[k])
        for k, ref in enumerate((out_hbm, query_hbm, key_hbm, value_hbm))
    ]
    load_cot = load(5, cot_hbm, cot_in)
    load_gate = load(6, gate_hbm, wide.at[0])
    load_up = load(7, up_hbm, wide.at[1])
    greet([(me, other) for other in others] + [(peer, place) for peer in peers])

    saves = []

    def save(from_ref, to_ref):
        copy = pltpu.make_async_copy(from_ref, to_ref, save_sem.at[len(saves)])
        copy.start()
        saves.append(copy)

    sent = []

    def start(copy):
        copy.start()
        sent.append(copy)

    def pass_block(buffer, sems, block, side, slot):
        return pltpu.make_async_remote_copy(
            src_ref=buffer.at[block],
            dst_ref=buffer.at[block],
            send_sem=sems[0].at[slot],
            recv_sem=sems[1].at[block],
            device_id=(me, place + side),
            device_id_type=mesh_id,
        )

    def inside(block):
        return (block >= 0) & (block <= last)

    norm_sems = (norm_send, norm_recv)
    cot_sems = (cot_send, cot_recv)

    def take(buffer, sems, distance):
        for side in (1, -1):
            other = place + side * distance

            @pl.when(inside(other))
            def _():
                pass_block(buffer, sems, other, side, other).wait_recv()

                @pl.when(inside(place - side))
                def _():
                    pass_block(buffer, sems, other, -side, other).start()

    def send_own(buffer, sems, side):
        return pass_block(buffer, sems, place, side, count + (side + 1) // 2)

    def cot_may_go(distance):
        for side in (1, -1):
            behind = place if side == 1 else last - place

            @pl.when((behind == distance) & inside(place + side))
            def _():
                if distance == 0:
                    send_own(norm, norm_sems, side).wait_send()
                else:
                    far_end = 0 if side == 1 else last
                    pass_block(norm, norm_sems, far_end, side, far_end).wait_send()
                send_own(cot, cot_sems, side).start()

    between = inside(place - 1) & inside(place + 1)

    load_x.wait()
    x[...] = x_in[...].T.astype(f32)
    norm[place] = rms_norm(x[...], attn_gain_ref[...].reshape(1, width)).astype(low)
    for side in (1, -1):

        @pl.when(inside(place + side))
        def _():
            send_own(norm, norm_sems, side).start()

    load_cot.wait()
    cot[place] = cot_in[...].T
    save(cot.at[place], own_cot_far)

    lane = lax.broadcasted_iota(jnp.int32, (1, lanes), 1)
    slot_of = place * slots + lane // HD
    lane_mask = jnp.where((slot_of < 5) | (slot_of == 6), 1.0, 0.0)
    for copy in load_thin:
        copy.wait()

    def lanes_of(who):
        return pl.ds(pl.multiple_of(who * lanes, lanes), lanes)

    def rows_of(who):
        return pl.ds(pl.multiple_of(who * height, height), height)

    proj[width:, lanes_of(place)] = jnp.zeros((padded - width, lanes), low)
    qkv_low[width:] = jnp.zeros((padded - width, 3 * lanes), low)
    blank[...] = jnp.zeros_like(blank)
    column = lax.broadcasted_iota(jnp.int32, (1, 128), 1)
    squares = jnp.zeros((1, 128), f32)

    def square_of(values, at):
        return jnp.where(column == at, total(total(values * values, 1), 0), 0.0)

    masked = (thin[0] * lane_mask).astype(low)
    proj[:width, lanes_of(place)] = masked

    def proj_copy(src, dst, sems, send_slot, recv_slot, device):
        return pltpu.make_async_remote_copy(
            src_ref=src,
            dst_ref=dst,
            send_sem=sems[0].at[send_slot],
            recv_sem=sems[1].at[recv_slot],
            device_id=device,
            device_id_type=mesh_id,
        )

    cross, aside = (cross_send, cross_recv), (side_send, side_recv)
    for k, other in enumerate(others):
        view = proj.at[rows_of(me), lanes_of(place)]
        start(proj_copy(view, view, cross, k, count - 2 - k, (me, other)))
    for k in range(3):
        qkv_low[:width, k * lanes : (k + 1) * lanes] = (thin[1 + k] * lane_mask).astype(low)
        squares = squares + square_of(thin[1 + k], k)
    squares = squares + square_of(thin[0], 6) + square_of(rel_ref[...], 3)
    save(qkv_low, qkv_low_far)

    onehot = onehot_rows(bucket_ref, line)
    vector = lax.dot_general(
        rel_ref[...],
        onehot,
        (((1,), (0,)), ((), ())),
        precision=highest,
        preferred_element_type=f32,
    )
    for slot in range(slots):
        spread = jnp.broadcast_to(vector[slot : slot + 1, :], (BLOCK, 2 * seq_len))
        tilt[slot] = pltpu.roll(spread, 2 * seq_len - BLOCK + 1, 1, stride=1, stride_axis=0)
    seg_row = segments_ref[...].astype(f32)
    seg_col[...] = jnp.broadcast_to(seg_row, (128, seq_len)).T

    arrivals = []
    for k, other in enumerate(others):
        view = proj.at[rows_of(me), lanes_of(other)]
        proj_copy(view, view, cross, k, k, (me, other)).wait_recv()
        at = k * (data_count - 1)
        for j, peer in enumerate(peers):
            start(proj_copy(view, view, aside, at + j, at + data_count - 2 - j, (peer, place)))
            come = proj.at[rows_of(peer), lanes_of(other)]
            arrivals.append(proj_copy(come, come, aside, at + j, at + j, (peer, place)))

    def own_rows(who):
        return pl.ds(pl.multiple_of(who * block_len, block_len), block_len)

    def project(block):
        qkv[own_rows(block)] = product(norm[block], qkv_low[:width]).astype(low)

    def project_at(distance):
        for side in (1, -1):
            other = place + side * distance

            @pl.when(inside(other))
            def _():
                project(other)

    project(place)
    load_gate.wait()
    gate_low[...] = wide[0].astype(low)
    squares = squares + square_of(wide[0], 4)
    load_down = load(6, down_hbm, wide.at[0])
    rows_used = pl.ds(0, width)
    save(gate_low, gate_up_far.at[rows_used, pl.ds(0, units)])
    load_up.wait()
    up_low[...] = wide[1].astype(low)
    squares = squares + square_of(wide[1], 5)
    save(up_low, gate_up_far.at[rows_used, pl.ds(units, units)])
    save(blank, gate_up_far.at[pl.ds(width, padded - width)])
    take(norm, norm_sems, 1)
    cot_may_go(0)
    project_at(1)
    load_down.wait()
    down_low[...] = wide[0].astype(low)
    squares = squares + square_of(wide[0], 7)
    save(down_low, down_far)
    squares_ref[...] = squares
    for distance in range(2, count):
        take(norm, norm_sems, distance)
        cot_may_go(distance - 1)
        project_at(distance)
    save(qkv, qkv_far)
    save(norm, norm_far)

    @pl.when(between)
    def _():
        take(cot, cot_sems, 1)

    steps = seq_len // BLOCK
    per = block_len // BLOCK
    table = [order[::-1] for order in turn_order(count)]

    def store_probs(t, block):
        rows = pl.ds(pl.multiple_of(block * BLOCK, BLOCK), BLOCK)
        return pltpu.make_async_copy(probs.at[t % 2], probs_far.at[:, rows], probs_sem.at[t % 2])

    def mix_copy(owner):
        return pltpu.make_async_remote_copy(
            src_ref=mixed.at[own_rows(owner)],
            dst_ref=own.at[:, lanes_of(place)],
            send_sem=mix_send.at[owner],
            recv_sem=mix_recv.at[place],
            device_id=(me, owner),
            device_id_type=mesh_id,
        )

    def attend_block(t, carry):
        owner = look_up(table, place, t // per)
        block = owner * per + t % per
        rows = pl.ds(pl.multiple_of(block * BLOCK, BLOCK), BLOCK)
        window = pl.ds(pl.multiple_of((steps - 1 - block) * BLOCK, BLOCK), seq_len)
        same_doc = seg_col[rows, 0:1] == seg_row
        queries = qkv[rows, 0:lanes]
        keys = qkv[:, lanes : 2 * lanes]
        values = qkv[:, 2 * lanes : 3 * lanes]
        result = jnp.zeros((BLOCK, lanes), f32)

        @pl.when(t >= 2)
        def _():
            store_probs(t, block).wait()

        for slot in range(slots):
            scores = right_inner(slot_lanes(queries, slot), keys) + tilt[slot, :, window]
            scores = jnp.where(same_doc, scores, -1e30)
            peak = jnp.max(scores, axis=-1, keepdims=True)
            raised = jnp.exp(scores - peak)
            weight = raised * (1.0 / jnp.sum(raised, axis=-1, keepdims=True))
            probs[t % 2, slot] = weight
            result = result + slot_lanes(product(weight.astype(low), values), slot)
        store_probs(t, block).start()
        mixed[rows] = result.astype(low)

        @pl.when((t % per == per - 1) & (owner != place))
        def _():
            mix_copy(owner).start()

        return carry

    lax.fori_loop(0, steps, attend_block, 0)
    own[:, lanes_of(place)] = mixed[own_rows(place)]

    @pl.when(between)
    def _():
        for distance in range(2, count):
            take(cot, cot_sems, distance)

    for arrival in arrivals:
        arrival.wait_recv()
    save(proj, proj_far)
    for k, other in enumerate(others):
        pltpu.make_async_remote_copy(
            src_ref=mixed.at[own_rows(other)],
            dst_ref=own.at[:, lanes_of(other)],
            send_sem=mix_send.at[other],
            recv_sem=mix_recv.at[other],
            device_id=(me, other),
            device_id_type=mesh_id,
        ).wait_recv()
    save(own, own_far)
    x[...] = x[...] + right_inner(own[...], proj[:width])
    save(x, middle_far)
    normed[...] = rms_norm(x[...], ff_gain_ref[...].reshape(1, width)).astype(low)
    save(normed, normed_far)

    @pl.when(jnp.logical_not(between))
    def _():
        for distance in range(1, count):
            take(cot, cot_sems, distance)

    save(cot, cot_far)
    for t in (0, 1):
        store_probs(t, 0).wait()
    for copy in saves:
        copy.wait()
    for copy in sent:
        copy.wait_send()
    for k, other in enumerate(others):
        mix_copy(other).wait_send()
    for buffer, sems in ((norm, norm_sems), (cot, cot_sems)):
        for side in (1, -1):
            behind = place if side == 1 else last - place
            unwaited = behind > 0 if buffer is norm else behind >= 0

            @pl.when(unwaited & inside(place + side))
            def _():
                send_own(buffer, sems, side).wait_send()

        for block in range(1, last) if buffer is norm else range(count):

            @pl.when((block != place) & between)
            def _():
                pass_block(buffer, sems, block, 1, block).wait_send()


def front(x, cot, weights, segments, bucket, rel_bias, attn_gain, ff_gain):
    count = lax.axis_size("mp")
    data_count = lax.axis_size("dp")
    query, key, value, out, gate, up, down = weights
    width, block_len = x.shape
    lanes = query.shape[1]
    slots = lanes // HD
    units = gate.shape[1]
    seq_len = count * block_len
    piece = 16 * data_count
    padded = (width + piece - 1) // piece * piece
    low, f32 = jnp.bfloat16, jnp.float32
    far = pl.BlockSpec(memory_space=pltpu.HBM)
    near = pl.BlockSpec(memory_space=pltpu.VMEM)
    dma = pltpu.SemaphoreType.DMA
    outs = [
        ((count, block_len, width), low),
        ((count, block_len, width), low),
        ((block_len, width), low),
        ((seq_len, 3 * lanes), low),
        ((slots, seq_len, seq_len), f32),
        ((block_len, count * lanes), low),
        ((block_len, width), f32),
        ((block_len, width), low),
        ((padded, count * lanes), low),
        ((padded, 3 * lanes), low),
        ((padded, 2 * units), low),
        ((width, units), low),
        ((1, 128), f32),
    ]
    scratch = [
        ((width, block_len), low),
        ((width, block_len), low),
        ((block_len, width), f32),
        ((count, block_len, width), low),
        ((count, block_len, width), low),
        ((4, width, lanes), f32),
        ((2, width, units), f32),
        ((width, units), low),
        ((width, units), low),
        ((width, units), low),
        ((padded - width, 2 * units), low),
        ((padded, count * lanes), low),
        ((padded, 3 * lanes), low),
        ((seq_len, 3 * lanes), low),
        ((slots, BLOCK, 2 * seq_len), f32),
        ((seq_len, 128), f32),
        ((2, slots, BLOCK, seq_len), f32),
        ((seq_len, lanes), low),
        ((block_len, count * lanes), low),
        ((block_len, width), low),
    ]
    sides = (count - 1) * (data_count - 1)
    return pl.pallas_call(
        functools.partial(front_kernel, data_count, count, slots),
        in_specs=[far] * 9 + [near] * 5,
        out_specs=[far] * 12 + [near],
        out_shape=[jax.ShapeDtypeStruct(shape, dtype) for shape, dtype in outs],
        scratch_shapes=[pltpu.VMEM(shape, dtype) for shape, dtype in scratch]
        + [
            pltpu.VMEM((1, 2 * seq_len), jnp.int32),
            dma((8,)),
            dma((16,)),
            dma((2,)),
            dma((count + 2,)),
            dma((count,)),
            dma((count + 2,)),
            dma((count,)),
            dma((count - 1,)),
            dma((count - 1,)),
            dma((sides,)),
            dma((sides,)),
            dma((count,)),
            dma((count,)),
        ],
        compiler_params=pltpu.CompilerParams(
            collective_id=0, has_side_effects=True, vmem_limit_bytes=60 << 20
        ),
        cost_estimate=pl.CostEstimate(
            flops=8 * slots * seq_len * seq_len * HD,
            bytes_accessed=300 << 20,
            transcendentals=slots * seq_len * seq_len,
        ),
        name="front",
    )(
        x, cot, query, key, value, out, gate, up, down,
        segments, bucket, rel_bias, attn_gain, ff_gain,
    )


def local(
    layer_in,
    segment_ids,
    bucket_table,
    attn_gain,
    query_weight,
    key_weight,
    value_weight,
    out_weight,
    rel_bias,
    ff_gain,
    gate_weight,
    up_weight,
    down_weight,
    cotangent,
):
    model_width = layer_in.shape[2]
    slots_here = rel_bias.shape[1]
    layer_in = layer_in[0]
    down_turned = down_weight.T
    out_turned = out_weight.T
    rel_turned = rel_bias.T
    (
        flat_norm,
        flat_cot,
        own_cot,
        qkv,
        probs,
        own_attended,
        middle,
        normed_ff_local,
        proj_all,
        qkv_low,
        gate_up_low,
        down_low,
        squares,
    ) = front(
        layer_in.T,
        cotangent[0].T,
        (query_weight, key_weight, value_weight, out_turned, gate_weight, up_weight, down_turned),
        segment_ids,
        bucket_table,
        rel_turned,
        attn_gain,
        ff_gain,
    )
    flat_norm = flat_norm.reshape(-1, model_width)
    out_terms, dn_ff, ff_pieces = feed_forward(normed_ff_local, flat_cot, gate_up_low, down_low)
    d_middle, dn_attn_terms, d_qkv_w, d_out_w, ff_grads = attend_back(
        dn_ff,
        middle,
        own_cot,
        ff_gain,
        proj_all,
        own_attended,
        qkv,
        probs,
        flat_norm,
        qkv_low,
        bucket_table,
        ff_pieces,
    )
    ff_branch = lax.psum_scatter(out_terms, "mp", scatter_dimension=0, tiled=True)
    dn_attn = lax.psum_scatter(dn_attn_terms, "mp", scatter_dimension=0, tiled=True)
    weights = (
        gate_weight,
        up_weight,
        down_turned,
        query_weight,
        key_weight,
        value_weight,
        out_turned,
    )
    *held, shared, own, tall = sum_weights(
        ff_grads, d_qkv_w, d_out_w, qkv_low, gate_up_low, squares, weights, model_width
    )
    results = update(held[:5], held[5:], rel_turned, attn_gain, ff_gain, shared, own, tall)
    news, along, across = results[:8], results[8:16], results[16:24]
    new_attn_gain, attn_gain_moment, new_ff_gain, ff_gain_moment = results[24:]
    gate, up, down, query, key, value, out, rel = zip(news, along, across)
    rel = (rel[0].T, rel[1], rel[2].reshape(slots_here))
    down = (down[0].T, down[2], down[1])
    out = (out[0].T, out[2], out[1])
    layer_out, input_grad = finish(middle, ff_branch, d_middle, dn_attn, layer_in.T, attn_gain)
    return (
        layer_out.T[None],
        input_grad.T[None],
        new_attn_gain,
        attn_gain_moment,
        *query,
        *key,
        *value,
        *out,
        *rel,
        new_ff_gain,
        ff_gain_moment,
        *gate,
        *up,
        *down,
    )


def solution(mesh):
    return jax.shard_map(
        local,
        mesh=mesh,
        in_specs=(
            P("dp", "mp", None),
            P("dp", None),
            P(),
            P(),
            P(None, "mp"),
            P(None, "mp"),
            P(None, "mp"),
            P("mp", None),
            P(None, "mp"),
            P(),
            P(None, "mp"),
            P(None, "mp"),
            P("mp", None),
            P("dp", "mp", None),
        ),
        out_specs=(
            P("dp", "mp", None),
            P("dp", "mp", None),
            P(),
            P(),
            P(None, "mp"),
            P(),
            P("mp"),
            P(None, "mp"),
            P(),
            P("mp"),
            P(None, "mp"),
            P(),
            P("mp"),
            P("mp", None),
            P("mp"),
            P(),
            P(None, "mp"),
            P(),
            P("mp"),
            P(),
            P(),
            P(None, "mp"),
            P(),
            P("mp"),
            P(None, "mp"),
            P(),
            P("mp"),
            P("mp", None),
            P("mp"),
            P(),
        ),
        check_vma=False,
    )
```

```python
import functools

import jax
import jax.numpy as jnp
from jax import lax
from jax.experimental import pallas as pl
from jax.experimental.pallas import tpu as pltpu
from jax.sharding import PartitionSpec as P

HD = 64
BUCKETS = 32
BLOCK = 128


highest = lax.Precision.HIGHEST
step_scale = 0.3


def rms_norm(values, gain):
    return values * lax.rsqrt(jnp.mean(values * values, axis=-1, keepdims=True) + 1e-06) * gain


def norm_back(values, gain, grad):
    scale = lax.rsqrt(jnp.mean(values * values, axis=-1, keepdims=True) + 1e-06)
    unit = values * scale
    pull = grad * gain
    return scale * (pull - unit * jnp.mean(pull * unit, axis=-1, keepdims=True))


def product(left_side, right_side):
    return jnp.dot(left_side, right_side, preferred_element_type=jnp.float32)


def left_inner(left_side, right_side):
    return lax.dot_general(
        left_side, right_side, (((0,), (0,)), ((), ())), preferred_element_type=jnp.float32
    )


def right_inner(left_side, right_side):
    return lax.dot_general(
        left_side, right_side, (((1,), (1,)), ((), ())), preferred_element_type=jnp.float32
    )


def slot_lanes(values, slot):
    lane = lax.broadcasted_iota(jnp.int32, values.shape, 1)
    return jnp.where((lane >= slot * HD) & (lane < (slot + 1) * HD), values, jnp.zeros_like(values))


class Butterfly:
    def __init__(self, order, base):
        self.order = order
        self.me = lax.axis_index("dp")
        self.line = lax.axis_index("mp")
        self.base = base
        self.offsets = []
        total = 0
        for s in range(len(order)):
            self.offsets.append(total)
            total += 1 << (len(order) - 1 - s)

    def bit(self, b):
        return (self.me // b) % 2

    def partner(self, s):
        b = self.order[s]
        return (self.me + b * (1 - 2 * self.bit(b)), self.line)

    def width(self, s):
        return 1 << (len(self.order) - 1 - s)

    def piece(self, s, j, mine):
        b = self.order[s]
        found = sum(k * self.bit(k) for k in self.order[:s])
        found = found + b * (self.bit(b) if mine else 1 - self.bit(b))
        for i, k in enumerate(self.order[s + 1 :]):
            found = found + k * ((j // (1 << i)) % 2)
        return found

    def copy(self, src, dst, sems, slot, s):
        return pltpu.make_async_remote_copy(
            src_ref=src,
            dst_ref=dst,
            send_sem=sems[0].at[self.base + slot],
            recv_sem=sems[1].at[self.base + slot],
            device_id=self.partner(s),
            device_id_type=pl.DeviceIdType.MESH,
        )

    def halve(self, s, source, landing, sems):
        at = self.offsets[s]
        return [
            self.copy(source(self.piece(s, j, False)), landing.at[at + j], sems, at + j, s)
            for j in range(self.width(s))
        ]

    def add(self, s, kept, landing, copies):
        at = self.offsets[s]
        for j, copy in enumerate(copies):
            copy.wait_recv()
            mine = kept(self.piece(s, j, True))
            mine[...] = (mine[...].astype(jnp.float32) + landing[at + j].astype(jnp.float32)).astype(
                jnp.bfloat16
            )

    def double(self, s, whole, sems, first=None):
        at = self.offsets[s]
        copies = []
        for j in range(self.width(s)):
            view = whole(self.piece(s, j, True))
            copies.append(self.copy(view if first is None else first, view, sems, at + j, s))
        return copies


def orders(data_count):
    bits = [1 << i for i in range(data_count.bit_length() - 1)]
    return (bits, bits[:1] + bits[:0:-1])


def greet(peers):
    barrier = pltpu.get_barrier_semaphore()
    for peer in peers:
        pl.semaphore_signal(barrier, inc=1, device_id=peer, device_id_type=pl.DeviceIdType.MESH)
    pl.semaphore_wait(barrier, len(peers))


def row_pieces(ref, data_count, at=0, lanes=None):
    rows = ref.shape[0] // data_count
    columns = pl.ds(at, ref.shape[1] if lanes is None else lanes)
    return lambda q: ref.at[pl.ds(pl.multiple_of(q * rows, rows), rows), columns]


def total(values, axis):
    return jnp.sum(values, axis=axis, keepdims=True)


def sum_weights_kernel(data_count, count, model_width, parts, *refs):
    ff_hbm, qkv_hbm, out_hbm, qkv_low, gate_up_low, squares_ref = refs[:6]
    weights_hbm, full, weights = refs[6:13], refs[13:18], refs[18:25]
    shared_ref, own_ref, tall_ref = refs[25:28]
    kept, landings = refs[28:30], refs[30:32]
    (
        cross,
        qkv_w,
        gate_up_w,
        tall,
        cols,
        gathered,
        load_sem,
        down_send,
        down_recv,
        up_send,
        up_recv,
        cross_send,
        cross_recv,
        share_send,
        share_recv,
    ) = refs[32:]
    me = lax.axis_index("dp")
    place = lax.axis_index("mp")
    span = data_count - 1
    ways = orders(data_count)
    stages = len(ways[0])
    down, up = (down_send, down_recv), (up_send, up_recv)
    padded, units = full[0].shape
    lanes = full[4].shape[1]
    height = padded // data_count
    f32 = jnp.float32

    whole = [row_pieces(ref, data_count) for ref in full]
    source = [row_pieces(ref, data_count) for ref in (qkv_hbm, out_hbm)]
    keep = [row_pieces(ref, data_count) for ref in kept]
    halvers = [Butterfly(ways[1 - i], i * span) for i in range(2)]
    doublers = [Butterfly(ways[way], k * span) for k, (_, _, _, way) in enumerate(parts)]
    views = [row_pieces(full[i], data_count, at, wide) for i, at, wide, _ in parts]

    loads = []

    def load(src, dst):
        copy = pltpu.make_async_copy(src, dst, load_sem.at[len(loads)])
        copy.start()
        loads.append(copy)

    early = [k for k, part in enumerate(parts) if part[0] < 3]
    late = [k for k, part in enumerate(parts) if part[0] >= 3]
    begin = {k: stages_left(parts[k], stages) - 1 for k in early}
    for k in early:
        i, at, wide, _ = parts[k]
        for j in range(doublers[k].width(begin[k])):
            q = doublers[k].piece(begin[k], j, True)
            load(row_pieces(ff_hbm.at[i], data_count, at, wide)(q), views[k](q))
    for i, fly in enumerate(halvers):
        for j in range(fly.width(0)):
            q = fly.piece(0, j, True)
            load(source[i](q), keep[i](q))
    load(qkv_low, qkv_w)
    load(gate_up_low, gate_up_w)
    others = [(place + k) % count for k in range(1, count)]
    greet([halvers[0].partner(s) for s in range(stages)] + [(me, other) for other in others])

    sent = []

    def start(copies):
        for copy in copies:
            copy.start()
        sent.extend(copies)
        return copies

    halves = [start(fly.halve(0, source[i], landings[i], down)) for i, fly in enumerate(halvers)]
    tall[...] = jnp.zeros_like(tall)
    cols[...] = jnp.zeros_like(cols)
    for copy in loads:
        copy.wait()
    fetched = []
    for i, (far_weight, near_weight) in enumerate(zip(weights_hbm, weights)):
        copy = pltpu.make_async_copy(far_weight, near_weight, load_sem.at[i])
        copy.start()
        fetched.append(copy)

    doubles = {}

    def spread(s, which):
        for k in which:
            doubles[k] = start(doublers[k].double(s, views[k], up))

    for k in early:
        spread(begin[k], [k])

    def note(k, q):
        i, start_lane, wide, _ = parts[k]
        rows = pl.ds(pl.multiple_of(q * height, height), height)
        grad = views[k](q)[...].astype(f32)
        if i == 3:
            at = lax.broadcasted_iota(jnp.int32, grad.shape, 0) + q * height
            grad = jnp.where(at < model_width, grad, 0.0)
        squares = grad * grad
        cols[i : i + 1, start_lane : start_lane + wide] += total(squares, 0)
        if i < 2:
            tall[rows, 3 + i : 4 + i] = total(squares, 1)
            weight = gate_up_w[rows, i * units : (i + 1) * units].astype(f32)
            tall[rows, 6:7] += total(grad * weight, 1)
        elif i == 3:
            for k in range(3):
                tall[rows, k : k + 1] = total(squares[:, k * lanes : (k + 1) * lanes], 1)
            tall[rows, 5:6] = total(grad * qkv_w[rows].astype(f32), 1)
        else:
            lane = 8 if i == 2 else 9
            tall[rows, lane : lane + 1] += total(squares, 1)

    for s in range(stages):
        for i, fly in enumerate(halvers):
            fly.add(s, keep[i], landings[i], halves[i])
            if s + 1 < stages:
                halves[i] = start(fly.halve(s + 1, keep[i], landings[i], down))
        if s == min(1, stages - 1):
            for k in early:
                if begin[k] > 0:
                    for copy in doubles[k]:
                        copy.wait_recv()
                    spread(0, [k])
    crossing = row_pieces(kept[1], data_count)(me)

    def lanes_of(other):
        return pl.ds(pl.multiple_of(other * lanes, lanes), lanes)

    start(
        [
            pltpu.make_async_remote_copy(
                src_ref=crossing.at[:, lanes_of(other)],
                dst_ref=cross.at[count - 2 - k],
                send_sem=cross_send.at[k],
                recv_sem=cross_recv.at[count - 2 - k],
                device_id=(me, other),
                device_id_type=pl.DeviceIdType.MESH,
            )
            for k, other in enumerate(others)
        ]
    )
    whole[3](me)[...] = keep[0](me)[...]
    spread(stages - 1, late[:1])
    summed = crossing[:, lanes_of(place)].astype(f32)
    for k in range(count - 1):
        pltpu.make_async_remote_copy(
            src_ref=cross.at[k],
            dst_ref=cross.at[k],
            send_sem=cross_send.at[k],
            recv_sem=cross_recv.at[k],
            device_id=(me, others[0]),
            device_id_type=pl.DeviceIdType.MESH,
        ).wait_recv()
        summed = summed + cross[k].astype(f32)
    whole[4](me)[...] = summed.astype(jnp.bfloat16)
    spread(stages - 1, late[1:])

    def note_pieces(k, s, mine):
        fly = doublers[k]

        def note_piece(j, carry):
            note(k, fly.piece(s, j, mine))
            return carry

        lax.fori_loop(0, fly.width(s), note_piece, 0)

    for k in early:
        note_pieces(k, 0, True)
    for k in late:
        note(k, me)
    for k in early:
        for copy in doubles[k]:
            copy.wait_recv()
        note_pieces(k, 0, False)
    for s in reversed(range(stages)):
        for k in late:
            for copy in doubles[k]:
                copy.wait_recv()
            if s > 0:
                doubles[k] = start(doublers[k].double(s - 1, views[k], up))
        for k in late:
            note_pieces(k, s, False)

    slots_rel = full[3][model_width : model_width + BUCKETS, :128].astype(f32)
    tall[:BUCKETS, 7:8] = total(slots_rel * slots_rel, 1)
    share = gathered.at[place]
    flat = tall[...].T[0:16]
    row = lax.broadcasted_iota(jnp.int32, flat.shape, 0)
    spare = jnp.concatenate([squares_ref[...], jnp.zeros((1, padded - 128), f32)], axis=1)
    share[...] = jnp.where(row == 10, spare, flat).astype(jnp.bfloat16)
    shares = start(
        [
            pltpu.make_async_remote_copy(
                src_ref=share,
                dst_ref=share,
                send_sem=share_send.at[k],
                recv_sem=share_recv.at[place],
                device_id=(me, other),
                device_id_type=pl.DeviceIdType.MESH,
            )
            for k, other in enumerate(others)
        ]
    )
    own_ref[...] = jnp.zeros_like(own_ref)
    own_ref[:, : cols.shape[1]] = cols[...]
    for k, other in enumerate(others):
        pltpu.make_async_remote_copy(
            src_ref=gathered.at[other],
            dst_ref=gathered.at[other],
            send_sem=share_send.at[k],
            recv_sem=share_recv.at[other],
            device_id=(me, other),
            device_id_type=pl.DeviceIdType.MESH,
        ).wait_recv()
    summed = gathered[0].astype(f32)
    for k in range(1, count):
        summed = summed + gathered[k].astype(f32)
    shared_ref[...] = summed
    tall_ref[...] = jnp.concatenate([summed, jnp.zeros((112, padded), f32)], axis=0).T
    for copy in fetched:
        copy.wait()
    for copy in sent:
        copy.wait_send()


def sum_weights(ff_grads, qkv, out, qkv_low, gate_up_low, squares, weights, model_width):
    count = lax.axis_size("mp")
    data_count = lax.axis_size("dp")
    far = pl.BlockSpec(memory_space=pltpu.HBM)
    near = pl.BlockSpec(memory_space=pltpu.VMEM)
    dma = pltpu.SemaphoreType.DMA
    low, f32 = jnp.bfloat16, jnp.float32
    span = data_count - 1
    units = ff_grads.shape[2]
    padded, wide = qkv.shape
    height = padded // data_count
    lanes = out.shape[1] // count
    full = [(padded, units)] * 3 + [(padded, wide), (padded, lanes)]
    parts = (*ff_parts(units), (3, 0, wide, 1), (4, 0, lanes, 0))
    n = len(parts)
    return pl.pallas_call(
        functools.partial(sum_weights_kernel, data_count, count, model_width, parts),
        out_shape=[pltpu.VMEM(s, low) for s in full]
        + [pltpu.VMEM(w.shape, f32) for w in weights]
        + [
            pltpu.VMEM((16, padded), f32),
            pltpu.VMEM((8, padded), f32),
            pltpu.VMEM((padded, 128), f32),
        ],
        in_specs=[far] * 5 + [near] + [far] * len(weights),
        out_specs=[near] * (8 + len(weights)),
        scratch_shapes=[pltpu.VMEM(a.shape, low) for a in (qkv, out)]
        + [pltpu.VMEM((span, height, a.shape[1]), low) for a in (qkv, out)]
        + [
            pltpu.VMEM((count - 1, height, lanes), low),
            pltpu.VMEM(qkv_low.shape, low),
            pltpu.VMEM(gate_up_low.shape, low),
            pltpu.VMEM((padded, 128), f32),
            pltpu.VMEM((8, (max(units, wide) + 127) // 128 * 128), f32),
            pltpu.VMEM((count, 16, padded), low),
            dma((3 * data_count + 5,)),
            dma((2 * span,)),
            dma((2 * span,)),
            dma((n * span,)),
            dma((n * span,)),
            dma((count - 1,)),
            dma((count - 1,)),
            dma((count - 1,)),
            dma((count,)),
        ],
        compiler_params=pltpu.CompilerParams(
            collective_id=2, has_side_effects=True, vmem_limit_bytes=30 << 20
        ),
        cost_estimate=pl.CostEstimate(
            flops=padded * units, bytes_accessed=200 << 20, transcendentals=0
        ),
        name="sum_weights",
    )(ff_grads, qkv, out, qkv_low, gate_up_low, squares, *weights)


def update_kernel(tensor_count, *refs):
    grads = refs[:5]
    weights, (rel_w, attn_w, ff_w) = refs[5:12], refs[12:15]
    shared_ref, own_ref, tall_ref = refs[15:18]
    news, rel_n = refs[18:25], refs[25]
    along, rel_r = refs[26:33], refs[33]
    across, rel_c = refs[34:41], refs[41]
    attn_n, attn_m, ff_n, ff_m = refs[42:46]
    first = pl.program_id(0) == 0
    height = news[0].shape[0]
    here_rows = pl.ds(pl.multiple_of(pl.program_id(0) * height, height), height)
    f32 = jnp.float32
    width = attn_w.shape[1]
    lanes = weights[3].shape[1]
    slots = rel_w.shape[0]
    tiny = 1e-30

    def step_rate(lane, size):
        return step_scale * jnp.sqrt(shared_ref[10:11, lane : lane + 1] / size)

    qkv = grads[3][here_rows].astype(f32)
    for k, (row, square, own, at) in enumerate(
        (
            (3, 4, 0, 0),
            (4, 5, 1, 0),
            (8, 7, 2, 0),
            (0, 0, 3, 0),
            (1, 1, 3, lanes),
            (2, 2, 3, 2 * lanes),
            (9, 6, 4, 0),
        )
    ):
        here = weights[k].shape[1]
        if own == 3:
            grad = qkv[:, at : at + lanes]
        else:
            grad = grads[own][here_rows].astype(f32)
        cols = here * tensor_count
        size = width * cols
        level = total(shared_ref[row : row + 1, :width], 1) / size + tiny
        rate = step_rate(square, size)
        row_factor = lax.rsqrt((tall_ref[here_rows, row : row + 1] / cols + tiny) / level) * rate
        col_moment = own_ref[own : own + 1, at : at + here] / width + tiny
        news[k][...] = weights[k][here_rows] - grad * row_factor * lax.rsqrt(col_moment)

        @pl.when(first)
        def _():
            along[k][...] = (shared_ref[row : row + 1, :width] / cols + tiny).reshape(width)
            across[k][...] = col_moment.reshape(here)

    @pl.when(first)
    def _():
        rel = grads[3][width : width + BUCKETS, :128].astype(f32)
        cols = slots * tensor_count
        size = BUCKETS * cols
        row_moment = shared_ref[7:8, :BUCKETS] / cols + tiny
        level = total(row_moment, 1) / BUCKETS
        row_factor = lax.rsqrt(row_moment / level) * step_rate(3, size)
        turned = rel.T[:slots]
        col_moment = total(turned * turned, 1) / BUCKETS + tiny
        rel_n[...] = rel_w[...] - turned * row_factor * lax.rsqrt(col_moment)
        rel_r[...] = row_moment.reshape(BUCKETS)
        rel_c[...] = (total(rel * rel, 0) / BUCKETS + tiny)[:, :slots]
        for gain, row, new, moment_out in ((attn_w, 5, attn_n, attn_m), (ff_w, 6, ff_n, ff_m)):
            value = gain[...]
            grad = shared_ref[row : row + 1, :width] / value
            moment = grad * grad + tiny
            rate = step_scale * jnp.sqrt(total(value * value, 1) / width)
            stepped = value - rate * grad * lax.rsqrt(total(moment, 1) / width)
            new[...] = stepped.reshape(width)
            moment_out[...] = moment.reshape(width)


def update(grads, weights, rel_w, attn_w, ff_w, shared, own, tall, chunks=4):
    tensor_count = lax.axis_size("mp")
    width = weights[0].shape[0]
    slots = rel_w.shape[0]
    f32 = jnp.float32

    def blocks(array):
        return pl.BlockSpec((width // chunks, array.shape[1]), lambda i: (i, 0))

    def fixed(rows, cols, at=0):
        return pl.BlockSpec((rows, cols), lambda i: (at, 0))

    def line(size):
        return pl.BlockSpec((size,), lambda i: (0,))

    matrices = [blocks(w) for w in weights]
    near = pl.BlockSpec(memory_space=pltpu.VMEM)
    rel_spec = fixed(slots, BUCKETS)
    columns = [w.shape[1] for w in weights]
    return pl.pallas_call(
        functools.partial(update_kernel, tensor_count),
        grid=(chunks,),
        in_specs=[
            *[near] * (len(grads) + len(weights)),
            rel_spec,
            fixed(1, width),
            fixed(1, width),
            near,
            near,
            near,
        ],
        out_specs=[*matrices, rel_spec]
        + [line(width)] * 7
        + [line(BUCKETS)]
        + [line(c) for c in columns]
        + [fixed(1, slots)]
        + [line(width)] * 4,
        out_shape=[jax.ShapeDtypeStruct(w.shape, f32) for w in weights]
        + [jax.ShapeDtypeStruct(rel_w.shape, f32)]
        + [jax.ShapeDtypeStruct((width,), f32)] * 7
        + [jax.ShapeDtypeStruct((BUCKETS,), f32)]
        + [jax.ShapeDtypeStruct((c,), f32) for c in columns]
        + [jax.ShapeDtypeStruct((1, slots), f32)]
        + [jax.ShapeDtypeStruct((width,), f32)] * 4,
        compiler_params=pltpu.CompilerParams(vmem_limit_bytes=16 << 20),
        cost_estimate=pl.CostEstimate(
            flops=40 * width * columns[0], bytes_accessed=36 * width * columns[0], transcendentals=0
        ),
        name="update",
    )(
        *grads, *weights, rel_w,
        attn_w.reshape(1, width), ff_w.reshape(1, width), shared, own, tall,
    )


def finish_kernel(middle_ref, ff_ref, d_middle_ref, dn_ref, x_ref, gain_ref, out_ref, grad_ref):
    f32, low = jnp.float32, jnp.bfloat16
    width = middle_ref.shape[1]
    out_ref[...] = (middle_ref[...] + ff_ref[...].astype(f32)).astype(low).T
    x = x_ref[...].T.astype(f32)
    back = norm_back(x, gain_ref[...].reshape(1, width), dn_ref[...].astype(f32))
    grad_ref[...] = (d_middle_ref[...] + back).astype(low).T


def finish(middle, ff, d_middle, dn, x, gain):
    positions, width = middle.shape
    rows = pl.BlockSpec((BLOCK, width), lambda i: (i, 0))
    columns = pl.BlockSpec((width, BLOCK), lambda i: (0, i))
    return pl.pallas_call(
        finish_kernel,
        grid=(positions // BLOCK,),
        in_specs=[rows] * 4 + [columns, pl.BlockSpec((width,), lambda i: (0,))],
        out_specs=[columns] * 2,
        out_shape=[jax.ShapeDtypeStruct((width, positions), jnp.bfloat16)] * 2,
        compiler_params=pltpu.CompilerParams(vmem_limit_bytes=58 << 20),
        cost_estimate=pl.CostEstimate(
            flops=20 * positions * width, bytes_accessed=18 * positions * width, transcendentals=0
        ),
        name="finish",
    )(middle, ff, d_middle, dn, x, gain)


def turn_order(count):
    return [sorted(range(count), key=lambda b: (abs(b - place), b < place)) for place in range(count)]


def look_up(table, row, column):
    found = jnp.int32(0)
    for r, entries in enumerate(table):
        for c, entry in enumerate(entries):
            found = jnp.where((row == r) & (column == c), jnp.int32(entry), found)
    return found


def feed_forward_kernel(
    data_count,
    count,
    parts,
    normed_hbm,
    cot_hbm,
    gate_up_hbm,
    down_hbm,
    out_hbm,
    dn_ref,
    pieces_hbm,
    normed,
    cot,
    gate_up,
    down,
    hidden,
    d_gate_up,
    outgoing,
    incoming,
    stage,
    grads,
    land_whole,
    land_most,
    land_rest,
    load_sem,
    stage_sem,
    gather_send,
    gather_recv,
    sum_send,
    sum_recv,
    down_send,
    down_recv,
):
    place = lax.axis_index("mp")
    row = lax.axis_index("dp")
    block_len, width = dn_ref.shape
    units = down.shape[1]
    part_len = block_len // parts
    last = count - 1
    has_left = place > 0
    has_right = place < last

    loads = [
        pltpu.make_async_copy(normed_hbm, normed.at[place], load_sem.at[0]),
        pltpu.make_async_copy(gate_up_hbm.at[pl.ds(0, width)], gate_up, load_sem.at[1]),
        pltpu.make_async_copy(down_hbm, down, load_sem.at[2]),
        pltpu.make_async_copy(cot_hbm, cot, load_sem.at[3]),
    ]
    for load in loads:
        load.start()

    ways = orders(data_count)
    span = data_count - 1
    most = land_most.shape[2]
    shares = (
        (0, 0, units, 0, land_whole.at[0]),
        (1, 0, units, 1, land_whole.at[1]),
        (2, 0, most, 0, land_most),
        (2, most, units - most, 1, land_rest),
    )
    flies = [Butterfly(ways[way], k * span) for k, (_, _, _, way, _) in enumerate(shares)]
    stages = len(ways[0])
    sems = (down_send, down_recv)
    views = [row_pieces(grads.at[i], data_count, at, lanes) for i, at, lanes, _, _ in shares]

    barrier = pltpu.get_barrier_semaphore()
    for s in range(stages):
        pl.semaphore_signal(
            barrier, inc=1, device_id=flies[0].partner(s), device_id_type=pl.DeviceIdType.MESH
        )
    for side, there in ((-1, has_left), (1, has_right)):

        @pl.when(there)
        def _():
            pl.semaphore_signal(
                barrier, inc=1, device_id=(row, place + side), device_id_type=pl.DeviceIdType.MESH
            )

    pl.semaphore_wait(barrier, stages + has_left.astype(jnp.int32) + has_right.astype(jnp.int32))

    def pass_block(block, side, slot):
        return pltpu.make_async_remote_copy(
            src_ref=normed.at[block],
            dst_ref=normed.at[block],
            send_sem=gather_send.at[slot],
            recv_sem=gather_recv.at[block],
            device_id=(row, place + side),
            device_id_type=pl.DeviceIdType.MESH,
        )

    def rows_of(part):
        return pl.ds(pl.multiple_of(part * part_len, part_len), part_len)

    def pass_sum(block, part, side, slot):
        return pltpu.make_async_remote_copy(
            src_ref=outgoing.at[block, rows_of(part)],
            dst_ref=incoming.at[slot, rows_of(part)],
            send_sem=sum_send.at[block, part],
            recv_sem=sum_recv.at[slot, part],
            device_id=(row, place + side),
            device_id_type=pl.DeviceIdType.MESH,
        )

    def landing(block, side):
        return jnp.where((side == -1) & (place + side == block), count, block)

    loads[0].wait()
    for side, there in ((-1, has_left), (1, has_right)):

        @pl.when(there)
        def _():
            pass_block(place, side, count + (side + 1) // 2).start()

    for load in loads[1:]:
        load.wait()

    def store_out(turn, block):
        return pltpu.make_async_copy(stage.at[turn % 2], out_hbm.at[block], stage_sem.at[turn % 2])

    table = turn_order(count)
    root = 0.7978845608028654

    def turn_body(turn, carry):
        block = look_up(table, place, turn)
        distance = jnp.abs(block - place)

        @pl.when((distance > 0) & ((block > place) | (place + distance > last)))
        def _():
            for side in (1, -1):
                other = place + side * distance

                @pl.when((other >= 0) & (other <= last))
                def _():
                    pass_block(other, 0, other).wait_recv()

                    @pl.when((place - side >= 0) & (place - side <= last))
                    def _():
                        pass_block(other, -side, other).start()

        acts = product(normed[block], gate_up[...])
        gate_act = acts[:, :units]
        up_act = acts[:, units:]
        squared = gate_act * gate_act
        bend = jnp.tanh(root * gate_act * (1.0 + 0.044715 * squared))
        half = 0.5 * (1.0 + bend)
        gelu = gate_act * half
        hidden[block] = (gelu * up_act).astype(jnp.bfloat16)
        d_hidden = product(cot[block], down[...])
        slope = half + 0.5 * gate_act * (1.0 - bend * bend) * (root * (1.0 + 0.134145 * squared))
        d_gate_up[block, :, :units] = (d_hidden * up_act * slope).astype(jnp.bfloat16)
        d_gate_up[block, :, units:] = (d_hidden * gelu).astype(jnp.bfloat16)
        term = right_inner(d_gate_up[block], gate_up[...])

        @pl.when(block == place)
        def _():
            dn_ref[...] = term

        @pl.when(block != place)
        def _():
            outgoing[block] = term.astype(jnp.bfloat16)

        for side, is_end in ((1, place == 0), (-1, place == last)):

            @pl.when(is_end & (block != place))
            def _():
                for part in range(parts):
                    pass_sum(block, part, side, landing(block, side)).start()

        @pl.when(turn >= 2)
        def _():
            store_out(turn, block).wait()

        stage[turn % 2] = right_inner(hidden[block], down[...]).astype(jnp.bfloat16)
        store_out(turn, block).start()
        return carry

    lax.fori_loop(0, count, turn_body, 0)

    def relay_side(key, side):
        owner = key if side == 1 else last - key
        through = (owner > place) & has_left if side == 1 else (owner < place) & has_right

        @pl.when(through)
        def _():
            def relay_part(part, carry):
                pass_sum(owner, part, side, owner).wait_recv()
                rows = rows_of(part)
                outgoing[owner, rows] = (
                    outgoing[owner, rows].astype(jnp.float32)
                    + incoming[owner, rows].astype(jnp.float32)
                ).astype(jnp.bfloat16)
                pass_sum(owner, part, side, landing(owner, side)).start()
                return carry

            lax.fori_loop(0, parts, relay_part, 0)

    def relay(key, between=None):
        for turn in (0, 1):
            for side in (1, -1):
                sooner = 2 * place <= last if side == 1 else 2 * place > last

                @pl.when(sooner if turn == 0 else jnp.logical_not(sooner))
                def _():
                    relay_side(key, side)

            if turn == 0 and between is not None:
                between()

    def flat(ref):
        return ref[...].reshape(count * block_len, ref.shape[2])

    sent = []

    def halve(k, s):
        copies = flies[k].halve(s, views[k], shares[k][4], sems)
        for copy in copies:
            copy.start()
        sent.extend(copies)
        return copies

    def add_halve(k, s, copies):
        flies[k].add(s, views[k], shares[k][4], copies)
        return halve(k, s + 1) if s + 1 < stages else None

    def weigh(i, left, right):
        grads[i, :width] = left_inner(left, right).astype(jnp.bfloat16)

    grads[:, width:] = jnp.zeros((3, grads.shape[1] - width, units), jnp.bfloat16)
    weigh(2, flat(cot), flat(hidden))
    flights = [None, None, halve(2, 0), halve(3, 0)]
    for key in range(1, last):
        relay(key)
    gate_side = d_gate_up[:, :, :units].reshape(count * block_len, units)
    weigh(0, flat(normed), gate_side)
    flights[0] = halve(0, 0)
    for k in (2, 3):
        flights[k] = add_halve(k, 0, flights[k])
    up_side = d_gate_up[:, :, units:].reshape(count * block_len, units)
    weigh(1, flat(normed), up_side)
    flights[1] = halve(1, 0)
    for k in (0, 1):
        flights[k] = add_halve(k, 0, flights[k])

    def halve_on():
        for s in range(1, stages - 1):
            for k in (2, 3, 0, 1):
                flights[k] = add_halve(k, s, flights[k])

    relay(last, halve_on)

    for side, there in ((1, has_left), (-1, has_right)):

        @pl.when(there)
        def _():
            slot = place if side == 1 else count

            def add_part(part, carry):
                pass_sum(place, part, side, slot).wait_recv()
                rows = rows_of(part)
                dn_ref[rows] += incoming[slot, rows].astype(jnp.float32)
                return carry

            lax.fori_loop(0, parts, add_part, 0)

    for k in (2, 3, 0, 1):
        add_halve(k, stages - 1, flights[k])
    mine = pl.ds(pl.multiple_of(row * pieces_hbm.shape[1], pieces_hbm.shape[1]), pieces_hbm.shape[1])
    save = pltpu.make_async_copy(grads.at[:, mine], pieces_hbm, load_sem.at[0])
    save.start()
    for copy in sent:
        copy.wait_send()

    for side, there in ((-1, has_left), (1, has_right)):

        @pl.when(there)
        def _():
            pass_block(place, side, count + (side + 1) // 2).wait_send()

    for block in range(count):

        @pl.when((block != place) & has_left & has_right)
        def _():
            pass_block(block, 1, block).wait_send()

        @pl.when(block != place)
        def _():
            for part in range(parts):
                pass_sum(block, part, 1, block).wait_send()

    for turn in (count - 2, count - 1):
        store_out(turn, 0).wait()
    save.wait()


def feed_forward(normed, cot_all, gate_up, down):
    count = lax.axis_size("mp")
    data_count = lax.axis_size("dp")
    block_len, width = normed.shape
    units = down.shape[1]
    padded = gate_up.shape[0]
    parts = 2
    low = jnp.bfloat16
    anywhere = pl.BlockSpec(memory_space=pl.ANY)
    dma = pltpu.SemaphoreType.DMA
    tokens = count * block_len
    height = padded // data_count
    span = data_count - 1
    most = (units // 2 + 127) // 128 * 128
    out_terms, dn, pieces = pl.pallas_call(
        functools.partial(feed_forward_kernel, data_count, count, parts),
        out_shape=[
            jax.ShapeDtypeStruct((count, block_len, width), low),
            jax.ShapeDtypeStruct((block_len, width), jnp.float32),
            jax.ShapeDtypeStruct((3, height, units), low),
        ],
        in_specs=[anywhere] * 4,
        out_specs=[anywhere, pl.BlockSpec(memory_space=pltpu.VMEM), anywhere],
        scratch_shapes=[
            pltpu.VMEM((count, block_len, width), low),
            pltpu.VMEM((count, block_len, width), low),
            pltpu.VMEM((width, 2 * units), low),
            pltpu.VMEM((width, units), low),
            pltpu.VMEM((count, block_len, units), low),
            pltpu.VMEM((count, block_len, 2 * units), low),
            pltpu.VMEM((count, block_len, width), low),
            pltpu.VMEM((count + 1, block_len, width), low),
            pltpu.VMEM((2, block_len, width), low),
            pltpu.VMEM((3, padded, units), low),
            pltpu.VMEM((2, span, height, units), low),
            pltpu.VMEM((span, height, most), low),
            pltpu.VMEM((span, height, units - most), low),
            dma((4,)),
            dma((2,)),
            dma((count + 2,)),
            dma((count,)),
            dma((count, parts)),
            dma((count + 1, parts)),
            dma((4 * span,)),
            dma((4 * span,)),
        ],
        compiler_params=pltpu.CompilerParams(
            collective_id=1, has_side_effects=True, vmem_limit_bytes=60 << 20
        ),
        cost_estimate=pl.CostEstimate(
            flops=18 * tokens * width * units,
            bytes_accessed=12 * width * units + 6 * tokens * width,
            transcendentals=tokens * units,
        ),
        name="feed_forward",
    )(normed, cot_all.reshape(count, block_len, width), gate_up, down)
    return out_terms.reshape(tokens, width), dn, pieces


def ff_parts(units):
    most = (units // 2 + 127) // 128 * 128
    return ((0, 0, units, 0), (1, 0, units, 1), (2, 0, most, 0), (2, most, units - most, 1))


def stages_left(part, stages):
    return min(2 if part[0] == 2 else 1, stages - 1)


def attend_back_kernel(
    data_count,
    count,
    slots,
    dn_hbm,
    middle_hbm,
    cot_hbm,
    gain_ref,
    proj_hbm,
    own_hbm,
    qkv_hbm,
    probs_hbm,
    norm_hbm,
    qkv_low_hbm,
    bucket_ref,
    ff_hbm,
    d_middle_hbm,
    terms_hbm,
    d_qkv_w_hbm,
    d_out_w_hbm,
    spread_hbm,
    dn,
    middle,
    cot,
    proj,
    own,
    qkv,
    probs,
    norm,
    qkv_low,
    d_own,
    grad,
    diag,
    dk,
    dv,
    d_qkv,
    terms,
    d_qkv_w,
    d_out_w,
    line,
    load_sem,
    probs_sem,
    cross_send,
    cross_recv,
    up_send,
    up_recv,
):
    place = lax.axis_index("mp")
    me = lax.axis_index("dp")
    block_len, width = dn.shape
    seq_len = qkv.shape[0]
    lanes = slots * HD
    padded = d_qkv_w.shape[0]
    steps = seq_len // BLOCK
    f32 = jnp.float32
    low = jnp.bfloat16

    loads = []

    def load(src, dst):
        copy = pltpu.make_async_copy(src, dst, load_sem.at[len(loads)])
        copy.start()
        loads.append(copy)

    load(dn_hbm, dn)
    load(middle_hbm, middle)
    load(cot_hbm, cot)
    load(proj_hbm, proj)
    load(own_hbm, own)
    load(qkv_hbm, qkv)
    load(norm_hbm, norm)
    load(qkv_low_hbm, qkv_low)
    height = padded // data_count
    mine = pl.ds(pl.multiple_of(me * height, height), height)
    load(ff_hbm, spread_hbm.at[:, mine])

    ways = orders(data_count)
    stages = len(ways[0])
    parts = ff_parts(spread_hbm.shape[2])
    span = data_count - 1
    flies = [Butterfly(ways[way], k * span) for k, (_, _, _, way) in enumerate(parts)]
    views = [row_pieces(spread_hbm.at[i], data_count, at, wide) for i, at, wide, _ in parts]
    others = [(place + k) % count for k in range(1, count)]
    greet([flies[0].partner(s) for s in range(1, stages)] + [(me, other) for other in others])
    sent = []

    def start(copies):
        for copy in copies:
            copy.start()
        sent.extend(copies)
        return copies

    flights = [
        start(
            fly.double(
                stages - 1, view, (up_send, up_recv), ff_hbm.at[i, :, pl.ds(at, wide)]
            )
        )
        for fly, view, (i, at, wide, _) in zip(flies, views, parts)
    ]

    table = turn_order(count)

    def fetch(t):
        per = block_len // BLOCK
        block = look_up(table, place, t // per) * per + t % per
        rows = pl.ds(pl.multiple_of(block * BLOCK, BLOCK), BLOCK)
        return block, pltpu.make_async_copy(
            probs_hbm.at[:, rows], probs.at[t % 2], probs_sem.at[t % 2]
        )

    fetch(0)[1].start()
    diag[...] = jnp.zeros_like(diag)
    dk[...] = jnp.zeros_like(dk)
    dv[...] = jnp.zeros_like(dv)
    for copy in loads[:3]:
        copy.wait()
    d_middle = cot[...].astype(f32) + norm_back(middle[...], gain_ref[...].reshape(1, width), dn[...])
    middle[...] = d_middle
    save_middle = pltpu.make_async_copy(middle, d_middle_hbm, load_sem.at[0])
    save_middle.start()
    cot[...] = d_middle.astype(low)
    loads[3].wait()
    d_all = product(cot[...], proj[:width]).astype(low)

    def own_rows(who):
        return pl.ds(pl.multiple_of(who * block_len, block_len), block_len)

    for k in range(count):
        d_own[k] = d_all[:, k * lanes : (k + 1) * lanes]
    start(
        [
            pltpu.make_async_remote_copy(
                src_ref=d_own.at[other],
                dst_ref=grad.at[own_rows(place)],
                send_sem=cross_send.at[k],
                recv_sem=cross_recv.at[place],
                device_id=(me, other),
                device_id_type=pl.DeviceIdType.MESH,
            )
            for k, other in enumerate(others)
        ]
    )
    grad[own_rows(place)] = d_own[place]
    loads[4].wait()
    d_out_w[width:] = jnp.zeros((padded - width, count * lanes), low)
    d_out_w[:width] = left_inner(cot[...], own[...]).astype(low)
    save_out = pltpu.make_async_copy(d_out_w, d_out_w_hbm, load_sem.at[1])
    save_out.start()
    loads[5].wait()

    def pass_on(s):
        for k, (fly, view) in enumerate(zip(flies, views)):
            for copy in flights[k]:
                copy.wait_recv()
            flights[k] = []
            if s > 1 and s - 1 >= stages_left(parts[k], stages):
                flights[k] = start(fly.double(s - 1, view, (up_send, up_recv)))

    def back_block(t, carry):
        per = block_len // BLOCK

        @pl.when((t > 0) & (t % per == 0))
        def _():
            who = look_up(table, place, t // per)
            pltpu.make_async_remote_copy(
                src_ref=d_own.at[0],
                dst_ref=grad.at[own_rows(who)],
                send_sem=cross_send.at[0],
                recv_sem=cross_recv.at[who],
                device_id=(me, who),
                device_id_type=pl.DeviceIdType.MESH,
            ).wait_recv()

        @pl.when(t + 1 < steps)
        def _():
            fetch(t + 1)[1].start()

        block, arrival = fetch(t)
        arrival.wait()
        rows = pl.ds(pl.multiple_of(block * BLOCK, BLOCK), BLOCK)
        window = pl.ds(pl.multiple_of((steps - 1 - block) * BLOCK, BLOCK), seq_len)
        queries = qkv[rows, 0:lanes]
        keys = qkv[:, lanes : 2 * lanes]
        values = qkv[:, 2 * lanes : 3 * lanes]
        d_query = jnp.zeros((BLOCK, lanes), f32)
        for slot in range(slots):
            weight = probs[t % 2, slot]
            slot_grad = slot_lanes(grad[rows], slot)
            d_probs = right_inner(slot_grad, values)
            delta = jnp.sum(weight * d_probs, axis=-1, keepdims=True)
            d_scores = (weight * (d_probs - delta)).astype(low)
            d_query = d_query + slot_lanes(product(d_scores, keys), slot)
            dk[...] += left_inner(slot_lanes(queries, slot), d_scores)
            dv[...] += left_inner(slot_grad, weight.astype(low))
            diag[slot, :, window] += d_scores.astype(f32)
        d_qkv[rows, 0:lanes] = d_query.astype(low)
        return carry

    loads[8].wait()
    pass_on(stages - 1)
    lax.fori_loop(0, steps, back_block, 0)
    for s in reversed(range(2, stages - 1)):
        pass_on(s)
    d_qkv[:, lanes : 2 * lanes] = dk[...].T.astype(low)
    d_qkv[:, 2 * lanes : 3 * lanes] = dv[...].T.astype(low)
    for copy in loads[6:8]:
        copy.wait()
    terms[...] = right_inner(d_qkv[...], qkv_low[:width]).astype(low)
    save_terms = pltpu.make_async_copy(terms, terms_hbm, load_sem.at[2])
    save_terms.start()
    d_qkv_w[:width] = left_inner(norm[...], d_qkv[...]).astype(low)
    d_qkv_w[width:] = jnp.zeros((padded - width, 3 * lanes), low)
    sums = []
    for slot in range(slots):
        level = diag[slot]
        rest = BLOCK // 2
        while rest >= 1:
            level = pltpu.roll(level[:rest], rest, 1) + level[rest:]
            rest //= 2
        sums.append(level)
    sums = jnp.concatenate(sums + [jnp.zeros((128 - slots, 2 * seq_len), f32)], axis=0)
    d_rel = lax.dot_general(
        onehot_rows(bucket_ref, line),
        sums,
        (((1,), (1,)), ((), ())),
        precision=highest,
        preferred_element_type=f32,
    )
    d_qkv_w[width : width + BUCKETS, :128] = d_rel.astype(low)
    save_qkv = pltpu.make_async_copy(d_qkv_w, d_qkv_w_hbm, load_sem.at[3])
    save_qkv.start()
    if stages > 1:
        pass_on(1)
    for copy in sent:
        copy.wait_send()
    for copy in (save_middle, save_out, save_terms, save_qkv):
        copy.wait()


def attend_back(dn, middle, cot, gain, proj_all, own, qkv, probs, norm, qkv_low, bucket, ff_pieces):
    count = lax.axis_size("mp")
    data_count = lax.axis_size("dp")
    seq_len = qkv.shape[0]
    slots = probs.shape[0]
    lanes = slots * HD
    block_len, width = dn.shape
    padded = qkv_low.shape[0]
    _, _, units = ff_pieces.shape
    far = pl.BlockSpec(memory_space=pltpu.HBM)
    near = pl.BlockSpec(memory_space=pltpu.VMEM)
    dma = pltpu.SemaphoreType.DMA
    low, f32 = jnp.bfloat16, jnp.float32
    span = data_count - 1
    scratch = [
        (dn.shape, f32),
        (middle.shape, f32),
        (cot.shape, low),
        (proj_all.shape, low),
        (own.shape, low),
        (qkv.shape, low),
        ((2, slots, BLOCK, seq_len), f32),
        (norm.shape, low),
        (qkv_low.shape, low),
        ((count, block_len, lanes), low),
        ((seq_len, lanes), low),
        ((slots, BLOCK, 2 * seq_len), f32),
        ((lanes, seq_len), f32),
        ((lanes, seq_len), f32),
        (qkv.shape, low),
        ((seq_len, width), low),
        ((padded, 3 * lanes), low),
        ((padded, count * lanes), low),
    ]
    return pl.pallas_call(
        functools.partial(attend_back_kernel, data_count, count, slots),
        in_specs=[far] * 3 + [near] + [far] * 6 + [near, far],
        out_specs=[far] * 5,
        out_shape=[
            jax.ShapeDtypeStruct((block_len, width), f32),
            jax.ShapeDtypeStruct((seq_len, width), low),
            jax.ShapeDtypeStruct((padded, 3 * lanes), low),
            jax.ShapeDtypeStruct((padded, count * lanes), low),
            jax.ShapeDtypeStruct((3, padded, units), low),
        ],
        scratch_shapes=[pltpu.VMEM(shape, dtype) for shape, dtype in scratch]
        + [
            pltpu.VMEM((1, 2 * seq_len), jnp.int32),
            dma((10,)),
            dma((2,)),
            dma((count - 1,)),
            dma((count,)),
            dma((4 * span,)),
            dma((4 * span,)),
        ],
        compiler_params=pltpu.CompilerParams(
            collective_id=3, has_side_effects=True, vmem_limit_bytes=56 << 20
        ),
        cost_estimate=pl.CostEstimate(
            flops=16 * slots * seq_len * seq_len * HD, bytes_accessed=140 << 20, transcendentals=0
        ),
        name="attend_back",
    )(dn, middle, cot, gain, proj_all, own, qkv, probs, norm, qkv_low, bucket, ff_pieces)


def onehot_rows(bucket_ref, line_ref):
    offsets = bucket_ref.shape[0]
    line_ref[...] = jnp.full(line_ref.shape, -1, jnp.int32)
    line_ref[:, :offsets] = bucket_ref[...].reshape(1, offsets)
    rows = lax.broadcasted_iota(jnp.int32, (BUCKETS, line_ref.shape[1]), 0)
    return jnp.where(rows == line_ref[...], 1.0, 0.0)


def front_kernel(
    data_count,
    count,
    slots,
    x_hbm,
    cot_hbm,
    query_hbm,
    key_hbm,
    value_hbm,
    out_hbm,
    gate_hbm,
    up_hbm,
    down_hbm,
    segments_ref,
    bucket_ref,
    rel_ref,
    attn_gain_ref,
    ff_gain_ref,
    norm_far,
    cot_far,
    own_cot_far,
    qkv_far,
    probs_far,
    own_far,
    middle_far,
    normed_far,
    proj_far,
    qkv_low_far,
    gate_up_far,
    down_far,
    squares_ref,
    x_in,
    cot_in,
    x,
    norm,
    cot,
    thin,
    wide,
    gate_low,
    up_low,
    down_low,
    blank,
    proj,
    qkv_low,
    qkv,
    tilt,
    seg_col,
    probs,
    mixed,
    own,
    normed,
    line,
    load_sem,
    save_sem,
    probs_sem,
    norm_send,
    norm_recv,
    cot_send,
    cot_recv,
    cross_send,
    cross_recv,
    side_send,
    side_recv,
    mix_send,
    mix_recv,
    cot_save,
):
    place = lax.axis_index("mp")
    me = lax.axis_index("dp")
    last = count - 1
    f32, low = jnp.float32, jnp.bfloat16
    block_len, width = x.shape
    seq_len = count * block_len
    lanes = slots * HD
    padded = proj.shape[0]
    height = padded // data_count
    units = gate_low.shape[1]
    mesh_id = pl.DeviceIdType.MESH
    others = [(place + k) % count for k in range(1, count)]
    peers = [(me + k) % data_count for k in range(1, data_count)]

    def load(k, from_ref, to_ref):
        copy = pltpu.make_async_copy(from_ref, to_ref, load_sem.at[k])
        copy.start()
        return copy

    load_x = load(0, x_hbm, x_in)
    load_thin = [
        load(1 + k, ref, thin.at[k])
        for k, ref in enumerate((out_hbm, query_hbm, key_hbm, value_hbm))
    ]
    load_cot = load(5, cot_hbm, cot_in)
    load_gate = load(6, gate_hbm, wide.at[0])
    load_up = load(7, up_hbm, wide.at[1])
    greet([(me, other) for other in others] + [(peer, place) for peer in peers])

    saves = []

    def save(from_ref, to_ref):
        copy = pltpu.make_async_copy(from_ref, to_ref, save_sem.at[len(saves)])
        copy.start()
        saves.append(copy)

    sent = []

    def start(copy):
        copy.start()
        sent.append(copy)

    def pass_block(buffer, sems, block, side, slot):
        return pltpu.make_async_remote_copy(
            src_ref=buffer.at[block],
            dst_ref=buffer.at[block],
            send_sem=sems[0].at[slot],
            recv_sem=sems[1].at[block],
            device_id=(me, place + side),
            device_id_type=mesh_id,
        )

    def inside(block):
        return (block >= 0) & (block <= last)

    norm_sems = (norm_send, norm_recv)
    cot_sems = (cot_send, cot_recv)

    def store_cot(block):
        return pltpu.make_async_copy(cot.at[block], cot_far.at[block], cot_save.at[block])

    def take(buffer, sems, distance):
        for side in (1, -1):
            other = place + side * distance

            @pl.when(inside(other))
            def _():
                pass_block(buffer, sems, other, side, other).wait_recv()

                @pl.when(inside(place - side))
                def _():
                    pass_block(buffer, sems, other, -side, other).start()

                if buffer is cot:
                    store_cot(other).start()

    def send_own(buffer, sems, side):
        return pass_block(buffer, sems, place, side, count + (side + 1) // 2)

    def cot_may_go(distance):
        for side in (1, -1):
            behind = place if side == 1 else last - place

            @pl.when((behind == distance) & inside(place + side))
            def _():
                if distance == 0:
                    send_own(norm, norm_sems, side).wait_send()
                else:
                    far_end = 0 if side == 1 else last
                    pass_block(norm, norm_sems, far_end, side, far_end).wait_send()
                send_own(cot, cot_sems, side).start()

    between = inside(place - 1) & inside(place + 1)

    load_x.wait()
    x[...] = x_in[...].T.astype(f32)
    norm[place] = rms_norm(x[...], attn_gain_ref[...].reshape(1, width)).astype(low)
    for side in (1, -1):

        @pl.when(inside(place + side))
        def _():
            send_own(norm, norm_sems, side).start()

    load_cot.wait()
    cot[place] = cot_in[...].T
    save(cot.at[place], own_cot_far)
    store_cot(place).start()

    lane = lax.broadcasted_iota(jnp.int32, (1, lanes), 1)
    slot_of = place * slots + lane // HD
    lane_mask = jnp.where((slot_of < 5) | (slot_of == 6), 1.0, 0.0)
    for copy in load_thin:
        copy.wait()

    def lanes_of(who):
        return pl.ds(pl.multiple_of(who * lanes, lanes), lanes)

    def rows_of(who):
        return pl.ds(pl.multiple_of(who * height, height), height)

    proj[width:, lanes_of(place)] = jnp.zeros((padded - width, lanes), low)
    qkv_low[width:] = jnp.zeros((padded - width, 3 * lanes), low)
    blank[...] = jnp.zeros_like(blank)
    column = lax.broadcasted_iota(jnp.int32, (1, 128), 1)
    squares = jnp.zeros((1, 128), f32)

    def square_of(values, at):
        return jnp.where(column == at, total(total(values * values, 1), 0), 0.0)

    masked = (thin[0] * lane_mask).astype(low)
    proj[:width, lanes_of(place)] = masked

    def proj_copy(src, dst, sems, send_slot, recv_slot, device):
        return pltpu.make_async_remote_copy(
            src_ref=src,
            dst_ref=dst,
            send_sem=sems[0].at[send_slot],
            recv_sem=sems[1].at[recv_slot],
            device_id=device,
            device_id_type=mesh_id,
        )

    cross, aside = (cross_send, cross_recv), (side_send, side_recv)
    for k, other in enumerate(others):
        view = proj.at[rows_of(me), lanes_of(place)]
        start(proj_copy(view, view, cross, k, count - 2 - k, (me, other)))
    for k in range(3):
        qkv_low[:width, k * lanes : (k + 1) * lanes] = (thin[1 + k] * lane_mask).astype(low)
        squares = squares + square_of(thin[1 + k], k)
    squares = squares + square_of(thin[0], 6) + square_of(rel_ref[...], 3)
    save(qkv_low, qkv_low_far)

    onehot = onehot_rows(bucket_ref, line)
    vector = lax.dot_general(
        rel_ref[...],
        onehot,
        (((1,), (0,)), ((), ())),
        precision=highest,
        preferred_element_type=f32,
    )
    for slot in range(slots):
        spread = jnp.broadcast_to(vector[slot : slot + 1, :], (BLOCK, 2 * seq_len))
        tilt[slot] = pltpu.roll(spread, 2 * seq_len - BLOCK + 1, 1, stride=1, stride_axis=0)
    seg_row = segments_ref[...].astype(f32)
    seg_col[...] = jnp.broadcast_to(seg_row, (128, seq_len)).T

    arrivals = []
    for k, other in enumerate(others):
        view = proj.at[rows_of(me), lanes_of(other)]
        proj_copy(view, view, cross, k, k, (me, other)).wait_recv()
        at = k * (data_count - 1)
        for j, peer in enumerate(peers):
            start(proj_copy(view, view, aside, at + j, at + data_count - 2 - j, (peer, place)))
            come = proj.at[rows_of(peer), lanes_of(other)]
            arrivals.append(proj_copy(come, come, aside, at + j, at + j, (peer, place)))

    def own_rows(who):
        return pl.ds(pl.multiple_of(who * block_len, block_len), block_len)

    def project(block):
        qkv[own_rows(block)] = product(norm[block], qkv_low[:width]).astype(low)

    def project_at(distance):
        for side in (1, -1):
            other = place + side * distance

            @pl.when(inside(other))
            def _():
                project(other)

    project(place)
    take(norm, norm_sems, 1)
    cot_may_go(0)
    project_at(1)
    load_gate.wait()
    gate_low[...] = wide[0].astype(low)
    squares = squares + square_of(wide[0], 4)
    load_down = load(6, down_hbm, wide.at[0])
    rows_used = pl.ds(0, width)
    save(gate_low, gate_up_far.at[rows_used, pl.ds(0, units)])
    load_up.wait()
    up_low[...] = wide[1].astype(low)
    squares = squares + square_of(wide[1], 5)
    save(up_low, gate_up_far.at[rows_used, pl.ds(units, units)])
    save(blank, gate_up_far.at[pl.ds(width, padded - width)])
    for distance in range(2, count):
        take(norm, norm_sems, distance)
        cot_may_go(distance - 1)
        project_at(distance)
        if distance == 2:
            load_down.wait()
            down_low[...] = wide[0].astype(low)
            squares = squares + square_of(wide[0], 7)
            save(down_low, down_far)
            squares_ref[...] = squares
    save(qkv, qkv_far)
    save(norm, norm_far)

    @pl.when(between)
    def _():
        take(cot, cot_sems, 1)

    steps = seq_len // BLOCK
    per = block_len // BLOCK
    table = [order[::-1] for order in turn_order(count)]

    def store_probs(t, block):
        rows = pl.ds(pl.multiple_of(block * BLOCK, BLOCK), BLOCK)
        return pltpu.make_async_copy(probs.at[t % 2], probs_far.at[:, rows], probs_sem.at[t % 2])

    def mix_copy(owner):
        return pltpu.make_async_remote_copy(
            src_ref=mixed.at[own_rows(owner)],
            dst_ref=own.at[:, lanes_of(place)],
            send_sem=mix_send.at[owner],
            recv_sem=mix_recv.at[place],
            device_id=(me, owner),
            device_id_type=mesh_id,
        )

    def attend_block(t, carry):
        owner = look_up(table, place, t // per)
        block = owner * per + t % per
        rows = pl.ds(pl.multiple_of(block * BLOCK, BLOCK), BLOCK)
        window = pl.ds(pl.multiple_of((steps - 1 - block) * BLOCK, BLOCK), seq_len)
        same_doc = seg_col[rows, 0:1] == seg_row
        queries = qkv[rows, 0:lanes]
        keys = qkv[:, lanes : 2 * lanes]
        values = qkv[:, 2 * lanes : 3 * lanes]
        result = jnp.zeros((BLOCK, lanes), f32)

        @pl.when(t >= 2)
        def _():
            store_probs(t, block).wait()

        for slot in range(slots):
            scores = right_inner(slot_lanes(queries, slot), keys) + tilt[slot, :, window]
            scores = jnp.where(same_doc, scores, -1e30)
            peak = jnp.max(scores, axis=-1, keepdims=True)
            raised = jnp.exp(scores - peak)
            weight = raised * (1.0 / jnp.sum(raised, axis=-1, keepdims=True))
            probs[t % 2, slot] = weight
            result = result + slot_lanes(product(weight.astype(low), values), slot)
        store_probs(t, block).start()
        mixed[rows] = result.astype(low)

        @pl.when((t % per == per - 1) & (owner != place))
        def _():
            mix_copy(owner).start()

        return carry

    lax.fori_loop(0, steps, attend_block, 0)
    own[:, lanes_of(place)] = mixed[own_rows(place)]

    @pl.when(between)
    def _():
        for distance in range(2, count):
            take(cot, cot_sems, distance)

    for arrival in arrivals:
        arrival.wait_recv()
    save(proj, proj_far)
    for k, other in enumerate(others):
        pltpu.make_async_remote_copy(
            src_ref=mixed.at[own_rows(other)],
            dst_ref=own.at[:, lanes_of(other)],
            send_sem=mix_send.at[other],
            recv_sem=mix_recv.at[other],
            device_id=(me, other),
            device_id_type=mesh_id,
        ).wait_recv()
    save(own, own_far)
    x[...] = x[...] + right_inner(own[...], proj[:width])
    save(x, middle_far)
    normed[...] = rms_norm(x[...], ff_gain_ref[...].reshape(1, width)).astype(low)
    save(normed, normed_far)

    @pl.when(jnp.logical_not(between))
    def _():
        for distance in range(1, count):
            take(cot, cot_sems, distance)

    for block in range(count):
        store_cot(block).wait()
    for t in (0, 1):
        store_probs(t, 0).wait()
    for copy in saves:
        copy.wait()
    for copy in sent:
        copy.wait_send()
    for k, other in enumerate(others):
        mix_copy(other).wait_send()
    for buffer, sems in ((norm, norm_sems), (cot, cot_sems)):
        for side in (1, -1):
            behind = place if side == 1 else last - place
            unwaited = behind > 0 if buffer is norm else behind >= 0

            @pl.when(unwaited & inside(place + side))
            def _():
                send_own(buffer, sems, side).wait_send()

        for block in range(1, last) if buffer is norm else range(count):

            @pl.when((block != place) & between)
            def _():
                pass_block(buffer, sems, block, 1, block).wait_send()


def front(x, cot, weights, segments, bucket, rel_bias, attn_gain, ff_gain):
    count = lax.axis_size("mp")
    data_count = lax.axis_size("dp")
    query, key, value, out, gate, up, down = weights
    width, block_len = x.shape
    lanes = query.shape[1]
    slots = lanes // HD
    units = gate.shape[1]
    seq_len = count * block_len
    piece = 16 * data_count
    padded = (width + piece - 1) // piece * piece
    low, f32 = jnp.bfloat16, jnp.float32
    far = pl.BlockSpec(memory_space=pltpu.HBM)
    near = pl.BlockSpec(memory_space=pltpu.VMEM)
    dma = pltpu.SemaphoreType.DMA
    outs = [
        ((count, block_len, width), low),
        ((count, block_len, width), low),
        ((block_len, width), low),
        ((seq_len, 3 * lanes), low),
        ((slots, seq_len, seq_len), f32),
        ((block_len, count * lanes), low),
        ((block_len, width), f32),
        ((block_len, width), low),
        ((padded, count * lanes), low),
        ((padded, 3 * lanes), low),
        ((padded, 2 * units), low),
        ((width, units), low),
        ((1, 128), f32),
    ]
    scratch = [
        ((width, block_len), low),
        ((width, block_len), low),
        ((block_len, width), f32),
        ((count, block_len, width), low),
        ((count, block_len, width), low),
        ((4, width, lanes), f32),
        ((2, width, units), f32),
        ((width, units), low),
        ((width, units), low),
        ((width, units), low),
        ((padded - width, 2 * units), low),
        ((padded, count * lanes), low),
        ((padded, 3 * lanes), low),
        ((seq_len, 3 * lanes), low),
        ((slots, BLOCK, 2 * seq_len), f32),
        ((seq_len, 128), f32),
        ((2, slots, BLOCK, seq_len), f32),
        ((seq_len, lanes), low),
        ((block_len, count * lanes), low),
        ((block_len, width), low),
    ]
    sides = (count - 1) * (data_count - 1)
    return pl.pallas_call(
        functools.partial(front_kernel, data_count, count, slots),
        in_specs=[far] * 9 + [near] * 5,
        out_specs=[far] * 12 + [near],
        out_shape=[jax.ShapeDtypeStruct(shape, dtype) for shape, dtype in outs],
        scratch_shapes=[pltpu.VMEM(shape, dtype) for shape, dtype in scratch]
        + [
            pltpu.VMEM((1, 2 * seq_len), jnp.int32),
            dma((8,)),
            dma((16,)),
            dma((2,)),
            dma((count + 2,)),
            dma((count,)),
            dma((count + 2,)),
            dma((count,)),
            dma((count - 1,)),
            dma((count - 1,)),
            dma((sides,)),
            dma((sides,)),
            dma((count,)),
            dma((count,)),
            dma((count,)),
        ],
        compiler_params=pltpu.CompilerParams(
            collective_id=0, has_side_effects=True, vmem_limit_bytes=60 << 20
        ),
        cost_estimate=pl.CostEstimate(
            flops=8 * slots * seq_len * seq_len * HD,
            bytes_accessed=300 << 20,
            transcendentals=slots * seq_len * seq_len,
        ),
        name="front",
    )(
        x, cot, query, key, value, out, gate, up, down,
        segments, bucket, rel_bias, attn_gain, ff_gain,
    )


def local(
    layer_in,
    segment_ids,
    bucket_table,
    attn_gain,
    query_weight,
    key_weight,
    value_weight,
    out_weight,
    rel_bias,
    ff_gain,
    gate_weight,
    up_weight,
    down_weight,
    cotangent,
):
    model_width = layer_in.shape[2]
    slots_here = rel_bias.shape[1]
    layer_in = layer_in[0]
    down_turned = down_weight.T
    out_turned = out_weight.T
    rel_turned = rel_bias.T
    (
        flat_norm,
        flat_cot,
        own_cot,
        qkv,
        probs,
        own_attended,
        middle,
        normed_ff_local,
        proj_all,
        qkv_low,
        gate_up_low,
        down_low,
        squares,
    ) = front(
        layer_in.T,
        cotangent[0].T,
        (query_weight, key_weight, value_weight, out_turned, gate_weight, up_weight, down_turned),
        segment_ids,
        bucket_table,
        rel_turned,
        attn_gain,
        ff_gain,
    )
    flat_norm = flat_norm.reshape(-1, model_width)
    out_terms, dn_ff, ff_pieces = feed_forward(normed_ff_local, flat_cot, gate_up_low, down_low)
    d_middle, dn_attn_terms, d_qkv_w, d_out_w, ff_grads = attend_back(
        dn_ff,
        middle,
        own_cot,
        ff_gain,
        proj_all,
        own_attended,
        qkv,
        probs,
        flat_norm,
        qkv_low,
        bucket_table,
        ff_pieces,
    )
    ff_branch = lax.psum_scatter(out_terms, "mp", scatter_dimension=0, tiled=True)
    dn_attn = lax.psum_scatter(dn_attn_terms, "mp", scatter_dimension=0, tiled=True)
    weights = (
        gate_weight,
        up_weight,
        down_turned,
        query_weight,
        key_weight,
        value_weight,
        out_turned,
    )
    *held, shared, own, tall = sum_weights(
        ff_grads, d_qkv_w, d_out_w, qkv_low, gate_up_low, squares, weights, model_width
    )
    results = update(held[:5], held[5:], rel_turned, attn_gain, ff_gain, shared, own, tall)
    news, along, across = results[:8], results[8:16], results[16:24]
    new_attn_gain, attn_gain_moment, new_ff_gain, ff_gain_moment = results[24:]
    gate, up, down, query, key, value, out, rel = zip(news, along, across)
    rel = (rel[0].T, rel[1], rel[2].reshape(slots_here))
    down = (down[0].T, down[2], down[1])
    out = (out[0].T, out[2], out[1])
    layer_out, input_grad = finish(middle, ff_branch, d_middle, dn_attn, layer_in.T, attn_gain)
    return (
        layer_out.T[None],
        input_grad.T[None],
        new_attn_gain,
        attn_gain_moment,
        *query,
        *key,
        *value,
        *out,
        *rel,
        new_ff_gain,
        ff_gain_moment,
        *gate,
        *up,
        *down,
    )


def solution(mesh):
    return jax.shard_map(
        local,
        mesh=mesh,
        in_specs=(
            P("dp", "mp", None),
            P("dp", None),
            P(),
            P(),
            P(None, "mp"),
            P(None, "mp"),
            P(None, "mp"),
            P("mp", None),
            P(None, "mp"),
            P(),
            P(None, "mp"),
            P(None, "mp"),
            P("mp", None),
            P("dp", "mp", None),
        ),
        out_specs=(
            P("dp", "mp", None),
            P("dp", "mp", None),
            P(),
            P(),
            P(None, "mp"),
            P(),
            P("mp"),
            P(None, "mp"),
            P(),
            P("mp"),
            P(None, "mp"),
            P(),
            P("mp"),
            P("mp", None),
            P("mp"),
            P(),
            P(None, "mp"),
            P(),
            P("mp"),
            P(),
            P(),
            P(None, "mp"),
            P(),
            P("mp"),
            P(None, "mp"),
            P(),
            P("mp"),
            P("mp", None),
            P("mp"),
            P(),
        ),
        check_vma=False,
    )
```

```python
import functools

import jax
import jax.numpy as jnp
from jax import lax
from jax.experimental import pallas as pl
from jax.experimental.pallas import tpu as pltpu
from jax.sharding import PartitionSpec as P

HD = 64
BUCKETS = 32
BLOCK = 128


highest = lax.Precision.HIGHEST
step_scale = 0.3


def rms_norm(values, gain):
    return values * lax.rsqrt(jnp.mean(values * values, axis=-1, keepdims=True) + 1e-06) * gain


def norm_back(values, gain, grad):
    scale = lax.rsqrt(jnp.mean(values * values, axis=-1, keepdims=True) + 1e-06)
    unit = values * scale
    pull = grad * gain
    return scale * (pull - unit * jnp.mean(pull * unit, axis=-1, keepdims=True))


def product(left_side, right_side):
    return jnp.dot(left_side, right_side, preferred_element_type=jnp.float32)


def left_inner(left_side, right_side):
    return lax.dot_general(
        left_side, right_side, (((0,), (0,)), ((), ())), preferred_element_type=jnp.float32
    )


def right_inner(left_side, right_side):
    return lax.dot_general(
        left_side, right_side, (((1,), (1,)), ((), ())), preferred_element_type=jnp.float32
    )


def slot_lanes(values, slot):
    lane = lax.broadcasted_iota(jnp.int32, values.shape, 1)
    return jnp.where((lane >= slot * HD) & (lane < (slot + 1) * HD), values, jnp.zeros_like(values))


class Butterfly:
    def __init__(self, order, base):
        self.order = order
        self.me = lax.axis_index("dp")
        self.line = lax.axis_index("mp")
        self.base = base
        self.offsets = []
        total = 0
        for s in range(len(order)):
            self.offsets.append(total)
            total += 1 << (len(order) - 1 - s)

    def bit(self, b):
        return (self.me // b) % 2

    def partner(self, s):
        b = self.order[s]
        return (self.me + b * (1 - 2 * self.bit(b)), self.line)

    def width(self, s):
        return 1 << (len(self.order) - 1 - s)

    def piece(self, s, j, mine):
        b = self.order[s]
        found = sum(k * self.bit(k) for k in self.order[:s])
        found = found + b * (self.bit(b) if mine else 1 - self.bit(b))
        for i, k in enumerate(self.order[s + 1 :]):
            found = found + k * ((j // (1 << i)) % 2)
        return found

    def copy(self, src, dst, sems, slot, s):
        return pltpu.make_async_remote_copy(
            src_ref=src,
            dst_ref=dst,
            send_sem=sems[0].at[self.base + slot],
            recv_sem=sems[1].at[self.base + slot],
            device_id=self.partner(s),
            device_id_type=pl.DeviceIdType.MESH,
        )

    def halve(self, s, source, landing, sems):
        at = self.offsets[s]
        return [
            self.copy(source(self.piece(s, j, False)), landing.at[at + j], sems, at + j, s)
            for j in range(self.width(s))
        ]

    def add(self, s, kept, landing, copies):
        at = self.offsets[s]
        for j, copy in enumerate(copies):
            copy.wait_recv()
            mine = kept(self.piece(s, j, True))
            mine[...] = (mine[...].astype(jnp.float32) + landing[at + j].astype(jnp.float32)).astype(
                jnp.bfloat16
            )

    def double(self, s, whole, sems, first=None):
        at = self.offsets[s]
        copies = []
        for j in range(self.width(s)):
            view = whole(self.piece(s, j, True))
            copies.append(self.copy(view if first is None else first, view, sems, at + j, s))
        return copies


def orders(data_count):
    bits = [1 << i for i in range(data_count.bit_length() - 1)]
    return (bits, bits[:1] + bits[:0:-1])


def greet(peers):
    barrier = pltpu.get_barrier_semaphore()
    for peer in peers:
        pl.semaphore_signal(barrier, inc=1, device_id=peer, device_id_type=pl.DeviceIdType.MESH)
    pl.semaphore_wait(barrier, len(peers))


def row_pieces(ref, data_count, at=0, lanes=None):
    rows = ref.shape[0] // data_count
    columns = pl.ds(at, ref.shape[1] if lanes is None else lanes)
    return lambda q: ref.at[pl.ds(pl.multiple_of(q * rows, rows), rows), columns]


def total(values, axis):
    return jnp.sum(values, axis=axis, keepdims=True)


def sum_weights_kernel(data_count, count, model_width, parts, *refs):
    ff_hbm, qkv_hbm, out_hbm, qkv_low, gate_up_low, squares_ref = refs[:6]
    weights_hbm, full, weights = refs[6:13], refs[13:18], refs[18:25]
    shared_ref, own_ref, tall_ref = refs[25:28]
    kept, landings = refs[28:30], refs[30:32]
    (
        cross,
        qkv_w,
        gate_up_w,
        tall,
        cols,
        gathered,
        load_sem,
        down_send,
        down_recv,
        up_send,
        up_recv,
        cross_send,
        cross_recv,
        share_send,
        share_recv,
    ) = refs[32:]
    me = lax.axis_index("dp")
    place = lax.axis_index("mp")
    span = data_count - 1
    ways = orders(data_count)
    stages = len(ways[0])
    down, up = (down_send, down_recv), (up_send, up_recv)
    padded, units = full[0].shape
    lanes = full[4].shape[1]
    height = padded // data_count
    f32 = jnp.float32

    whole = [row_pieces(ref, data_count) for ref in full]
    source = [row_pieces(ref, data_count) for ref in (qkv_hbm, out_hbm)]
    keep = [row_pieces(ref, data_count) for ref in kept]
    halvers = [Butterfly(ways[1 - i], i * span) for i in range(2)]
    doublers = [Butterfly(ways[way], k * span) for k, (_, _, _, way) in enumerate(parts)]
    views = [row_pieces(full[i], data_count, at, wide) for i, at, wide, _ in parts]

    loads = []

    def load(src, dst):
        copy = pltpu.make_async_copy(src, dst, load_sem.at[len(loads)])
        copy.start()
        loads.append(copy)

    early = [k for k, part in enumerate(parts) if part[0] < 3]
    late = [k for k, part in enumerate(parts) if part[0] >= 3]
    begin = {k: stages_left(parts[k], stages) - 1 for k in early}
    for k in early:
        i, at, wide, _ = parts[k]
        for j in range(doublers[k].width(begin[k])):
            q = doublers[k].piece(begin[k], j, True)
            load(row_pieces(ff_hbm.at[i], data_count, at, wide)(q), views[k](q))
    for i, fly in enumerate(halvers):
        for j in range(fly.width(0)):
            q = fly.piece(0, j, True)
            load(source[i](q), keep[i](q))
    load(qkv_low, qkv_w)
    load(gate_up_low, gate_up_w)
    others = [(place + k) % count for k in range(1, count)]
    greet([halvers[0].partner(s) for s in range(stages)] + [(me, other) for other in others])

    sent = []

    def start(copies):
        for copy in copies:
            copy.start()
        sent.extend(copies)
        return copies

    halves = [start(fly.halve(0, source[i], landings[i], down)) for i, fly in enumerate(halvers)]
    tall[...] = jnp.zeros_like(tall)
    cols[...] = jnp.zeros_like(cols)
    for copy in loads:
        copy.wait()
    fetched = []
    for i, (far_weight, near_weight) in enumerate(zip(weights_hbm, weights)):
        copy = pltpu.make_async_copy(far_weight, near_weight, load_sem.at[i])
        copy.start()
        fetched.append(copy)

    doubles = {}

    def spread(s, which):
        for k in which:
            doubles[k] = start(doublers[k].double(s, views[k], up))

    for k in early:
        spread(begin[k], [k])

    def note(k, q):
        i, start_lane, wide, _ = parts[k]
        rows = pl.ds(pl.multiple_of(q * height, height), height)
        grad = views[k](q)[...].astype(f32)
        if i == 3:
            at = lax.broadcasted_iota(jnp.int32, grad.shape, 0) + q * height
            grad = jnp.where(at < model_width, grad, 0.0)
        squares = grad * grad
        cols[i : i + 1, start_lane : start_lane + wide] += total(squares, 0)
        if i < 2:
            tall[rows, 3 + i : 4 + i] = total(squares, 1)
            weight = gate_up_w[rows, i * units : (i + 1) * units].astype(f32)
            tall[rows, 6:7] += total(grad * weight, 1)
        elif i == 3:
            for k in range(3):
                tall[rows, k : k + 1] = total(squares[:, k * lanes : (k + 1) * lanes], 1)
            tall[rows, 5:6] = total(grad * qkv_w[rows].astype(f32), 1)
        else:
            lane = 8 if i == 2 else 9
            tall[rows, lane : lane + 1] += total(squares, 1)

    for s in range(stages):
        for i, fly in enumerate(halvers):
            fly.add(s, keep[i], landings[i], halves[i])
            if s + 1 < stages:
                halves[i] = start(fly.halve(s + 1, keep[i], landings[i], down))
        if s == min(1, stages - 1):
            for k in early:
                if begin[k] > 0:
                    for copy in doubles[k]:
                        copy.wait_recv()
                    spread(0, [k])
    crossing = row_pieces(kept[1], data_count)(me)

    def lanes_of(other):
        return pl.ds(pl.multiple_of(other * lanes, lanes), lanes)

    start(
        [
            pltpu.make_async_remote_copy(
                src_ref=crossing.at[:, lanes_of(other)],
                dst_ref=cross.at[count - 2 - k],
                send_sem=cross_send.at[k],
                recv_sem=cross_recv.at[count - 2 - k],
                device_id=(me, other),
                device_id_type=pl.DeviceIdType.MESH,
            )
            for k, other in enumerate(others)
        ]
    )
    whole[3](me)[...] = keep[0](me)[...]
    spread(stages - 1, late[:1])
    summed = crossing[:, lanes_of(place)].astype(f32)
    for k in range(count - 1):
        pltpu.make_async_remote_copy(
            src_ref=cross.at[k],
            dst_ref=cross.at[k],
            send_sem=cross_send.at[k],
            recv_sem=cross_recv.at[k],
            device_id=(me, others[0]),
            device_id_type=pl.DeviceIdType.MESH,
        ).wait_recv()
        summed = summed + cross[k].astype(f32)
    whole[4](me)[...] = summed.astype(jnp.bfloat16)
    spread(stages - 1, late[1:])

    def note_pieces(k, s, mine):
        fly = doublers[k]

        def note_piece(j, carry):
            note(k, fly.piece(s, j, mine))
            return carry

        lax.fori_loop(0, fly.width(s), note_piece, 0)

    for k in early:
        note_pieces(k, 0, True)
    for k in late:
        note(k, me)
    for k in early:
        for copy in doubles[k]:
            copy.wait_recv()
        note_pieces(k, 0, False)
    for s in reversed(range(stages)):
        for k in late:
            for copy in doubles[k]:
                copy.wait_recv()
            if s > 0:
                doubles[k] = start(doublers[k].double(s - 1, views[k], up))
        for k in late:
            note_pieces(k, s, False)

    slots_rel = full[3][model_width : model_width + BUCKETS, :128].astype(f32)
    tall[:BUCKETS, 7:8] = total(slots_rel * slots_rel, 1)
    share = gathered.at[place]
    flat = tall[...].T[0:16]
    row = lax.broadcasted_iota(jnp.int32, flat.shape, 0)
    spare = jnp.concatenate([squares_ref[...], jnp.zeros((1, padded - 128), f32)], axis=1)
    share[...] = jnp.where(row == 10, spare, flat).astype(jnp.bfloat16)
    shares = start(
        [
            pltpu.make_async_remote_copy(
                src_ref=share,
                dst_ref=share,
                send_sem=share_send.at[k],
                recv_sem=share_recv.at[place],
                device_id=(me, other),
                device_id_type=pl.DeviceIdType.MESH,
            )
            for k, other in enumerate(others)
        ]
    )
    own_ref[...] = jnp.zeros_like(own_ref)
    own_ref[:, : cols.shape[1]] = cols[...]
    for k, other in enumerate(others):
        pltpu.make_async_remote_copy(
            src_ref=gathered.at[other],
            dst_ref=gathered.at[other],
            send_sem=share_send.at[k],
            recv_sem=share_recv.at[other],
            device_id=(me, other),
            device_id_type=pl.DeviceIdType.MESH,
        ).wait_recv()
    summed = gathered[0].astype(f32)
    for k in range(1, count):
        summed = summed + gathered[k].astype(f32)
    shared_ref[...] = summed
    tall_ref[...] = jnp.concatenate([summed, jnp.zeros((112, padded), f32)], axis=0).T
    for copy in fetched:
        copy.wait()
    for copy in sent:
        copy.wait_send()


def sum_weights(ff_grads, qkv, out, qkv_low, gate_up_low, squares, weights, model_width):
    count = lax.axis_size("mp")
    data_count = lax.axis_size("dp")
    far = pl.BlockSpec(memory_space=pltpu.HBM)
    near = pl.BlockSpec(memory_space=pltpu.VMEM)
    dma = pltpu.SemaphoreType.DMA
    low, f32 = jnp.bfloat16, jnp.float32
    span = data_count - 1
    units = ff_grads.shape[2]
    padded, wide = qkv.shape
    height = padded // data_count
    lanes = out.shape[1] // count
    full = [(padded, units)] * 3 + [(padded, wide), (padded, lanes)]
    parts = (*ff_parts(units), (3, 0, wide, 1), (4, 0, lanes, 0))
    n = len(parts)
    return pl.pallas_call(
        functools.partial(sum_weights_kernel, data_count, count, model_width, parts),
        out_shape=[pltpu.VMEM(s, low) for s in full]
        + [pltpu.VMEM(w.shape, f32) for w in weights]
        + [
            pltpu.VMEM((16, padded), f32),
            pltpu.VMEM((8, padded), f32),
            pltpu.VMEM((padded, 128), f32),
        ],
        in_specs=[far] * 5 + [near] + [far] * len(weights),
        out_specs=[near] * (8 + len(weights)),
        scratch_shapes=[pltpu.VMEM(a.shape, low) for a in (qkv, out)]
        + [pltpu.VMEM((span, height, a.shape[1]), low) for a in (qkv, out)]
        + [
            pltpu.VMEM((count - 1, height, lanes), low),
            pltpu.VMEM(qkv_low.shape, low),
            pltpu.VMEM(gate_up_low.shape, low),
            pltpu.VMEM((padded, 128), f32),
            pltpu.VMEM((8, (max(units, wide) + 127) // 128 * 128), f32),
            pltpu.VMEM((count, 16, padded), low),
            dma((3 * data_count + 5,)),
            dma((2 * span,)),
            dma((2 * span,)),
            dma((n * span,)),
            dma((n * span,)),
            dma((count - 1,)),
            dma((count - 1,)),
            dma((count - 1,)),
            dma((count,)),
        ],
        compiler_params=pltpu.CompilerParams(
            collective_id=2, has_side_effects=True, vmem_limit_bytes=30 << 20
        ),
        cost_estimate=pl.CostEstimate(
            flops=padded * units, bytes_accessed=200 << 20, transcendentals=0
        ),
        name="sum_weights",
    )(ff_grads, qkv, out, qkv_low, gate_up_low, squares, *weights)


def update_kernel(tensor_count, *refs):
    grads = refs[:5]
    weights, (rel_w, attn_w, ff_w) = refs[5:12], refs[12:15]
    shared_ref, own_ref, tall_ref = refs[15:18]
    news, rel_n = refs[18:25], refs[25]
    along, rel_r = refs[26:33], refs[33]
    across, rel_c = refs[34:41], refs[41]
    attn_n, attn_m, ff_n, ff_m = refs[42:46]
    first = pl.program_id(0) == 0
    height = news[0].shape[0]
    here_rows = pl.ds(pl.multiple_of(pl.program_id(0) * height, height), height)
    f32 = jnp.float32
    width = attn_w.shape[1]
    lanes = weights[3].shape[1]
    slots = rel_w.shape[0]
    tiny = 1e-30

    def step_rate(lane, size):
        return step_scale * jnp.sqrt(shared_ref[10:11, lane : lane + 1] / size)

    qkv = grads[3][here_rows].astype(f32)
    for k, (row, square, own, at) in enumerate(
        (
            (3, 4, 0, 0),
            (4, 5, 1, 0),
            (8, 7, 2, 0),
            (0, 0, 3, 0),
            (1, 1, 3, lanes),
            (2, 2, 3, 2 * lanes),
            (9, 6, 4, 0),
        )
    ):
        here = weights[k].shape[1]
        if own == 3:
            grad = qkv[:, at : at + lanes]
        else:
            grad = grads[own][here_rows].astype(f32)
        cols = here * tensor_count
        size = width * cols
        level = total(shared_ref[row : row + 1, :width], 1) / size + tiny
        rate = step_rate(square, size)
        row_factor = lax.rsqrt((tall_ref[here_rows, row : row + 1] / cols + tiny) / level) * rate
        col_moment = own_ref[own : own + 1, at : at + here] / width + tiny
        news[k][...] = weights[k][here_rows] - grad * row_factor * lax.rsqrt(col_moment)

        @pl.when(first)
        def _():
            along[k][...] = (shared_ref[row : row + 1, :width] / cols + tiny).reshape(width)
            across[k][...] = col_moment.reshape(here)

    @pl.when(first)
    def _():
        rel = grads[3][width : width + BUCKETS, :128].astype(f32)
        cols = slots * tensor_count
        size = BUCKETS * cols
        row_moment = shared_ref[7:8, :BUCKETS] / cols + tiny
        level = total(row_moment, 1) / BUCKETS
        row_factor = lax.rsqrt(row_moment / level) * step_rate(3, size)
        turned = rel.T[:slots]
        col_moment = total(turned * turned, 1) / BUCKETS + tiny
        rel_n[...] = rel_w[...] - turned * row_factor * lax.rsqrt(col_moment)
        rel_r[...] = row_moment.reshape(BUCKETS)
        rel_c[...] = (total(rel * rel, 0) / BUCKETS + tiny)[:, :slots]
        for gain, row, new, moment_out in ((attn_w, 5, attn_n, attn_m), (ff_w, 6, ff_n, ff_m)):
            value = gain[...]
            grad = shared_ref[row : row + 1, :width] / value
            moment = grad * grad + tiny
            rate = step_scale * jnp.sqrt(total(value * value, 1) / width)
            stepped = value - rate * grad * lax.rsqrt(total(moment, 1) / width)
            new[...] = stepped.reshape(width)
            moment_out[...] = moment.reshape(width)


def update(grads, weights, rel_w, attn_w, ff_w, shared, own, tall, chunks=4):
    tensor_count = lax.axis_size("mp")
    width = weights[0].shape[0]
    slots = rel_w.shape[0]
    f32 = jnp.float32

    def blocks(array):
        return pl.BlockSpec((width // chunks, array.shape[1]), lambda i: (i, 0))

    def fixed(rows, cols, at=0):
        return pl.BlockSpec((rows, cols), lambda i: (at, 0))

    def line(size):
        return pl.BlockSpec((size,), lambda i: (0,))

    matrices = [blocks(w) for w in weights]
    near = pl.BlockSpec(memory_space=pltpu.VMEM)
    rel_spec = fixed(slots, BUCKETS)
    columns = [w.shape[1] for w in weights]
    return pl.pallas_call(
        functools.partial(update_kernel, tensor_count),
        grid=(chunks,),
        in_specs=[
            *[near] * (len(grads) + len(weights)),
            rel_spec,
            fixed(1, width),
            fixed(1, width),
            near,
            near,
            near,
        ],
        out_specs=[*matrices, rel_spec]
        + [line(width)] * 7
        + [line(BUCKETS)]
        + [line(c) for c in columns]
        + [fixed(1, slots)]
        + [line(width)] * 4,
        out_shape=[jax.ShapeDtypeStruct(w.shape, f32) for w in weights]
        + [jax.ShapeDtypeStruct(rel_w.shape, f32)]
        + [jax.ShapeDtypeStruct((width,), f32)] * 7
        + [jax.ShapeDtypeStruct((BUCKETS,), f32)]
        + [jax.ShapeDtypeStruct((c,), f32) for c in columns]
        + [jax.ShapeDtypeStruct((1, slots), f32)]
        + [jax.ShapeDtypeStruct((width,), f32)] * 4,
        compiler_params=pltpu.CompilerParams(vmem_limit_bytes=16 << 20),
        cost_estimate=pl.CostEstimate(
            flops=40 * width * columns[0], bytes_accessed=36 * width * columns[0], transcendentals=0
        ),
        name="update",
    )(
        *grads, *weights, rel_w,
        attn_w.reshape(1, width), ff_w.reshape(1, width), shared, own, tall,
    )


def finish_out_kernel(middle_ref, ff_ref, out_ref):
    out_ref[...] = (middle_ref[...] + ff_ref[...].astype(jnp.float32)).astype(jnp.bfloat16).T


def finish_grad_kernel(d_middle_ref, dn_ref, x_ref, gain_ref, grad_ref):
    f32 = jnp.float32
    x = x_ref[...].T.astype(f32)
    gain = gain_ref[...].reshape(1, x.shape[1])
    back = norm_back(x, gain, dn_ref[...].astype(f32))
    grad_ref[...] = (d_middle_ref[...] + back).astype(jnp.bfloat16).T


def finish(kernel, name, rows_in, columns_in, lines_in):
    positions, width = rows_in[0].shape
    rows = pl.BlockSpec((BLOCK, width), lambda i: (i, 0))
    columns = pl.BlockSpec((width, BLOCK), lambda i: (0, i))
    line = pl.BlockSpec((width,), lambda i: (0,))
    return pl.pallas_call(
        kernel,
        grid=(positions // BLOCK,),
        in_specs=[rows] * len(rows_in) + [columns] * len(columns_in) + [line] * len(lines_in),
        out_specs=columns,
        out_shape=jax.ShapeDtypeStruct((width, positions), jnp.bfloat16),
        compiler_params=pltpu.CompilerParams(vmem_limit_bytes=58 << 20),
        cost_estimate=pl.CostEstimate(
            flops=20 * positions * width, bytes_accessed=9 * positions * width, transcendentals=0
        ),
        name=name,
    )(*rows_in, *columns_in, *lines_in)


def turn_order(count):
    return [sorted(range(count), key=lambda b: (abs(b - place), b < place)) for place in range(count)]


def look_up(table, row, column):
    found = jnp.int32(0)
    for r, entries in enumerate(table):
        for c, entry in enumerate(entries):
            found = jnp.where((row == r) & (column == c), jnp.int32(entry), found)
    return found


def feed_forward_kernel(
    data_count,
    count,
    parts,
    normed_hbm,
    cot_hbm,
    gate_up_hbm,
    down_hbm,
    out_hbm,
    dn_ref,
    pieces_hbm,
    normed,
    cot,
    gate_up,
    down,
    hidden,
    d_gate_up,
    outgoing,
    incoming,
    stage,
    grads,
    land_whole,
    land_most,
    land_rest,
    load_sem,
    stage_sem,
    gather_send,
    gather_recv,
    sum_send,
    sum_recv,
    down_send,
    down_recv,
):
    place = lax.axis_index("mp")
    row = lax.axis_index("dp")
    block_len, width = dn_ref.shape
    units = down.shape[1]
    part_len = block_len // parts
    last = count - 1
    has_left = place > 0
    has_right = place < last

    loads = [
        pltpu.make_async_copy(normed_hbm, normed.at[place], load_sem.at[0]),
        pltpu.make_async_copy(gate_up_hbm.at[pl.ds(0, width)], gate_up, load_sem.at[1]),
        pltpu.make_async_copy(down_hbm, down, load_sem.at[2]),
        pltpu.make_async_copy(cot_hbm, cot, load_sem.at[3]),
    ]
    for load in loads:
        load.start()

    ways = orders(data_count)
    span = data_count - 1
    most = land_most.shape[2]
    shares = (
        (0, 0, units, 0, land_whole.at[0]),
        (1, 0, units, 1, land_whole.at[1]),
        (2, 0, most, 0, land_most),
        (2, most, units - most, 1, land_rest),
    )
    flies = [Butterfly(ways[way], k * span) for k, (_, _, _, way, _) in enumerate(shares)]
    stages = len(ways[0])
    sems = (down_send, down_recv)
    views = [row_pieces(grads.at[i], data_count, at, lanes) for i, at, lanes, _, _ in shares]

    barrier = pltpu.get_barrier_semaphore()
    for s in range(stages):
        pl.semaphore_signal(
            barrier, inc=1, device_id=flies[0].partner(s), device_id_type=pl.DeviceIdType.MESH
        )
    for side, there in ((-1, has_left), (1, has_right)):

        @pl.when(there)
        def _():
            pl.semaphore_signal(
                barrier, inc=1, device_id=(row, place + side), device_id_type=pl.DeviceIdType.MESH
            )

    pl.semaphore_wait(barrier, stages + has_left.astype(jnp.int32) + has_right.astype(jnp.int32))

    def pass_block(block, side, slot):
        return pltpu.make_async_remote_copy(
            src_ref=normed.at[block],
            dst_ref=normed.at[block],
            send_sem=gather_send.at[slot],
            recv_sem=gather_recv.at[block],
            device_id=(row, place + side),
            device_id_type=pl.DeviceIdType.MESH,
        )

    def rows_of(part):
        return pl.ds(pl.multiple_of(part * part_len, part_len), part_len)

    def pass_sum(block, part, side, slot):
        return pltpu.make_async_remote_copy(
            src_ref=outgoing.at[block, rows_of(part)],
            dst_ref=incoming.at[slot, rows_of(part)],
            send_sem=sum_send.at[block, part],
            recv_sem=sum_recv.at[slot, part],
            device_id=(row, place + side),
            device_id_type=pl.DeviceIdType.MESH,
        )

    def landing(block, side):
        return jnp.where((side == -1) & (place + side == block), count, block)

    loads[0].wait()
    for side, there in ((-1, has_left), (1, has_right)):

        @pl.when(there)
        def _():
            pass_block(place, side, count + (side + 1) // 2).start()

    for load in loads[1:]:
        load.wait()

    def store_out(turn, block):
        return pltpu.make_async_copy(stage.at[turn % 2], out_hbm.at[block], stage_sem.at[turn % 2])

    table = turn_order(count)
    root = 0.7978845608028654

    def turn_body(turn, carry):
        block = look_up(table, place, turn)
        distance = jnp.abs(block - place)

        @pl.when((distance > 0) & ((block > place) | (place + distance > last)))
        def _():
            for side in (1, -1):
                other = place + side * distance

                @pl.when((other >= 0) & (other <= last))
                def _():
                    pass_block(other, 0, other).wait_recv()

                    @pl.when((place - side >= 0) & (place - side <= last))
                    def _():
                        pass_block(other, -side, other).start()

        acts = product(normed[block], gate_up[...])
        gate_act = acts[:, :units]
        up_act = acts[:, units:]
        squared = gate_act * gate_act
        bend = jnp.tanh(root * gate_act * (1.0 + 0.044715 * squared))
        half = 0.5 * (1.0 + bend)
        gelu = gate_act * half
        hidden[block] = (gelu * up_act).astype(jnp.bfloat16)
        d_hidden = product(cot[block], down[...])
        slope = half + 0.5 * gate_act * (1.0 - bend * bend) * (root * (1.0 + 0.134145 * squared))
        d_gate_up[block, :, :units] = (d_hidden * up_act * slope).astype(jnp.bfloat16)
        d_gate_up[block, :, units:] = (d_hidden * gelu).astype(jnp.bfloat16)
        term = right_inner(d_gate_up[block], gate_up[...])

        @pl.when(block == place)
        def _():
            dn_ref[...] = term

        @pl.when(block != place)
        def _():
            outgoing[block] = term.astype(jnp.bfloat16)

        for side, is_end in ((1, place == 0), (-1, place == last)):

            @pl.when(is_end & (block != place))
            def _():
                for part in range(parts):
                    pass_sum(block, part, side, landing(block, side)).start()

        @pl.when(turn >= 2)
        def _():
            store_out(turn, block).wait()

        stage[turn % 2] = right_inner(hidden[block], down[...]).astype(jnp.bfloat16)
        store_out(turn, block).start()
        return carry

    lax.fori_loop(0, count, turn_body, 0)

    def relay_side(key, side):
        owner = key if side == 1 else last - key
        through = (owner > place) & has_left if side == 1 else (owner < place) & has_right

        @pl.when(through)
        def _():
            def relay_part(part, carry):
                pass_sum(owner, part, side, owner).wait_recv()
                rows = rows_of(part)
                outgoing[owner, rows] = (
                    outgoing[owner, rows].astype(jnp.float32)
                    + incoming[owner, rows].astype(jnp.float32)
                ).astype(jnp.bfloat16)
                pass_sum(owner, part, side, landing(owner, side)).start()
                return carry

            lax.fori_loop(0, parts, relay_part, 0)

    def relay(key, between=None):
        for turn in (0, 1):
            for side in (1, -1):
                sooner = 2 * place <= last if side == 1 else 2 * place > last

                @pl.when(sooner if turn == 0 else jnp.logical_not(sooner))
                def _():
                    relay_side(key, side)

            if turn == 0 and between is not None:
                between()

    def flat(ref):
        return ref[...].reshape(count * block_len, ref.shape[2])

    sent = []

    def halve(k, s):
        copies = flies[k].halve(s, views[k], shares[k][4], sems)
        for copy in copies:
            copy.start()
        sent.extend(copies)
        return copies

    def add_halve(k, s, copies):
        flies[k].add(s, views[k], shares[k][4], copies)
        return halve(k, s + 1) if s + 1 < stages else None

    def weigh(i, left, right):
        grads[i, :width] = left_inner(left, right).astype(jnp.bfloat16)

    grads[:, width:] = jnp.zeros((3, grads.shape[1] - width, units), jnp.bfloat16)
    weigh(2, flat(cot), flat(hidden))
    flights = [None, None, halve(2, 0), halve(3, 0)]
    for key in range(1, last):
        relay(key)
    gate_side = d_gate_up[:, :, :units].reshape(count * block_len, units)
    weigh(0, flat(normed), gate_side)
    flights[0] = halve(0, 0)
    for k in (2, 3):
        flights[k] = add_halve(k, 0, flights[k])
    up_side = d_gate_up[:, :, units:].reshape(count * block_len, units)
    weigh(1, flat(normed), up_side)
    flights[1] = halve(1, 0)
    for k in (0, 1):
        flights[k] = add_halve(k, 0, flights[k])

    def halve_on():
        for s in range(1, stages - 1):
            for k in (2, 3, 0, 1):
                flights[k] = add_halve(k, s, flights[k])

    relay(last, halve_on)

    for side, there in ((1, has_left), (-1, has_right)):

        @pl.when(there)
        def _():
            slot = place if side == 1 else count

            def add_part(part, carry):
                pass_sum(place, part, side, slot).wait_recv()
                rows = rows_of(part)
                dn_ref[rows] += incoming[slot, rows].astype(jnp.float32)
                return carry

            lax.fori_loop(0, parts, add_part, 0)

    for k in (2, 3, 0, 1):
        add_halve(k, stages - 1, flights[k])
    mine = pl.ds(pl.multiple_of(row * pieces_hbm.shape[1], pieces_hbm.shape[1]), pieces_hbm.shape[1])
    save = pltpu.make_async_copy(grads.at[:, mine], pieces_hbm, load_sem.at[0])
    save.start()
    for copy in sent:
        copy.wait_send()

    for side, there in ((-1, has_left), (1, has_right)):

        @pl.when(there)
        def _():
            pass_block(place, side, count + (side + 1) // 2).wait_send()

    for block in range(count):

        @pl.when((block != place) & has_left & has_right)
        def _():
            pass_block(block, 1, block).wait_send()

        @pl.when(block != place)
        def _():
            for part in range(parts):
                pass_sum(block, part, 1, block).wait_send()

    for turn in (count - 2, count - 1):
        store_out(turn, 0).wait()
    save.wait()


def feed_forward(normed, cot_all, gate_up, down):
    count = lax.axis_size("mp")
    data_count = lax.axis_size("dp")
    block_len, width = normed.shape
    units = down.shape[1]
    padded = gate_up.shape[0]
    parts = 2
    low = jnp.bfloat16
    anywhere = pl.BlockSpec(memory_space=pl.ANY)
    dma = pltpu.SemaphoreType.DMA
    tokens = count * block_len
    height = padded // data_count
    span = data_count - 1
    most = (units // 2 + 127) // 128 * 128
    out_terms, dn, pieces = pl.pallas_call(
        functools.partial(feed_forward_kernel, data_count, count, parts),
        out_shape=[
            jax.ShapeDtypeStruct((count, block_len, width), low),
            jax.ShapeDtypeStruct((block_len, width), jnp.float32),
            jax.ShapeDtypeStruct((3, height, units), low),
        ],
        in_specs=[anywhere] * 4,
        out_specs=[anywhere, pl.BlockSpec(memory_space=pltpu.VMEM), anywhere],
        scratch_shapes=[
            pltpu.VMEM((count, block_len, width), low),
            pltpu.VMEM((count, block_len, width), low),
            pltpu.VMEM((width, 2 * units), low),
            pltpu.VMEM((width, units), low),
            pltpu.VMEM((count, block_len, units), low),
            pltpu.VMEM((count, block_len, 2 * units), low),
            pltpu.VMEM((count, block_len, width), low),
            pltpu.VMEM((count + 1, block_len, width), low),
            pltpu.VMEM((2, block_len, width), low),
            pltpu.VMEM((3, padded, units), low),
            pltpu.VMEM((2, span, height, units), low),
            pltpu.VMEM((span, height, most), low),
            pltpu.VMEM((span, height, units - most), low),
            dma((4,)),
            dma((2,)),
            dma((count + 2,)),
            dma((count,)),
            dma((count, parts)),
            dma((count + 1, parts)),
            dma((4 * span,)),
            dma((4 * span,)),
        ],
        compiler_params=pltpu.CompilerParams(
            collective_id=1, has_side_effects=True, vmem_limit_bytes=60 << 20
        ),
        cost_estimate=pl.CostEstimate(
            flops=18 * tokens * width * units,
            bytes_accessed=12 * width * units + 6 * tokens * width,
            transcendentals=tokens * units,
        ),
        name="feed_forward",
    )(normed, cot_all.reshape(count, block_len, width), gate_up, down)
    return out_terms.reshape(tokens, width), dn, pieces


def ff_parts(units):
    most = (units // 2 + 127) // 128 * 128
    return ((0, 0, units, 0), (1, 0, units, 1), (2, 0, most, 0), (2, most, units - most, 1))


def stages_left(part, stages):
    return min(2 if part[0] == 2 else 1, stages - 1)


def attend_back_kernel(
    data_count,
    count,
    slots,
    dn_hbm,
    middle_hbm,
    cot_hbm,
    gain_ref,
    proj_hbm,
    own_hbm,
    qkv_hbm,
    probs_hbm,
    norm_hbm,
    qkv_low_hbm,
    bucket_ref,
    ff_hbm,
    d_middle_hbm,
    terms_hbm,
    d_qkv_w_hbm,
    d_out_w_hbm,
    spread_hbm,
    dn,
    middle,
    cot,
    proj,
    own,
    qkv,
    probs,
    norm,
    qkv_low,
    d_own,
    grad,
    diag,
    dk,
    dv,
    d_qkv,
    terms,
    d_qkv_w,
    d_out_w,
    line,
    load_sem,
    probs_sem,
    cross_send,
    cross_recv,
    up_send,
    up_recv,
):
    place = lax.axis_index("mp")
    me = lax.axis_index("dp")
    block_len, width = dn.shape
    seq_len = qkv.shape[0]
    lanes = slots * HD
    padded = d_qkv_w.shape[0]
    steps = seq_len // BLOCK
    f32 = jnp.float32
    low = jnp.bfloat16

    loads = []

    def load(src, dst):
        copy = pltpu.make_async_copy(src, dst, load_sem.at[len(loads)])
        copy.start()
        loads.append(copy)

    load(dn_hbm, dn)
    load(middle_hbm, middle)
    load(cot_hbm, cot)
    load(proj_hbm, proj)
    load(own_hbm, own)
    load(qkv_hbm, qkv)
    load(norm_hbm, norm)
    load(qkv_low_hbm, qkv_low)
    height = padded // data_count
    mine = pl.ds(pl.multiple_of(me * height, height), height)
    load(ff_hbm, spread_hbm.at[:, mine])

    ways = orders(data_count)
    stages = len(ways[0])
    parts = ff_parts(spread_hbm.shape[2])
    span = data_count - 1
    flies = [Butterfly(ways[way], k * span) for k, (_, _, _, way) in enumerate(parts)]
    views = [row_pieces(spread_hbm.at[i], data_count, at, wide) for i, at, wide, _ in parts]
    others = [(place + k) % count for k in range(1, count)]
    greet([flies[0].partner(s) for s in range(1, stages)] + [(me, other) for other in others])
    sent = []

    def start(copies):
        for copy in copies:
            copy.start()
        sent.extend(copies)
        return copies

    flights = [
        start(
            fly.double(
                stages - 1, view, (up_send, up_recv), ff_hbm.at[i, :, pl.ds(at, wide)]
            )
        )
        for fly, view, (i, at, wide, _) in zip(flies, views, parts)
    ]

    table = turn_order(count)

    def fetch(t):
        per = block_len // BLOCK
        block = look_up(table, place, t // per) * per + t % per
        rows = pl.ds(pl.multiple_of(block * BLOCK, BLOCK), BLOCK)
        return block, pltpu.make_async_copy(
            probs_hbm.at[:, rows], probs.at[t % 2], probs_sem.at[t % 2]
        )

    fetch(0)[1].start()
    diag[...] = jnp.zeros_like(diag)
    dk[...] = jnp.zeros_like(dk)
    dv[...] = jnp.zeros_like(dv)
    for copy in loads[:3]:
        copy.wait()
    d_middle = cot[...].astype(f32) + norm_back(middle[...], gain_ref[...].reshape(1, width), dn[...])
    middle[...] = d_middle
    save_middle = pltpu.make_async_copy(middle, d_middle_hbm, load_sem.at[0])
    save_middle.start()
    cot[...] = d_middle.astype(low)
    loads[3].wait()
    d_all = product(cot[...], proj[:width]).astype(low)

    def own_rows(who):
        return pl.ds(pl.multiple_of(who * block_len, block_len), block_len)

    for k in range(count):
        d_own[k] = d_all[:, k * lanes : (k + 1) * lanes]
    start(
        [
            pltpu.make_async_remote_copy(
                src_ref=d_own.at[other],
                dst_ref=grad.at[own_rows(place)],
                send_sem=cross_send.at[k],
                recv_sem=cross_recv.at[place],
                device_id=(me, other),
                device_id_type=pl.DeviceIdType.MESH,
            )
            for k, other in enumerate(others)
        ]
    )
    grad[own_rows(place)] = d_own[place]
    loads[4].wait()
    d_out_w[width:] = jnp.zeros((padded - width, count * lanes), low)
    d_out_w[:width] = left_inner(cot[...], own[...]).astype(low)
    save_out = pltpu.make_async_copy(d_out_w, d_out_w_hbm, load_sem.at[1])
    save_out.start()
    loads[5].wait()

    def pass_on(s):
        for k, (fly, view) in enumerate(zip(flies, views)):
            for copy in flights[k]:
                copy.wait_recv()
            flights[k] = []
            if s > 1 and s - 1 >= stages_left(parts[k], stages):
                flights[k] = start(fly.double(s - 1, view, (up_send, up_recv)))

    def back_block(t, carry):
        per = block_len // BLOCK

        @pl.when((t > 0) & (t % per == 0))
        def _():
            who = look_up(table, place, t // per)
            pltpu.make_async_remote_copy(
                src_ref=d_own.at[0],
                dst_ref=grad.at[own_rows(who)],
                send_sem=cross_send.at[0],
                recv_sem=cross_recv.at[who],
                device_id=(me, who),
                device_id_type=pl.DeviceIdType.MESH,
            ).wait_recv()

        @pl.when(t + 1 < steps)
        def _():
            fetch(t + 1)[1].start()

        block, arrival = fetch(t)
        arrival.wait()
        rows = pl.ds(pl.multiple_of(block * BLOCK, BLOCK), BLOCK)
        window = pl.ds(pl.multiple_of((steps - 1 - block) * BLOCK, BLOCK), seq_len)
        queries = qkv[rows, 0:lanes]
        keys = qkv[:, lanes : 2 * lanes]
        values = qkv[:, 2 * lanes : 3 * lanes]
        d_query = jnp.zeros((BLOCK, lanes), f32)
        for slot in range(slots):
            weight = probs[t % 2, slot]
            slot_grad = slot_lanes(grad[rows], slot)
            d_probs = right_inner(slot_grad, values)
            delta = jnp.sum(weight * d_probs, axis=-1, keepdims=True)
            d_scores = (weight * (d_probs - delta)).astype(low)
            d_query = d_query + slot_lanes(product(d_scores, keys), slot)
            dk[...] += left_inner(slot_lanes(queries, slot), d_scores)
            dv[...] += left_inner(slot_grad, weight.astype(low))
            diag[slot, :, window] += d_scores.astype(f32)
        d_qkv[rows, 0:lanes] = d_query.astype(low)
        return carry

    loads[8].wait()
    pass_on(stages - 1)
    lax.fori_loop(0, steps, back_block, 0)
    for s in reversed(range(2, stages - 1)):
        pass_on(s)
    d_qkv[:, lanes : 2 * lanes] = dk[...].T.astype(low)
    d_qkv[:, 2 * lanes : 3 * lanes] = dv[...].T.astype(low)
    for copy in loads[6:8]:
        copy.wait()
    terms[...] = right_inner(d_qkv[...], qkv_low[:width]).astype(low)
    save_terms = pltpu.make_async_copy(terms, terms_hbm, load_sem.at[2])
    save_terms.start()
    d_qkv_w[:width] = left_inner(norm[...], d_qkv[...]).astype(low)
    d_qkv_w[width:] = jnp.zeros((padded - width, 3 * lanes), low)
    sums = []
    for slot in range(slots):
        level = diag[slot]
        rest = BLOCK // 2
        while rest >= 1:
            level = pltpu.roll(level[:rest], rest, 1) + level[rest:]
            rest //= 2
        sums.append(level)
    sums = jnp.concatenate(sums + [jnp.zeros((128 - slots, 2 * seq_len), f32)], axis=0)
    d_rel = lax.dot_general(
        onehot_rows(bucket_ref, line),
        sums,
        (((1,), (1,)), ((), ())),
        precision=highest,
        preferred_element_type=f32,
    )
    d_qkv_w[width : width + BUCKETS, :128] = d_rel.astype(low)
    save_qkv = pltpu.make_async_copy(d_qkv_w, d_qkv_w_hbm, load_sem.at[3])
    save_qkv.start()
    if stages > 1:
        pass_on(1)
    for copy in sent:
        copy.wait_send()
    for copy in (save_middle, save_out, save_terms, save_qkv):
        copy.wait()


def attend_back(dn, middle, cot, gain, proj_all, own, qkv, probs, norm, qkv_low, bucket, ff_pieces):
    count = lax.axis_size("mp")
    data_count = lax.axis_size("dp")
    seq_len = qkv.shape[0]
    slots = probs.shape[0]
    lanes = slots * HD
    block_len, width = dn.shape
    padded = qkv_low.shape[0]
    _, _, units = ff_pieces.shape
    far = pl.BlockSpec(memory_space=pltpu.HBM)
    near = pl.BlockSpec(memory_space=pltpu.VMEM)
    dma = pltpu.SemaphoreType.DMA
    low, f32 = jnp.bfloat16, jnp.float32
    span = data_count - 1
    scratch = [
        (dn.shape, f32),
        (middle.shape, f32),
        (cot.shape, low),
        (proj_all.shape, low),
        (own.shape, low),
        (qkv.shape, low),
        ((2, slots, BLOCK, seq_len), f32),
        (norm.shape, low),
        (qkv_low.shape, low),
        ((count, block_len, lanes), low),
        ((seq_len, lanes), low),
        ((slots, BLOCK, 2 * seq_len), f32),
        ((lanes, seq_len), f32),
        ((lanes, seq_len), f32),
        (qkv.shape, low),
        ((seq_len, width), low),
        ((padded, 3 * lanes), low),
        ((padded, count * lanes), low),
    ]
    return pl.pallas_call(
        functools.partial(attend_back_kernel, data_count, count, slots),
        in_specs=[far] * 3 + [near] + [far] * 6 + [near, far],
        out_specs=[far] * 5,
        out_shape=[
            jax.ShapeDtypeStruct((block_len, width), f32),
            jax.ShapeDtypeStruct((seq_len, width), low),
            jax.ShapeDtypeStruct((padded, 3 * lanes), low),
            jax.ShapeDtypeStruct((padded, count * lanes), low),
            jax.ShapeDtypeStruct((3, padded, units), low),
        ],
        scratch_shapes=[pltpu.VMEM(shape, dtype) for shape, dtype in scratch]
        + [
            pltpu.VMEM((1, 2 * seq_len), jnp.int32),
            dma((10,)),
            dma((2,)),
            dma((count - 1,)),
            dma((count,)),
            dma((4 * span,)),
            dma((4 * span,)),
        ],
        compiler_params=pltpu.CompilerParams(
            collective_id=3, has_side_effects=True, vmem_limit_bytes=56 << 20
        ),
        cost_estimate=pl.CostEstimate(
            flops=16 * slots * seq_len * seq_len * HD, bytes_accessed=140 << 20, transcendentals=0
        ),
        name="attend_back",
    )(dn, middle, cot, gain, proj_all, own, qkv, probs, norm, qkv_low, bucket, ff_pieces)


def onehot_rows(bucket_ref, line_ref):
    offsets = bucket_ref.shape[0]
    line_ref[...] = jnp.full(line_ref.shape, -1, jnp.int32)
    line_ref[:, :offsets] = bucket_ref[...].reshape(1, offsets)
    rows = lax.broadcasted_iota(jnp.int32, (BUCKETS, line_ref.shape[1]), 0)
    return jnp.where(rows == line_ref[...], 1.0, 0.0)


def front_kernel(
    data_count,
    count,
    slots,
    x_hbm,
    cot_hbm,
    query_hbm,
    key_hbm,
    value_hbm,
    out_hbm,
    gate_hbm,
    up_hbm,
    down_hbm,
    segments_ref,
    bucket_ref,
    rel_ref,
    attn_gain_ref,
    ff_gain_ref,
    norm_far,
    cot_far,
    own_cot_far,
    qkv_far,
    probs_far,
    own_far,
    middle_far,
    normed_far,
    proj_far,
    qkv_low_far,
    gate_up_far,
    down_far,
    squares_ref,
    x_in,
    cot_in,
    x,
    norm,
    cot,
    thin,
    wide,
    gate_low,
    up_low,
    down_low,
    blank,
    proj,
    qkv_low,
    qkv,
    tilt,
    seg_col,
    probs,
    mixed,
    own,
    normed,
    line,
    load_sem,
    save_sem,
    probs_sem,
    norm_send,
    norm_recv,
    cot_send,
    cot_recv,
    cross_send,
    cross_recv,
    side_send,
    side_recv,
    mix_send,
    mix_recv,
    cot_save,
):
    place = lax.axis_index("mp")
    me = lax.axis_index("dp")
    last = count - 1
    f32, low = jnp.float32, jnp.bfloat16
    block_len, width = x.shape
    seq_len = count * block_len
    lanes = slots * HD
    padded = proj.shape[0]
    height = padded // data_count
    units = gate_low.shape[1]
    mesh_id = pl.DeviceIdType.MESH
    others = [(place + k) % count for k in range(1, count)]
    peers = [(me + k) % data_count for k in range(1, data_count)]

    def load(k, from_ref, to_ref):
        copy = pltpu.make_async_copy(from_ref, to_ref, load_sem.at[k])
        copy.start()
        return copy

    load_x = load(0, x_hbm, x_in)
    load_thin = [
        load(1 + k, ref, thin.at[k])
        for k, ref in enumerate((out_hbm, query_hbm, key_hbm, value_hbm))
    ]
    load_cot = load(5, cot_hbm, cot_in)
    load_gate = load(6, gate_hbm, wide.at[0])
    load_up = load(7, up_hbm, wide.at[1])
    greet([(me, other) for other in others] + [(peer, place) for peer in peers])

    saves = []

    def save(from_ref, to_ref):
        copy = pltpu.make_async_copy(from_ref, to_ref, save_sem.at[len(saves)])
        copy.start()
        saves.append(copy)

    sent = []

    def start(copy):
        copy.start()
        sent.append(copy)

    def pass_block(buffer, sems, block, side, slot):
        return pltpu.make_async_remote_copy(
            src_ref=buffer.at[block],
            dst_ref=buffer.at[block],
            send_sem=sems[0].at[slot],
            recv_sem=sems[1].at[block],
            device_id=(me, place + side),
            device_id_type=mesh_id,
        )

    def inside(block):
        return (block >= 0) & (block <= last)

    norm_sems = (norm_send, norm_recv)
    cot_sems = (cot_send, cot_recv)

    def store_cot(block):
        return pltpu.make_async_copy(cot.at[block], cot_far.at[block], cot_save.at[block])

    def take(buffer, sems, distance):
        for side in (1, -1):
            other = place + side * distance

            @pl.when(inside(other))
            def _():
                pass_block(buffer, sems, other, side, other).wait_recv()

                @pl.when(inside(place - side))
                def _():
                    pass_block(buffer, sems, other, -side, other).start()

                if buffer is cot:
                    store_cot(other).start()

    def send_own(buffer, sems, side):
        return pass_block(buffer, sems, place, side, count + (side + 1) // 2)

    def cot_may_go(distance):
        for side in (1, -1):
            behind = place if side == 1 else last - place

            @pl.when((behind == distance) & inside(place + side))
            def _():
                if distance == 0:
                    send_own(norm, norm_sems, side).wait_send()
                else:
                    far_end = 0 if side == 1 else last
                    pass_block(norm, norm_sems, far_end, side, far_end).wait_send()
                send_own(cot, cot_sems, side).start()

    between = inside(place - 1) & inside(place + 1)

    load_x.wait()
    x[...] = x_in[...].T.astype(f32)
    norm[place] = rms_norm(x[...], attn_gain_ref[...].reshape(1, width)).astype(low)
    for side in (1, -1):

        @pl.when(inside(place + side))
        def _():
            send_own(norm, norm_sems, side).start()

    load_cot.wait()
    cot[place] = cot_in[...].T
    save(cot.at[place], own_cot_far)
    store_cot(place).start()

    lane = lax.broadcasted_iota(jnp.int32, (1, lanes), 1)
    slot_of = place * slots + lane // HD
    lane_mask = jnp.where((slot_of < 5) | (slot_of == 6), 1.0, 0.0)
    for copy in load_thin:
        copy.wait()

    def lanes_of(who):
        return pl.ds(pl.multiple_of(who * lanes, lanes), lanes)

    def rows_of(who):
        return pl.ds(pl.multiple_of(who * height, height), height)

    proj[width:, lanes_of(place)] = jnp.zeros((padded - width, lanes), low)
    qkv_low[width:] = jnp.zeros((padded - width, 3 * lanes), low)
    blank[...] = jnp.zeros_like(blank)
    column = lax.broadcasted_iota(jnp.int32, (1, 128), 1)
    squares = jnp.zeros((1, 128), f32)

    def square_of(values, at):
        return jnp.where(column == at, total(total(values * values, 1), 0), 0.0)

    masked = (thin[0] * lane_mask).astype(low)
    proj[:width, lanes_of(place)] = masked

    def proj_copy(src, dst, sems, send_slot, recv_slot, device):
        return pltpu.make_async_remote_copy(
            src_ref=src,
            dst_ref=dst,
            send_sem=sems[0].at[send_slot],
            recv_sem=sems[1].at[recv_slot],
            device_id=device,
            device_id_type=mesh_id,
        )

    cross, aside = (cross_send, cross_recv), (side_send, side_recv)
    for k, other in enumerate(others):
        view = proj.at[rows_of(me), lanes_of(place)]
        start(proj_copy(view, view, cross, k, count - 2 - k, (me, other)))
    for k in range(3):
        qkv_low[:width, k * lanes : (k + 1) * lanes] = (thin[1 + k] * lane_mask).astype(low)
        squares = squares + square_of(thin[1 + k], k)
    squares = squares + square_of(thin[0], 6) + square_of(rel_ref[...], 3)
    save(qkv_low, qkv_low_far)

    onehot = onehot_rows(bucket_ref, line)
    vector = lax.dot_general(
        rel_ref[...],
        onehot,
        (((1,), (0,)), ((), ())),
        precision=highest,
        preferred_element_type=f32,
    )
    for slot in range(slots):
        spread = jnp.broadcast_to(vector[slot : slot + 1, :], (BLOCK, 2 * seq_len))
        tilt[slot] = pltpu.roll(spread, 2 * seq_len - BLOCK + 1, 1, stride=1, stride_axis=0)
    seg_row = segments_ref[...].astype(f32)
    seg_col[...] = jnp.broadcast_to(seg_row, (128, seq_len)).T

    arrivals = []
    for k, other in enumerate(others):
        view = proj.at[rows_of(me), lanes_of(other)]
        proj_copy(view, view, cross, k, k, (me, other)).wait_recv()
        at = k * (data_count - 1)
        for j, peer in enumerate(peers):
            start(proj_copy(view, view, aside, at + j, at + data_count - 2 - j, (peer, place)))
            come = proj.at[rows_of(peer), lanes_of(other)]
            arrivals.append(proj_copy(come, come, aside, at + j, at + j, (peer, place)))

    def own_rows(who):
        return pl.ds(pl.multiple_of(who * block_len, block_len), block_len)

    def project(block):
        qkv[own_rows(block)] = product(norm[block], qkv_low[:width]).astype(low)

    def project_at(distance):
        for side in (1, -1):
            other = place + side * distance

            @pl.when(inside(other))
            def _():
                project(other)

    project(place)
    take(norm, norm_sems, 1)
    cot_may_go(0)
    project_at(1)
    load_gate.wait()
    gate_low[...] = wide[0].astype(low)
    squares = squares + square_of(wide[0], 4)
    load_down = load(6, down_hbm, wide.at[0])
    rows_used = pl.ds(0, width)
    save(gate_low, gate_up_far.at[rows_used, pl.ds(0, units)])
    load_up.wait()
    up_low[...] = wide[1].astype(low)
    squares = squares + square_of(wide[1], 5)
    save(up_low, gate_up_far.at[rows_used, pl.ds(units, units)])
    save(blank, gate_up_far.at[pl.ds(width, padded - width)])
    for distance in range(2, count):
        take(norm, norm_sems, distance)
        cot_may_go(distance - 1)
        project_at(distance)
        if distance == 2:
            load_down.wait()
            down_low[...] = wide[0].astype(low)
            squares = squares + square_of(wide[0], 7)
            save(down_low, down_far)
            squares_ref[...] = squares
    save(qkv, qkv_far)
    save(norm, norm_far)

    @pl.when(between)
    def _():
        take(cot, cot_sems, 1)

    steps = seq_len // BLOCK
    per = block_len // BLOCK
    table = [order[::-1] for order in turn_order(count)]

    def store_probs(t, block):
        rows = pl.ds(pl.multiple_of(block * BLOCK, BLOCK), BLOCK)
        return pltpu.make_async_copy(probs.at[t % 2], probs_far.at[:, rows], probs_sem.at[t % 2])

    def mix_copy(owner):
        return pltpu.make_async_remote_copy(
            src_ref=mixed.at[own_rows(owner)],
            dst_ref=own.at[:, lanes_of(place)],
            send_sem=mix_send.at[owner],
            recv_sem=mix_recv.at[place],
            device_id=(me, owner),
            device_id_type=mesh_id,
        )

    def attend_block(t, carry):
        owner = look_up(table, place, t // per)
        block = owner * per + t % per
        rows = pl.ds(pl.multiple_of(block * BLOCK, BLOCK), BLOCK)
        window = pl.ds(pl.multiple_of((steps - 1 - block) * BLOCK, BLOCK), seq_len)
        same_doc = seg_col[rows, 0:1] == seg_row
        queries = qkv[rows, 0:lanes]
        keys = qkv[:, lanes : 2 * lanes]
        values = qkv[:, 2 * lanes : 3 * lanes]
        result = jnp.zeros((BLOCK, lanes), f32)

        @pl.when(t >= 2)
        def _():
            store_probs(t, block).wait()

        for slot in range(slots):
            scores = right_inner(slot_lanes(queries, slot), keys) + tilt[slot, :, window]
            scores = jnp.where(same_doc, scores, -1e30)
            peak = jnp.max(scores, axis=-1, keepdims=True)
            raised = jnp.exp(scores - peak)
            weight = raised * (1.0 / jnp.sum(raised, axis=-1, keepdims=True))
            probs[t % 2, slot] = weight
            result = result + slot_lanes(product(weight.astype(low), values), slot)
        store_probs(t, block).start()
        mixed[rows] = result.astype(low)

        @pl.when((t % per == per - 1) & (owner != place))
        def _():
            mix_copy(owner).start()

        return carry

    lax.fori_loop(0, steps, attend_block, 0)
    own[:, lanes_of(place)] = mixed[own_rows(place)]

    @pl.when(between)
    def _():
        for distance in range(2, count):
            take(cot, cot_sems, distance)

    for arrival in arrivals:
        arrival.wait_recv()
    save(proj, proj_far)
    for k, other in enumerate(others):
        pltpu.make_async_remote_copy(
            src_ref=mixed.at[own_rows(other)],
            dst_ref=own.at[:, lanes_of(other)],
            send_sem=mix_send.at[other],
            recv_sem=mix_recv.at[other],
            device_id=(me, other),
            device_id_type=mesh_id,
        ).wait_recv()
    save(own, own_far)
    x[...] = x[...] + right_inner(own[...], proj[:width])
    save(x, middle_far)
    normed[...] = rms_norm(x[...], ff_gain_ref[...].reshape(1, width)).astype(low)
    save(normed, normed_far)

    @pl.when(jnp.logical_not(between))
    def _():
        for distance in range(1, count):
            take(cot, cot_sems, distance)

    for block in range(count):
        store_cot(block).wait()
    for t in (0, 1):
        store_probs(t, 0).wait()
    for copy in saves:
        copy.wait()
    for copy in sent:
        copy.wait_send()
    for k, other in enumerate(others):
        mix_copy(other).wait_send()
    for buffer, sems in ((norm, norm_sems), (cot, cot_sems)):
        for side in (1, -1):
            behind = place if side == 1 else last - place
            unwaited = behind > 0 if buffer is norm else behind >= 0

            @pl.when(unwaited & inside(place + side))
            def _():
                send_own(buffer, sems, side).wait_send()

        for block in range(1, last) if buffer is norm else range(count):

            @pl.when((block != place) & between)
            def _():
                pass_block(buffer, sems, block, 1, block).wait_send()


def front(x, cot, weights, segments, bucket, rel_bias, attn_gain, ff_gain):
    count = lax.axis_size("mp")
    data_count = lax.axis_size("dp")
    query, key, value, out, gate, up, down = weights
    width, block_len = x.shape
    lanes = query.shape[1]
    slots = lanes // HD
    units = gate.shape[1]
    seq_len = count * block_len
    piece = 16 * data_count
    padded = (width + piece - 1) // piece * piece
    low, f32 = jnp.bfloat16, jnp.float32
    far = pl.BlockSpec(memory_space=pltpu.HBM)
    near = pl.BlockSpec(memory_space=pltpu.VMEM)
    dma = pltpu.SemaphoreType.DMA
    outs = [
        ((count, block_len, width), low),
        ((count, block_len, width), low),
        ((block_len, width), low),
        ((seq_len, 3 * lanes), low),
        ((slots, seq_len, seq_len), f32),
        ((block_len, count * lanes), low),
        ((block_len, width), f32),
        ((block_len, width), low),
        ((padded, count * lanes), low),
        ((padded, 3 * lanes), low),
        ((padded, 2 * units), low),
        ((width, units), low),
        ((1, 128), f32),
    ]
    scratch = [
        ((width, block_len), low),
        ((width, block_len), low),
        ((block_len, width), f32),
        ((count, block_len, width), low),
        ((count, block_len, width), low),
        ((4, width, lanes), f32),
        ((2, width, units), f32),
        ((width, units), low),
        ((width, units), low),
        ((width, units), low),
        ((padded - width, 2 * units), low),
        ((padded, count * lanes), low),
        ((padded, 3 * lanes), low),
        ((seq_len, 3 * lanes), low),
        ((slots, BLOCK, 2 * seq_len), f32),
        ((seq_len, 128), f32),
        ((2, slots, BLOCK, seq_len), f32),
        ((seq_len, lanes), low),
        ((block_len, count * lanes), low),
        ((block_len, width), low),
    ]
    sides = (count - 1) * (data_count - 1)
    return pl.pallas_call(
        functools.partial(front_kernel, data_count, count, slots),
        in_specs=[far] * 9 + [near] * 5,
        out_specs=[far] * 12 + [near],
        out_shape=[jax.ShapeDtypeStruct(shape, dtype) for shape, dtype in outs],
        scratch_shapes=[pltpu.VMEM(shape, dtype) for shape, dtype in scratch]
        + [
            pltpu.VMEM((1, 2 * seq_len), jnp.int32),
            dma((8,)),
            dma((16,)),
            dma((2,)),
            dma((count + 2,)),
            dma((count,)),
            dma((count + 2,)),
            dma((count,)),
            dma((count - 1,)),
            dma((count - 1,)),
            dma((sides,)),
            dma((sides,)),
            dma((count,)),
            dma((count,)),
            dma((count,)),
        ],
        compiler_params=pltpu.CompilerParams(
            collective_id=0, has_side_effects=True, vmem_limit_bytes=60 << 20
        ),
        cost_estimate=pl.CostEstimate(
            flops=8 * slots * seq_len * seq_len * HD,
            bytes_accessed=300 << 20,
            transcendentals=slots * seq_len * seq_len,
        ),
        name="front",
    )(
        x, cot, query, key, value, out, gate, up, down,
        segments, bucket, rel_bias, attn_gain, ff_gain,
    )


def local(
    layer_in,
    segment_ids,
    bucket_table,
    attn_gain,
    query_weight,
    key_weight,
    value_weight,
    out_weight,
    rel_bias,
    ff_gain,
    gate_weight,
    up_weight,
    down_weight,
    cotangent,
):
    model_width = layer_in.shape[2]
    slots_here = rel_bias.shape[1]
    layer_in = layer_in[0]
    down_turned = down_weight.T
    out_turned = out_weight.T
    rel_turned = rel_bias.T
    (
        flat_norm,
        flat_cot,
        own_cot,
        qkv,
        probs,
        own_attended,
        middle,
        normed_ff_local,
        proj_all,
        qkv_low,
        gate_up_low,
        down_low,
        squares,
    ) = front(
        layer_in.T,
        cotangent[0].T,
        (query_weight, key_weight, value_weight, out_turned, gate_weight, up_weight, down_turned),
        segment_ids,
        bucket_table,
        rel_turned,
        attn_gain,
        ff_gain,
    )
    flat_norm = flat_norm.reshape(-1, model_width)
    out_terms, dn_ff, ff_pieces = feed_forward(normed_ff_local, flat_cot, gate_up_low, down_low)
    d_middle, dn_attn_terms, d_qkv_w, d_out_w, ff_grads = attend_back(
        dn_ff,
        middle,
        own_cot,
        ff_gain,
        proj_all,
        own_attended,
        qkv,
        probs,
        flat_norm,
        qkv_low,
        bucket_table,
        ff_pieces,
    )
    ff_branch = lax.psum_scatter(out_terms, "mp", scatter_dimension=0, tiled=True)
    dn_attn = lax.psum_scatter(dn_attn_terms, "mp", scatter_dimension=0, tiled=True)
    weights = (
        gate_weight,
        up_weight,
        down_turned,
        query_weight,
        key_weight,
        value_weight,
        out_turned,
    )
    *held, shared, own, tall = sum_weights(
        ff_grads, d_qkv_w, d_out_w, qkv_low, gate_up_low, squares, weights, model_width
    )
    results = update(held[:5], held[5:], rel_turned, attn_gain, ff_gain, shared, own, tall)
    news, along, across = results[:8], results[8:16], results[16:24]
    new_attn_gain, attn_gain_moment, new_ff_gain, ff_gain_moment = results[24:]
    gate, up, down, query, key, value, out, rel = zip(news, along, across)
    rel = (rel[0].T, rel[1], rel[2].reshape(slots_here))
    down = (down[0].T, down[2], down[1])
    out = (out[0].T, out[2], out[1])
    ff_gain_moment, ff_branch = lax.optimization_barrier((ff_gain_moment, ff_branch))
    layer_out = finish(finish_out_kernel, "finish_out", (middle, ff_branch), (), ())
    input_grad = finish(
        finish_grad_kernel, "finish_grad", (d_middle, dn_attn), (layer_in.T,), (attn_gain,)
    )
    return (
        layer_out.T[None],
        input_grad.T[None],
        new_attn_gain,
        attn_gain_moment,
        *query,
        *key,
        *value,
        *out,
        *rel,
        new_ff_gain,
        ff_gain_moment,
        *gate,
        *up,
        *down,
    )


def solution(mesh):
    return jax.shard_map(
        local,
        mesh=mesh,
        in_specs=(
            P("dp", "mp", None),
            P("dp", None),
            P(),
            P(),
            P(None, "mp"),
            P(None, "mp"),
            P(None, "mp"),
            P("mp", None),
            P(None, "mp"),
            P(),
            P(None, "mp"),
            P(None, "mp"),
            P("mp", None),
            P("dp", "mp", None),
        ),
        out_specs=(
            P("dp", "mp", None),
            P("dp", "mp", None),
            P(),
            P(),
            P(None, "mp"),
            P(),
            P("mp"),
            P(None, "mp"),
            P(),
            P("mp"),
            P(None, "mp"),
            P(),
            P("mp"),
            P("mp", None),
            P("mp"),
            P(),
            P(None, "mp"),
            P(),
            P("mp"),
            P(),
            P(),
            P(None, "mp"),
            P(),
            P("mp"),
            P(None, "mp"),
            P(),
            P("mp"),
            P("mp", None),
            P("mp"),
            P(),
        ),
        check_vma=False,
    )
```
